32 devices in a mesh: slab: 8 (over y, x, core), comp: 4 (over z).
Axes of the slice: x: 2, y: 2, z: 4, core: 2. Of those that a mesh axis runs over, the one named last changes fastest.
Arguments:
- current_field: float32 [3, 64, 64, 256], P(None, 'slab', 'comp'), may hold values from -6 to 6
- earlier_field: float32 [3, 64, 64, 256], P(None, 'slab', 'comp'), may hold values from -6 to 6
- wave_coef: float32 [64, 64, 256], P('slab', 'comp'), may hold values from 0.05 to 0.24
- layer_mask: int32 [64, 64, 256], P('slab', 'comp'), may hold values from 0 to 2
- point_xyz: float32 [3, 32768], P(None, ('slab', 'comp')), may hold values from 0 to 4
- point_owner: int32 [32768, 1], P(('slab', 'comp')), may hold values from 0 to 31; in each aligned block of 1024 rows (0 to 1023, 1024 to 2047, ...) at most 64 rows name the same one
- cell_offset: int32 [32768], P(('slab', 'comp')), may hold values from 0 to 32767
- wave_vector: float32 [3, 4096], P(None, 'comp'), may hold values from -8 to 8
- frequency: float32 [4096], P('comp'), may hold values from 0.5 to 8
- amplitude: float32 [3, 4096], P(None, 'comp'), may hold values from -0.09375 to 0.09375
- phase_index: int32 [4096], P('comp'), may hold values from 0 to 255
- phase_table: float32 [256], replicated, may hold values from -3.140625 to 3.140625
Outputs:
- final_field: float32 [3, 64, 64, 256], P(None, 'slab', 'comp')
- prior_field: float32 [3, 64, 64, 256], P(None, 'slab', 'comp')
The draws below stay inside these ranges and needn't reach their ends.
Inputs may be any that keep to these rules, and one draw needn't show every extreme that they name: `point_owner`: the device at position s of slab and c of comp is numbered s times the size of comp plus c. Among the rows of one device at most 64 points name one owner.
All inputs are finite; a program needn't handle non-finite values.
Results may differ from the reference program's by a relative error of at most 0.0003.
Values sent between devices are 32-bit elements; how exact they have to be, the bound alone decides.
No kernel may reach another device: no remote copies, remote signals or barrier semaphores. Data moves between devices by JAX's collectives and lax.ppermute only.
A program may use at most 192 MiB of HBM per device.

```python
import math
import jax
import jax.numpy as jnp
import numpy as np
from jax import lax

CX = 8
CY = 16
NZ = 256
PT_DEV = 1024
K = 4096
NPH = 256
STEPS = 3
CAP = 64
NX = 64
NY = 64
POINTS = 32768
N_COMP = 4
DEVICES = 32


def set_ends(values, stream_key, low, top_value):
    longest = values.shape.index(max(values.shape))
    spots = []
    for shift in (0, 1):
        where = [jax.random.randint(jax.random.fold_in(stream_key, axis), (), 0, length) for axis, length in enumerate(values.shape)]
        where[longest] = (where[longest] + shift) % values.shape[longest]
        spots.append(tuple(where))
    return values.at[spots[0]].set(low).at[spots[1]].set(top_value)


def block_levels(own_key, shape, cuts, smallest, largest):
    level, own = 1.0, jax.random.fold_in(own_key, 6)
    for axis_at, shards_of in cuts:
        draws = jnp.exp(jax.random.uniform(jax.random.fold_in(own, axis_at), (shards_of,), jnp.float32, smallest / len(cuts), largest / len(cuts)))
        level = level * jnp.repeat(draws, shape[axis_at] // shards_of).reshape([-1 if axis == axis_at else 1 for axis in range(len(shape))])
    return level


def routed_block(rng, own, number, rows, amount, top, most, lean):
    ranking = jax.random.permutation(rng, amount)
    heavy_load, ordinary = shares(amount, rows * top, most, lean, True), shares(amount, rows * top, most, lean, False)
    places = jnp.arange(amount)

    def named(tallies, turn):
        used = int((tallies > 0).sum())
        fixed = max(1, used // 4)
        moved = fixed + (places - fixed + turn * (used - fixed)) % max(1, amount - fixed)
        return jnp.zeros((amount,), jnp.int32).at[ranking[jnp.where(places < fixed, places, moved)]].set(jnp.asarray(tallies, jnp.int32))

    tallies = jnp.where(number % 4 == 0, named(heavy_load, number // 4), named(ordinary, number - number // 4 - 1))
    mixed = jax.random.permutation(jax.random.fold_in(own, 3), amount)
    donor, sink = mixed[0:amount // 2 * 2:2], mixed[1:amount // 2 * 2:2]
    margin = jnp.minimum(tallies[donor] - 1, most - tallies[sink]) // 2
    margin = jnp.where((donor == ranking[0]) | (sink == ranking[0]) | (tallies[sink] == 0), 0, jnp.maximum(margin, 0))
    moved = jax.random.randint(jax.random.fold_in(own, 4), (amount // 2,), 0, 1 << 20) % (margin + 1)
    tallies = tallies.at[donor].add(-moved).at[sink].add(moved)
    items = jnp.searchsorted(jnp.cumsum(tallies), jnp.arange(rows * top), side="right").astype(jnp.int32)
    listing = items.reshape(top, rows).T
    listing = listing[jax.random.permutation(jax.random.fold_in(own, 1), rows)]
    turn = jax.random.randint(jax.random.fold_in(own, 2), (rows, 1), 0, top)
    return jnp.take_along_axis(listing, (jnp.arange(top)[None, :] + turn) % top, axis=1)


def shares(amount, total, most, slope, full):
    loads = [(1 << 20) // math.isqrt(standing ** slope) + 1 for standing in range(1, amount + 1)]
    largest = most if full else min(most, max(-(-total // amount), total * loads[0] // sum(loads)))
    least = 1 if total - largest >= amount - 1 else 0
    given, rest = [largest] + [least] * (amount - 1), total - largest - least * (amount - 1)
    while rest > 0:
        movable = [i for i in range(1, amount) if given[i] < largest] or [i for i in range(1, amount) if given[i] < most]
        mass, left = sum([loads[i] for i in movable]), rest
        for i in movable:
            addition = min(most - given[i], max(1, left * loads[i] // mass), rest)
            given[i] = given[i] + addition
            rest = rest - addition
    return np.array(given)


def noise(own_key, shape, width, limit, split=(), dtype=jnp.bfloat16):
    loudness = block_levels(own_key, shape, split, -0.22, 0.18) if split else 1.0
    values = jax.random.normal(own_key, shape, jnp.float32) * width * loudness
    return jnp.minimum(jnp.maximum(values, -limit), limit).astype(dtype)


def setup_inputs(seed: int = 0) -> dict:
    seeds = jax.random.split(jax.random.key(seed), 13)
    current_field = noise(seeds[0], (3, NX, NY, NZ), 1.0, 6.0, ((1, 8), (2, 4)), jnp.float32)
    earlier_field = noise(seeds[1], (3, NX, NY, NZ), 1.0, 6.0, ((1, 8), (2, 4)), jnp.float32)
    wave_coef = jnp.clip(jnp.exp(math.log(0.24) - 1.5686159 * jax.random.uniform(seeds[2], (NX, NY, NZ), jnp.float32) ** block_levels(seeds[2], (NX, NY, NZ), ((0, 8), (1, 4)), -0.2, 0.2)), 0.05, 0.24)
    layer_mask = set_ends(jax.random.randint(seeds[3], (NX, NY, NZ), 0, 3), jax.random.fold_in(seeds[3], 1), 0, 2).astype(jnp.int32)
    point_xyz = jnp.clip(4.0 * jax.random.uniform(seeds[4], (3, POINTS), jnp.float32) ** block_levels(seeds[4], (3, POINTS), ((1, 32),), -0.2, 0.2), 0.0, 4.0)
    point_owner_keys = jax.random.split(jax.random.fold_in(seeds[5], 1), POINTS // PT_DEV)
    point_owner_turns = jax.random.permutation(jax.random.fold_in(seeds[5], 3), POINTS // PT_DEV)
    point_owner = jax.vmap(lambda own, number: routed_block(jax.random.fold_in(seeds[5], 2), own, number, PT_DEV, DEVICES, 1, CAP, 2))(point_owner_keys, point_owner_turns).reshape((POINTS, 1))
    cell_offset = set_ends(jax.random.randint(seeds[6], (POINTS,), 0, CX * CY * NZ), jax.random.fold_in(seeds[6], 1), 0, (CX * CY * NZ) - 1).astype(jnp.int32)
    wave_vector = jnp.clip(jax.random.uniform(seeds[7], (3, K), jnp.float32, -8.0, 8.0) * block_levels(seeds[7], (3, K), ((1, 4),), -0.4, 0.0), -8.0, 8.0)
    frequency = jnp.clip(jnp.exp(math.log(8.0) - 2.7725887 * jax.random.uniform(seeds[8], (K,), jnp.float32) ** block_levels(seeds[8], (K,), ((0, 4),), -0.2, 0.2)), 0.5, 8.0)
    amplitude = noise(seeds[9], (3, K), K ** -0.5, 0.09375, ((1, 4),), jnp.float32)
    phase_index = set_ends(jax.random.randint(seeds[10], (K,), 0, NPH), jax.random.fold_in(seeds[10], 1), 0, NPH - 1).astype(jnp.int32)
    phase_table = jnp.clip(jax.random.uniform(seeds[11], (NPH,), jnp.float32, -3.140625, 3.140625), -3.140625, 3.140625)
    return {"current_field": current_field, "earlier_field": earlier_field, "wave_coef": wave_coef, "layer_mask": layer_mask, "point_xyz": point_xyz, "point_owner": point_owner, "cell_offset": cell_offset, "wave_vector": wave_vector, "frequency": frequency, "amplitude": amplitude, "phase_index": phase_index, "phase_table": phase_table}


step_size = 0.05
near_weight = 4.0 / 3.0
far_weight = -1.0 / 12.0
centre_weight = -7.5


def shifted(padded, axis_pos, offset):
    result = padded
    for dim_pos in (1, 2, 3):
        first_cell = 2 + offset if dim_pos == axis_pos else 2
        result = lax.slice_in_dim(result, first_cell, first_cell + padded.shape[dim_pos] - 4, axis=dim_pos)
    return result


def laplace_four(padded):
    summed = centre_weight * shifted(padded, 0, 0)
    for axis_pos in (1, 2, 3):
        summed = summed + near_weight * (shifted(padded, axis_pos, 1) + shifted(padded, axis_pos, -1))
        summed = summed + far_weight * (shifted(padded, axis_pos, 2) + shifted(padded, axis_pos, -2))
    return summed


def incident_terms(comp_block, coords):
    angles = comp_block[0][:, None] * coords[0][None, :] + comp_block[1][:, None] * coords[1][None, :] + comp_block[2][:, None] * coords[2][None, :]
    cosine = jnp.cos(angles)
    sine_part = jnp.sin(angles)
    moments = step_size * (jnp.arange(STEPS) + 1).astype(jnp.float32)
    delays = moments[:, None] * comp_block[3][None, :] - comp_block[7][None, :]
    block_width = comp_block.shape[1]
    left_cos = (jnp.cos(delays)[:, None, :] * comp_block[4:7][None, :, :]).reshape(STEPS * 3, block_width)
    left_sin = (jnp.sin(delays)[:, None, :] * comp_block[4:7][None, :, :]).reshape(STEPS * 3, block_width)
    first_part = jnp.dot(left_cos, cosine, precision=lax.Precision.HIGHEST, preferred_element_type=jnp.float32)
    second_part = jnp.dot(left_sin, sine_part, precision=lax.Precision.HIGHEST, preferred_element_type=jnp.float32)
    return first_part + second_part


def reference(current_field, earlier_field, wave_coef, layer_mask, point_xyz, point_owner, cell_offset, wave_vector, frequency, amplitude, phase_index, phase_table):
    phases = phase_table[phase_index]
    comp_block = jnp.concatenate([wave_vector, frequency[None, :], amplitude, phases[None, :]], axis=0)
    groups = jnp.transpose(point_xyz.reshape(3, DEVICES, PT_DEV), (1, 0, 2))
    incident = lax.map(lambda coords: incident_terms(comp_block, coords), groups)
    incident = jnp.transpose(incident, (1, 0, 2)).reshape(STEPS * 3, POINTS)
    owners = point_owner[:, 0]
    slab_pos = owners // N_COMP
    comp_pos = owners % N_COMP
    local_x = cell_offset // (CY * NZ)
    local_y = (cell_offset // NZ) % CY
    local_z = cell_offset % NZ
    flat_cell = (((slab_pos * CX + local_x) * NY + comp_pos * CY + local_y) * NZ + local_z).astype(jnp.int32)
    forcing = jnp.zeros((STEPS * 3, NX * NY * NZ), jnp.float32).at[:, flat_cell].add(incident)
    sign_field = ((layer_mask == 1).astype(jnp.float32) - (layer_mask == 2).astype(jnp.float32))[None]
    current = current_field
    earlier = earlier_field
    for step_index in range(STEPS):
        padded = jnp.pad(current, ((0, 0), (2, 2), (2, 2), (2, 2)))
        source = forcing[3 * step_index:3 * step_index + 3].reshape(3, NX, NY, NZ)
        following = 2.0 * current - earlier + wave_coef[None] * laplace_four(padded) + sign_field * source
        earlier = current
        current = following
    return current, earlier
```

```python
import jax
import jax.numpy as jnp
from jax import lax
from jax.experimental import pallas as pl
from jax.experimental.pallas import tpu as pltpu
from jax.sharding import PartitionSpec as P

STEPS = 3
step_size = 0.05
near_weight = 4.0 / 3.0
far_weight = -1.0 / 12.0
centre_weight = -7.5
inv_two_pi = 0.15915494309189535
round_magic = 12582912.0

SIN_C = (4.4428679, -7.30744342, 3.59478806, -0.78437398)
COS_C = (1.4142135, -6.97885099, 5.73946117, -1.88356299, 0.31069819)

F32 = jnp.float32
BF16 = jnp.bfloat16


def horner(coefs, z):
    out = coefs[-1] * z + coefs[-2]
    for c in coefs[-3::-1]:
        out = out * z + c
    return out


def sincos_turns(u):
    r = u - ((u + round_magic) - round_magic)
    z = r * r
    s = r * horner(SIN_C, z)
    c = horner(COS_C, z)
    return s * c, 1.0 - s * s


def split_three(x):
    hi = x.astype(BF16).astype(F32)
    rest = x - hi
    mid = rest.astype(BF16).astype(F32)
    return hi, mid, rest - mid


def row_ids(shape):
    return lax.broadcasted_iota(jnp.int32, shape, 0)


def incident_kernel(slot_count, owner_count, par_ref, xyz_ref, own_ref, off_ref, out_ref, x8_ref, acc_ref):
    comps = par_ref.shape[1]
    points = xyz_ref.shape[1]
    kc = 256
    tile = 256
    x8_ref[...] = jnp.zeros(x8_ref.shape, F32)
    x8_ref[0:3, :] = xyz_ref[...]
    xhi, xmid, xlo = split_three(x8_ref[...])
    right = jnp.concatenate([xhi, xmid, xlo, xhi, xmid, xhi], axis=0).astype(BF16)
    acc_ref[...] = jnp.zeros(acc_ref.shape, F32)
    rows8 = row_ids((8, kc))
    times = step_size * (rows8 + 1).astype(F32)
    rows16 = row_ids((16, kc))
    comp_row = rows16 % 3

    def body(step, carry):
        blk = par_ref[:, pl.ds(pl.multiple_of(step * kc, kc), kc)]
        kv = jnp.where(rows8 < 3, blk * inv_two_pi, 0.0)
        khi, kmid, klo = split_three(kv)
        left = jnp.concatenate([khi, khi, khi, kmid, kmid, klo], axis=0).astype(BF16)
        delays = times * blk[3:4, :] - blk[7:8, :]
        sd, cd = sincos_turns(delays * inv_two_pi)
        amp = jnp.where(comp_row == 0, blk[4:5, :], jnp.where(comp_row == 1, blk[5:6, :], blk[6:7, :]))
        amp = jnp.where(rows16 < 9, amp, 0.0)

        def rows_of(t):
            w = amp * jnp.where(rows16 < 3, t[0:1, :], jnp.where(rows16 < 6, t[1:2, :], t[2:3, :]))
            hi = w.astype(BF16)
            lo = (w - hi.astype(F32)).astype(BF16)
            return jnp.concatenate([hi, lo], axis=0)

        lc = rows_of(cd)
        ls = rows_of(sd)
        for t in range(points // tile):
            cols = slice(t * tile, (t + 1) * tile)
            u = lax.dot_general(left, right[:, cols], (((0,), (0,)), ((), ())), preferred_element_type=F32)
            highs, lows = [], []
            for j in range(kc // 32):
                for value in sincos_turns(u[32 * j : 32 * j + 32]):
                    high = value.astype(BF16)
                    highs.append(high)
                    lows.append((value - high.astype(F32)).astype(BF16))
            part = jnp.dot(ls, jnp.concatenate(highs[0::2], axis=0), preferred_element_type=F32)
            part += jnp.dot(lc, jnp.concatenate(highs[1::2], axis=0), preferred_element_type=F32)
            part += jnp.dot(ls, jnp.concatenate(lows[0::2], axis=0), preferred_element_type=F32)
            part += jnp.dot(lc, jnp.concatenate(lows[1::2], axis=0), preferred_element_type=F32)
            acc_ref[:, cols] += part
        return carry

    lax.fori_loop(0, comps // kc, body, 0)
    vals = acc_ref[0:16, :] + acc_ref[16:32, :]
    prow = row_ids((16, points))
    vals = jnp.where(prow == 9, off_ref[...].astype(F32), vals)
    v1, v2, v3 = split_three(vals)
    vals3 = jnp.concatenate([v1, v2, v3], axis=0).astype(BF16)
    lanes = -(-owner_count // 128) * 128
    lane = lax.broadcasted_iota(jnp.int32, (points, lanes), 1)
    named = own_ref[...] == lane
    lower = lax.broadcasted_iota(jnp.int32, (points, points), 1) < row_ids((points, points))
    before = jnp.dot(lower.astype(F32).astype(BF16), named.astype(F32).astype(BF16), preferred_element_type=F32)
    slot = jnp.sum(jnp.where(named, before + (lane * slot_count).astype(F32), 0.0), axis=1, keepdims=True)
    slot = slot.astype(jnp.int32)
    width = 512
    slots = out_ref.shape[1]
    for t in range(slots // width):
        spot = lax.broadcasted_iota(jnp.int32, (points, width), 1) + t * width
        one_hot = (slot == spot).astype(F32).astype(BF16)
        got = jnp.dot(vals3, one_hot, preferred_element_type=F32)
        out_ref[:, t * width : (t + 1) * width] = got[0:16] + got[16:32] + got[32:48]


def scatter_kernel(nz, val_ref, out_ref):
    count = val_ref.shape[1]
    rows = out_ref.shape[1]
    chunk = 256
    out_ref[...] = jnp.zeros(out_ref.shape, F32)

    def body(step, carry):
        blk = val_ref[:, pl.ds(pl.multiple_of(step * chunk, chunk), chunk)]
        off = blk[9:10, :].astype(jnp.int32)
        row = off // nz
        lz = off - row * nz
        zt = (row_ids((nz, chunk)) == lz).astype(F32).astype(BF16)
        mask = (row_ids((rows, chunk)) == row).astype(F32).astype(BF16)
        hi = blk.astype(BF16)
        lo = (blk - hi.astype(F32)).astype(BF16)
        for i in range(9):
            left = jnp.concatenate([mask * hi[i : i + 1, :], mask * lo[i : i + 1, :]], axis=0)
            got = lax.dot_general(left, zt, (((1,), (1,)), ((), ())), preferred_element_type=F32)
            out_ref[i] += got[0:rows] + got[rows:]
        return carry

    lax.fori_loop(0, count // chunk, body, 0)


def with_halo(block, sides, width):
    for axis, dim in sides:
        count = lax.axis_size(axis)
        forward = [(i, i + 1) for i in range(count - 1)]
        backward = [(target, source) for source, target in forward]
        low = lax.ppermute(
            lax.slice_in_dim(block, block.shape[dim] - width, None, axis=dim), axis, forward
        )
        high = lax.ppermute(lax.slice_in_dim(block, 0, width, axis=dim), axis, backward)
        block = jnp.concatenate([low, block, high], axis=dim)
    return block


def shifted(padded, axis_pos, offset):
    result = padded
    for dim_pos in (1, 2, 3):
        first_cell = 2 + offset if dim_pos == axis_pos else 2
        result = lax.slice_in_dim(
            result, first_cell, first_cell + padded.shape[dim_pos] - 4, axis=dim_pos
        )
    return result


def laplace_four(padded):
    summed = centre_weight * shifted(padded, 0, 0)
    for axis_pos in (1, 2, 3):
        summed = summed + near_weight * (
            shifted(padded, axis_pos, 1) + shifted(padded, axis_pos, -1)
        )
        summed = summed + far_weight * (
            shifted(padded, axis_pos, 2) + shifted(padded, axis_pos, -2)
        )
    return summed


def local(
    current_field,
    earlier_field,
    wave_coef,
    layer_mask,
    point_xyz,
    point_owner,
    cell_offset,
    wave_vector,
    frequency,
    amplitude,
    phase_index,
    phase_table,
):
    table_size = phase_table.shape[0]
    matches = (phase_index[None, :] == jnp.arange(table_size)[:, None]).astype(F32)
    phases = jnp.dot(
        phase_table[None, :], matches, precision=lax.Precision.HIGHEST, preferred_element_type=F32
    )[0]
    own_block = jnp.concatenate(
        [wave_vector, frequency[None, :], amplitude, phases[None, :]], axis=0
    )
    point_count = point_xyz.shape[1]
    slab_count = lax.axis_size("slab")
    comp_count = lax.axis_size("comp")
    device_count = slab_count * comp_count
    slot_count = max(2, 2 * point_count // device_count)
    rows_out = STEPS * 3
    blocks = [own_block]
    for shift in range(1, comp_count):
        ring = [(i, (i + shift) % comp_count) for i in range(comp_count)]
        blocks.append(lax.ppermute(own_block, "comp", ring))
    params = jnp.concatenate(blocks, axis=1)
    slots = device_count * slot_count
    packed = pl.pallas_call(
        lambda *refs: incident_kernel(slot_count, device_count, *refs),
        out_shape=jax.ShapeDtypeStruct((16, slots), F32),
        scratch_shapes=[pltpu.VMEM((8, point_count), F32), pltpu.VMEM((32, point_count), F32)],
        name="incident",
    )(params, point_xyz, point_owner, cell_offset[None, :])
    rows_sent = rows_out + 1
    sent = jnp.transpose(
        packed[:rows_sent].reshape(rows_sent, device_count, slot_count), (1, 0, 2)
    ).reshape(device_count, rows_sent * slot_count)
    got = lax.all_to_all(sent, ("slab", "comp"), split_axis=0, concat_axis=0, tiled=True)
    arrived = jnp.transpose(
        got.reshape(device_count, rows_sent, slot_count), (1, 0, 2)
    ).reshape(rows_sent, slots)
    cx, cy, nz = current_field.shape[1:]
    forcing = pl.pallas_call(
        lambda *refs: scatter_kernel(nz, *refs),
        out_shape=jax.ShapeDtypeStruct((rows_out, cx * cy, nz), F32),
        name="scatter",
    )(arrived)
    forcing = forcing.reshape(rows_out, cx, cy, nz)
    sign_field = ((layer_mask == 1).astype(F32) - (layer_mask == 2).astype(F32))[None]
    current = current_field
    earlier = earlier_field
    for step_index in range(STEPS):
        widened = with_halo(current, (("slab", 1), ("comp", 2)), 2)
        padded = jnp.pad(widened, ((0, 0), (0, 0), (0, 0), (2, 2)))
        source = forcing[3 * step_index : 3 * step_index + 3]
        following = (
            2.0 * current - earlier + wave_coef[None] * laplace_four(padded) + sign_field * source
        )
        earlier = current
        current = following
    return (current, earlier)


def solution(mesh):
    in_specs = (
        P(None, "slab", "comp", None),
        P(None, "slab", "comp", None),
        P("slab", "comp", None),
        P("slab", "comp", None),
        P(None, ("slab", "comp")),
        P(("slab", "comp"), None),
        P(("slab", "comp")),
        P(None, "comp"),
        P("comp"),
        P(None, "comp"),
        P("comp"),
        P(),
    )
    out_specs = (P(None, "slab", "comp", None), P(None, "slab", "comp", None))
    return jax.shard_map(local, mesh=mesh, in_specs=in_specs, out_specs=out_specs, check_vma=False)
```

```python
import jax
import jax.numpy as jnp
from jax import lax
from jax.experimental import pallas as pl
from jax.experimental.pallas import tpu as pltpu
from jax.sharding import PartitionSpec as P

STEPS = 3
step_size = 0.05
near_weight = 4.0 / 3.0
far_weight = -1.0 / 12.0
centre_weight = -7.5
inv_two_pi = 0.15915494309189535
round_magic = 12582912.0

SIN_C = (4.442834854125977, -7.306587219238281, 3.588636875152588, -0.7713118195533752)
HALF = 64

F32 = jnp.float32
BF16 = jnp.bfloat16


def horner(coefs, z):
    out = coefs[-1] * z + coefs[-2]
    for c in coefs[-3::-1]:
        out = out * z + c
    return out


def sin_versine(u):
    r = u - jnp.round(u)
    s = r * horner(SIN_C, r * r)
    q = s * s
    w = 2.0 - q
    return s * (w * lax.rsqrt(w)), q


def split_three(x):
    hi = x.astype(BF16).astype(F32)
    rest = x - hi
    mid = rest.astype(BF16).astype(F32)
    return hi, mid, rest - mid


def row_ids(shape):
    return lax.broadcasted_iota(jnp.int32, shape, 0)


def incident_kernel(slot_stride, par_ref, xyz_ref, own_ref, off_ref, out_ref, x8_ref, acc_ref):
    comps = par_ref.shape[1]
    points = xyz_ref.shape[1]
    owners = out_ref.shape[0]
    kc = 256
    tile = 256
    x8_ref[...] = jnp.zeros(x8_ref.shape, F32)
    x8_ref[0:3, :] = xyz_ref[...]
    xhi, xmid, xlo = split_three(x8_ref[...])
    right = jnp.concatenate([xhi, xmid, xlo, xhi, xmid, xhi], axis=0).astype(BF16)
    acc_ref[...] = jnp.zeros(acc_ref.shape, F32)
    rows8 = row_ids((8, kc))
    times = step_size * (rows8 + 1).astype(F32)
    rows16 = row_ids((16, kc))
    comp_row = jnp.where(rows16 < 6, rows16 % 3, (rows16 + 2) % 3)
    valued = (rows16 < 10) & (rows16 != 6)

    def body(step, total):
        blk = par_ref[:, pl.ds(pl.multiple_of(step * kc, kc), kc)]
        kv = jnp.where(rows8 < 3, blk * inv_two_pi, 0.0)
        khi, kmid, klo = split_three(kv)
        left = jnp.concatenate([khi, khi, khi, kmid, kmid, klo], axis=0).astype(BF16)
        delays = times * blk[3:4, :] - blk[7:8, :]
        sd, qd = sin_versine(delays * inv_two_pi)
        amp = jnp.where(comp_row == 0, blk[4:5, :], jnp.where(comp_row == 1, blk[5:6, :], blk[6:7, :]))
        amp = jnp.where(valued, amp, 0.0)

        def rows_of(t):
            w = amp * jnp.where(rows16 < 3, t[0:1, :], jnp.where(rows16 < 6, t[1:2, :], t[2:3, :]))
            hi = w.astype(BF16)
            lo = (w - hi.astype(F32)).astype(BF16)
            return w, jnp.concatenate([hi, lo], axis=0)

        wc, lc = rows_of(qd - 1.0)
        ls = rows_of(sd)[1]
        for t in range(points // tile):
            cols = slice(t * tile, (t + 1) * tile)
            u = lax.dot_general(left, right[:, cols], (((0,), (0,)), ((), ())), preferred_element_type=F32)
            highs, lows = [], []
            for j in range(kc // 32):
                for value in sin_versine(u[32 * j : 32 * j + 32]):
                    high = value.astype(BF16)
                    highs.append(high)
                    lows.append((value - high.astype(F32)).astype(BF16))
            part = jnp.dot(ls, jnp.concatenate(highs[0::2], axis=0), preferred_element_type=F32)
            part += jnp.dot(lc, jnp.concatenate(highs[1::2], axis=0), preferred_element_type=F32)
            part += jnp.dot(ls, jnp.concatenate(lows[0::2], axis=0), preferred_element_type=F32)
            part += jnp.dot(lc, jnp.concatenate(lows[1::2], axis=0), preferred_element_type=F32)
            acc_ref[:, cols] += part
        return total - wc

    total = lax.fori_loop(0, comps // kc, body, jnp.zeros((16, kc), F32))
    vals = acc_ref[0:16, :] + acc_ref[16:32, :] + jnp.sum(total, axis=1, keepdims=True)
    vals = jnp.where(row_ids((16, points)) == 6, off_ref[...].astype(F32), vals)
    v1, v2, v3 = split_three(vals)
    vals3 = jnp.concatenate([v1, v2, v3], axis=0).astype(BF16)
    owner_id = row_ids((owners, points))
    named = own_ref[...] == owner_id
    earlier = row_ids((points, points)) < lax.broadcasted_iota(jnp.int32, (points, points), 1)
    before = jnp.dot(named.astype(F32).astype(BF16), earlier.astype(F32).astype(BF16), preferred_element_type=F32)
    slot = jnp.sum(jnp.where(named, before + (owner_id * slot_stride).astype(F32), 0.0), axis=0, keepdims=True)
    slot = slot.astype(jnp.int32)
    width = 8 * slot_stride
    left_half = lax.broadcasted_iota(jnp.int32, (8, 2 * slot_stride), 1) < slot_stride
    for t in range(owners // 8):
        spot = row_ids((width, points)) + t * width
        one_hot = (slot == spot).astype(F32).astype(BF16)
        got = lax.dot_general(vals3, one_hot, (((1,), (1,)), ((), ())), preferred_element_type=F32)
        got = got[0:16] + got[16:32] + got[32:48]
        for pair in range(4):
            cols = slice(pair * 2 * slot_stride, (pair + 1) * 2 * slot_stride)
            low, high = got[0:8, cols], got[8:16, cols]
            out_ref[8 * t + 2 * pair] = jnp.where(left_half, low, pltpu.roll(high, slot_stride, 1))
            out_ref[8 * t + 2 * pair + 1] = jnp.where(left_half, pltpu.roll(low, slot_stride, 1), high)


def scatter_kernel(nz, val_ref, out_ref):
    sources = val_ref.shape[0]
    rows = out_ref.shape[1]
    chunk = 256
    lanes = val_ref.shape[2]
    left_half = lax.broadcasted_iota(jnp.int32, (8, lanes), 1) < lanes // 2
    out_ref[...] = jnp.zeros(out_ref.shape, F32)

    def body(step, carry):
        lows, highs = [], []
        for pair in range(2):
            even, odd = val_ref[4 * step + 2 * pair], val_ref[4 * step + 2 * pair + 1]
            lows.append(jnp.where(left_half, even, pltpu.roll(odd, lanes // 2, 1)))
            highs.append(jnp.where(left_half, pltpu.roll(even, lanes // 2, 1), odd))
        low = jnp.concatenate(lows, axis=1)
        blk = jnp.concatenate([low, jnp.concatenate(highs, axis=1)], axis=0)
        off = blk[6:7, :].astype(jnp.int32)
        row = off // nz
        lz = off - row * nz
        zt = (row_ids((nz, chunk)) == lz).astype(F32).astype(BF16)
        mask = (row_ids((rows, chunk)) == row).astype(F32).astype(BF16)
        hi = blk.astype(BF16)
        lo = (blk - hi.astype(F32)).astype(BF16)
        for i in range(9):
            r = i if i < 6 else i + 1
            left = jnp.concatenate([mask * hi[r : r + 1, :], mask * lo[r : r + 1, :]], axis=0)
            got = lax.dot_general(left, zt, (((1,), (1,)), ((), ())), preferred_element_type=F32)
            out_ref[i] += got[0:rows] + got[rows:]
        return carry

    lax.fori_loop(0, sources // 4, body, 0)


def with_halo(block, sides, width):
    for axis, dim in sides:
        count = lax.axis_size(axis)
        forward = [(i, i + 1) for i in range(count - 1)]
        backward = [(target, source) for source, target in forward]
        low = lax.ppermute(
            lax.slice_in_dim(block, block.shape[dim] - width, None, axis=dim), axis, forward
        )
        high = lax.ppermute(lax.slice_in_dim(block, 0, width, axis=dim), axis, backward)
        block = jnp.concatenate([low, block, high], axis=dim)
    return block


def shifted(padded, axis_pos, offset):
    result = padded
    for dim_pos in (1, 2, 3):
        first_cell = 2 + offset if dim_pos == axis_pos else 2
        result = lax.slice_in_dim(
            result, first_cell, first_cell + padded.shape[dim_pos] - 4, axis=dim_pos
        )
    return result


def laplace_four(padded):
    summed = centre_weight * shifted(padded, 0, 0)
    for axis_pos in (1, 2, 3):
        summed = summed + near_weight * (
            shifted(padded, axis_pos, 1) + shifted(padded, axis_pos, -1)
        )
        summed = summed + far_weight * (
            shifted(padded, axis_pos, 2) + shifted(padded, axis_pos, -2)
        )
    return summed


def local(
    current_field,
    earlier_field,
    wave_coef,
    layer_mask,
    point_xyz,
    point_owner,
    cell_offset,
    wave_vector,
    frequency,
    amplitude,
    phase_index,
    phase_table,
):
    table_size = phase_table.shape[0]
    matches = (phase_index[None, :] == jnp.arange(table_size)[:, None]).astype(F32)
    phases = jnp.dot(
        phase_table[None, :], matches, precision=lax.Precision.HIGHEST, preferred_element_type=F32
    )[0]
    own_block = jnp.concatenate(
        [wave_vector, frequency[None, :], amplitude, phases[None, :]], axis=0
    )
    point_count = point_xyz.shape[1]
    slab_count = lax.axis_size("slab")
    comp_count = lax.axis_size("comp")
    device_count = slab_count * comp_count
    slot_count = max(2, 2 * point_count // device_count)
    rows_out = STEPS * 3
    blocks = [own_block]
    for shift in range(1, comp_count):
        ring = [(i, (i + shift) % comp_count) for i in range(comp_count)]
        blocks.append(lax.ppermute(own_block, "comp", ring))
    params = jnp.concatenate(blocks, axis=1)
    assert slot_count <= HALF and device_count % 8 == 0
    packed = pl.pallas_call(
        lambda *refs: incident_kernel(HALF, *refs),
        out_shape=jax.ShapeDtypeStruct((device_count, 8, 2 * HALF), F32),
        scratch_shapes=[pltpu.VMEM((8, point_count), F32), pltpu.VMEM((32, point_count), F32)],
        name="incident",
    )(params, point_xyz, point_owner.reshape(1, point_count), cell_offset.reshape(1, point_count))
    arrived = lax.all_to_all(packed, ("slab", "comp"), split_axis=0, concat_axis=0, tiled=True)
    cx, cy, nz = current_field.shape[1:]
    forcing = pl.pallas_call(
        lambda *refs: scatter_kernel(nz, *refs),
        out_shape=jax.ShapeDtypeStruct((rows_out, cx * cy, nz), F32),
        name="scatter",
    )(arrived)
    forcing = forcing.reshape(rows_out, cx, cy, nz)
    sign_field = ((layer_mask == 1).astype(F32) - (layer_mask == 2).astype(F32))[None]
    current = current_field
    earlier = earlier_field
    for step_index in range(STEPS):
        widened = with_halo(current, (("slab", 1), ("comp", 2)), 2)
        padded = jnp.pad(widened, ((0, 0), (0, 0), (0, 0), (2, 2)))
        source = forcing[3 * step_index : 3 * step_index + 3]
        following = (
            2.0 * current - earlier + wave_coef[None] * laplace_four(padded) + sign_field * source
        )
        earlier = current
        current = following
    return (current, earlier)


def solution(mesh):
    in_specs = (
        P(None, "slab", "comp", None),
        P(None, "slab", "comp", None),
        P("slab", "comp", None),
        P("slab", "comp", None),
        P(None, ("slab", "comp")),
        P(("slab", "comp"), None),
        P(("slab", "comp")),
        P(None, "comp"),
        P("comp"),
        P(None, "comp"),
        P("comp"),
        P(),
    )
    out_specs = (P(None, "slab", "comp", None), P(None, "slab", "comp", None))
    return jax.shard_map(local, mesh=mesh, in_specs=in_specs, out_specs=out_specs, check_vma=False)
```

```python
import jax
import jax.numpy as jnp
from jax import lax
from jax.experimental import pallas as pl
from jax.experimental.pallas import tpu as pltpu
from jax.sharding import PartitionSpec as P

STEPS = 3
step_size = 0.05
near_weight = 4.0 / 3.0
far_weight = -1.0 / 12.0
centre_weight = -7.5
inv_two_pi = 0.15915494309189535
round_magic = 12582912.0

SIN_C = (4.442834854125977, -7.306587219238281, 3.588636875152588, -0.7713118195533752)
HALF = 64

F32 = jnp.float32
BF16 = jnp.bfloat16


def horner(coefs, z):
    out = coefs[-1] * z + coefs[-2]
    for c in coefs[-3::-1]:
        out = out * z + c
    return out


def sin_versine(u):
    r = u - jnp.round(u)
    s = r * horner(SIN_C, r * r)
    q = s * s
    w = 2.0 - q
    return s * (w * lax.rsqrt(w)), q


def split_three(x):
    hi = x.astype(BF16).astype(F32)
    rest = x - hi
    mid = rest.astype(BF16).astype(F32)
    return hi, mid, rest - mid


def row_ids(shape):
    return lax.broadcasted_iota(jnp.int32, shape, 0)


def add_components(par_refs, xyz_ref, x8_ref, acc_ref):
    points = xyz_ref.shape[1]
    kc = 256
    tile = 256
    x8_ref[...] = jnp.zeros(x8_ref.shape, F32)
    x8_ref[0:3, :] = xyz_ref[...]
    xhi, xmid, xlo = split_three(x8_ref[...])
    right = jnp.concatenate([xhi, xmid, xlo, xhi, xmid, xhi], axis=0).astype(BF16)
    rows8 = row_ids((8, kc))
    times = step_size * (rows8 + 1).astype(F32)
    rows16 = row_ids((16, kc))
    comp_row = jnp.where(rows16 < 6, rows16 % 3, (rows16 + 2) % 3)
    valued = (rows16 < 10) & (rows16 != 6)

    def body(par_ref, step, total):
        blk = par_ref[:, pl.ds(pl.multiple_of(step * kc, kc), kc)]
        kv = jnp.where(rows8 < 3, blk * inv_two_pi, 0.0)
        khi, kmid, klo = split_three(kv)
        left = jnp.concatenate([khi, khi, khi, kmid, kmid, klo], axis=0).astype(BF16)
        delays = times * blk[3:4, :] - blk[7:8, :]
        sd, qd = sin_versine(delays * inv_two_pi)
        amp = jnp.where(comp_row == 0, blk[4:5, :], jnp.where(comp_row == 1, blk[5:6, :], blk[6:7, :]))
        amp = jnp.where(valued, amp, 0.0)

        def rows_of(t):
            w = amp * jnp.where(rows16 < 3, t[0:1, :], jnp.where(rows16 < 6, t[1:2, :], t[2:3, :]))
            hi = w.astype(BF16)
            lo = (w - hi.astype(F32)).astype(BF16)
            return w, jnp.concatenate([hi, lo], axis=0)

        wc, lc = rows_of(qd - 1.0)
        ls = rows_of(sd)[1]
        for t in range(points // tile):
            cols = slice(t * tile, (t + 1) * tile)
            u = lax.dot_general(left, right[:, cols], (((0,), (0,)), ((), ())), preferred_element_type=F32)
            highs, lows = [], []
            for j in range(kc // 32):
                for value in sin_versine(u[32 * j : 32 * j + 32]):
                    high = value.astype(BF16)
                    highs.append(high)
                    lows.append((value - high.astype(F32)).astype(BF16))
            part = jnp.dot(ls, jnp.concatenate(highs[0::2], axis=0), preferred_element_type=F32)
            part += jnp.dot(lc, jnp.concatenate(highs[1::2], axis=0), preferred_element_type=F32)
            part += jnp.dot(ls, jnp.concatenate(lows[0::2], axis=0), preferred_element_type=F32)
            part += jnp.dot(lc, jnp.concatenate(lows[1::2], axis=0), preferred_element_type=F32)
            acc_ref[:, cols] += part
        return total - wc

    total = jnp.zeros((16, kc), F32)
    for par_ref in par_refs:
        steps = par_ref.shape[1] // kc
        total = lax.fori_loop(0, steps, lambda step, t, ref=par_ref: body(ref, step, t), total)
    return total


def first_incident_kernel(count, *refs):
    par_refs, (xyz_ref, acc_ref, total_ref, x8_ref) = refs[:count], refs[count:]
    acc_ref[...] = jnp.zeros(acc_ref.shape, F32)
    total_ref[...] = add_components(par_refs, xyz_ref, x8_ref, acc_ref)


def last_incident_kernel(count, slot_stride, *refs):
    par_refs, refs = refs[:count], refs[count:]
    first_ref, first_total_ref, xyz_ref, own_ref, off_ref, out_ref, x8_ref, acc_ref = refs
    points = xyz_ref.shape[1]
    owners = out_ref.shape[0]
    acc_ref[...] = first_ref[...]
    total = add_components(par_refs, xyz_ref, x8_ref, acc_ref) + first_total_ref[...]
    vals = acc_ref[0:16, :] + acc_ref[16:32, :] + jnp.sum(total, axis=1, keepdims=True)
    vals = jnp.where(row_ids((16, points)) == 6, off_ref[...].astype(F32), vals)
    v1, v2, v3 = split_three(vals)
    vals3 = jnp.concatenate([v1, v2, v3], axis=0).astype(BF16)
    owner_id = row_ids((owners, points))
    named = own_ref[...] == owner_id
    earlier = row_ids((points, points)) < lax.broadcasted_iota(jnp.int32, (points, points), 1)
    before = jnp.dot(named.astype(F32).astype(BF16), earlier.astype(F32).astype(BF16), preferred_element_type=F32)
    slot = jnp.sum(jnp.where(named, before + (owner_id * slot_stride).astype(F32), 0.0), axis=0, keepdims=True)
    slot = slot.astype(jnp.int32)
    width = 8 * slot_stride
    left_half = lax.broadcasted_iota(jnp.int32, (8, 2 * slot_stride), 1) < slot_stride
    for t in range(owners // 8):
        spot = row_ids((width, points)) + t * width
        one_hot = (slot == spot).astype(F32).astype(BF16)
        got = lax.dot_general(vals3, one_hot, (((1,), (1,)), ((), ())), preferred_element_type=F32)
        got = got[0:16] + got[16:32] + got[32:48]
        for pair in range(4):
            cols = slice(pair * 2 * slot_stride, (pair + 1) * 2 * slot_stride)
            low, high = got[0:8, cols], got[8:16, cols]
            out_ref[8 * t + 2 * pair] = jnp.where(left_half, low, pltpu.roll(high, slot_stride, 1))
            out_ref[8 * t + 2 * pair + 1] = jnp.where(left_half, pltpu.roll(low, slot_stride, 1), high)


TILE = 8
DEEP = 6
MID = 4
NEAR = 2


def half_turn(tile):
    return pltpu.roll(tile, TILE // 2, 0)


def scatter_kernel(par_ref, val_ref, mask_ref, out_ref, face_ref, acc_ref):
    sources = val_ref.shape[0]
    cx, cy, nz = mask_ref.shape
    rows = cx * cy
    chunk = 256
    lanes = val_ref.shape[2]
    left_half = lax.broadcasted_iota(jnp.int32, (8, lanes), 1) < lanes // 2
    acc_ref[...] = jnp.zeros(acc_ref.shape, F32)

    def body(step, carry):
        lows, highs = [], []
        for pair in range(2):
            even, odd = val_ref[4 * step + 2 * pair], val_ref[4 * step + 2 * pair + 1]
            lows.append(jnp.where(left_half, even, pltpu.roll(odd, lanes // 2, 1)))
            highs.append(jnp.where(left_half, pltpu.roll(even, lanes // 2, 1), odd))
        low = jnp.concatenate(lows, axis=1)
        blk = jnp.concatenate([low, jnp.concatenate(highs, axis=1)], axis=0)
        off = blk[6:7, :].astype(jnp.int32)
        row = off // nz
        lz = off - row * nz
        zt = (row_ids((nz, chunk)) == lz).astype(F32).astype(BF16)
        mask = (row_ids((rows, chunk)) == row).astype(F32).astype(BF16)
        hi = blk.astype(BF16)
        lo = (blk - hi.astype(F32)).astype(BF16)
        for i in range(9):
            r = i if i < 6 else i + 1
            left = jnp.concatenate([mask * hi[r : r + 1, :], mask * lo[r : r + 1, :]], axis=0)
            got = lax.dot_general(left, zt, (((1,), (1,)), ((), ())), preferred_element_type=F32)
            acc_ref[i] += got[0:rows] + got[rows:]
        return carry

    lax.fori_loop(0, sources // 4, body, 0)
    sign = (mask_ref[...] == 1).astype(F32) - (mask_ref[...] == 2).astype(F32)
    for i in range(9):
        out_ref[i] = acc_ref[i].reshape(cx, cy, nz) * sign
    parity = par_ref[0]
    upper = row_ids((TILE, nz)) >= TILE // 2
    for high, place in ((True, parity), (False, 1 - parity)):
        ys = slice(cy - TILE, cy) if high else slice(0, TILE)
        keep = upper if high else ~upper
        for i in range(3):
            for x in range(cx):
                face_ref[place, i, x] = jnp.where(keep, out_ref[i, x, ys], half_turn(out_ref[3 + i, x, ys]))


def pair_list(count, odd):
    first = 1 if odd else 0
    pairs = [(i, i + 1) for i in range(first, count - 1, 2)]
    return pairs + [(j, i) for i, j in pairs]


def swap_faces(faces, axis):
    count = lax.axis_size(axis)
    return [lax.ppermute(faces[k], axis, pair_list(count, k)) for k in (0, 1)]


def field_face_kernel(par_ref, cur_ref, ear_ref, coef_ref, out_ref):
    _, cx, cy, nz = cur_ref.shape
    parity = par_ref[0]
    upper = row_ids((TILE, nz)) >= TILE // 2
    for high, place in ((True, parity), (False, 1 - parity)):
        ys = slice(cy - TILE, cy) if high else slice(0, TILE)
        keep = upper if high else ~upper
        for x in range(cx):
            for i in range(3):
                out_ref[place, i, x] = cur_ref[i, x, ys]
            out_ref[place, 3, x] = jnp.where(keep, ear_ref[0, x, ys], half_turn(ear_ref[1, x, ys]))
            out_ref[place, 4, x] = jnp.where(keep, ear_ref[2, x, ys], half_turn(coef_ref[x, ys]))


def face_tile(ref, name, x):
    if name < 3:
        return ref[name, x]
    tile = ref[3 + (name - 3) // 2, x]
    return half_turn(tile) if name in (4, 6) else tile


def select_side(parity, even_ref, odd_ref, high):
    from_even = (parity == 0) if high else (parity == 1)

    def read(get):
        return jnp.where(from_even, get(even_ref), get(odd_ref))

    return read


FIELD_PLAN = [(DEEP, MID)] * 3 + [(MID, NEAR)] * 4
FORCE_PLAN = [(MID, NEAR)] * 3 + [(NEAR, 0)] * 3


def plan_tiles(plan, cy):
    out = []
    for name, (planes, corners) in enumerate(plan):
        for dist in range(1, planes + 1):
            for part in list(range(cy // TILE)) + ([-1] if dist <= corners else []):
                out.append((name, dist, part, len(out)))
    return out


def side_kernel(plan, own_tile, halo_tile, cx, cy, nz, px_ref, py_ref, even_ref, odd_ref, out_ref):
    upper = row_ids((TILE, nz)) >= TILE // 2
    low = select_side(py_ref[0], even_ref, odd_ref, False)
    high = select_side(py_ref[0], even_ref, odd_ref, True)
    parity = px_ref[0]
    for is_high, place in ((True, parity), (False, 1 - parity)):
        for name, dist, part, at in plan_tiles(plan, cy):
            x = cx - dist if is_high else dist - 1
            if part >= 0:
                tile = own_tile(name, x, slice(part * TILE, (part + 1) * TILE))
            else:
                tile = jnp.where(
                    upper,
                    low(lambda ref: halo_tile(ref, name, x)),
                    high(lambda ref: halo_tile(ref, name, x)),
                )
            out_ref[place, at] = tile


def field_side_kernel(px_ref, py_ref, cur_ref, ear_ref, coef_ref, even_ref, odd_ref, out_ref):
    _, cx, cy, nz = cur_ref.shape

    def own_tile(name, x, ys):
        if name < 3:
            return cur_ref[name, x, ys]
        return ear_ref[name - 3, x, ys] if name < 6 else coef_ref[x, ys]

    side_kernel(FIELD_PLAN, own_tile, face_tile, cx, cy, nz, px_ref, py_ref, even_ref, odd_ref, out_ref)


def force_side_kernel(px_ref, py_ref, force_ref, even_ref, odd_ref, out_ref):
    _, cx, cy, nz = force_ref.shape
    side_kernel(
        FORCE_PLAN,
        lambda name, x, ys: force_ref[name, x, ys],
        lambda ref, name, x: ref[name, x],
        cx, cy, nz, px_ref, py_ref, even_ref, odd_ref, out_ref,
    )


def laplacian(plane, x_near, x_far):
    rows, nz = plane.shape
    lane = lax.broadcasted_iota(jnp.int32, (rows, nz), 1)

    def along_z(k):
        below = jnp.where(lane >= k, pltpu.roll(plane, k, 1), 0.0)
        return below + jnp.where(lane < nz - k, pltpu.roll(plane, nz - k, 1), 0.0)

    def along_y(k):
        return pltpu.roll(plane, k, 0) + pltpu.roll(plane, rows - k, 0)

    near = x_near + along_y(1) + along_z(1)
    far = x_far + along_y(2) + along_z(2)
    return centre_weight * plane + near_weight * near + far_weight * far


def laplacian_at(ref, i, x):
    return laplacian(ref[i, x], ref[i, x - 1] + ref[i, x + 1], ref[i, x - 2] + ref[i, x + 2])


def first_wave_kernel(
    px_ref, py_ref, cur_ref, ear_ref, coef_ref, ye_ref, yo_ref, xe_ref, xo_ref,
    next_ref, now_ref, wide_coef_ref, u_ref, e_ref, c_ref,
):
    _, cx, cy, nz = cur_ref.shape
    own = slice(TILE, TILE + cy)
    lower, higher = slice(0, TILE), slice(TILE + cy, 2 * TILE + cy)
    low = select_side(py_ref[0], ye_ref, yo_ref, False)
    high = select_side(py_ref[0], ye_ref, yo_ref, True)

    def put(name, x, rows, value):
        if name < 3:
            u_ref[name, DEEP + x, rows] = value
        elif name < 6:
            e_ref[name - 3, MID + x, rows] = value
        else:
            c_ref[MID + x, rows] = value

    for x in range(cx):
        for name in range(7):
            value = cur_ref[name, x] if name < 3 else ear_ref[name - 3, x] if name < 6 else coef_ref[x]
            put(name, x, own, value)
            put(name, x, lower, low(lambda ref: face_tile(ref, name, x)))
            put(name, x, higher, high(lambda ref: face_tile(ref, name, x)))
    for is_high in (False, True):
        read = select_side(px_ref[0], xe_ref, xo_ref, is_high)
        for name, dist, part, at in plan_tiles(FIELD_PLAN, cy):
            x = cx - 1 + dist if is_high else -dist
            tile = read(lambda ref: ref[at])
            if part >= 0:
                put(name, x, slice(TILE * (part + 1), TILE * (part + 2)), tile)
            else:
                put(name, x, lower, tile)
                put(name, x, higher, tile)

    def plane(x, carry):
        coef = c_ref[x]
        for i in range(3):
            at = x + DEEP - MID
            next_ref[i, x] = 2.0 * u_ref[i, at] - e_ref[i, x] + coef * laplacian_at(u_ref, i, at)
        return carry

    lax.fori_loop(0, cx + 2 * MID, plane, 0)
    for i in range(3):
        now_ref[i] = u_ref[i, DEEP - NEAR : DEEP + cx + NEAR]
    wide_coef_ref[...] = c_ref[MID - NEAR : MID + cx + NEAR]


def last_wave_kernel(
    px_ref, py_ref, next_ref, now_ref, coef_ref, force_ref, ye_ref, yo_ref, xe_ref, xo_ref,
    final_ref, prior_ref, one_ref, two_ref,
):
    _, cx, cy, nz = force_ref.shape
    own = slice(TILE, TILE + cy)
    lower, higher = slice(0, TILE), slice(TILE + cy, 2 * TILE + cy)
    low = select_side(py_ref[0], ye_ref, yo_ref, False)
    high = select_side(py_ref[0], ye_ref, yo_ref, True)
    one_ref[...] = next_ref[...]
    for i in range(3):
        for x in range(cx):
            one_ref[i, MID + x, own] += force_ref[i, x]
            two_ref[i, NEAR + x, own] = force_ref[3 + i, x]
            for rows, read in ((lower, low), (higher, high)):
                tile = read(lambda ref: ref[i, x])
                one_ref[i, MID + x, rows] += tile
                two_ref[i, NEAR + x, rows] = half_turn(tile)
    for is_high in (False, True):
        read = select_side(px_ref[0], xe_ref, xo_ref, is_high)
        for name, dist, part, at in plan_tiles(FORCE_PLAN, cy):
            x = cx - 1 + dist if is_high else -dist
            tile = read(lambda ref: ref[at])
            if name >= 3:
                two_ref[name - 3, NEAR + x, slice(TILE * (part + 1), TILE * (part + 2))] = tile
            elif part >= 0:
                one_ref[name, MID + x, slice(TILE * (part + 1), TILE * (part + 2))] += tile
            else:
                one_ref[name, MID + x, lower] += tile
                one_ref[name, MID + x, higher] += tile

    def second(x, carry):
        coef = coef_ref[x]
        for i in range(3):
            at = x + MID - NEAR
            lap = laplacian_at(one_ref, i, at)
            two_ref[i, x] = 2.0 * one_ref[i, at] - now_ref[i, x] + coef * lap + two_ref[i, x]
        return carry

    lax.fori_loop(0, cx + 2 * NEAR, second, 0)

    def third(x, carry):
        coef = coef_ref[x + NEAR]
        for i in range(3):
            at = x + NEAR
            plane = two_ref[i, at]
            moved = 2.0 * plane - one_ref[i, x + MID] + coef * laplacian_at(two_ref, i, at)
            final_ref[i, x] = moved[TILE : TILE + cy] + force_ref[6 + i, x]
            prior_ref[i, x] = plane[TILE : TILE + cy]
        return carry

    lax.fori_loop(0, cx, third, 0)


def local(
    current_field,
    earlier_field,
    wave_coef,
    layer_mask,
    point_xyz,
    point_owner,
    cell_offset,
    wave_vector,
    frequency,
    amplitude,
    phase_index,
    phase_table,
):
    table_size = phase_table.shape[0]
    matches = (phase_index[None, :] == jnp.arange(table_size)[:, None]).astype(F32)
    phases = jnp.dot(
        phase_table[None, :], matches, precision=lax.Precision.HIGHEST, preferred_element_type=F32
    )[0]
    own_block = jnp.concatenate(
        [wave_vector, frequency[None, :], amplitude, phases[None, :]], axis=0
    )
    point_count = point_xyz.shape[1]
    slab_count = lax.axis_size("slab")
    comp_count = lax.axis_size("comp")
    device_count = slab_count * comp_count
    slot_count = max(2, 2 * point_count // device_count)
    _, cx, cy, nz = current_field.shape
    assert slot_count <= HALF and device_count % 8 == 0
    assert cx >= DEEP and cy >= 2 * TILE and cy % TILE == 0
    wide = cy + 2 * TILE
    smem = pl.BlockSpec(memory_space=pltpu.SMEM)
    vmem = pl.BlockSpec(memory_space=pltpu.VMEM)

    def call(kernel, name, operands, shapes, scratch=(), scalars=0):
        shapes = [jax.ShapeDtypeStruct(shape, F32) for shape in shapes]
        return pl.pallas_call(
            kernel,
            out_shape=shapes,
            in_specs=[smem] * scalars + [vmem] * (len(operands) - scalars),
            out_specs=[vmem] * len(shapes),
            scratch_shapes=[pltpu.VMEM(shape, F32) for shape in scratch],
            name=name,
        )(*operands)

    px = (lax.axis_index("slab") % 2).astype(jnp.int32).reshape(1)
    py = (lax.axis_index("comp") % 2).astype(jnp.int32).reshape(1)
    if comp_count == 4:
        near_block = lax.ppermute(own_block, "comp", pair_list(4, 0))
        first_blocks = [own_block, near_block]
        ring = pair_list(4, 1) + [(0, 3), (3, 0)]
        far_block = lax.ppermute(jnp.concatenate(first_blocks, axis=1), "comp", ring)
        last_blocks = [far_block]
    else:
        first_blocks = [own_block]
        last_blocks = [
            lax.ppermute(own_block, "comp", [(i, (i + k) % comp_count) for i in range(comp_count)])
            for k in range(1, comp_count)
        ]
    fields = (current_field, earlier_field, wave_coef)
    (faces,) = call(field_face_kernel, "field_faces", (py, *fields), [(2, 5, cx, TILE, nz)], scalars=1)
    ye, yo = swap_faces(faces, "comp")
    (sum_one, total_one) = call(
        lambda *refs: first_incident_kernel(len(first_blocks), *refs),
        "incident_first",
        (*first_blocks, point_xyz),
        [(32, point_count), (16, 256)],
        [(8, point_count)],
    )
    field_tiles = len(plan_tiles(FIELD_PLAN, cy))
    (sides,) = call(
        field_side_kernel, "field_sides", (px, py, *fields, ye, yo), [(2, field_tiles, TILE, nz)], scalars=2
    )
    xe, xo = swap_faces(sides, "slab")
    (packed,) = call(
        lambda *refs: last_incident_kernel(len(last_blocks), HALF, *refs),
        "incident_last",
        (
            *last_blocks, sum_one, total_one, point_xyz,
            point_owner.reshape(1, point_count), cell_offset.reshape(1, point_count),
        ),
        [(device_count, 8, 2 * HALF)],
        [(8, point_count), (32, point_count)],
    )
    arrived = lax.all_to_all(packed, ("slab", "comp"), split_axis=0, concat_axis=0, tiled=True)
    force, force_faces = call(
        scatter_kernel,
        "scatter",
        (py, arrived, layer_mask),
        [(9, cx, cy, nz), (2, 3, cx, TILE, nz)],
        [(9, cx * cy, nz)],
        scalars=1,
    )
    fye, fyo = swap_faces(force_faces, "comp")
    force_tiles = len(plan_tiles(FORCE_PLAN, cy))
    (force_sides,) = call(
        force_side_kernel, "force_sides", (px, py, force, fye, fyo), [(2, force_tiles, TILE, nz)], scalars=2
    )
    fxe, fxo = swap_faces(force_sides, "slab")
    following, now, wide_coef = call(
        first_wave_kernel,
        "first_wave",
        (px, py, *fields, ye, yo, xe, xo),
        [(3, cx + 2 * MID, wide, nz), (3, cx + 2 * NEAR, wide, nz), (cx + 2 * NEAR, wide, nz)],
        [(3, cx + 2 * DEEP, wide, nz), (3, cx + 2 * MID, wide, nz), (cx + 2 * MID, wide, nz)],
        scalars=2,
    )
    final, prior = call(
        last_wave_kernel,
        "last_wave",
        (px, py, following, now, wide_coef, force, fye, fyo, fxe, fxo),
        [current_field.shape, current_field.shape],
        [(3, cx + 2 * MID, wide, nz), (3, cx + 2 * NEAR, wide, nz)],
        scalars=2,
    )
    return (final, prior)


def solution(mesh):
    in_specs = (
        P(None, "slab", "comp", None),
        P(None, "slab", "comp", None),
        P("slab", "comp", None),
        P("slab", "comp", None),
        P(None, ("slab", "comp")),
        P(("slab", "comp"), None),
        P(("slab", "comp")),
        P(None, "comp"),
        P("comp"),
        P(None, "comp"),
        P("comp"),
        P(),
    )
    out_specs = (P(None, "slab", "comp", None), P(None, "slab", "comp", None))
    return jax.shard_map(local, mesh=mesh, in_specs=in_specs, out_specs=out_specs, check_vma=False)
```

```python
import jax
import jax.numpy as jnp
from jax import lax
from jax.experimental import pallas as pl
from jax.experimental.pallas import tpu as pltpu
from jax.sharding import PartitionSpec as P

step_size = 0.05
near_weight = 4.0 / 3.0
far_weight = -1.0 / 12.0
centre_weight = -7.5
inv_two_pi = 0.15915494309189535

SIN_C = (4.442834854125977, -7.306587219238281, 3.588636875152588, -0.7713118195533752)
HALF = 64
VMEM_GRANT = 16 * 2**20

F32 = jnp.float32
BF16 = jnp.bfloat16


def horner(coefs, z):
    out = coefs[-1] * z + coefs[-2]
    for c in coefs[-3::-1]:
        out = out * z + c
    return out


def sin_versine(u):
    r = u - jnp.round(u)
    s = r * horner(SIN_C, r * r)
    q = s * s
    w = 2.0 - q
    return s * (w * lax.rsqrt(w)), q


def split_three(x):
    hi = x.astype(BF16).astype(F32)
    rest = x - hi
    mid = rest.astype(BF16).astype(F32)
    return hi, mid, rest - mid


def row_ids(shape):
    return lax.broadcasted_iota(jnp.int32, shape, 0)


def add_components(par_refs, xyz_ref, x8_ref, acc_ref):
    points = xyz_ref.shape[1]
    kc = 256
    tile = 256
    x8_ref[...] = jnp.zeros(x8_ref.shape, F32)
    x8_ref[0:3, :] = xyz_ref[...]
    xhi, xmid, xlo = split_three(x8_ref[...])
    right = jnp.concatenate([xhi, xmid, xlo, xhi, xmid, xhi], axis=0).astype(BF16)
    rows8 = row_ids((8, kc))
    times = step_size * (rows8 + 1).astype(F32)
    rows16 = row_ids((16, kc))
    comp_row = jnp.where(rows16 < 6, rows16 % 3, (rows16 + 2) % 3)
    valued = (rows16 < 10) & (rows16 != 6)

    def body(par_ref, step, total):
        blk = par_ref[:, pl.ds(pl.multiple_of(step * kc, kc), kc)]
        kv = jnp.where(rows8 < 3, blk * inv_two_pi, 0.0)
        khi, kmid, klo = split_three(kv)
        left = jnp.concatenate([khi, khi, khi, kmid, kmid, klo], axis=0).astype(BF16)
        delays = times * blk[3:4, :] - blk[7:8, :]
        sd, qd = sin_versine(delays * inv_two_pi)
        amp = jnp.where(comp_row == 0, blk[4:5, :], jnp.where(comp_row == 1, blk[5:6, :], blk[6:7, :]))
        amp = jnp.where(valued, amp, 0.0)

        def rows_of(t):
            w = amp * jnp.where(rows16 < 3, t[0:1, :], jnp.where(rows16 < 6, t[1:2, :], t[2:3, :]))
            hi = w.astype(BF16)
            lo = (w - hi.astype(F32)).astype(BF16)
            return w, jnp.concatenate([hi, lo], axis=0)

        wc, lc = rows_of(qd - 1.0)
        ls = rows_of(sd)[1]
        for t in range(points // tile):
            cols = slice(t * tile, (t + 1) * tile)
            u = lax.dot_general(left, right[:, cols], (((0,), (0,)), ((), ())), preferred_element_type=F32)
            highs, lows = [], []
            for j in range(kc // 32):
                for value in sin_versine(u[32 * j : 32 * j + 32]):
                    high = value.astype(BF16)
                    highs.append(high)
                    lows.append((value - high.astype(F32)).astype(BF16))
            part = jnp.dot(ls, jnp.concatenate(highs[0::2], axis=0), preferred_element_type=F32)
            part += jnp.dot(lc, jnp.concatenate(highs[1::2], axis=0), preferred_element_type=F32)
            part += jnp.dot(ls, jnp.concatenate(lows[0::2], axis=0), preferred_element_type=F32)
            part += jnp.dot(lc, jnp.concatenate(lows[1::2], axis=0), preferred_element_type=F32)
            acc_ref[:, cols] += part
        return total - wc

    total = jnp.zeros((16, kc), F32)
    for par_ref in par_refs:
        steps = par_ref.shape[1] // kc
        total = lax.fori_loop(0, steps, lambda step, t, ref=par_ref: body(ref, step, t), total)
    return total


def first_incident_kernel(count, *refs):
    par_refs, (xyz_ref, acc_ref, total_ref, x8_ref) = refs[:count], refs[count:]
    acc_ref[...] = jnp.zeros(acc_ref.shape, F32)
    total_ref[...] = add_components(par_refs, xyz_ref, x8_ref, acc_ref)


def last_incident_kernel(count, slot_stride, *refs):
    par_refs, refs = refs[:count], refs[count:]
    first_ref, first_total_ref, xyz_ref, own_ref, off_ref, out_ref, x8_ref, acc_ref = refs
    points = xyz_ref.shape[1]
    owners = out_ref.shape[0]
    acc_ref[...] = first_ref[...]
    total = add_components(par_refs, xyz_ref, x8_ref, acc_ref) + first_total_ref[...]
    vals = acc_ref[0:16, :] + acc_ref[16:32, :] + jnp.sum(total, axis=1, keepdims=True)
    vals = jnp.where(row_ids((16, points)) == 6, off_ref[...].astype(F32), vals)
    v1, v2, v3 = split_three(vals)
    vals3 = jnp.concatenate([v1, v2, v3], axis=0).astype(BF16)
    owner_id = row_ids((owners, points))
    named = own_ref[...] == owner_id
    earlier = row_ids((points, points)) < lax.broadcasted_iota(jnp.int32, (points, points), 1)
    before = jnp.dot(named.astype(F32).astype(BF16), earlier.astype(F32).astype(BF16), preferred_element_type=F32)
    slot = jnp.sum(jnp.where(named, before + (owner_id * slot_stride).astype(F32), 0.0), axis=0, keepdims=True)
    slot = slot.astype(jnp.int32)
    width = 8 * slot_stride
    left_half = lax.broadcasted_iota(jnp.int32, (8, 2 * slot_stride), 1) < slot_stride
    for t in range(owners // 8):
        spot = row_ids((width, points)) + t * width
        one_hot = (slot == spot).astype(F32).astype(BF16)
        got = lax.dot_general(vals3, one_hot, (((1,), (1,)), ((), ())), preferred_element_type=F32)
        got = got[0:16] + got[16:32] + got[32:48]
        for pair in range(4):
            cols = slice(pair * 2 * slot_stride, (pair + 1) * 2 * slot_stride)
            low, high = got[0:8, cols], got[8:16, cols]
            out_ref[8 * t + 2 * pair] = jnp.where(left_half, low, pltpu.roll(high, slot_stride, 1))
            out_ref[8 * t + 2 * pair + 1] = jnp.where(left_half, pltpu.roll(low, slot_stride, 1), high)


TILE = 8
DEEP = 6
MID = 4
NEAR = 2


def half_turn(tile):
    return pltpu.roll(tile, TILE // 2, 0)


def scatter_kernel(par_ref, val_ref, mask_ref, out_ref, even_out, odd_out, acc_ref):
    sources = val_ref.shape[0]
    cx, cy, nz = mask_ref.shape
    rows = cx * cy
    chunk = 256
    lanes = val_ref.shape[2]
    left_half = lax.broadcasted_iota(jnp.int32, (8, lanes), 1) < lanes // 2
    acc_ref[...] = jnp.zeros(acc_ref.shape, F32)

    def body(step, carry):
        lows, highs = [], []
        for pair in range(2):
            even, odd = val_ref[4 * step + 2 * pair], val_ref[4 * step + 2 * pair + 1]
            lows.append(jnp.where(left_half, even, pltpu.roll(odd, lanes // 2, 1)))
            highs.append(jnp.where(left_half, pltpu.roll(even, lanes // 2, 1), odd))
        low = jnp.concatenate(lows, axis=1)
        blk = jnp.concatenate([low, jnp.concatenate(highs, axis=1)], axis=0)
        off = blk[6:7, :].astype(jnp.int32)
        row = off // nz
        lz = off - row * nz
        zt = (row_ids((nz, chunk)) == lz).astype(F32).astype(BF16)
        mask = (row_ids((rows, chunk)) == row).astype(F32).astype(BF16)
        hi = blk.astype(BF16)
        lo = (blk - hi.astype(F32)).astype(BF16)
        for i in range(9):
            r = i if i < 6 else i + 1
            left = jnp.concatenate([mask * hi[r : r + 1, :], mask * lo[r : r + 1, :]], axis=0)
            got = lax.dot_general(left, zt, (((1,), (1,)), ((), ())), preferred_element_type=F32)
            acc_ref[i] += got[0:rows] + got[rows:]
        return carry

    lax.fori_loop(0, sources // 4, body, 0)
    sign = (mask_ref[...] == 1).astype(F32) - (mask_ref[...] == 2).astype(F32)
    for i in range(9):
        out_ref[i] = acc_ref[i].reshape(cx, cy, nz) * sign
    upper = row_ids((TILE, nz)) >= TILE // 2

    def write(high, face_ref):
        ys = slice(cy - TILE, cy) if high else slice(0, TILE)
        keep = upper if high else ~upper
        for i in range(3):
            for x in range(cx):
                face_ref[i, x] = jnp.where(keep, out_ref[i, x, ys], half_turn(out_ref[3 + i, x, ys]))

    write_faces(par_ref[0], write, even_out, odd_out)


def write_faces(parity, write, even_out, odd_out):
    @pl.when(parity == 0)
    def _():
        write(True, even_out)
        write(False, odd_out)

    @pl.when(parity != 0)
    def _():
        write(False, even_out)
        write(True, odd_out)


def pair_list(count, odd):
    first = 1 if odd else 0
    pairs = [(i, i + 1) for i in range(first, count - 1, 2)]
    return pairs + [(j, i) for i, j in pairs]


def swap_faces(faces, axis):
    count = lax.axis_size(axis)
    out = []
    for k in (0, 1):
        out.append(lax.ppermute(faces[k], axis, pair_list(count, k)))
    return out


def field_face_kernel(par_ref, cur_ref, ear_ref, coef_ref, even_out, odd_out):
    _, cx, cy, nz = cur_ref.shape
    upper = row_ids((TILE, nz)) >= TILE // 2

    def write(high, face_ref):
        ys = slice(cy - TILE, cy) if high else slice(0, TILE)
        keep = upper if high else ~upper
        for x in range(cx):
            for i in range(3):
                face_ref[i, x] = cur_ref[i, x, ys]
            face_ref[3, x] = jnp.where(keep, ear_ref[0, x, ys], half_turn(ear_ref[1, x, ys]))
            face_ref[4, x] = jnp.where(keep, ear_ref[2, x, ys], half_turn(coef_ref[x, ys]))

    write_faces(par_ref[0], write, even_out, odd_out)


def face_tile(ref, name, x):
    if name < 3:
        return ref[name, x]
    tile = ref[3 + (name - 3) // 2, x]
    return half_turn(tile) if name in (4, 6) else tile


def select_side(parity, even_ref, odd_ref, high):
    from_even = (parity == 0) if high else (parity == 1)

    def read(get):
        return jnp.where(from_even, get(even_ref), get(odd_ref))

    return read


FIELD_PLAN = [(DEEP, MID)] * 3 + [(MID, NEAR)] * 4
FORCE_PLAN = [(MID, NEAR)] * 3 + [(NEAR, 0)] * 3


def plan_tiles(plan, cy):
    out = []
    for name, (planes, corners) in enumerate(plan):
        for dist in range(1, planes + 1):
            for part in list(range(cy // TILE)) + ([-1] if dist <= corners else []):
                out.append((name, dist, part, len(out)))
    return out


def side_kernel(plan, own_tile, halo_tile, cx, cy, nz, px_ref, py_ref, even_ref, odd_ref, even_out, odd_out):
    upper = row_ids((TILE, nz)) >= TILE // 2
    low = select_side(py_ref[0], even_ref, odd_ref, False)
    high = select_side(py_ref[0], even_ref, odd_ref, True)

    def write(is_high, face_ref):
        for name, dist, part, at in plan_tiles(plan, cy):
            x = cx - dist if is_high else dist - 1
            if part >= 0:
                tile = own_tile(name, x, slice(part * TILE, (part + 1) * TILE))
            else:
                tile = jnp.where(
                    upper,
                    low(lambda ref: halo_tile(ref, name, x)),
                    high(lambda ref: halo_tile(ref, name, x)),
                )
            face_ref[at] = tile

    write_faces(px_ref[0], write, even_out, odd_out)


def field_side_kernel(px_ref, py_ref, cur_ref, ear_ref, coef_ref, *refs):
    _, cx, cy, nz = cur_ref.shape

    def own_tile(name, x, ys):
        if name < 3:
            return cur_ref[name, x, ys]
        return ear_ref[name - 3, x, ys] if name < 6 else coef_ref[x, ys]

    side_kernel(FIELD_PLAN, own_tile, face_tile, cx, cy, nz, px_ref, py_ref, *refs)


def force_side_kernel(px_ref, py_ref, force_ref, *refs):
    _, cx, cy, nz = force_ref.shape
    side_kernel(
        FORCE_PLAN,
        lambda name, x, ys: force_ref[name, x, ys],
        lambda ref, name, x: ref[name, x],
        cx, cy, nz, px_ref, py_ref, *refs,
    )


def laplacian(plane, x_near, x_far):
    rows, nz = plane.shape
    lane = lax.broadcasted_iota(jnp.int32, (rows, nz), 1)

    def along_z(k):
        below = jnp.where(lane >= k, pltpu.roll(plane, k, 1), 0.0)
        return below + jnp.where(lane < nz - k, pltpu.roll(plane, nz - k, 1), 0.0)

    def along_y(k):
        return pltpu.roll(plane, k, 0) + pltpu.roll(plane, rows - k, 0)

    near = x_near + along_y(1) + along_z(1)
    far = x_far + along_y(2) + along_z(2)
    return centre_weight * plane + near_weight * near + far_weight * far


def laplacian_at(ref, i, x):
    return laplacian(ref[i, x], ref[i, x - 1] + ref[i, x + 1], ref[i, x - 2] + ref[i, x + 2])


def first_wave_kernel(
    px_ref, py_ref, cur_ref, ear_ref, coef_ref, ye_ref, yo_ref, xe_ref, xo_ref,
    next_ref, now_ref, wide_coef_ref, u_ref, e_ref, c_ref,
):
    _, cx, cy, _ = cur_ref.shape
    own = slice(TILE, TILE + cy)
    lower, higher = slice(0, TILE), slice(TILE + cy, 2 * TILE + cy)
    low = select_side(py_ref[0], ye_ref, yo_ref, False)
    high = select_side(py_ref[0], ye_ref, yo_ref, True)

    def put(name, x, rows, value):
        if name < 3:
            u_ref[name, DEEP + x, rows] = value
        elif name < 6:
            e_ref[name - 3, MID + x, rows] = value
        else:
            c_ref[MID + x, rows] = value

    for x in range(cx):
        for name in range(7):
            value = cur_ref[name, x] if name < 3 else ear_ref[name - 3, x] if name < 6 else coef_ref[x]
            put(name, x, own, value)
            put(name, x, lower, low(lambda ref: face_tile(ref, name, x)))
            put(name, x, higher, high(lambda ref: face_tile(ref, name, x)))
    for is_high in (False, True):
        read = select_side(px_ref[0], xe_ref, xo_ref, is_high)
        for name, dist, part, at in plan_tiles(FIELD_PLAN, cy):
            x = cx - 1 + dist if is_high else -dist
            tile = read(lambda ref: ref[at])
            if part >= 0:
                put(name, x, slice(TILE * (part + 1), TILE * (part + 2)), tile)
            else:
                put(name, x, lower, tile)
                put(name, x, higher, tile)

    def plane(x, carry):
        coef = c_ref[x]
        for i in range(3):
            at = x + DEEP - MID
            next_ref[i, x] = 2.0 * u_ref[i, at] - e_ref[i, x] + coef * laplacian_at(u_ref, i, at)
        return carry

    lax.fori_loop(0, cx + 2 * MID, plane, 0)
    for i in range(3):
        now_ref[i] = u_ref[i, DEEP - NEAR : DEEP + cx + NEAR]
    wide_coef_ref[...] = c_ref[MID - NEAR : MID + cx + NEAR]


def last_wave_kernel(
    px_ref, py_ref, next_ref, now_ref, coef_ref, force_ref, ye_ref, yo_ref, xe_ref, xo_ref,
    final_ref, prior_ref, one_ref, two_ref,
):
    _, cx, cy, _ = force_ref.shape
    own = slice(TILE, TILE + cy)
    lower, higher = slice(0, TILE), slice(TILE + cy, 2 * TILE + cy)
    low = select_side(py_ref[0], ye_ref, yo_ref, False)
    high = select_side(py_ref[0], ye_ref, yo_ref, True)
    one_ref[...] = next_ref[...]
    for i in range(3):
        for x in range(cx):
            one_ref[i, MID + x, own] += force_ref[i, x]
            two_ref[i, NEAR + x, own] = force_ref[3 + i, x]
            for rows, read in ((lower, low), (higher, high)):
                tile = read(lambda ref: ref[i, x])
                one_ref[i, MID + x, rows] += tile
                two_ref[i, NEAR + x, rows] = half_turn(tile)
    for is_high in (False, True):
        read = select_side(px_ref[0], xe_ref, xo_ref, is_high)
        for name, dist, part, at in plan_tiles(FORCE_PLAN, cy):
            x = cx - 1 + dist if is_high else -dist
            tile = read(lambda ref: ref[at])
            if name >= 3:
                two_ref[name - 3, NEAR + x, slice(TILE * (part + 1), TILE * (part + 2))] = tile
            elif part >= 0:
                one_ref[name, MID + x, slice(TILE * (part + 1), TILE * (part + 2))] += tile
            else:
                one_ref[name, MID + x, lower] += tile
                one_ref[name, MID + x, higher] += tile

    def second(x, carry):
        coef = coef_ref[x]
        for i in range(3):
            at = x + MID - NEAR
            lap = laplacian_at(one_ref, i, at)
            two_ref[i, x] = 2.0 * one_ref[i, at] - now_ref[i, x] + coef * lap + two_ref[i, x]
        return carry

    lax.fori_loop(0, cx + 2 * NEAR, second, 0)

    def third(x, carry):
        coef = coef_ref[x + NEAR]
        for i in range(3):
            at = x + NEAR
            plane = two_ref[i, at]
            moved = 2.0 * plane - one_ref[i, x + MID] + coef * laplacian_at(two_ref, i, at)
            final_ref[i, x] = moved[TILE : TILE + cy] + force_ref[6 + i, x]
            prior_ref[i, x] = plane[TILE : TILE + cy]
        return carry

    lax.fori_loop(0, cx, third, 0)


def local(
    current_field,
    earlier_field,
    wave_coef,
    layer_mask,
    point_xyz,
    point_owner,
    cell_offset,
    wave_vector,
    frequency,
    amplitude,
    phase_index,
    phase_table,
):
    table_size = phase_table.shape[0]
    matches = (phase_index[None, :] == jnp.arange(table_size)[:, None]).astype(F32)
    phases = jnp.dot(
        phase_table[None, :], matches, precision=lax.Precision.HIGHEST, preferred_element_type=F32
    )[0]
    own_block = jnp.concatenate(
        [wave_vector, frequency[None, :], amplitude, phases[None, :]], axis=0
    )
    point_count = point_xyz.shape[1]
    slab_count = lax.axis_size("slab")
    comp_count = lax.axis_size("comp")
    device_count = slab_count * comp_count
    slot_count = max(2, 2 * point_count // device_count)
    _, cx, cy, nz = current_field.shape
    assert slot_count <= HALF and device_count % 8 == 0
    assert cx >= DEEP and cy >= 2 * TILE and cy % TILE == 0
    wide = cy + 2 * TILE
    smem = pl.BlockSpec(memory_space=pltpu.SMEM)
    vmem = pl.BlockSpec(memory_space=pltpu.VMEM)

    def call(kernel, operands, shapes, scratch=(), scalars=0):
        shapes = [jax.ShapeDtypeStruct(shape, F32) for shape in shapes]
        return pl.pallas_call(
            kernel,
            out_shape=shapes,
            in_specs=[smem] * scalars + [vmem] * (len(operands) - scalars),
            out_specs=[vmem] * len(shapes),
            scratch_shapes=[pltpu.VMEM(shape, F32) for shape in scratch],
            compiler_params=pltpu.CompilerParams(vmem_limit_bytes=VMEM_GRANT),
        )(*operands)

    px = (lax.axis_index("slab") % 2).astype(jnp.int32).reshape(1)
    py = (lax.axis_index("comp") % 2).astype(jnp.int32).reshape(1)
    if comp_count == 4:
        near_block = lax.ppermute(own_block, "comp", pair_list(4, 0))
        first_blocks = [own_block, near_block]
        ring = pair_list(4, 1) + [(0, 3), (3, 0)]
        far_block = lax.ppermute(jnp.concatenate(first_blocks, axis=1), "comp", ring)
        last_blocks = [far_block]
    else:
        first_blocks = [own_block]
        last_blocks = [
            lax.ppermute(own_block, "comp", [(i, (i + k) % comp_count) for i in range(comp_count)])
            for k in range(1, comp_count)
        ]
    fields = (current_field, earlier_field, wave_coef)
    faces = call(field_face_kernel, (py, *fields), [(5, cx, TILE, nz)] * 2, scalars=1)
    ye, yo = swap_faces(faces, "comp")
    (sum_one, total_one) = call(
        lambda *refs: first_incident_kernel(len(first_blocks), *refs),
        (*first_blocks, point_xyz),
        [(32, point_count), (16, 256)],
        [(8, point_count)],
    )
    field_tiles = len(plan_tiles(FIELD_PLAN, cy))
    sides = call(field_side_kernel, (px, py, *fields, ye, yo), [(field_tiles, TILE, nz)] * 2, scalars=2)
    xe, xo = swap_faces(sides, "slab")
    (packed,) = call(
        lambda *refs: last_incident_kernel(len(last_blocks), HALF, *refs),
        (
            *last_blocks, sum_one, total_one, point_xyz,
            point_owner.reshape(1, point_count), cell_offset.reshape(1, point_count),
        ),
        [(device_count, 8, 2 * HALF)],
        [(8, point_count), (32, point_count)],
    )
    arrived = lax.all_to_all(packed, ("slab", "comp"), split_axis=0, concat_axis=0, tiled=True)
    force, *force_faces = call(
        scatter_kernel,
        (py, arrived, layer_mask),
        [(9, cx, cy, nz)] + [(3, cx, TILE, nz)] * 2,
        [(9, cx * cy, nz)],
        scalars=1,
    )
    fye, fyo = swap_faces(force_faces, "comp")
    force_tiles = len(plan_tiles(FORCE_PLAN, cy))
    force_sides = call(force_side_kernel, (px, py, force, fye, fyo), [(force_tiles, TILE, nz)] * 2, scalars=2)
    fxe, fxo = swap_faces(force_sides, "slab")
    following, now, wide_coef = call(
        first_wave_kernel,
        (px, py, *fields, ye, yo, xe, xo),
        [(3, cx + 2 * MID, wide, nz), (3, cx + 2 * NEAR, wide, nz), (cx + 2 * NEAR, wide, nz)],
        [(3, cx + 2 * DEEP, wide, nz), (3, cx + 2 * MID, wide, nz), (cx + 2 * MID, wide, nz)],
        scalars=2,
    )
    final, prior = call(
        last_wave_kernel,
        (px, py, following, now, wide_coef, force, fye, fyo, fxe, fxo),
        [current_field.shape, current_field.shape],
        [(3, cx + 2 * MID, wide, nz), (3, cx + 2 * NEAR, wide, nz)],
        scalars=2,
    )
    return (final, prior)


def solution(mesh):
    in_specs = (
        P(None, "slab", "comp", None),
        P(None, "slab", "comp", None),
        P("slab", "comp", None),
        P("slab", "comp", None),
        P(None, ("slab", "comp")),
        P(("slab", "comp"), None),
        P(("slab", "comp")),
        P(None, "comp"),
        P("comp"),
        P(None, "comp"),
        P("comp"),
        P(),
    )
    out_specs = (P(None, "slab", "comp", None), P(None, "slab", "comp", None))
    return jax.shard_map(local, mesh=mesh, in_specs=in_specs, out_specs=out_specs, check_vma=False)
```

```python
import jax
import jax.numpy as jnp
from jax import lax
from jax.experimental import pallas as pl
from jax.experimental.pallas import tpu as pltpu
from jax.sharding import PartitionSpec as P

step_size = 0.05
near_weight = 4.0 / 3.0
far_weight = -1.0 / 12.0
centre_weight = -7.5
inv_two_pi = 0.15915494309189535

LEAD = -0.7713118195533752
SIN_C = (4.442834854125977 / LEAD, -7.306587219238281 / LEAD, 3.588636875152588 / LEAD)
SIN_SCALE = LEAD * abs(LEAD)
VER_SCALE = LEAD * LEAD
HALF = 64
OWN_TILES = 5
SIDE_TILES = 4
HIGH_LIST = OWN_TILES
LOW_LIST = OWN_TILES + SIDE_TILES
LIST_ROWS = 16
VMEM_GRANT = 16 * 2**20

F32 = jnp.float32
BF16 = jnp.bfloat16


def sin_versine(u):
    r = u - jnp.round(u)
    z = r * r
    s = r * (((z + SIN_C[2]) * z + SIN_C[1]) * z + SIN_C[0])
    q = s * s
    w = 2.0 / VER_SCALE - q
    return s * (w * lax.rsqrt(w)), q


def split_three(x):
    hi = x.astype(BF16).astype(F32)
    rest = x - hi
    mid = rest.astype(BF16).astype(F32)
    return hi, mid, rest - mid


def row_ids(shape):
    return lax.broadcasted_iota(jnp.int32, shape, 0)


def add_components(par_refs, xyz_ref, x8_ref, acc_ref):
    points = xyz_ref.shape[1]
    kc = 256
    tile = 256
    x8_ref[...] = jnp.zeros(x8_ref.shape, F32)
    x8_ref[0:3, :] = xyz_ref[...]
    xhi, xmid, xlo = split_three(x8_ref[...])
    right = jnp.concatenate([xhi, xmid, xlo, xhi, xmid, xhi], axis=0).astype(BF16)
    rows8 = row_ids((8, kc))
    times = step_size * (rows8 + 1).astype(F32)
    rows16 = row_ids((16, kc))
    comp_row = jnp.where(rows16 < 6, rows16 % 3, (rows16 + 2) % 3)
    valued = (rows16 < 10) & (rows16 != 6)

    def body(par_ref, step, total):
        blk = par_ref[:, pl.ds(pl.multiple_of(step * kc, kc), kc)]
        kv = jnp.where(rows8 < 3, blk * inv_two_pi, 0.0)
        khi, kmid, klo = split_three(kv)
        left = jnp.concatenate([khi, khi, khi, kmid, kmid, klo], axis=0).astype(BF16)
        delays = times * blk[3:4, :] - blk[7:8, :]
        sd, qd = sin_versine(delays * inv_two_pi)
        sd, cd = SIN_SCALE * sd, 1.0 - VER_SCALE * qd
        amp = jnp.where(comp_row == 0, blk[4:5, :], jnp.where(comp_row == 1, blk[5:6, :], blk[6:7, :]))
        amp = jnp.where(valued, amp, 0.0)

        def rows_of(t):
            w = amp * jnp.where(rows16 < 3, t[0:1, :], jnp.where(rows16 < 6, t[1:2, :], t[2:3, :]))
            hi = w.astype(BF16)
            lo = (w - hi.astype(F32)).astype(BF16)
            return w, jnp.concatenate([hi, lo], axis=0)

        wc = rows_of(cd)[0]
        lc = rows_of(-VER_SCALE * cd)[1]
        ls = rows_of(SIN_SCALE * sd)[1]
        for t in range(points // tile):
            cols = slice(t * tile, (t + 1) * tile)
            u = lax.dot_general(left, right[:, cols], (((0,), (0,)), ((), ())), preferred_element_type=F32)
            highs, lows = [], []
            for j in range(kc // 32):
                for value in sin_versine(u[32 * j : 32 * j + 32]):
                    high = value.astype(BF16)
                    highs.append(high)
                    lows.append((value - high.astype(F32)).astype(BF16))
            part = jnp.dot(ls, jnp.concatenate(highs[0::2], axis=0), preferred_element_type=F32)
            part += jnp.dot(lc, jnp.concatenate(highs[1::2], axis=0), preferred_element_type=F32)
            part += jnp.dot(ls, jnp.concatenate(lows[0::2], axis=0), preferred_element_type=F32)
            part += jnp.dot(lc, jnp.concatenate(lows[1::2], axis=0), preferred_element_type=F32)
            acc_ref[:, cols] += part
        return total + wc

    total = jnp.zeros((16, kc), F32)
    for par_ref in par_refs:
        steps = par_ref.shape[1] // kc
        total = lax.fori_loop(0, steps, lambda step, t, ref=par_ref: body(ref, step, t), total)
    return total


def first_incident_kernel(count, *refs):
    par_refs, (xyz_ref, acc_ref, total_ref, x8_ref) = refs[:count], refs[count:]
    acc_ref[...] = jnp.zeros(acc_ref.shape, F32)
    total_ref[...] = add_components(par_refs, xyz_ref, x8_ref, acc_ref)


def last_incident_kernel(count, step, *refs):
    par_refs, refs = refs[:count], refs[count:]
    first_ref, first_total_ref, xyz_ref, own_ref, off_ref, out_ref, x8_ref, acc_ref = refs
    points = xyz_ref.shape[1]
    owners = out_ref.shape[0]
    acc_ref[...] = first_ref[...]
    total = add_components(par_refs, xyz_ref, x8_ref, acc_ref) + first_total_ref[...]
    vals = acc_ref[0:16, :] + acc_ref[16:32, :] + jnp.sum(total, axis=1, keepdims=True)
    vals = jnp.where(row_ids((16, points)) == 6, off_ref[...].astype(F32), vals)
    v1, v2, v3 = split_three(vals)
    named = own_ref[...] == row_ids((owners, points))
    named_one = named.astype(F32).astype(BF16)
    earlier = row_ids((points, points)) < lax.broadcasted_iota(jnp.int32, (points, points), 1)
    before = jnp.dot(named_one, earlier.astype(F32).astype(BF16), preferred_element_type=F32)
    rank = jnp.sum(jnp.where(named, before, 0.0), axis=0, keepdims=True).astype(jnp.int32)
    terms = [v.astype(BF16) for v in (v1, v2, v3)]
    tiles = 0.0
    for odd in (0, 1):
        left = jnp.concatenate(
            [named_one * t[2 * j + odd : 2 * j + odd + 1, :] for t in terms for j in range(OWN_TILES)], axis=0
        )
        spots = (row_ids((2 * HALF, points)) == rank + odd * HALF).astype(F32).astype(BF16)
        got = lax.dot_general(left, spots, (((1,), (1,)), ((), ())), preferred_element_type=F32)
        size = OWN_TILES * owners
        tiles = tiles + (got[0:size] + got[size : 2 * size] + got[2 * size :])
    owner_row = row_ids((owners, 2 * HALF))
    for j in range(OWN_TILES):
        tile = tiles[j * owners : (j + 1) * owners]
        out_ref[:, j, :] = tile
        if j < SIDE_TILES:
            above = pltpu.roll(tile, owners - step, 0)
            out_ref[:, HIGH_LIST + j, :] = jnp.where(owner_row < owners - step, above, 0.0)
            out_ref[:, LOW_LIST + j, :] = jnp.where(owner_row >= step, pltpu.roll(tile, step, 0), 0.0)
    for j in range(LOW_LIST + SIDE_TILES, LIST_ROWS):
        out_ref[:, j, :] = jnp.zeros((owners, 2 * HALF), F32)


TILE = 8
DEEP = 6
MID = 4
NEAR = 2


def half_turn(tile):
    return pltpu.roll(tile, TILE // 2, 0)


def scatter_kernel(par_ref, val_ref, sign_ref, zero_out, one_out, two_out, even_out, odd_out, zero_ref, one_ref, two_ref):
    sources, _, lanes = val_ref.shape
    _, cx, cy, nz = two_out.shape
    rows, mid, near = cx * cy, MID * cy, NEAR * cy
    chunk = 2 * lanes
    left_half = lax.broadcasted_iota(jnp.int32, (LIST_ROWS, lanes), 1) < lanes // 2
    for ref in (zero_ref, one_ref, two_ref):
        ref[...] = jnp.zeros(ref.shape, F32)

    def body(step, carry):
        evens, odds = [], []
        for pair in range(2):
            first, second = val_ref[4 * step + 2 * pair], val_ref[4 * step + 2 * pair + 1]
            evens.append(jnp.where(left_half, first, pltpu.roll(second, lanes // 2, 1)))
            odds.append(jnp.where(left_half, pltpu.roll(first, lanes // 2, 1), second))
        values = [jnp.concatenate(evens, axis=1), jnp.concatenate(odds, axis=1)]
        high = [v.astype(BF16) for v in values]
        low = [(v - h.astype(F32)).astype(BF16) for v, h in zip(values, high)]

        def spread(base, r, mask, zt, ref, i, start):
            at = base + r // 2
            left = jnp.concatenate([mask * t[r % 2][at : at + 1, :] for t in (high, low)], axis=0)
            got = lax.dot_general(left, zt, (((1,), (1,)), ((), ())), preferred_element_type=F32)
            size = mask.shape[0]
            ref[i, start : start + size] += got[0:size] + got[size:]

        for base, count, shift in ((0, rows, 0), (HIGH_LIST, mid, 0), (LOW_LIST, mid, rows - mid)):
            off = values[0][base + 3 : base + 4, :].astype(jnp.int32)
            row = off // nz
            zt = (row_ids((nz, chunk)) == off - row * nz).astype(F32).astype(BF16)
            mask = (row_ids((count, chunk)) == row - shift).astype(F32).astype(BF16)
            for i in range(3):
                if base == 0:
                    spread(base, i, mask, zt, zero_ref, i, mid)
                    spread(base, 3 + i, mask, zt, one_ref, i, near)
                    spread(base, 7 + i, mask, zt, two_ref, i, 0)
                elif base == HIGH_LIST:
                    spread(base, i, mask, zt, zero_ref, i, mid + rows)
                    spread(base, 3 + i, mask[0:near], zt, one_ref, i, near + rows)
                else:
                    spread(base, i, mask, zt, zero_ref, i, 0)
                    spread(base, 3 + i, mask[mid - near :], zt, one_ref, i, 0)
        return carry

    lax.fori_loop(0, sources // 4, body, 0)
    sign = sign_ref[...]
    for i in range(3):
        zero_out[i] = zero_ref[i].reshape(zero_out.shape[1:]) * sign
        one_out[i] = one_ref[i].reshape(one_out.shape[1:]) * sign[MID - NEAR : MID + cx + NEAR]
        two_out[i] = two_ref[i].reshape(two_out.shape[1:]) * sign[MID : MID + cx]
    at = row_ids((TILE, nz))

    def write(is_high, face_ref):
        ys = slice(cy - TILE, cy) if is_high else slice(0, TILE)
        half = at >= TILE // 2 if is_high else at < TILE // 2
        corner = at < NEAR if is_high else at >= TILE - NEAR
        for i in range(3):
            for x in range(cx):
                tile = jnp.where(half, zero_out[i, MID + x, ys], half_turn(one_out[i, NEAR + x, ys]))
                if x < 2 * NEAR:
                    moved = pltpu.roll(zero_out[i, MID + corner_plane(x, cx), ys], NEAR if is_high else TILE - NEAR, 0)
                    tile = jnp.where(corner, moved, tile)
                face_ref[i, x] = tile

    write_faces(par_ref[0], write, even_out, odd_out)


def corner_plane(x, cx):
    return x - NEAR if x < NEAR else cx + x - NEAR


def write_faces(parity, write, even_out, odd_out):
    @pl.when(parity == 0)
    def _():
        write(True, even_out)
        write(False, odd_out)

    @pl.when(parity != 0)
    def _():
        write(False, even_out)
        write(True, odd_out)


def pair_list(count, odd):
    first = 1 if odd else 0
    pairs = [(i, i + 1) for i in range(first, count - 1, 2)]
    return pairs + [(j, i) for i, j in pairs]


def swap_faces(faces, axis):
    count = lax.axis_size(axis)
    out = []
    for k in (0, 1):
        out.append(lax.ppermute(faces[k], axis, pair_list(count, k)))
    return out


def field_face_kernel(par_ref, cur_ref, ear_ref, coef_ref, even_out, odd_out):
    _, cx, cy, nz = cur_ref.shape
    upper = row_ids((TILE, nz)) >= TILE // 2

    def write(high, face_ref):
        ys = slice(cy - TILE, cy) if high else slice(0, TILE)
        keep = upper if high else ~upper
        for x in range(cx):
            for i in range(3):
                face_ref[i, x] = cur_ref[i, x, ys]
            face_ref[3, x] = jnp.where(keep, ear_ref[0, x, ys], half_turn(ear_ref[1, x, ys]))
            face_ref[4, x] = jnp.where(keep, ear_ref[2, x, ys], half_turn(coef_ref[x, ys]))

    write_faces(par_ref[0], write, even_out, odd_out)


def face_tile(ref, name, x):
    if name < 3:
        return ref[name, x]
    tile = ref[3 + (name - 3) // 2, x]
    return half_turn(tile) if name in (4, 6) else tile


def select_side(parity, even_ref, odd_ref, high):
    from_even = (parity == 0) if high else (parity == 1)

    def read(get):
        return jnp.where(from_even, get(even_ref), get(odd_ref))

    return read


FIELD_PLAN = [(DEEP, MID)] * 3 + [(MID, NEAR)] * 4 + [(MID, 0)]


def plan_tiles(plan, cy):
    out = []
    for name, (planes, corners) in enumerate(plan):
        for dist in range(1, planes + 1):
            for part in list(range(cy // TILE)) + ([-1] if dist <= corners else []):
                out.append((name, dist, part, len(out)))
    return out


def side_kernel(plan, own_tile, halo_tile, cx, cy, nz, px_ref, py_ref, even_ref, odd_ref, even_out, odd_out):
    upper = row_ids((TILE, nz)) >= TILE // 2
    low = select_side(py_ref[0], even_ref, odd_ref, False)
    high = select_side(py_ref[0], even_ref, odd_ref, True)

    def write(is_high, face_ref):
        for name, dist, part, at in plan_tiles(plan, cy):
            x = cx - dist if is_high else dist - 1
            if part >= 0:
                tile = own_tile(name, x, slice(part * TILE, (part + 1) * TILE))
            else:
                tile = jnp.where(
                    upper,
                    low(lambda ref: halo_tile(ref, name, x)),
                    high(lambda ref: halo_tile(ref, name, x)),
                )
            face_ref[at] = tile

    write_faces(px_ref[0], write, even_out, odd_out)


def sign_of(mask):
    return (mask == 1).astype(F32) - (mask == 2).astype(F32)


def field_side_kernel(px_ref, py_ref, cur_ref, ear_ref, coef_ref, mask_ref, *refs):
    _, cx, cy, nz = cur_ref.shape

    def own_tile(name, x, ys):
        if name < 3:
            return cur_ref[name, x, ys]
        if name < 6:
            return ear_ref[name - 3, x, ys]
        return coef_ref[x, ys] if name == 6 else sign_of(mask_ref[x, ys])

    side_kernel(FIELD_PLAN, own_tile, face_tile, cx, cy, nz, px_ref, py_ref, *refs)


def laplacian(plane, x_near, x_far):
    rows, nz = plane.shape
    width = 128
    lane = lax.broadcasted_iota(jnp.int32, (rows, width), 1)
    parts = [plane[:, k : k + width] for k in range(0, nz, width)]

    def along_z(k):
        up = [pltpu.roll(p, k, 1) for p in parts]
        down = [pltpu.roll(p, width - k, 1) for p in parts]
        out = []
        for j in range(len(parts)):
            below = jnp.where(lane >= k, up[j], up[j - 1] if j else 0.0)
            above = jnp.where(lane < width - k, down[j], down[j + 1] if j + 1 < len(parts) else 0.0)
            out.append(below + above)
        return jnp.concatenate(out, axis=1)

    def along_y(k):
        return pltpu.roll(plane, k, 0) + pltpu.roll(plane, rows - k, 0)

    near = x_near + along_y(1) + along_z(1)
    far = x_far + along_y(2) + along_z(2)
    return centre_weight * plane + near_weight * near + far_weight * far


def laplacian_at(ref, i, x):
    return laplacian(ref[i, x], ref[i, x - 1] + ref[i, x + 1], ref[i, x - 2] + ref[i, x + 2])


def first_wave_kernel(
    px_ref, py_ref, cur_ref, ear_ref, coef_ref, mask_ref, ye_ref, yo_ref, xe_ref, xo_ref,
    final_ref, prior_ref, wide_coef_ref, wide_sign_ref, u_ref, e_ref, c_ref, one_ref, two_ref,
):
    _, cx, cy, _ = cur_ref.shape
    own = slice(TILE, TILE + cy)
    lower, higher = slice(0, TILE), slice(TILE + cy, 2 * TILE + cy)
    low = select_side(py_ref[0], ye_ref, yo_ref, False)
    high = select_side(py_ref[0], ye_ref, yo_ref, True)

    def put(name, x, rows, value):
        if name < 3:
            u_ref[name, DEEP + x, rows] = value
        elif name < 6:
            e_ref[name - 3, MID + x, rows] = value
        elif name == 6:
            c_ref[MID + x, rows] = value
        else:
            wide_sign_ref[MID + x, slice(rows.start - TILE, rows.stop - TILE)] = value

    for x in range(cx):
        for name in range(7):
            value = cur_ref[name, x] if name < 3 else ear_ref[name - 3, x] if name < 6 else coef_ref[x]
            put(name, x, own, value)
            put(name, x, lower, low(lambda ref: face_tile(ref, name, x)))
            put(name, x, higher, high(lambda ref: face_tile(ref, name, x)))
        put(7, x, own, sign_of(mask_ref[x]))
    for is_high in (False, True):
        read = select_side(px_ref[0], xe_ref, xo_ref, is_high)
        for name, dist, part, at in plan_tiles(FIELD_PLAN, cy):
            x = cx - 1 + dist if is_high else -dist
            tile = read(lambda ref: ref[at])
            if part >= 0:
                put(name, x, slice(TILE * (part + 1), TILE * (part + 2)), tile)
            else:
                put(name, x, lower, tile)
                put(name, x, higher, tile)

    def first(x, carry):
        for i in range(3):
            at = x + DEEP - MID
            one_ref[i, x] = 2.0 * u_ref[i, at] - e_ref[i, x] + c_ref[x] * laplacian_at(u_ref, i, at)
        return carry

    def second(x, carry):
        at = x + MID - NEAR
        coef = c_ref[at]
        wide_coef_ref[x] = coef
        for i in range(3):
            lap = laplacian_at(one_ref, i, at)
            two_ref[i, x] = 2.0 * one_ref[i, at] - u_ref[i, x + DEEP - NEAR] + coef * lap
        return carry

    def third(x, carry):
        for i in range(3):
            at = x + NEAR
            plane = two_ref[i, at]
            moved = 2.0 * plane - one_ref[i, x + MID] + c_ref[x + MID] * laplacian_at(two_ref, i, at)
            final_ref[i, x] = moved[own]
            prior_ref[i, x] = plane[own]
        return carry

    lax.fori_loop(0, cx + 2 * MID, first, 0)
    lax.fori_loop(0, cx + 2 * NEAR, second, 0)
    lax.fori_loop(0, cx, third, 0)


def last_wave_kernel(
    py_ref, free_final_ref, free_prior_ref, coef_ref, zero_in, one_in, two_in, ye_ref, yo_ref,
    final_ref, prior_ref, one_ref, two_ref,
):
    _, cx, cy, _ = two_in.shape
    own = slice(TILE, TILE + cy)
    lower, higher = slice(0, TILE), slice(TILE + cy, 2 * TILE + cy)
    low = select_side(py_ref[0], ye_ref, yo_ref, False)
    high = select_side(py_ref[0], ye_ref, yo_ref, True)
    for i in range(3):
        for x in range(cx + 2 * MID):
            one_ref[i, x, own] = zero_in[i, x]
        for x in range(cx + 2 * NEAR):
            two_ref[i, x, own] = one_in[i, x]
        for x in range(cx):
            for rows, read, turn in ((lower, low, TILE - NEAR), (higher, high, NEAR)):
                tile = read(lambda ref: ref[i, x])
                one_ref[i, MID + x, rows] = tile
                two_ref[i, NEAR + x, rows] = half_turn(tile)
                if x < 2 * NEAR:
                    one_ref[i, MID + corner_plane(x, cx), rows] = pltpu.roll(tile, turn, 0)

    def second(x, carry):
        coef = coef_ref[x]
        for i in range(3):
            at = x + MID - NEAR
            two_ref[i, x] = 2.0 * one_ref[i, at] + coef * laplacian_at(one_ref, i, at) + two_ref[i, x]
        return carry

    lax.fori_loop(0, cx + 2 * NEAR, second, 0)

    def third(x, carry):
        coef = coef_ref[x + NEAR]
        for i in range(3):
            at = x + NEAR
            plane = two_ref[i, at]
            moved = 2.0 * plane - one_ref[i, x + MID] + coef * laplacian_at(two_ref, i, at)
            final_ref[i, x] = free_final_ref[i, x] + (moved[own] + two_in[i, x])
            prior_ref[i, x] = free_prior_ref[i, x] + plane[own]
        return carry

    lax.fori_loop(0, cx, third, 0)


def staged(kernel, positions, operand_count):
    def run(*refs):
        refs, stages, sems = refs[: -len(positions) - 1], refs[-len(positions) - 1 : -1], refs[-1]
        ins = list(refs[:operand_count])
        copies = []
        for k, (at, stage) in enumerate(zip(positions, stages)):
            copies.append(pltpu.make_async_copy(ins[at], stage, sems.at[k]))
            ins[at] = stage
        for copy in copies:
            copy.start()
        for copy in copies:
            copy.wait()
        kernel(*ins, *refs[operand_count:])

    return run


def local(
    current_field,
    earlier_field,
    wave_coef,
    layer_mask,
    point_xyz,
    point_owner,
    cell_offset,
    wave_vector,
    frequency,
    amplitude,
    phase_index,
    phase_table,
):
    table_size = phase_table.shape[0]
    matches = (phase_index[None, :] == jnp.arange(table_size)[:, None]).astype(F32)
    phases = jnp.dot(
        phase_table[None, :], matches, precision=lax.Precision.HIGHEST, preferred_element_type=F32
    )[0]
    own_block = jnp.concatenate(
        [wave_vector, frequency[None, :], amplitude, phases[None, :]], axis=0
    )
    point_count = point_xyz.shape[1]
    slab_count = lax.axis_size("slab")
    comp_count = lax.axis_size("comp")
    device_count = slab_count * comp_count
    slot_count = max(2, 2 * point_count // device_count)
    _, cx, cy, nz = current_field.shape
    assert slot_count <= HALF and device_count % 8 == 0
    assert cx >= DEEP and cy >= 2 * TILE and cy % TILE == 0
    wide = cy + 2 * TILE
    smem = pl.BlockSpec(memory_space=pltpu.SMEM)
    vmem = pl.BlockSpec(memory_space=pltpu.VMEM)

    def call(kernel, operands, shapes, scratch=(), scalars=0, from_hbm=(), to_hbm=False):
        shapes = [(pltpu.HBM if to_hbm else jax.ShapeDtypeStruct)(shape, F32) for shape in shapes]
        operands = list(operands)
        in_specs = [smem] * scalars + [vmem] * (len(operands) - scalars)
        scratch_shapes = [pltpu.VMEM(shape, F32) for shape in scratch]
        if from_hbm:
            for at in from_hbm:
                operands[at] = pltpu.with_memory_space_constraint(operands[at], pltpu.HBM)
                in_specs[at] = pl.BlockSpec(memory_space=pltpu.HBM)
                scratch_shapes.append(pltpu.VMEM(operands[at].shape, operands[at].dtype))
            scratch_shapes.append(pltpu.SemaphoreType.DMA((len(from_hbm),)))
            kernel = staged(kernel, from_hbm, len(operands))
        return pl.pallas_call(
            kernel,
            out_shape=shapes,
            in_specs=in_specs,
            out_specs=[vmem] * len(shapes),
            scratch_shapes=scratch_shapes,
            compiler_params=pltpu.CompilerParams(vmem_limit_bytes=VMEM_GRANT),
        )(*operands)

    px = (lax.axis_index("slab") % 2).astype(jnp.int32).reshape(1)
    py = (lax.axis_index("comp") % 2).astype(jnp.int32).reshape(1)
    if comp_count == 4:
        near_block = lax.ppermute(own_block, "comp", pair_list(4, 0))
        first_blocks = [own_block, near_block]
        ring = pair_list(4, 1) + [(0, 3), (3, 0)]
        far_block = lax.ppermute(jnp.concatenate(first_blocks, axis=1), "comp", ring)
        last_blocks = [far_block]
    else:
        first_blocks = [own_block]
        last_blocks = [
            lax.ppermute(own_block, "comp", [(i, (i + k) % comp_count) for i in range(comp_count)])
            for k in range(1, comp_count)
        ]
    fields = (current_field, earlier_field, wave_coef)
    faces = call(field_face_kernel, (py, *fields), [(5, cx, TILE, nz)] * 2, scalars=1, from_hbm=(1, 2, 3))
    ye, yo = swap_faces(faces, "comp")
    (sum_one, total_one) = call(
        lambda *refs: first_incident_kernel(len(first_blocks), *refs),
        (*first_blocks, point_xyz),
        [(32, point_count), (16, 256)],
        [(8, point_count)],
    )
    field_tiles = len(plan_tiles(FIELD_PLAN, cy))
    sides = call(
        field_side_kernel,
        (px, py, *fields, layer_mask, ye, yo),
        [(field_tiles, TILE, nz)] * 2,
        scalars=2,
        from_hbm=(2, 3, 4, 5),
    )
    xe, xo = swap_faces(sides, "slab")
    (packed,) = call(
        lambda *refs: last_incident_kernel(len(last_blocks), comp_count, *refs),
        (
            *last_blocks, sum_one, total_one, point_xyz,
            point_owner.reshape(1, point_count), cell_offset.reshape(1, point_count),
        ),
        [(device_count, LIST_ROWS, 2 * HALF)],
        [(8, point_count), (32, point_count)],
    )
    arrived = lax.all_to_all(packed, ("slab", "comp"), split_axis=0, concat_axis=0, tiled=True)
    free_final, free_prior, wide_coef, wide_sign = call(
        first_wave_kernel,
        (px, py, *fields, layer_mask, ye, yo, xe, xo),
        [current_field.shape, current_field.shape, (cx + 2 * NEAR, wide, nz), (cx + 2 * MID, cy, nz)],
        [
            (3, cx + 2 * DEEP, wide, nz), (3, cx + 2 * MID, wide, nz), (cx + 2 * MID, wide, nz),
            (3, cx + 2 * MID, wide, nz), (3, cx + 2 * NEAR, wide, nz),
        ],
        scalars=2,
        from_hbm=(2, 3, 4, 5),
        to_hbm=True,
    )
    *force, face_even, face_odd = call(
        scatter_kernel,
        (py, arrived, wide_sign),
        [(3, cx + 2 * MID, cy, nz), (3, cx + 2 * NEAR, cy, nz), (3, cx, cy, nz)] + [(3, cx, TILE, nz)] * 2,
        [(3, (cx + 2 * MID) * cy, nz), (3, (cx + 2 * NEAR) * cy, nz), (3, cx * cy, nz)],
        scalars=1,
        from_hbm=(2,),
    )
    fye, fyo = swap_faces((face_even, face_odd), "comp")
    final, prior = call(
        last_wave_kernel,
        (py, free_final, free_prior, wide_coef, *force, fye, fyo),
        [current_field.shape, current_field.shape],
        [(3, cx + 2 * MID, wide, nz), (3, cx + 2 * NEAR, wide, nz)],
        scalars=1,
        from_hbm=(1, 2, 3),
    )
    return (final, prior)


def solution(mesh):
    in_specs = (
        P(None, "slab", "comp", None),
        P(None, "slab", "comp", None),
        P("slab", "comp", None),
        P("slab", "comp", None),
        P(None, ("slab", "comp")),
        P(("slab", "comp"), None),
        P(("slab", "comp")),
        P(None, "comp"),
        P("comp"),
        P(None, "comp"),
        P("comp"),
        P(),
    )
    out_specs = (P(None, "slab", "comp", None), P(None, "slab", "comp", None))
    return jax.shard_map(local, mesh=mesh, in_specs=in_specs, out_specs=out_specs, check_vma=False)
```

```python
import jax
import jax.numpy as jnp
from jax import lax
from jax.experimental import pallas as pl
from jax.experimental.pallas import tpu as pltpu
from jax.sharding import PartitionSpec as P

step_size = 0.05
near_weight = 4.0 / 3.0
far_weight = -1.0 / 12.0
centre_weight = -7.5
inv_two_pi = 0.15915494309189535

LEAD = -0.7713118195533752
SIN_C = (4.442834854125977 / LEAD, -7.306587219238281 / LEAD, 3.588636875152588 / LEAD)
SIN_SCALE = LEAD * abs(LEAD)
VER_SCALE = LEAD * LEAD
HALF = 64
OWN_TILES = 5
SIDE_TILES = 4
HIGH_LIST = OWN_TILES
LOW_LIST = OWN_TILES + SIDE_TILES
LIST_ROWS = 16
VMEM_GRANT = 16 * 2**20

F32 = jnp.float32
BF16 = jnp.bfloat16


def sin_versine(u):
    r = u - jnp.round(u)
    z = r * r
    s = r * (((z + SIN_C[2]) * z + SIN_C[1]) * z + SIN_C[0])
    q = s * s
    w = 2.0 / VER_SCALE - q
    return s * (w * lax.rsqrt(w)), q


def split_three(x):
    hi = x.astype(BF16).astype(F32)
    rest = x - hi
    mid = rest.astype(BF16).astype(F32)
    return hi, mid, rest - mid


def row_ids(shape):
    return lax.broadcasted_iota(jnp.int32, shape, 0)


def add_components(par_refs, xyz_ref, x8_ref, acc_ref):
    points = xyz_ref.shape[1]
    kc = 256
    tile = 256
    x8_ref[...] = jnp.zeros(x8_ref.shape, F32)
    x8_ref[0:3, :] = xyz_ref[...]
    xhi, xmid, xlo = split_three(x8_ref[...])
    right = jnp.concatenate([xhi, xmid, xlo, xhi, xmid, xhi], axis=0).astype(BF16)
    rows8 = row_ids((8, kc))
    times = step_size * (rows8 + 1).astype(F32)
    rows16 = row_ids((16, kc))
    comp_row = jnp.where(rows16 < 6, rows16 % 3, (rows16 + 2) % 3)
    valued = (rows16 < 10) & (rows16 != 6)

    def body(par_ref, step, total):
        blk = par_ref[:, pl.ds(pl.multiple_of(step * kc, kc), kc)]
        kv = jnp.where(rows8 < 3, blk * inv_two_pi, 0.0)
        khi, kmid, klo = split_three(kv)
        left = jnp.concatenate([khi, khi, khi, kmid, kmid, klo], axis=0).astype(BF16)
        delays = times * blk[3:4, :] - blk[7:8, :]
        sd, qd = sin_versine(delays * inv_two_pi)
        sd, cd = SIN_SCALE * sd, 1.0 - VER_SCALE * qd
        amp = jnp.where(comp_row == 0, blk[4:5, :], jnp.where(comp_row == 1, blk[5:6, :], blk[6:7, :]))
        amp = jnp.where(valued, amp, 0.0)

        def rows_of(t):
            w = amp * jnp.where(rows16 < 3, t[0:1, :], jnp.where(rows16 < 6, t[1:2, :], t[2:3, :]))
            hi = w.astype(BF16)
            lo = (w - hi.astype(F32)).astype(BF16)
            return w, jnp.concatenate([hi, lo], axis=0)

        wc = rows_of(cd)[0]
        lc = rows_of(-VER_SCALE * cd)[1]
        ls = rows_of(SIN_SCALE * sd)[1]
        for t in range(points // tile):
            cols = slice(t * tile, (t + 1) * tile)
            u = lax.dot_general(left, right[:, cols], (((0,), (0,)), ((), ())), preferred_element_type=F32)
            highs, lows = [], []
            for j in range(kc // 32):
                for value in sin_versine(u[32 * j : 32 * j + 32]):
                    high = value.astype(BF16)
                    highs.append(high)
                    lows.append((value - high.astype(F32)).astype(BF16))
            part = jnp.dot(ls, jnp.concatenate(highs[0::2], axis=0), preferred_element_type=F32)
            part += jnp.dot(lc, jnp.concatenate(highs[1::2], axis=0), preferred_element_type=F32)
            part += jnp.dot(ls, jnp.concatenate(lows[0::2], axis=0), preferred_element_type=F32)
            part += jnp.dot(lc, jnp.concatenate(lows[1::2], axis=0), preferred_element_type=F32)
            acc_ref[:, cols] += part
        return total + wc

    total = jnp.zeros((16, kc), F32)
    for par_ref in par_refs:
        steps = par_ref.shape[1] // kc
        total = lax.fori_loop(0, steps, lambda step, t, ref=par_ref: body(ref, step, t), total)
    return total


def first_incident_kernel(count, *refs):
    par_refs, (xyz_ref, acc_ref, total_ref, x8_ref) = refs[:count], refs[count:]
    acc_ref[...] = jnp.zeros(acc_ref.shape, F32)
    total_ref[...] = add_components(par_refs, xyz_ref, x8_ref, acc_ref)


def last_incident_kernel(count, step, *refs):
    par_refs, refs = refs[:count], refs[count:]
    first_ref, first_total_ref, xyz_ref, own_ref, off_ref, out_ref, x8_ref, acc_ref = refs
    points = xyz_ref.shape[1]
    owners = out_ref.shape[0]
    acc_ref[...] = first_ref[...]
    total = add_components(par_refs, xyz_ref, x8_ref, acc_ref) + first_total_ref[...]
    vals = acc_ref[0:16, :] + acc_ref[16:32, :] + jnp.sum(total, axis=1, keepdims=True)
    vals = jnp.where(row_ids((16, points)) == 6, off_ref[...].astype(F32), vals)
    v1, v2, v3 = split_three(vals)
    named = own_ref[...] == row_ids((owners, points))
    named_one = named.astype(F32).astype(BF16)
    earlier = row_ids((points, points)) < lax.broadcasted_iota(jnp.int32, (points, points), 1)
    before = jnp.dot(named_one, earlier.astype(F32).astype(BF16), preferred_element_type=F32)
    rank = jnp.sum(jnp.where(named, before, 0.0), axis=0, keepdims=True).astype(jnp.int32)
    terms = [v.astype(BF16) for v in (v1, v2, v3)]
    tiles = 0.0
    for odd in (0, 1):
        left = jnp.concatenate(
            [named_one * t[2 * j + odd : 2 * j + odd + 1, :] for t in terms for j in range(OWN_TILES)], axis=0
        )
        spots = (row_ids((2 * HALF, points)) == rank + odd * HALF).astype(F32).astype(BF16)
        got = lax.dot_general(left, spots, (((1,), (1,)), ((), ())), preferred_element_type=F32)
        size = OWN_TILES * owners
        tiles = tiles + (got[0:size] + got[size : 2 * size] + got[2 * size :])
    owner_row = row_ids((owners, 2 * HALF))
    for j in range(OWN_TILES):
        tile = tiles[j * owners : (j + 1) * owners]
        out_ref[:, j, :] = tile
        if j < SIDE_TILES:
            above = pltpu.roll(tile, owners - step, 0)
            out_ref[:, HIGH_LIST + j, :] = jnp.where(owner_row < owners - step, above, 0.0)
            out_ref[:, LOW_LIST + j, :] = jnp.where(owner_row >= step, pltpu.roll(tile, step, 0), 0.0)
    for j in range(LOW_LIST + SIDE_TILES, LIST_ROWS):
        out_ref[:, j, :] = jnp.zeros((owners, 2 * HALF), F32)


TILE = 8
DEEP = 6
MID = 4
NEAR = 2


def half_turn(tile):
    return pltpu.roll(tile, TILE // 2, 0)


def scatter_lists(val_ref, jobs, cy, nz):
    sources, _, lanes = val_ref.shape
    chunk = 2 * lanes
    left_half = lax.broadcasted_iota(jnp.int32, (LIST_ROWS, lanes), 1) < lanes // 2
    for ref in {id(job[4]): job[4] for job in jobs}.values():
        ref[...] = jnp.zeros(ref.shape, F32)

    def body(step, carry):
        evens, odds = [], []
        for pair in range(2):
            first, second = val_ref[4 * step + 2 * pair], val_ref[4 * step + 2 * pair + 1]
            evens.append(jnp.where(left_half, first, pltpu.roll(second, lanes // 2, 1)))
            odds.append(jnp.where(left_half, pltpu.roll(first, lanes // 2, 1), second))
        values = [jnp.concatenate(evens, axis=1), jnp.concatenate(odds, axis=1)]
        high = [v.astype(BF16) for v in values]
        low = [(v - h.astype(F32)).astype(BF16) for v, h in zip(values, high)]
        for base in (0, HIGH_LIST, LOW_LIST):
            own_jobs = [job for job in jobs if job[0] == base]
            off = values[0][base + 3 : base + 4, :].astype(jnp.int32)
            row = off // nz
            zt = (row_ids((nz, chunk)) == off - row * nz).astype(F32).astype(BF16)
            masks, left = {}, []
            for _, ranks, plane, planes, ref, start in own_jobs:
                if (plane, planes) not in masks:
                    ids = row_ids((planes * cy, chunk)) + plane * cy
                    masks[plane, planes] = (ids == row).astype(F32).astype(BF16)
                for r in ranks:
                    at = base + r // 2
                    left += [masks[plane, planes] * t[r % 2][at : at + 1, :] for t in (high, low)]
            left = jnp.concatenate(left, axis=0)
            got = lax.dot_general(left, zt, (((1,), (1,)), ((), ())), preferred_element_type=F32)
            at = 0
            for _, ranks, _, planes, ref, start in own_jobs:
                size = planes * cy
                for i in range(len(ranks)):
                    ref[i, start : start + size] += got[at : at + size] + got[at + size : at + 2 * size]
                    at += 2 * size
        return carry

    lax.fori_loop(0, sources // 4, body, 0)


STEP_ROWS = ((0, 1, 2), (3, 4, 5), (7, 8, 9))


def near_scatter_kernel(par_ref, val_ref, sign_ref, zero_out, one_out, even_out, odd_out, zero_ref, one_ref):
    _, cx, cy, nz = one_out.shape
    jobs = (
        (0, STEP_ROWS[0], 0, cx, zero_ref, NEAR * cy),
        (0, STEP_ROWS[1], 0, cx, one_ref, 0),
        (HIGH_LIST, STEP_ROWS[0], 0, NEAR, zero_ref, (NEAR + cx) * cy),
        (LOW_LIST, STEP_ROWS[0], cx - NEAR, NEAR, zero_ref, 0),
    )
    scatter_lists(val_ref, jobs, cy, nz)
    sign = sign_ref[...]
    for i in range(3):
        zero_out[i] = zero_ref[i].reshape(zero_out.shape[1:]) * sign[MID - NEAR : MID + cx + NEAR]
        one_out[i] = one_ref[i].reshape(one_out.shape[1:]) * sign[MID : MID + cx]
    at = row_ids((TILE, nz))

    def write(is_high, face_ref):
        ys = slice(cy - TILE, cy) if is_high else slice(0, TILE)
        half = at >= TILE // 2 if is_high else at < TILE // 2
        corner = at < NEAR if is_high else at >= TILE - NEAR
        for i in range(3):
            for x in range(cx):
                tile = jnp.where(half, zero_out[i, NEAR + x, ys], half_turn(one_out[i, x, ys]))
                if x < 2 * NEAR:
                    moved = pltpu.roll(zero_out[i, NEAR + corner_plane(x, cx), ys], NEAR if is_high else TILE - NEAR, 0)
                    tile = jnp.where(corner, moved, tile)
                face_ref[i, x] = tile

    write_faces(par_ref[0], write, even_out, odd_out)


def rest_scatter_kernel(val_ref, sign_ref, zero_out, one_out, two_out, zero_ref, one_ref, two_ref):
    _, cx, cy, nz = two_out.shape
    jobs = (
        (0, STEP_ROWS[2], 0, cx, two_ref, 0),
        (HIGH_LIST, STEP_ROWS[0], NEAR, MID - NEAR, zero_ref, NEAR * cy),
        (LOW_LIST, STEP_ROWS[0], cx - MID, MID - NEAR, zero_ref, 0),
        (HIGH_LIST, STEP_ROWS[1], 0, NEAR, one_ref, NEAR * cy),
        (LOW_LIST, STEP_ROWS[1], cx - NEAR, NEAR, one_ref, 0),
    )
    scatter_lists(val_ref, jobs, cy, nz)
    sign = sign_ref[...]
    last = cx + 2 * MID
    far = jnp.concatenate([sign[0 : MID - NEAR], sign[last - (MID - NEAR) :]], axis=0)
    side = jnp.concatenate([sign[MID - NEAR : MID], sign[MID + cx : MID + cx + NEAR]], axis=0)
    for i in range(3):
        zero_out[i] = zero_ref[i].reshape(zero_out.shape[1:]) * far
        one_out[i] = one_ref[i].reshape(one_out.shape[1:]) * side
        two_out[i] = two_ref[i].reshape(two_out.shape[1:]) * sign[MID : MID + cx]


def corner_plane(x, cx):
    return x - NEAR if x < NEAR else cx + x - NEAR


def write_faces(parity, write, even_out, odd_out):
    @pl.when(parity == 0)
    def _():
        write(True, even_out)
        write(False, odd_out)

    @pl.when(parity != 0)
    def _():
        write(False, even_out)
        write(True, odd_out)


def pair_list(count, odd):
    first = 1 if odd else 0
    pairs = [(i, i + 1) for i in range(first, count - 1, 2)]
    return pairs + [(j, i) for i, j in pairs]


def swap_faces(faces, axis):
    count = lax.axis_size(axis)
    out = []
    for k in (0, 1):
        out.append(lax.ppermute(faces[k], axis, pair_list(count, k)))
    return out


def field_face_kernel(par_ref, cur_ref, ear_ref, coef_ref, even_out, odd_out):
    _, cx, cy, nz = cur_ref.shape
    upper = row_ids((TILE, nz)) >= TILE // 2

    def write(high, face_ref):
        ys = slice(cy - TILE, cy) if high else slice(0, TILE)
        keep = upper if high else ~upper
        for x in range(cx):
            for i in range(3):
                face_ref[i, x] = cur_ref[i, x, ys]
            face_ref[3, x] = jnp.where(keep, ear_ref[0, x, ys], half_turn(ear_ref[1, x, ys]))
            face_ref[4, x] = jnp.where(keep, ear_ref[2, x, ys], half_turn(coef_ref[x, ys]))

    write_faces(par_ref[0], write, even_out, odd_out)


def face_tile(ref, name, x):
    if name < 3:
        return ref[name, x]
    tile = ref[3 + (name - 3) // 2, x]
    return half_turn(tile) if name in (4, 6) else tile


def select_side(parity, even_ref, odd_ref, high):
    from_even = (parity == 0) if high else (parity == 1)

    def read(get):
        return jnp.where(from_even, get(even_ref), get(odd_ref))

    return read


FIELD_PLAN = [(DEEP, MID)] * 3 + [(MID, NEAR)] * 4 + [(MID, 0)]


def plan_tiles(plan, cy):
    out = []
    for name, (planes, corners) in enumerate(plan):
        for dist in range(1, planes + 1):
            for part in list(range(cy // TILE)) + ([-1] if dist <= corners else []):
                out.append((name, dist, part, len(out)))
    return out


def side_kernel(plan, own_tile, halo_tile, cx, cy, nz, px_ref, py_ref, even_ref, odd_ref, even_out, odd_out):
    upper = row_ids((TILE, nz)) >= TILE // 2
    low = select_side(py_ref[0], even_ref, odd_ref, False)
    high = select_side(py_ref[0], even_ref, odd_ref, True)

    def write(is_high, face_ref):
        for name, dist, part, at in plan_tiles(plan, cy):
            x = cx - dist if is_high else dist - 1
            if part >= 0:
                tile = own_tile(name, x, slice(part * TILE, (part + 1) * TILE))
            else:
                tile = jnp.where(
                    upper,
                    low(lambda ref: halo_tile(ref, name, x)),
                    high(lambda ref: halo_tile(ref, name, x)),
                )
            face_ref[at] = tile

    write_faces(px_ref[0], write, even_out, odd_out)


def sign_of(mask):
    return (mask == 1).astype(F32) - (mask == 2).astype(F32)


def field_side_kernel(px_ref, py_ref, cur_ref, ear_ref, coef_ref, mask_ref, *refs):
    _, cx, cy, nz = cur_ref.shape

    def own_tile(name, x, ys):
        if name < 3:
            return cur_ref[name, x, ys]
        if name < 6:
            return ear_ref[name - 3, x, ys]
        return coef_ref[x, ys] if name == 6 else sign_of(mask_ref[x, ys])

    side_kernel(FIELD_PLAN, own_tile, face_tile, cx, cy, nz, px_ref, py_ref, *refs)


LANES = 128


def put_rows(ref, index, rows, value):
    for h in range(value.shape[1] // LANES):
        ref[(*index, h, rows)] = value[:, h * LANES : (h + 1) * LANES]


def laplacian_rows(ref, i, x, start, count):
    tiles = ref.shape[2]
    lane = lax.broadcasted_iota(jnp.int32, (count, LANES), 1)

    def rows(h, dx, dy):
        return ref[i, x + dx, h, pl.ds(start + dy, count)]

    centre = [rows(h, 0, 0) for h in range(tiles)]
    out = [centre_weight * c for c in centre]
    for k, weight in ((1, near_weight), (2, far_weight)):
        up = [pltpu.roll(c, k, 1) for c in centre]
        down = [pltpu.roll(c, LANES - k, 1) for c in centre]
        for h in range(tiles):
            below = jnp.where(lane >= k, up[h], up[h - 1] if h else 0.0)
            above = jnp.where(lane < LANES - k, down[h], down[h + 1] if h + 1 < tiles else 0.0)
            across = (rows(h, -k, 0) + rows(h, k, 0)) + (rows(h, 0, -k) + rows(h, 0, k))
            out[h] = out[h] + weight * (across + (below + above))
    return centre, out


def run_planes(first, last, body):
    lax.fori_loop(first, last, lambda x, carry: (body(x), carry)[1], 0, unroll=2)


def first_wave_kernel(
    px_ref, py_ref, cur_ref, ear_ref, coef_ref, mask_ref, ye_ref, yo_ref, xe_ref, xo_ref,
    final_ref, prior_ref, wide_coef_ref, wide_sign_ref, u_ref, e_ref, c_ref, one_ref, two_ref,
):
    _, cx, cy, _ = cur_ref.shape
    own = slice(TILE, TILE + cy)
    lower, higher = slice(0, TILE), slice(TILE + cy, 2 * TILE + cy)
    low = select_side(py_ref[0], ye_ref, yo_ref, False)
    high = select_side(py_ref[0], ye_ref, yo_ref, True)

    def put(name, x, rows, value):
        if name < 3:
            put_rows(u_ref, (name, DEEP + x), rows, value)
        elif name < 6:
            put_rows(e_ref, (name - 3, MID + x), rows, value)
        elif name == 6:
            put_rows(c_ref, (MID + x,), rows, value)
            if -NEAR <= x < cx + NEAR:
                put_rows(wide_coef_ref, (NEAR + x,), rows, value)
        else:
            wide_sign_ref[MID + x, slice(rows.start - TILE, rows.stop - TILE)] = value

    for x in range(cx):
        for name in range(7):
            value = cur_ref[name, x] if name < 3 else ear_ref[name - 3, x] if name < 6 else coef_ref[x]
            put(name, x, own, value)
            put(name, x, lower, low(lambda ref: face_tile(ref, name, x)))
            put(name, x, higher, high(lambda ref: face_tile(ref, name, x)))
        put(7, x, own, sign_of(mask_ref[x]))
    for is_high in (False, True):
        read = select_side(px_ref[0], xe_ref, xo_ref, is_high)
        for name, dist, part, at in plan_tiles(FIELD_PLAN, cy):
            x = cx - 1 + dist if is_high else -dist
            tile = read(lambda ref: ref[at])
            if part >= 0:
                put(name, x, slice(TILE * (part + 1), TILE * (part + 2)), tile)
            else:
                put(name, x, lower, tile)
                put(name, x, higher, tile)

    begin = px_ref[1]
    deep = cy + TILE

    def first(start, count):
        def body(x):
            for i in range(3):
                centre, lap = laplacian_rows(u_ref, i, x + DEEP - MID, start, count)
                for h, (c, l) in enumerate(zip(centre, lap)):
                    rows = pl.ds(start, count)
                    one_ref[i, x, h, rows] = 2.0 * c - e_ref[i, x, h, rows] + c_ref[x, h, rows] * l

        return body

    def second(start, count):
        def body(x):
            for i in range(3):
                centre, lap = laplacian_rows(one_ref, i, x + MID - NEAR, start, count)
                for h, (c, l) in enumerate(zip(centre, lap)):
                    rows = pl.ds(start, count)
                    moved = 2.0 * c - u_ref[i, x + DEEP - NEAR, h, rows]
                    two_ref[i, x, h, rows] = moved + c_ref[x + MID - NEAR, h, rows] * l

        return body

    def third(x):
        for i in range(3):
            centre, lap = laplacian_rows(two_ref, i, x + NEAR, TILE, cy)
            for h, (c, l) in enumerate(zip(centre, lap)):
                lanes = slice(h * LANES, (h + 1) * LANES)
                moved = 2.0 * c - one_ref[i, x + MID, h, own]
                final_ref[i, x, :, lanes] = moved + c_ref[x + MID, h, own] * l
                prior_ref[i, x, :, lanes] = c

    run_planes(0, NEAR, first(TILE, cy))
    run_planes(NEAR, cx + 2 * MID - NEAR, first(begin, deep))
    run_planes(cx + 2 * MID - NEAR, cx + 2 * MID, first(TILE, cy))
    run_planes(0, NEAR, second(TILE, cy))
    run_planes(NEAR, cx + NEAR, second(begin, deep))
    run_planes(cx + NEAR, cx + 2 * NEAR, second(TILE, cy))
    run_planes(0, cx, third)


def last_wave_kernel(
    px_ref, py_ref, free_final_ref, free_prior_ref, coef_ref, zero_in, zero_far_in, one_in, one_side_in, two_in,
    ye_ref, yo_ref, final_ref, prior_ref, one_ref, two_ref,
):
    _, cx, cy, _ = two_in.shape
    own = slice(TILE, TILE + cy)
    lower, higher = slice(0, TILE), slice(TILE + cy, 2 * TILE + cy)
    low = select_side(py_ref[0], ye_ref, yo_ref, False)
    high = select_side(py_ref[0], ye_ref, yo_ref, True)
    for i in range(3):
        for x in range(cx + 2 * NEAR):
            put_rows(one_ref, (i, x + MID - NEAR), own, zero_in[i, x])
        for k in range(NEAR):
            put_rows(one_ref, (i, k), own, zero_far_in[i, k])
            put_rows(one_ref, (i, cx + 2 * MID - NEAR + k), own, zero_far_in[i, NEAR + k])
            put_rows(two_ref, (i, k), own, one_side_in[i, k])
            put_rows(two_ref, (i, cx + NEAR + k), own, one_side_in[i, NEAR + k])
        for x in range(cx):
            put_rows(two_ref, (i, NEAR + x), own, one_in[i, x])
            for rows, read, turn in ((lower, low, TILE - NEAR), (higher, high, NEAR)):
                tile = read(lambda ref: ref[i, x])
                put_rows(one_ref, (i, MID + x), rows, tile)
                put_rows(two_ref, (i, NEAR + x), rows, half_turn(tile))
                if x < 2 * NEAR:
                    put_rows(one_ref, (i, MID + corner_plane(x, cx)), rows, pltpu.roll(tile, turn, 0))

    def second(start, count):
        def body(x):
            for i in range(3):
                centre, lap = laplacian_rows(one_ref, i, x + MID - NEAR, start, count)
                for h, (c, l) in enumerate(zip(centre, lap)):
                    rows = pl.ds(start, count)
                    two_ref[i, x, h, rows] = 2.0 * c + coef_ref[x, h, rows] * l + two_ref[i, x, h, rows]

        return body

    def third(x):
        for i in range(3):
            centre, lap = laplacian_rows(two_ref, i, x + NEAR, TILE, cy)
            for h, (c, l) in enumerate(zip(centre, lap)):
                lanes = slice(h * LANES, (h + 1) * LANES)
                moved = 2.0 * c - one_ref[i, x + MID, h, own] + coef_ref[x + NEAR, h, own] * l
                final_ref[i, x, :, lanes] = free_final_ref[i, x, :, lanes] + (moved + two_in[i, x, :, lanes])
                prior_ref[i, x, :, lanes] = free_prior_ref[i, x, :, lanes] + c

    run_planes(0, NEAR, second(TILE, cy))
    run_planes(NEAR, cx + NEAR, second(px_ref[1], cy + TILE))
    run_planes(cx + NEAR, cx + 2 * NEAR, second(TILE, cy))
    run_planes(0, cx, third)


def staged(kernel, positions, operand_count):
    def run(*refs):
        refs, stages, sems = refs[: -len(positions) - 1], refs[-len(positions) - 1 : -1], refs[-1]
        ins = list(refs[:operand_count])
        copies = []
        for k, (at, stage) in enumerate(zip(positions, stages)):
            copies.append(pltpu.make_async_copy(ins[at], stage, sems.at[k]))
            ins[at] = stage
        for copy in copies:
            copy.start()
        for copy in copies:
            copy.wait()
        kernel(*ins, *refs[operand_count:])

    return run


def local(
    current_field,
    earlier_field,
    wave_coef,
    layer_mask,
    point_xyz,
    point_owner,
    cell_offset,
    wave_vector,
    frequency,
    amplitude,
    phase_index,
    phase_table,
):
    table_size = phase_table.shape[0]
    matches = (phase_index[None, :] == jnp.arange(table_size)[:, None]).astype(F32)
    phases = jnp.dot(
        phase_table[None, :], matches, precision=lax.Precision.HIGHEST, preferred_element_type=F32
    )[0]
    own_block = jnp.concatenate(
        [wave_vector, frequency[None, :], amplitude, phases[None, :]], axis=0
    )
    point_count = point_xyz.shape[1]
    slab_count = lax.axis_size("slab")
    comp_count = lax.axis_size("comp")
    device_count = slab_count * comp_count
    slot_count = max(2, 2 * point_count // device_count)
    _, cx, cy, nz = current_field.shape
    assert slot_count <= HALF and device_count % 8 == 0
    assert cx >= DEEP and cy >= 2 * TILE and cy % TILE == 0
    wide = cy + 2 * TILE
    assert nz % LANES == 0 and MID == 2 * NEAR

    def plane_stack(*lead):
        return (*lead, nz // LANES, wide, LANES)

    smem = pl.BlockSpec(memory_space=pltpu.SMEM)
    vmem = pl.BlockSpec(memory_space=pltpu.VMEM)

    def call(kernel, operands, shapes, scratch=(), scalars=0, from_hbm=(), to_hbm=False):
        shapes = [(pltpu.HBM if to_hbm else jax.ShapeDtypeStruct)(shape, F32) for shape in shapes]
        operands = list(operands)
        in_specs = [smem] * scalars + [vmem] * (len(operands) - scalars)
        scratch_shapes = [pltpu.VMEM(shape, F32) for shape in scratch]
        if from_hbm:
            for at in from_hbm:
                operands[at] = pltpu.with_memory_space_constraint(operands[at], pltpu.HBM)
                in_specs[at] = pl.BlockSpec(memory_space=pltpu.HBM)
                scratch_shapes.append(pltpu.VMEM(operands[at].shape, operands[at].dtype))
            scratch_shapes.append(pltpu.SemaphoreType.DMA((len(from_hbm),)))
            kernel = staged(kernel, from_hbm, len(operands))
        return pl.pallas_call(
            kernel,
            out_shape=shapes,
            in_specs=in_specs,
            out_specs=[vmem] * len(shapes),
            scratch_shapes=scratch_shapes,
            compiler_params=pltpu.CompilerParams(vmem_limit_bytes=VMEM_GRANT),
        )(*operands)

    px = jnp.stack([lax.axis_index("slab") % 2, TILE // 2]).astype(jnp.int32)
    py = (lax.axis_index("comp") % 2).astype(jnp.int32).reshape(1)
    if comp_count == 4:
        near_block = lax.ppermute(own_block, "comp", pair_list(4, 0))
        first_blocks = [own_block, near_block]
        ring = pair_list(4, 1) + [(0, 3), (3, 0)]
        far_block = lax.ppermute(jnp.concatenate(first_blocks, axis=1), "comp", ring)
        last_blocks = [far_block]
    else:
        first_blocks = [own_block]
        last_blocks = [
            lax.ppermute(own_block, "comp", [(i, (i + k) % comp_count) for i in range(comp_count)])
            for k in range(1, comp_count)
        ]
    fields = (current_field, earlier_field, wave_coef)
    faces = call(field_face_kernel, (py, *fields), [(5, cx, TILE, nz)] * 2, scalars=1, from_hbm=(1, 2, 3))
    ye, yo = swap_faces(faces, "comp")
    (sum_one, total_one) = call(
        lambda *refs: first_incident_kernel(len(first_blocks), *refs),
        (*first_blocks, point_xyz),
        [(32, point_count), (16, 256)],
        [(8, point_count)],
    )
    field_tiles = len(plan_tiles(FIELD_PLAN, cy))
    sides = call(
        field_side_kernel,
        (px, py, *fields, layer_mask, ye, yo),
        [(field_tiles, TILE, nz)] * 2,
        scalars=2,
        from_hbm=(2, 3, 4, 5),
    )
    xe, xo = swap_faces(sides, "slab")
    (packed,) = call(
        lambda *refs: last_incident_kernel(len(last_blocks), comp_count, *refs),
        (
            *last_blocks, sum_one, total_one, point_xyz,
            point_owner.reshape(1, point_count), cell_offset.reshape(1, point_count),
        ),
        [(device_count, LIST_ROWS, 2 * HALF)],
        [(8, point_count), (32, point_count)],
    )
    arrived = lax.all_to_all(packed, ("slab", "comp"), split_axis=0, concat_axis=0, tiled=True)
    free_final, free_prior, wide_coef, wide_sign = call(
        first_wave_kernel,
        (px, py, *fields, layer_mask, ye, yo, xe, xo),
        [current_field.shape, current_field.shape, plane_stack(cx + 2 * NEAR), (cx + 2 * MID, cy, nz)],
        [
            plane_stack(3, cx + 2 * DEEP), plane_stack(3, cx + 2 * MID), plane_stack(cx + 2 * MID),
            plane_stack(3, cx + 2 * MID), plane_stack(3, cx + 2 * NEAR),
        ],
        scalars=2,
        from_hbm=(2, 3, 4, 5),
        to_hbm=True,
    )
    zero, one, face_even, face_odd = call(
        near_scatter_kernel,
        (py, arrived, wide_sign),
        [(3, cx + 2 * NEAR, cy, nz), (3, cx, cy, nz)] + [(3, cx, TILE, nz)] * 2,
        [(3, (cx + 2 * NEAR) * cy, nz), (3, cx * cy, nz)],
        scalars=1,
        from_hbm=(2,),
    )
    fye, fyo = swap_faces((face_even, face_odd), "comp")
    zero_far, one_side, two = call(
        rest_scatter_kernel,
        (arrived, wide_sign),
        [(3, 2 * NEAR, cy, nz), (3, 2 * NEAR, cy, nz), (3, cx, cy, nz)],
        [(3, 2 * NEAR * cy, nz), (3, 2 * NEAR * cy, nz), (3, cx * cy, nz)],
        from_hbm=(1,),
    )
    final, prior = call(
        last_wave_kernel,
        (px, py, free_final, free_prior, wide_coef, zero, zero_far, one, one_side, two, fye, fyo),
        [current_field.shape, current_field.shape],
        [plane_stack(3, cx + 2 * MID), plane_stack(3, cx + 2 * NEAR)],
        scalars=2,
        from_hbm=(2, 3, 4),
    )
    return (final, prior)


def solution(mesh):
    in_specs = (
        P(None, "slab", "comp", None),
        P(None, "slab", "comp", None),
        P("slab", "comp", None),
        P("slab", "comp", None),
        P(None, ("slab", "comp")),
        P(("slab", "comp"), None),
        P(("slab", "comp")),
        P(None, "comp"),
        P("comp"),
        P(None, "comp"),
        P("comp"),
        P(),
    )
    out_specs = (P(None, "slab", "comp", None), P(None, "slab", "comp", None))
    return jax.shard_map(local, mesh=mesh, in_specs=in_specs, out_specs=out_specs, check_vma=False)
```

```python
import jax
import jax.numpy as jnp
from jax import lax
from jax.experimental import pallas as pl
from jax.experimental.pallas import tpu as pltpu
from jax.sharding import PartitionSpec as P

step_size = 0.05
near_weight = 4.0 / 3.0
far_weight = -1.0 / 12.0
centre_weight = -7.5
inv_two_pi = 0.15915494309189535

LEAD = -0.7713118195533752
SIN_C = (4.442834854125977 / LEAD, -7.306587219238281 / LEAD, 3.588636875152588 / LEAD)
SIN_SCALE = LEAD * abs(LEAD)
VER_SCALE = LEAD * LEAD
HALF = 64
OWN_TILES = 5
SIDE_TILES = 4
HIGH_LIST = OWN_TILES
LOW_LIST = OWN_TILES + SIDE_TILES
LIST_ROWS = OWN_TILES + 2 * SIDE_TILES
VMEM_GRANT = 16 * 2**20

F32 = jnp.float32
BF16 = jnp.bfloat16


def sin_versine(u):
    r = u - jnp.round(u)
    z = r * r
    s = r * (((z + SIN_C[2]) * z + SIN_C[1]) * z + SIN_C[0])
    q = s * s
    w = 2.0 / VER_SCALE - q
    return s * (w * lax.rsqrt(w)), q


def split_three(x):
    hi = x.astype(BF16).astype(F32)
    rest = x - hi
    mid = rest.astype(BF16).astype(F32)
    return hi, mid, rest - mid


def row_ids(shape):
    return lax.broadcasted_iota(jnp.int32, shape, 0)


def add_components(par_refs, xyz_ref, x8_ref, acc_ref):
    points = xyz_ref.shape[1]
    kc = 256
    tile = 256
    x8_ref[...] = jnp.zeros(x8_ref.shape, F32)
    x8_ref[0:3, :] = xyz_ref[...]
    xhi, xmid, xlo = split_three(x8_ref[...])
    right = jnp.concatenate([xhi, xmid, xlo, xhi, xmid, xhi], axis=0).astype(BF16)
    rows8 = row_ids((8, kc))
    times = step_size * (rows8 + 1).astype(F32)
    rows16 = row_ids((16, kc))
    comp_row = jnp.where(rows16 < 6, rows16 % 3, (rows16 + 2) % 3)
    valued = (rows16 < 10) & (rows16 != 6)

    def body(par_ref, step, total):
        blk = par_ref[:, pl.ds(pl.multiple_of(step * kc, kc), kc)]
        kv = jnp.where(rows8 < 3, blk * inv_two_pi, 0.0)
        khi, kmid, klo = split_three(kv)
        left = jnp.concatenate([khi, khi, khi, kmid, kmid, klo], axis=0).astype(BF16)
        delays = times * blk[3:4, :] - blk[7:8, :]
        sd, qd = sin_versine(delays * inv_two_pi)
        sd, cd = SIN_SCALE * sd, 1.0 - VER_SCALE * qd
        amp = jnp.where(comp_row == 0, blk[4:5, :], jnp.where(comp_row == 1, blk[5:6, :], blk[6:7, :]))
        amp = jnp.where(valued, amp, 0.0)

        def rows_of(t):
            w = amp * jnp.where(rows16 < 3, t[0:1, :], jnp.where(rows16 < 6, t[1:2, :], t[2:3, :]))
            hi = w.astype(BF16)
            lo = (w - hi.astype(F32)).astype(BF16)
            return w, jnp.concatenate([hi, lo], axis=0)

        wc = rows_of(cd)[0]
        lc = rows_of(-VER_SCALE * cd)[1]
        ls = rows_of(SIN_SCALE * sd)[1]
        for t in range(points // tile):
            cols = slice(t * tile, (t + 1) * tile)
            u = lax.dot_general(left, right[:, cols], (((0,), (0,)), ((), ())), preferred_element_type=F32)
            highs, lows = [], []
            for j in range(kc // 32):
                for value in sin_versine(u[32 * j : 32 * j + 32]):
                    high = value.astype(BF16)
                    highs.append(high)
                    lows.append((value - high.astype(F32)).astype(BF16))
            part = jnp.dot(ls, jnp.concatenate(highs[0::2], axis=0), preferred_element_type=F32)
            part += jnp.dot(lc, jnp.concatenate(highs[1::2], axis=0), preferred_element_type=F32)
            part += jnp.dot(ls, jnp.concatenate(lows[0::2], axis=0), preferred_element_type=F32)
            part += jnp.dot(lc, jnp.concatenate(lows[1::2], axis=0), preferred_element_type=F32)
            acc_ref[:, cols] += part
        return total + wc

    total = jnp.zeros((16, kc), F32)
    for par_ref in par_refs:
        steps = par_ref.shape[1] // kc
        total = lax.fori_loop(0, steps, lambda step, t, ref=par_ref: body(ref, step, t), total)
    return total


def first_incident_kernel(count, *refs):
    par_refs, (xyz_ref, acc_ref, total_ref, x8_ref) = refs[:count], refs[count:]
    acc_ref[...] = jnp.zeros(acc_ref.shape, F32)
    total_ref[...] = add_components(par_refs, xyz_ref, x8_ref, acc_ref)


def last_incident_kernel(count, step, *refs):
    par_refs, refs = refs[:count], refs[count:]
    first_ref, first_total_ref, xyz_ref, own_ref, off_ref, out_ref, x8_ref, acc_ref = refs
    points = xyz_ref.shape[1]
    owners = out_ref.shape[0]
    acc_ref[...] = first_ref[...]
    total = add_components(par_refs, xyz_ref, x8_ref, acc_ref) + first_total_ref[...]
    vals = acc_ref[0:16, :] + acc_ref[16:32, :] + jnp.sum(total, axis=1, keepdims=True)
    vals = jnp.where(row_ids((16, points)) == 6, off_ref[...].astype(F32), vals)
    v1, v2, v3 = split_three(vals)
    named = own_ref[...] == row_ids((owners, points))
    named_one = named.astype(F32).astype(BF16)
    earlier = row_ids((points, points)) < lax.broadcasted_iota(jnp.int32, (points, points), 1)
    before = jnp.dot(named_one, earlier.astype(F32).astype(BF16), preferred_element_type=F32)
    rank = jnp.sum(jnp.where(named, before, 0.0), axis=0, keepdims=True).astype(jnp.int32)
    terms = [v.astype(BF16) for v in (v1, v2, v3)]
    tiles = 0.0
    for odd in (0, 1):
        left = jnp.concatenate(
            [named_one * t[2 * j + odd : 2 * j + odd + 1, :] for t in terms for j in range(OWN_TILES)], axis=0
        )
        spots = (row_ids((2 * HALF, points)) == rank + odd * HALF).astype(F32).astype(BF16)
        got = lax.dot_general(left, spots, (((1,), (1,)), ((), ())), preferred_element_type=F32)
        size = OWN_TILES * owners
        tiles = tiles + (got[0:size] + got[size : 2 * size] + got[2 * size :])
    owner_row = row_ids((owners, 2 * HALF))

    def put(j, tile):
        out_ref[:, 0, 2 * HALF * j : 2 * HALF * (j + 1)] = tile

    for j in range(OWN_TILES):
        tile = tiles[j * owners : (j + 1) * owners]
        put(j, tile)
        if j < SIDE_TILES:
            above = pltpu.roll(tile, owners - step, 0)
            put(HIGH_LIST + j, jnp.where(owner_row < owners - step, above, 0.0))
            put(LOW_LIST + j, jnp.where(owner_row >= step, pltpu.roll(tile, step, 0), 0.0))


TILE = 8
DEEP = 6
MID = 4
NEAR = 2


def half_turn(tile):
    return pltpu.roll(tile, TILE // 2, 0)


ROWS_HELD = 16


def scatter_lists(val_ref, even_ref, odd_ref, jobs, cy, nz):
    lanes = 2 * HALF
    sources = val_ref.shape[0]
    groups = sources // 2
    chunk = 2 * lanes
    left_half = lax.broadcasted_iota(jnp.int32, (groups, lanes), 1) < lanes // 2
    for ref in {id(job[4]): job[4] for job in jobs}.values():
        ref[...] = jnp.zeros(ref.shape, F32)
    for j in range(LIST_ROWS):
        rows = val_ref[:, 0, lanes * j : lanes * (j + 1)]
        first, second = rows[0:groups], rows[groups:]
        at = pl.ds(j, groups, stride=ROWS_HELD)
        even_ref[at, :] = jnp.where(left_half, first, pltpu.roll(second, lanes // 2, 1))
        odd_ref[at, :] = jnp.where(left_half, pltpu.roll(first, lanes // 2, 1), second)

    def body(step, carry):
        evens, odds = [], []
        for pair in range(2):
            at = pl.ds(pl.multiple_of((2 * step + pair) * ROWS_HELD, ROWS_HELD), ROWS_HELD)
            evens.append(even_ref[at, :])
            odds.append(odd_ref[at, :])
        values = [jnp.concatenate(evens, axis=1), jnp.concatenate(odds, axis=1)]
        high = [v.astype(BF16) for v in values]
        low = [(v - h.astype(F32)).astype(BF16) for v, h in zip(values, high)]
        for base in (0, HIGH_LIST, LOW_LIST):
            own_jobs = [job for job in jobs if job[0] == base]
            off = values[0][base + 3 : base + 4, :].astype(jnp.int32)
            row = off // nz
            zt = (row_ids((nz, chunk)) == off - row * nz).astype(F32).astype(BF16)
            masks, left = {}, []
            for _, ranks, plane, planes, ref, start in own_jobs:
                if (plane, planes) not in masks:
                    ids = row_ids((planes * cy, chunk)) + plane * cy
                    masks[plane, planes] = (ids == row).astype(F32).astype(BF16)
                for r in ranks:
                    at = base + r // 2
                    left += [masks[plane, planes] * t[r % 2][at : at + 1, :] for t in (high, low)]
            left = jnp.concatenate(left, axis=0)
            got = lax.dot_general(left, zt, (((1,), (1,)), ((), ())), preferred_element_type=F32)
            at = 0
            for _, ranks, _, planes, ref, start in own_jobs:
                size = planes * cy
                for i in range(len(ranks)):
                    ref[i, start : start + size] += got[at : at + size] + got[at + size : at + 2 * size]
                    at += 2 * size
        return carry

    lax.fori_loop(0, groups // 2, body, 0)


STEP_ROWS = ((0, 1, 2), (3, 4, 5), (7, 8, 9))


def near_scatter_kernel(
    ready, par_ref, val_ref, sign_ref, zero_out, one_out, even_out, odd_out, zero_ref, one_ref, even_ref, odd_ref
):
    _, cx, cy, nz = one_out.shape
    jobs = (
        (0, STEP_ROWS[0], 0, cx, zero_ref, NEAR * cy),
        (0, STEP_ROWS[1], 0, cx, one_ref, 0),
        (HIGH_LIST, STEP_ROWS[0], 0, NEAR, zero_ref, (NEAR + cx) * cy),
        (LOW_LIST, STEP_ROWS[0], cx - NEAR, NEAR, zero_ref, 0),
    )
    scatter_lists(val_ref, even_ref, odd_ref, jobs, cy, nz)
    ready()
    sign = sign_ref[...]
    for i in range(3):
        zero_out[i] = zero_ref[i].reshape(zero_out.shape[1:]) * sign[MID - NEAR : MID + cx + NEAR]
        one_out[i] = one_ref[i].reshape(one_out.shape[1:]) * sign[MID : MID + cx]
    at = row_ids((TILE, nz))

    def write(is_high, face_ref):
        ys = slice(cy - TILE, cy) if is_high else slice(0, TILE)
        half = at >= TILE // 2 if is_high else at < TILE // 2
        corner = at < NEAR if is_high else at >= TILE - NEAR
        for i in range(3):
            for x in range(cx):
                tile = jnp.where(half, zero_out[i, NEAR + x, ys], half_turn(one_out[i, x, ys]))
                if x < 2 * NEAR:
                    moved = pltpu.roll(zero_out[i, NEAR + corner_plane(x, cx), ys], NEAR if is_high else TILE - NEAR, 0)
                    tile = jnp.where(corner, moved, tile)
                face_ref[i, x] = tile

    write_faces(par_ref[0], write, even_out, odd_out)


def rest_scatter_kernel(
    ready, val_ref, sign_ref, zero_out, one_out, two_out, zero_ref, one_ref, two_ref, even_ref, odd_ref
):
    _, cx, cy, nz = two_out.shape
    jobs = (
        (0, STEP_ROWS[2], 0, cx, two_ref, 0),
        (HIGH_LIST, STEP_ROWS[0], NEAR, MID - NEAR, zero_ref, NEAR * cy),
        (LOW_LIST, STEP_ROWS[0], cx - MID, MID - NEAR, zero_ref, 0),
        (HIGH_LIST, STEP_ROWS[1], 0, NEAR, one_ref, NEAR * cy),
        (LOW_LIST, STEP_ROWS[1], cx - NEAR, NEAR, one_ref, 0),
    )
    scatter_lists(val_ref, even_ref, odd_ref, jobs, cy, nz)
    ready()
    sign = sign_ref[...]
    last = cx + 2 * MID
    far = jnp.concatenate([sign[0 : MID - NEAR], sign[last - (MID - NEAR) :]], axis=0)
    side = jnp.concatenate([sign[MID - NEAR : MID], sign[MID + cx : MID + cx + NEAR]], axis=0)
    for i in range(3):
        zero_out[i] = zero_ref[i].reshape(zero_out.shape[1:]) * far
        one_out[i] = one_ref[i].reshape(one_out.shape[1:]) * side
        two_out[i] = two_ref[i].reshape(two_out.shape[1:]) * sign[MID : MID + cx]


def corner_plane(x, cx):
    return x - NEAR if x < NEAR else cx + x - NEAR


def write_faces(parity, write, even_out, odd_out):
    @pl.when(parity == 0)
    def _():
        write(True, even_out)
        write(False, odd_out)

    @pl.when(parity != 0)
    def _():
        write(False, even_out)
        write(True, odd_out)


def pair_list(count, odd):
    first = 1 if odd else 0
    pairs = [(i, i + 1) for i in range(first, count - 1, 2)]
    return pairs + [(j, i) for i, j in pairs]


def swap_faces(faces, axis):
    count = lax.axis_size(axis)
    out = []
    for k in (0, 1):
        out.append(lax.ppermute(faces[k], axis, pair_list(count, k)))
    return out


def prepare_kernel(
    ready, par_ref, cur_ref, ear_ref, coef_ref, wave_ref, freq_ref, amp_ref, index_ref, table_ref,
    block_out, even_out, odd_out,
):
    entries = table_ref.shape[1]
    comps = index_ref.shape[1]
    picked = (row_ids((entries, comps)) == index_ref[...]).astype(F32).astype(BF16)
    terms = jnp.concatenate(list(split_three(jnp.broadcast_to(table_ref[...], (TILE, entries)))), axis=0).astype(BF16)
    phase = jnp.dot(terms, picked, preferred_element_type=F32)
    block_out[0:3, :] = wave_ref[...]
    block_out[3:4, :] = freq_ref[...]
    block_out[4:7, :] = amp_ref[...]
    block_out[7:8, :] = phase[0:1] + phase[TILE : TILE + 1] + phase[2 * TILE : 2 * TILE + 1]
    ready()
    _, cx, cy, nz = cur_ref.shape
    upper = row_ids((TILE, nz)) >= TILE // 2

    def write(high, face_ref):
        ys = slice(cy - TILE, cy) if high else slice(0, TILE)
        keep = upper if high else ~upper
        for x in range(cx):
            for i in range(3):
                face_ref[i, x] = cur_ref[i, x, ys]
            face_ref[3, x] = jnp.where(keep, ear_ref[0, x, ys], half_turn(ear_ref[1, x, ys]))
            face_ref[4, x] = jnp.where(keep, ear_ref[2, x, ys], half_turn(coef_ref[x, ys]))

    write_faces(par_ref[0], write, even_out, odd_out)


def face_tile(ref, name, x):
    if name < 3:
        return ref[name, x]
    tile = ref[3 + (name - 3) // 2, x]
    return half_turn(tile) if name in (4, 6) else tile


def select_side(parity, even_ref, odd_ref, high):
    from_even = (parity == 0) if high else (parity == 1)

    def read(get):
        return jnp.where(from_even, get(even_ref), get(odd_ref))

    return read


FIELD_PLAN = [(DEEP, MID)] * 3 + [(MID, NEAR)] * 4 + [(MID, 0)]


def plan_tiles(plan, cy):
    out = []
    for name, (planes, corners) in enumerate(plan):
        for dist in range(1, planes + 1):
            for part in list(range(cy // TILE)) + ([-1] if dist <= corners else []):
                out.append((name, dist, part, len(out)))
    return out


def side_kernel(plan, own_tile, halo_tile, cx, cy, nz, px_ref, py_ref, even_ref, odd_ref, even_out, odd_out):
    upper = row_ids((TILE, nz)) >= TILE // 2
    low = select_side(py_ref[0], even_ref, odd_ref, False)
    high = select_side(py_ref[0], even_ref, odd_ref, True)

    def write(is_high, face_ref):
        for name, dist, part, at in plan_tiles(plan, cy):
            x = cx - dist if is_high else dist - 1
            if part >= 0:
                tile = own_tile(name, x, slice(part * TILE, (part + 1) * TILE))
            else:
                tile = jnp.where(
                    upper,
                    low(lambda ref: halo_tile(ref, name, x)),
                    high(lambda ref: halo_tile(ref, name, x)),
                )
            face_ref[at] = tile

    write_faces(px_ref[0], write, even_out, odd_out)


def sign_of(mask):
    return (mask == 1).astype(F32) - (mask == 2).astype(F32)


def field_side_kernel(ready, px_ref, py_ref, cur_ref, ear_ref, coef_ref, mask_ref, *refs):
    _, cx, cy, nz = cur_ref.shape
    ready()

    def own_tile(name, x, ys):
        if name < 3:
            return cur_ref[name, x, ys]
        if name < 6:
            return ear_ref[name - 3, x, ys]
        return coef_ref[x, ys] if name == 6 else sign_of(mask_ref[x, ys])

    side_kernel(FIELD_PLAN, own_tile, face_tile, cx, cy, nz, px_ref, py_ref, *refs)


LANES = 128


def put_rows(ref, index, rows, value):
    for h in range(value.shape[1] // LANES):
        ref[(*index, h, rows)] = value[:, h * LANES : (h + 1) * LANES]


def laplacian_rows(ref, i, x, start, count):
    tiles = ref.shape[2]
    lane = lax.broadcasted_iota(jnp.int32, (count, LANES), 1)

    def rows(h, dx, dy):
        return ref[i, x + dx, h, pl.ds(start + dy, count)]

    centre = [rows(h, 0, 0) for h in range(tiles)]
    out = [centre_weight * c for c in centre]
    for k, weight in ((1, near_weight), (2, far_weight)):
        up = [pltpu.roll(c, k, 1) for c in centre]
        down = [pltpu.roll(c, LANES - k, 1) for c in centre]
        for h in range(tiles):
            below = jnp.where(lane >= k, up[h], up[h - 1] if h else 0.0)
            above = jnp.where(lane < LANES - k, down[h], down[h + 1] if h + 1 < tiles else 0.0)
            across = (rows(h, -k, 0) + rows(h, k, 0)) + (rows(h, 0, -k) + rows(h, 0, k))
            out[h] = out[h] + weight * (across + (below + above))
    return centre, out


def run_planes(first, last, body):
    lax.fori_loop(first, last, lambda x, carry: (body(x), carry)[1], 0, unroll=2)


def first_wave_kernel(
    ready, px_ref, py_ref, cur_ref, ear_ref, coef_ref, mask_ref, ye_ref, yo_ref, xe_ref, xo_ref,
    final_ref, prior_ref, wide_coef_ref, wide_sign_ref, u_ref, e_ref, c_ref, one_ref, two_ref,
):
    _, cx, cy, _ = cur_ref.shape
    own = slice(TILE, TILE + cy)
    lower, higher = slice(0, TILE), slice(TILE + cy, 2 * TILE + cy)
    low = select_side(py_ref[0], ye_ref, yo_ref, False)
    high = select_side(py_ref[0], ye_ref, yo_ref, True)
    ready()

    def put(name, x, rows, value):
        if name < 3:
            put_rows(u_ref, (name, DEEP + x), rows, value)
        elif name < 6:
            put_rows(e_ref, (name - 3, MID + x), rows, value)
        elif name == 6:
            put_rows(c_ref, (MID + x,), rows, value)
            if -NEAR <= x < cx + NEAR:
                put_rows(wide_coef_ref, (NEAR + x,), rows, value)
        else:
            wide_sign_ref[MID + x, slice(rows.start - TILE, rows.stop - TILE)] = value

    for x in range(cx):
        for name in range(7):
            value = cur_ref[name, x] if name < 3 else ear_ref[name - 3, x] if name < 6 else coef_ref[x]
            put(name, x, own, value)
            put(name, x, lower, low(lambda ref: face_tile(ref, name, x)))
            put(name, x, higher, high(lambda ref: face_tile(ref, name, x)))
        put(7, x, own, sign_of(mask_ref[x]))
    for is_high in (False, True):
        read = select_side(px_ref[0], xe_ref, xo_ref, is_high)
        for name, dist, part, at in plan_tiles(FIELD_PLAN, cy):
            x = cx - 1 + dist if is_high else -dist
            tile = read(lambda ref: ref[at])
            if part >= 0:
                put(name, x, slice(TILE * (part + 1), TILE * (part + 2)), tile)
            else:
                put(name, x, lower, tile)
                put(name, x, higher, tile)

    begin = px_ref[1]
    deep = cy + TILE

    def first(start, count):
        def body(x):
            for i in range(3):
                centre, lap = laplacian_rows(u_ref, i, x + DEEP - MID, start, count)
                for h, (c, l) in enumerate(zip(centre, lap)):
                    rows = pl.ds(start, count)
                    one_ref[i, x, h, rows] = 2.0 * c - e_ref[i, x, h, rows] + c_ref[x, h, rows] * l

        return body

    def second(start, count):
        def body(x):
            for i in range(3):
                centre, lap = laplacian_rows(one_ref, i, x + MID - NEAR, start, count)
                for h, (c, l) in enumerate(zip(centre, lap)):
                    rows = pl.ds(start, count)
                    moved = 2.0 * c - u_ref[i, x + DEEP - NEAR, h, rows]
                    two_ref[i, x, h, rows] = moved + c_ref[x + MID - NEAR, h, rows] * l

        return body

    def third(x):
        for i in range(3):
            centre, lap = laplacian_rows(two_ref, i, x + NEAR, TILE, cy)
            for h, (c, l) in enumerate(zip(centre, lap)):
                lanes = slice(h * LANES, (h + 1) * LANES)
                moved = 2.0 * c - one_ref[i, x + MID, h, own]
                final_ref[i, x, :, lanes] = moved + c_ref[x + MID, h, own] * l
                prior_ref[i, x, :, lanes] = c

    run_planes(0, NEAR, first(TILE, cy))
    run_planes(NEAR, cx + 2 * MID - NEAR, first(begin, deep))
    run_planes(cx + 2 * MID - NEAR, cx + 2 * MID, first(TILE, cy))
    run_planes(0, NEAR, second(TILE, cy))
    run_planes(NEAR, cx + NEAR, second(begin, deep))
    run_planes(cx + NEAR, cx + 2 * NEAR, second(TILE, cy))
    run_planes(0, cx, third)


def last_wave_kernel(
    ready, px_ref, py_ref, free_final_ref, free_prior_ref, coef_ref, zero_in, zero_far_in, one_in, one_side_in, two_in,
    ye_ref, yo_ref, final_ref, prior_ref, one_ref, two_ref,
):
    _, cx, cy, _ = two_in.shape
    own = slice(TILE, TILE + cy)
    lower, higher = slice(0, TILE), slice(TILE + cy, 2 * TILE + cy)
    low = select_side(py_ref[0], ye_ref, yo_ref, False)
    high = select_side(py_ref[0], ye_ref, yo_ref, True)
    for i in range(3):
        for x in range(cx + 2 * NEAR):
            put_rows(one_ref, (i, x + MID - NEAR), own, zero_in[i, x])
        for k in range(NEAR):
            put_rows(one_ref, (i, k), own, zero_far_in[i, k])
            put_rows(one_ref, (i, cx + 2 * MID - NEAR + k), own, zero_far_in[i, NEAR + k])
            put_rows(two_ref, (i, k), own, one_side_in[i, k])
            put_rows(two_ref, (i, cx + NEAR + k), own, one_side_in[i, NEAR + k])
        for x in range(cx):
            put_rows(two_ref, (i, NEAR + x), own, one_in[i, x])
            for rows, read, turn in ((lower, low, TILE - NEAR), (higher, high, NEAR)):
                tile = read(lambda ref: ref[i, x])
                put_rows(one_ref, (i, MID + x), rows, tile)
                put_rows(two_ref, (i, NEAR + x), rows, half_turn(tile))
                if x < 2 * NEAR:
                    put_rows(one_ref, (i, MID + corner_plane(x, cx)), rows, pltpu.roll(tile, turn, 0))

    def second(start, count):
        def body(x):
            for i in range(3):
                centre, lap = laplacian_rows(one_ref, i, x + MID - NEAR, start, count)
                for h, (c, l) in enumerate(zip(centre, lap)):
                    rows = pl.ds(start, count)
                    two_ref[i, x, h, rows] = 2.0 * c + coef_ref[x, h, rows] * l + two_ref[i, x, h, rows]

        return body

    def third(x):
        for i in range(3):
            centre, lap = laplacian_rows(two_ref, i, x + NEAR, TILE, cy)
            for h, (c, l) in enumerate(zip(centre, lap)):
                lanes = slice(h * LANES, (h + 1) * LANES)
                moved = 2.0 * c - one_ref[i, x + MID, h, own] + coef_ref[x + NEAR, h, own] * l
                final_ref[i, x, :, lanes] = free_final_ref[i, x, :, lanes] + (moved + two_in[i, x, :, lanes])
                prior_ref[i, x, :, lanes] = free_prior_ref[i, x, :, lanes] + c

    ready()
    run_planes(0, NEAR, second(TILE, cy))
    run_planes(NEAR, cx + NEAR, second(px_ref[1], cy + TILE))
    run_planes(cx + NEAR, cx + 2 * NEAR, second(TILE, cy))
    run_planes(0, cx, third)


def staged(kernel, positions, operand_count):
    def run(*refs):
        refs, stages, sems = refs[: -len(positions) - 1], refs[-len(positions) - 1 : -1], refs[-1]
        ins = list(refs[:operand_count])
        copies = []
        for k, (at, stage) in enumerate(zip(positions, stages)):
            copies.append(pltpu.make_async_copy(ins[at], stage, sems.at[k]))
            ins[at] = stage
        for copy in copies:
            copy.start()

        def ready():
            for copy in copies:
                copy.wait()

        kernel(ready, *ins, *refs[operand_count:])

    return run


def local(
    current_field,
    earlier_field,
    wave_coef,
    layer_mask,
    point_xyz,
    point_owner,
    cell_offset,
    wave_vector,
    frequency,
    amplitude,
    phase_index,
    phase_table,
):
    point_count = point_xyz.shape[1]
    slab_count = lax.axis_size("slab")
    comp_count = lax.axis_size("comp")
    device_count = slab_count * comp_count
    slot_count = max(2, 2 * point_count // device_count)
    _, cx, cy, nz = current_field.shape
    assert slot_count <= HALF and device_count % 8 == 0
    assert cx >= DEEP and cy >= 2 * TILE and cy % TILE == 0
    wide = cy + 2 * TILE
    assert nz % LANES == 0 and MID == 2 * NEAR

    def plane_stack(*lead):
        return (*lead, nz // LANES, wide, LANES)

    smem = pl.BlockSpec(memory_space=pltpu.SMEM)
    vmem = pl.BlockSpec(memory_space=pltpu.VMEM)

    def call(kernel, operands, shapes, scratch=(), scalars=0, from_hbm=(), to_hbm=False):
        shapes = [(pltpu.HBM if to_hbm else jax.ShapeDtypeStruct)(shape, F32) for shape in shapes]
        operands = list(operands)
        in_specs = [smem] * scalars + [vmem] * (len(operands) - scalars)
        scratch_shapes = [pltpu.VMEM(shape, F32) for shape in scratch]
        if from_hbm:
            for at in from_hbm:
                operands[at] = pltpu.with_memory_space_constraint(operands[at], pltpu.HBM)
                in_specs[at] = pl.BlockSpec(memory_space=pltpu.HBM)
                scratch_shapes.append(pltpu.VMEM(operands[at].shape, operands[at].dtype))
            scratch_shapes.append(pltpu.SemaphoreType.DMA((len(from_hbm),)))
            kernel = staged(kernel, from_hbm, len(operands))
        return pl.pallas_call(
            kernel,
            out_shape=shapes,
            in_specs=in_specs,
            out_specs=[vmem] * len(shapes),
            scratch_shapes=scratch_shapes,
            compiler_params=pltpu.CompilerParams(vmem_limit_bytes=VMEM_GRANT),
        )(*operands)

    px = jnp.stack([lax.axis_index("slab") % 2, TILE // 2]).astype(jnp.int32)
    py = (lax.axis_index("comp") % 2).astype(jnp.int32).reshape(1)
    fields = (current_field, earlier_field, wave_coef)
    local_comps = frequency.shape[0]
    own_block, *faces = call(
        prepare_kernel,
        (
            py, *fields, wave_vector, frequency.reshape(1, local_comps), amplitude,
            phase_index.reshape(1, local_comps), phase_table.reshape(1, -1),
        ),
        [(8, local_comps)] + [(5, cx, TILE, nz)] * 2,
        scalars=1,
        from_hbm=(1, 2, 3),
    )
    if comp_count == 4:
        near_block = lax.ppermute(own_block, "comp", pair_list(4, 0))
        first_blocks = [own_block, near_block]
        ring = pair_list(4, 1) + [(0, 3), (3, 0)]
        far_block = lax.ppermute(jnp.concatenate(first_blocks, axis=1), "comp", ring)
        last_blocks = [far_block]
    else:
        first_blocks = [own_block]
        last_blocks = [
            lax.ppermute(own_block, "comp", [(i, (i + k) % comp_count) for i in range(comp_count)])
            for k in range(1, comp_count)
        ]
    ye, yo = swap_faces(faces, "comp")
    (sum_one, total_one) = call(
        lambda *refs: first_incident_kernel(len(first_blocks), *refs),
        (*first_blocks, point_xyz),
        [(32, point_count), (16, 256)],
        [(8, point_count)],
    )
    field_tiles = len(plan_tiles(FIELD_PLAN, cy))
    sides = call(
        field_side_kernel,
        (px, py, *fields, layer_mask, ye, yo),
        [(field_tiles, TILE, nz)] * 2,
        scalars=2,
        from_hbm=(2, 3, 4, 5),
    )
    xe, xo = swap_faces(sides, "slab")
    (packed,) = call(
        lambda *refs: last_incident_kernel(len(last_blocks), comp_count, *refs),
        (
            *last_blocks, sum_one, total_one, point_xyz,
            point_owner.reshape(1, point_count), cell_offset.reshape(1, point_count),
        ),
        [(device_count, 1, LIST_ROWS * 2 * HALF)],
        [(8, point_count), (32, point_count)],
    )
    arrived = lax.all_to_all(packed, ("slab", "comp"), split_axis=0, concat_axis=0, tiled=True)
    free_final, free_prior, wide_coef, wide_sign = call(
        first_wave_kernel,
        (px, py, *fields, layer_mask, ye, yo, xe, xo),
        [current_field.shape, current_field.shape, plane_stack(cx + 2 * NEAR), (cx + 2 * MID, cy, nz)],
        [
            plane_stack(3, cx + 2 * DEEP), plane_stack(3, cx + 2 * MID), plane_stack(cx + 2 * MID),
            plane_stack(3, cx + 2 * MID), plane_stack(3, cx + 2 * NEAR),
        ],
        scalars=2,
        from_hbm=(2, 3, 4, 5),
        to_hbm=True,
    )
    held = (device_count // 2 * ROWS_HELD, 2 * HALF)
    zero, one, face_even, face_odd = call(
        near_scatter_kernel,
        (py, arrived, wide_sign),
        [(3, cx + 2 * NEAR, cy, nz), (3, cx, cy, nz)] + [(3, cx, TILE, nz)] * 2,
        [(3, (cx + 2 * NEAR) * cy, nz), (3, cx * cy, nz), held, held],
        scalars=1,
        from_hbm=(2,),
    )
    fye, fyo = swap_faces((face_even, face_odd), "comp")
    zero_far, one_side, two = call(
        rest_scatter_kernel,
        (arrived, wide_sign),
        [(3, 2 * NEAR, cy, nz), (3, 2 * NEAR, cy, nz), (3, cx, cy, nz)],
        [(3, 2 * NEAR * cy, nz), (3, 2 * NEAR * cy, nz), (3, cx * cy, nz), held, held],
        from_hbm=(1,),
    )
    final, prior = call(
        last_wave_kernel,
        (px, py, free_final, free_prior, wide_coef, zero, zero_far, one, one_side, two, fye, fyo),
        [current_field.shape, current_field.shape],
        [plane_stack(3, cx + 2 * MID), plane_stack(3, cx + 2 * NEAR)],
        scalars=2,
        from_hbm=(2, 3, 4),
    )
    return (final, prior)


def solution(mesh):
    in_specs = (
        P(None, "slab", "comp", None),
        P(None, "slab", "comp", None),
        P("slab", "comp", None),
        P("slab", "comp", None),
        P(None, ("slab", "comp")),
        P(("slab", "comp"), None),
        P(("slab", "comp")),
        P(None, "comp"),
        P("comp"),
        P(None, "comp"),
        P("comp"),
        P(),
    )
    out_specs = (P(None, "slab", "comp", None), P(None, "slab", "comp", None))
    return jax.shard_map(local, mesh=mesh, in_specs=in_specs, out_specs=out_specs, check_vma=False)
```

```python
import jax
import jax.numpy as jnp
from jax import lax
from jax.experimental import pallas as pl
from jax.experimental.pallas import tpu as pltpu
from jax.sharding import PartitionSpec as P

step_size = 0.05
near_weight = 4.0 / 3.0
far_weight = -1.0 / 12.0
centre_weight = -7.5
inv_two_pi = 0.15915494309189535

LEAD = -0.7713118195533752
SIN_C = (4.442834854125977 / LEAD, -7.306587219238281 / LEAD, 3.588636875152588 / LEAD)
SIN_SCALE = LEAD * abs(LEAD)
VER_SCALE = LEAD * LEAD
HALF = 64
OWN_TILES = 5
SIDE_TILES = 4
HIGH_LIST = OWN_TILES
LOW_LIST = OWN_TILES + SIDE_TILES
LIST_ROWS = OWN_TILES + 2 * SIDE_TILES
VMEM_GRANT = 16 * 2**20

F32 = jnp.float32
BF16 = jnp.bfloat16


def sin_versine(u):
    r = u - jnp.round(u)
    z = r * r
    s = r * (((z + SIN_C[2]) * z + SIN_C[1]) * z + SIN_C[0])
    q = s * s
    w = 2.0 / VER_SCALE - q
    return s * (w * lax.rsqrt(w)), q


def split_three(x):
    hi = x.astype(BF16).astype(F32)
    rest = x - hi
    mid = rest.astype(BF16).astype(F32)
    return hi, mid, rest - mid


def row_ids(shape):
    return lax.broadcasted_iota(jnp.int32, shape, 0)


def add_components(par_refs, xyz_ref, x8_ref, acc_ref):
    points = xyz_ref.shape[1]
    kc = 256
    tile = 256
    x8_ref[...] = jnp.zeros(x8_ref.shape, F32)
    x8_ref[0:3, :] = xyz_ref[...]
    xhi, xmid, xlo = split_three(x8_ref[...])
    right = jnp.concatenate([xhi, xmid, xlo, xhi, xmid, xhi], axis=0).astype(BF16)
    rows8 = row_ids((8, kc))
    times = step_size * (rows8 + 1).astype(F32)
    rows16 = row_ids((16, kc))
    comp_row = jnp.where(rows16 < 6, rows16 % 3, (rows16 + 2) % 3)
    valued = (rows16 < 10) & (rows16 != 6)

    def body(par_ref, step, total):
        blk = par_ref[:, pl.ds(pl.multiple_of(step * kc, kc), kc)]
        kv = jnp.where(rows8 < 3, blk * inv_two_pi, 0.0)
        khi, kmid, klo = split_three(kv)
        left = jnp.concatenate([khi, khi, khi, kmid, kmid, klo], axis=0).astype(BF16)
        delays = times * blk[3:4, :] - blk[7:8, :]
        sd, qd = sin_versine(delays * inv_two_pi)
        sd, cd = SIN_SCALE * sd, 1.0 - VER_SCALE * qd
        amp = jnp.where(comp_row == 0, blk[4:5, :], jnp.where(comp_row == 1, blk[5:6, :], blk[6:7, :]))
        amp = jnp.where(valued, amp, 0.0)

        def rows_of(t):
            w = amp * jnp.where(rows16 < 3, t[0:1, :], jnp.where(rows16 < 6, t[1:2, :], t[2:3, :]))
            hi = w.astype(BF16)
            lo = (w - hi.astype(F32)).astype(BF16)
            return w, jnp.concatenate([hi, lo], axis=0)

        wc = rows_of(cd)[0]
        lc = rows_of(-VER_SCALE * cd)[1]
        ls = rows_of(SIN_SCALE * sd)[1]
        for t in range(points // tile):
            cols = slice(t * tile, (t + 1) * tile)
            u = lax.dot_general(left, right[:, cols], (((0,), (0,)), ((), ())), preferred_element_type=F32)
            highs, lows = [], []
            for j in range(kc // 32):
                for value in sin_versine(u[32 * j : 32 * j + 32]):
                    high = value.astype(BF16)
                    highs.append(high)
                    lows.append((value - high.astype(F32)).astype(BF16))
            part = jnp.dot(ls, jnp.concatenate(highs[0::2], axis=0), preferred_element_type=F32)
            part += jnp.dot(lc, jnp.concatenate(highs[1::2], axis=0), preferred_element_type=F32)
            part += jnp.dot(ls, jnp.concatenate(lows[0::2], axis=0), preferred_element_type=F32)
            part += jnp.dot(lc, jnp.concatenate(lows[1::2], axis=0), preferred_element_type=F32)
            acc_ref[:, cols] += part
        return total + wc

    total = jnp.zeros((16, kc), F32)
    for par_ref in par_refs:
        steps = par_ref.shape[1] // kc
        total = lax.fori_loop(0, steps, lambda step, t, ref=par_ref: body(ref, step, t), total)
    return total


def first_incident_kernel(count, ready, *refs):
    ready()
    par_refs, (xyz_ref, acc_ref, total_ref, x8_ref) = refs[:count], refs[count:]
    acc_ref[...] = jnp.zeros(acc_ref.shape, F32)
    total_ref[...] = add_components(par_refs, xyz_ref, x8_ref, acc_ref)


def last_incident_kernel(count, step, ready, *refs):
    ready()
    par_refs, refs = refs[:count], refs[count:]
    first_ref, first_total_ref, xyz_ref, own_ref, off_ref, out_ref, x8_ref, acc_ref = refs
    points = xyz_ref.shape[1]
    owners = out_ref.shape[0]
    acc_ref[...] = first_ref[...]
    total = add_components(par_refs, xyz_ref, x8_ref, acc_ref) + first_total_ref[...]
    vals = acc_ref[0:16, :] + acc_ref[16:32, :] + jnp.sum(total, axis=1, keepdims=True)
    vals = jnp.where(row_ids((16, points)) == 6, off_ref[...].astype(F32), vals)
    v1, v2, v3 = split_three(vals)
    named = own_ref[...] == row_ids((owners, points))
    named_one = named.astype(F32).astype(BF16)
    earlier = row_ids((points, points)) < lax.broadcasted_iota(jnp.int32, (points, points), 1)
    before = jnp.dot(named_one, earlier.astype(F32).astype(BF16), preferred_element_type=F32)
    rank = jnp.sum(jnp.where(named, before, 0.0), axis=0, keepdims=True).astype(jnp.int32)
    terms = [v.astype(BF16) for v in (v1, v2, v3)]
    tiles = 0.0
    for odd in (0, 1):
        left = jnp.concatenate(
            [named_one * t[2 * j + odd : 2 * j + odd + 1, :] for t in terms for j in range(OWN_TILES)], axis=0
        )
        spots = (row_ids((2 * HALF, points)) == rank + odd * HALF).astype(F32).astype(BF16)
        got = lax.dot_general(left, spots, (((1,), (1,)), ((), ())), preferred_element_type=F32)
        size = OWN_TILES * owners
        tiles = tiles + (got[0:size] + got[size : 2 * size] + got[2 * size :])
    owner_row = row_ids((owners, 2 * HALF))

    def put(j, tile):
        out_ref[:, 0, 2 * HALF * j : 2 * HALF * (j + 1)] = tile

    for j in range(OWN_TILES):
        tile = tiles[j * owners : (j + 1) * owners]
        put(j, tile)
        if j < SIDE_TILES:
            above = pltpu.roll(tile, owners - step, 0)
            put(HIGH_LIST + j, jnp.where(owner_row < owners - step, above, 0.0))
            put(LOW_LIST + j, jnp.where(owner_row >= step, pltpu.roll(tile, step, 0), 0.0))


TILE = 8
DEEP = 6
MID = 4
NEAR = 2


def half_turn(tile):
    return pltpu.roll(tile, TILE // 2, 0)


ROWS_HELD = 16


def scatter_lists(val_ref, even_ref, odd_ref, jobs, cy, nz):
    lanes = 2 * HALF
    sources = val_ref.shape[0]
    groups = sources // 2
    chunk = 2 * lanes
    left_half = lax.broadcasted_iota(jnp.int32, (groups, lanes), 1) < lanes // 2
    for ref in {id(job[4]): job[4] for job in jobs}.values():
        ref[...] = jnp.zeros(ref.shape, F32)
    for j in range(LIST_ROWS):
        rows = val_ref[:, 0, lanes * j : lanes * (j + 1)]
        first, second = rows[0:groups], rows[groups:]
        at = pl.ds(j, groups, stride=ROWS_HELD)
        even_ref[at, :] = jnp.where(left_half, first, pltpu.roll(second, lanes // 2, 1))
        odd_ref[at, :] = jnp.where(left_half, pltpu.roll(first, lanes // 2, 1), second)

    def body(step, carry):
        evens, odds = [], []
        for pair in range(2):
            at = pl.ds(pl.multiple_of((2 * step + pair) * ROWS_HELD, ROWS_HELD), ROWS_HELD)
            evens.append(even_ref[at, :])
            odds.append(odd_ref[at, :])
        values = [jnp.concatenate(evens, axis=1), jnp.concatenate(odds, axis=1)]
        high = [v.astype(BF16) for v in values]
        low = [(v - h.astype(F32)).astype(BF16) for v, h in zip(values, high)]
        for base in (0, HIGH_LIST, LOW_LIST):
            own_jobs = [job for job in jobs if job[0] == base]
            off = values[0][base + 3 : base + 4, :].astype(jnp.int32)
            row = off // nz
            zt = (row_ids((nz, chunk)) == off - row * nz).astype(F32).astype(BF16)
            masks, left = {}, []
            for _, ranks, plane, planes, ref, start in own_jobs:
                if (plane, planes) not in masks:
                    ids = row_ids((planes * cy, chunk)) + plane * cy
                    masks[plane, planes] = (ids == row).astype(F32).astype(BF16)
                for r in ranks:
                    at = base + r // 2
                    left += [masks[plane, planes] * t[r % 2][at : at + 1, :] for t in (high, low)]
            left = jnp.concatenate(left, axis=0)
            got = lax.dot_general(left, zt, (((1,), (1,)), ((), ())), preferred_element_type=F32)
            at = 0
            for _, ranks, _, planes, ref, start in own_jobs:
                size = planes * cy
                for i in range(len(ranks)):
                    ref[i, start : start + size] += got[at : at + size] + got[at + size : at + 2 * size]
                    at += 2 * size
        return carry

    lax.fori_loop(0, groups // 2, body, 0)


STEP_ROWS = ((0, 1, 2), (3, 4, 5), (7, 8, 9))


def near_scatter_kernel(
    ready, par_ref, val_ref, sign_ref, zero_out, one_out, even_out, odd_out, zero_ref, one_ref, even_ref, odd_ref
):
    _, cx, cy, nz = one_out.shape
    jobs = (
        (0, STEP_ROWS[0], 0, cx, zero_ref, NEAR * cy),
        (0, STEP_ROWS[1], 0, cx, one_ref, 0),
        (HIGH_LIST, STEP_ROWS[0], 0, NEAR, zero_ref, (NEAR + cx) * cy),
        (LOW_LIST, STEP_ROWS[0], cx - NEAR, NEAR, zero_ref, 0),
    )
    scatter_lists(val_ref, even_ref, odd_ref, jobs, cy, nz)
    ready()
    sign = sign_ref[...]
    for i in range(3):
        zero_out[i] = zero_ref[i].reshape(zero_out.shape[1:]) * sign[MID - NEAR : MID + cx + NEAR]
        one_out[i] = one_ref[i].reshape(one_out.shape[1:]) * sign[MID : MID + cx]
    at = row_ids((TILE, nz))

    def write(is_high, face_ref):
        ys = slice(cy - TILE, cy) if is_high else slice(0, TILE)
        half = at >= TILE // 2 if is_high else at < TILE // 2
        corner = at < NEAR if is_high else at >= TILE - NEAR
        for i in range(3):
            for x in range(cx):
                tile = jnp.where(half, zero_out[i, NEAR + x, ys], half_turn(one_out[i, x, ys]))
                if x < 2 * NEAR:
                    moved = pltpu.roll(zero_out[i, NEAR + corner_plane(x, cx), ys], NEAR if is_high else TILE - NEAR, 0)
                    tile = jnp.where(corner, moved, tile)
                face_ref[i, x] = tile

    write_faces(par_ref[0], write, even_out, odd_out)


def rest_scatter_kernel(
    ready, val_ref, sign_ref, zero_out, one_out, two_out, zero_ref, one_ref, two_ref, even_ref, odd_ref
):
    _, cx, cy, nz = two_out.shape
    jobs = (
        (0, STEP_ROWS[2], 0, cx, two_ref, 0),
        (HIGH_LIST, STEP_ROWS[0], NEAR, MID - NEAR, zero_ref, NEAR * cy),
        (LOW_LIST, STEP_ROWS[0], cx - MID, MID - NEAR, zero_ref, 0),
        (HIGH_LIST, STEP_ROWS[1], 0, NEAR, one_ref, NEAR * cy),
        (LOW_LIST, STEP_ROWS[1], cx - NEAR, NEAR, one_ref, 0),
    )
    scatter_lists(val_ref, even_ref, odd_ref, jobs, cy, nz)
    ready()
    sign = sign_ref[...]
    last = cx + 2 * MID
    far = jnp.concatenate([sign[0 : MID - NEAR], sign[last - (MID - NEAR) :]], axis=0)
    side = jnp.concatenate([sign[MID - NEAR : MID], sign[MID + cx : MID + cx + NEAR]], axis=0)
    for i in range(3):
        zero_out[i] = zero_ref[i].reshape(zero_out.shape[1:]) * far
        one_out[i] = one_ref[i].reshape(one_out.shape[1:]) * side
        two_out[i] = two_ref[i].reshape(two_out.shape[1:]) * sign[MID : MID + cx]


def corner_plane(x, cx):
    return x - NEAR if x < NEAR else cx + x - NEAR


def write_faces(parity, write, even_out, odd_out):
    @pl.when(parity == 0)
    def _():
        write(True, even_out)
        write(False, odd_out)

    @pl.when(parity != 0)
    def _():
        write(False, even_out)
        write(True, odd_out)


def pair_list(count, odd):
    first = 1 if odd else 0
    pairs = [(i, i + 1) for i in range(first, count - 1, 2)]
    return pairs + [(j, i) for i, j in pairs]


def swap_faces(faces, axis):
    count = lax.axis_size(axis)
    out = []
    for k in (0, 1):
        out.append(lax.ppermute(faces[k], axis, pair_list(count, k)))
    return out


def prepare_kernel(
    ready, par_ref, cur_ref, ear_ref, coef_ref, wave_ref, freq_ref, amp_ref, index_ref, table_ref,
    block_out, even_out, odd_out,
):
    ready()
    entries = table_ref.shape[1]
    comps = index_ref.shape[1]
    picked = (row_ids((entries, comps)) == index_ref[...]).astype(F32).astype(BF16)
    terms = jnp.concatenate(list(split_three(jnp.broadcast_to(table_ref[...], (TILE, entries)))), axis=0).astype(BF16)
    phase = jnp.dot(terms, picked, preferred_element_type=F32)
    block_out[0:3, :] = wave_ref[...]
    block_out[3:4, :] = freq_ref[...]
    block_out[4:7, :] = amp_ref[...]
    block_out[7:8, :] = phase[0:1] + phase[TILE : TILE + 1] + phase[2 * TILE : 2 * TILE + 1]
    _, cx, cy, nz = cur_ref.shape
    upper = row_ids((TILE, nz)) >= TILE // 2

    def write(high, face_ref):
        ys = slice(cy - TILE, cy) if high else slice(0, TILE)
        keep = upper if high else ~upper
        for x in range(cx):
            for i in range(3):
                face_ref[i, x] = cur_ref[i, x, ys]
            face_ref[3, x] = jnp.where(keep, ear_ref[0, x, ys], half_turn(ear_ref[1, x, ys]))
            face_ref[4, x] = jnp.where(keep, ear_ref[2, x, ys], half_turn(coef_ref[x, ys]))

    write_faces(par_ref[0], write, even_out, odd_out)


def face_tile(ref, name, x):
    if name < 3:
        return ref[name, x]
    tile = ref[3 + (name - 3) // 2, x]
    return half_turn(tile) if name in (4, 6) else tile


def select_side(parity, even_ref, odd_ref, high):
    from_even = (parity == 0) if high else (parity == 1)

    def read(get):
        return jnp.where(from_even, get(even_ref), get(odd_ref))

    return read


FIELD_PLAN = [(DEEP, MID)] * 3 + [(MID, NEAR)] * 4 + [(MID, 0)]
SIDE_PLANES = sum(planes for planes, _ in FIELD_PLAN)
CORNERS = [(name, dist) for name, (_, corners) in enumerate(FIELD_PLAN) for dist in range(1, corners + 1)]


def side_plane(name, dist, is_high):
    planes = FIELD_PLAN[name][0]
    first = sum(n for n, _ in FIELD_PLAN[:name])
    return first + (dist - 1 if is_high else planes - dist)


def corner_place(k, cy):
    per_plane = cy // TILE
    start = k % per_plane * TILE
    return SIDE_PLANES + k // per_plane, slice(start, start + TILE)


def side_planes_sent(cy):
    return SIDE_PLANES + -(-len(CORNERS) // (cy // TILE))


def sign_of(mask):
    return (mask == 1).astype(F32) - (mask == 2).astype(F32)


def field_side_kernel(
    ready, px_ref, py_ref, cur_ref, ear_ref, coef_ref, mask_ref, even_ref, odd_ref, even_out, odd_out,
    corner_ref, sign_ref, sems,
):
    _, cx, cy, nz = cur_ref.shape
    upper = row_ids((TILE, nz)) >= TILE // 2
    low = select_side(py_ref[0], even_ref, odd_ref, False)
    high = select_side(py_ref[0], even_ref, odd_ref, True)
    sources = [cur_ref.at[i] for i in range(3)] + [ear_ref.at[i] for i in range(3)] + [coef_ref]

    def copies_of(is_high, face, out):
        out_copies = []
        for name, source in enumerate(sources):
            planes = FIELD_PLAN[name][0]
            x = cx - planes if is_high else 0
            first = sum(n for n, _ in FIELD_PLAN[:name])
            out_copies.append(
                pltpu.make_async_copy(
                    source.at[pl.ds(x, planes)], out.at[pl.ds(first, planes)], sems.at[face, name]
                )
            )
        return out_copies

    def late_copies(face, out):
        signs = pl.ds(SIDE_PLANES - MID, MID)
        rest = pl.ds(SIDE_PLANES, corner_ref.shape[1])
        return [
            pltpu.make_async_copy(sign_ref.at[face], out.at[signs], sems.at[face, len(sources)]),
            pltpu.make_async_copy(corner_ref.at[face], out.at[rest], sems.at[face, len(sources) + 1]),
        ]

    def run(high_out, low_out):
        faces = ((True, 0, high_out), (False, 1, low_out))
        early = [copy for is_high, face, out in faces for copy in copies_of(is_high, face, out)]
        for copy in early:
            copy.start()
        for is_high, face, _ in faces:
            for k, (name, dist) in enumerate(CORNERS):
                x = cx - dist if is_high else dist - 1
                below = low(lambda ref: face_tile(ref, name, x))
                above = high(lambda ref: face_tile(ref, name, x))
                plane, rows = corner_place(k, cy)
                corner_ref[face, plane - SIDE_PLANES, rows] = jnp.where(upper, below, above)
        ready()
        for is_high, face, _ in faces:
            for k in range(MID):
                sign_ref[face, k] = sign_of(mask_ref[cx - MID + k if is_high else k])
        late = [copy for _, face, out in faces for copy in late_copies(face, out)]
        for copy in late:
            copy.start()
        for copy in early + late:
            copy.wait()

    @pl.when(px_ref[0] == 0)
    def _():
        run(even_out, odd_out)

    @pl.when(px_ref[0] != 0)
    def _():
        run(odd_out, even_out)


LANES = 128


def put_rows(ref, index, rows, value):
    for h in range(value.shape[1] // LANES):
        ref[(*index, h, rows)] = value[:, h * LANES : (h + 1) * LANES]


def laplacian_rows(ref, i, x, start, count):
    tiles = ref.shape[2]
    lane = lax.broadcasted_iota(jnp.int32, (count, LANES), 1)

    def rows(h, dx, dy):
        return ref[i, x + dx, h, pl.ds(start + dy, count)]

    centre = [rows(h, 0, 0) for h in range(tiles)]
    out = [centre_weight * c for c in centre]
    for k, weight in ((1, near_weight), (2, far_weight)):
        up = [pltpu.roll(c, k, 1) for c in centre]
        down = [pltpu.roll(c, LANES - k, 1) for c in centre]
        for h in range(tiles):
            below = jnp.where(lane >= k, up[h], up[h - 1] if h else 0.0)
            above = jnp.where(lane < LANES - k, down[h], down[h + 1] if h + 1 < tiles else 0.0)
            across = (rows(h, -k, 0) + rows(h, k, 0)) + (rows(h, 0, -k) + rows(h, 0, k))
            out[h] = out[h] + weight * (across + (below + above))
    return centre, out


def run_planes(first, last, body):
    lax.fori_loop(first, last, lambda x, carry: (body(x), carry)[1], 0, unroll=2)


def first_wave_kernel(
    ready, px_ref, py_ref, cur_ref, ear_ref, coef_ref, mask_ref, ye_ref, yo_ref, xe_ref, xo_ref,
    final_ref, prior_ref, wide_coef_ref, wide_sign_ref, u_ref, e_ref, c_ref, one_ref, two_ref,
):
    _, cx, cy, _ = cur_ref.shape
    own = slice(TILE, TILE + cy)
    lower, higher = slice(0, TILE), slice(TILE + cy, 2 * TILE + cy)
    low = select_side(py_ref[0], ye_ref, yo_ref, False)
    high = select_side(py_ref[0], ye_ref, yo_ref, True)
    ready()

    def put(name, x, rows, value):
        if name < 3:
            put_rows(u_ref, (name, DEEP + x), rows, value)
        elif name < 6:
            put_rows(e_ref, (name - 3, MID + x), rows, value)
        elif name == 6:
            put_rows(c_ref, (MID + x,), rows, value)
            if -NEAR <= x < cx + NEAR:
                put_rows(wide_coef_ref, (NEAR + x,), rows, value)
        else:
            wide_sign_ref[MID + x, slice(rows.start - TILE, rows.stop - TILE)] = value

    for x in range(cx):
        for name in range(7):
            value = cur_ref[name, x] if name < 3 else ear_ref[name - 3, x] if name < 6 else coef_ref[x]
            put(name, x, own, value)
            put(name, x, lower, low(lambda ref: face_tile(ref, name, x)))
            put(name, x, higher, high(lambda ref: face_tile(ref, name, x)))
        put(7, x, own, sign_of(mask_ref[x]))
    for is_high in (False, True):
        read = select_side(px_ref[0], xe_ref, xo_ref, is_high)
        for name, (planes, _) in enumerate(FIELD_PLAN):
            for dist in range(1, planes + 1):
                x = cx - 1 + dist if is_high else -dist
                put(name, x, own, read(lambda ref: ref[side_plane(name, dist, is_high)]))
        for k, (name, dist) in enumerate(CORNERS):
            x = cx - 1 + dist if is_high else -dist
            plane, rows = corner_place(k, cy)
            tile = read(lambda ref: ref[plane, rows])
            put(name, x, lower, tile)
            put(name, x, higher, tile)

    begin = px_ref[1]
    deep = cy + TILE

    def first(start, count):
        def body(x):
            for i in range(3):
                centre, lap = laplacian_rows(u_ref, i, x + DEEP - MID, start, count)
                for h, (c, l) in enumerate(zip(centre, lap)):
                    rows = pl.ds(start, count)
                    one_ref[i, x, h, rows] = 2.0 * c - e_ref[i, x, h, rows] + c_ref[x, h, rows] * l

        return body

    def second(start, count):
        def body(x):
            for i in range(3):
                centre, lap = laplacian_rows(one_ref, i, x + MID - NEAR, start, count)
                for h, (c, l) in enumerate(zip(centre, lap)):
                    rows = pl.ds(start, count)
                    moved = 2.0 * c - u_ref[i, x + DEEP - NEAR, h, rows]
                    two_ref[i, x, h, rows] = moved + c_ref[x + MID - NEAR, h, rows] * l

        return body

    def third(x):
        for i in range(3):
            centre, lap = laplacian_rows(two_ref, i, x + NEAR, TILE, cy)
            for h, (c, l) in enumerate(zip(centre, lap)):
                lanes = slice(h * LANES, (h + 1) * LANES)
                moved = 2.0 * c - one_ref[i, x + MID, h, own]
                final_ref[i, x, :, lanes] = moved + c_ref[x + MID, h, own] * l
                prior_ref[i, x, :, lanes] = c

    run_planes(0, NEAR, first(TILE, cy))
    run_planes(NEAR, cx + 2 * MID - NEAR, first(begin, deep))
    run_planes(cx + 2 * MID - NEAR, cx + 2 * MID, first(TILE, cy))
    run_planes(0, NEAR, second(TILE, cy))
    run_planes(NEAR, cx + NEAR, second(begin, deep))
    run_planes(cx + NEAR, cx + 2 * NEAR, second(TILE, cy))
    run_planes(0, cx, third)


def last_wave_kernel(
    ready, px_ref, py_ref, free_final_ref, free_prior_ref, coef_ref, zero_in, zero_far_in, one_in, one_side_in, two_in,
    ye_ref, yo_ref, final_ref, prior_ref, one_ref, two_ref,
):
    _, cx, cy, _ = two_in.shape
    own = slice(TILE, TILE + cy)
    lower, higher = slice(0, TILE), slice(TILE + cy, 2 * TILE + cy)
    low = select_side(py_ref[0], ye_ref, yo_ref, False)
    high = select_side(py_ref[0], ye_ref, yo_ref, True)
    for i in range(3):
        for x in range(cx + 2 * NEAR):
            put_rows(one_ref, (i, x + MID - NEAR), own, zero_in[i, x])
        for k in range(NEAR):
            put_rows(one_ref, (i, k), own, zero_far_in[i, k])
            put_rows(one_ref, (i, cx + 2 * MID - NEAR + k), own, zero_far_in[i, NEAR + k])
            put_rows(two_ref, (i, k), own, one_side_in[i, k])
            put_rows(two_ref, (i, cx + NEAR + k), own, one_side_in[i, NEAR + k])
        for x in range(cx):
            put_rows(two_ref, (i, NEAR + x), own, one_in[i, x])
            for rows, read, turn in ((lower, low, TILE - NEAR), (higher, high, NEAR)):
                tile = read(lambda ref: ref[i, x])
                put_rows(one_ref, (i, MID + x), rows, tile)
                put_rows(two_ref, (i, NEAR + x), rows, half_turn(tile))
                if x < 2 * NEAR:
                    put_rows(one_ref, (i, MID + corner_plane(x, cx)), rows, pltpu.roll(tile, turn, 0))

    def second(start, count):
        def body(x):
            for i in range(3):
                centre, lap = laplacian_rows(one_ref, i, x + MID - NEAR, start, count)
                for h, (c, l) in enumerate(zip(centre, lap)):
                    rows = pl.ds(start, count)
                    two_ref[i, x, h, rows] = 2.0 * c + coef_ref[x, h, rows] * l + two_ref[i, x, h, rows]

        return body

    def third(x):
        for i in range(3):
            centre, lap = laplacian_rows(two_ref, i, x + NEAR, TILE, cy)
            for h, (c, l) in enumerate(zip(centre, lap)):
                lanes = slice(h * LANES, (h + 1) * LANES)
                moved = 2.0 * c - one_ref[i, x + MID, h, own] + coef_ref[x + NEAR, h, own] * l
                final_ref[i, x, :, lanes] = free_final_ref[i, x, :, lanes] + (moved + two_in[i, x, :, lanes])
                prior_ref[i, x, :, lanes] = free_prior_ref[i, x, :, lanes] + c

    ready()
    run_planes(0, NEAR, second(TILE, cy))
    run_planes(NEAR, cx + NEAR, second(px_ref[1], cy + TILE))
    run_planes(cx + NEAR, cx + 2 * NEAR, second(TILE, cy))
    run_planes(0, cx, third)


def staged(kernel, positions, operand_count):
    def run(*refs):
        refs, stages, sems = refs[: -len(positions) - 1], refs[-len(positions) - 1 : -1], refs[-1]
        ins = list(refs[:operand_count])
        copies = []
        for k, (at, stage) in enumerate(zip(positions, stages)):
            copies.append(pltpu.make_async_copy(ins[at], stage, sems.at[k]))
            ins[at] = stage
        for copy in copies:
            copy.start()

        def ready():
            for copy in copies:
                copy.wait()

        kernel(ready, *ins, *refs[operand_count:])

    return run


def local(
    current_field,
    earlier_field,
    wave_coef,
    layer_mask,
    point_xyz,
    point_owner,
    cell_offset,
    wave_vector,
    frequency,
    amplitude,
    phase_index,
    phase_table,
):
    point_count = point_xyz.shape[1]
    slab_count = lax.axis_size("slab")
    comp_count = lax.axis_size("comp")
    device_count = slab_count * comp_count
    slot_count = max(2, 2 * point_count // device_count)
    _, cx, cy, nz = current_field.shape
    assert slot_count <= HALF and device_count % 8 == 0
    assert cx >= DEEP and cy >= 2 * TILE and cy % TILE == 0
    wide = cy + 2 * TILE
    assert nz % LANES == 0 and MID == 2 * NEAR

    def plane_stack(*lead):
        return (*lead, nz // LANES, wide, LANES)

    smem = pl.BlockSpec(memory_space=pltpu.SMEM)
    vmem = pl.BlockSpec(memory_space=pltpu.VMEM)

    def call(kernel, operands, shapes, scratch=(), scalars=0, from_hbm=(), left_in_hbm=(), to_hbm=False, raw_outputs=False):
        shapes = [(pltpu.HBM if to_hbm else jax.ShapeDtypeStruct)(shape, F32) for shape in shapes]
        operands = list(operands)
        in_specs = [smem] * scalars + [vmem] * (len(operands) - scalars)
        scratch_shapes = [pltpu.VMEM(shape, F32) if isinstance(shape, tuple) else shape for shape in scratch]
        hbm = pl.BlockSpec(memory_space=pltpu.HBM)
        for at in left_in_hbm:
            operands[at] = pltpu.with_memory_space_constraint(operands[at], pltpu.HBM)
            in_specs[at] = hbm
        if from_hbm:
            for at in from_hbm:
                operands[at] = pltpu.with_memory_space_constraint(operands[at], pltpu.HBM)
                in_specs[at] = hbm
                scratch_shapes.append(pltpu.VMEM(operands[at].shape, operands[at].dtype))
            scratch_shapes.append(pltpu.SemaphoreType.DMA((len(from_hbm),)))
            kernel = staged(kernel, from_hbm, len(operands))
        return pl.pallas_call(
            kernel,
            out_shape=shapes,
            in_specs=in_specs,
            out_specs=[hbm if raw_outputs else vmem] * len(shapes),
            scratch_shapes=scratch_shapes,
            compiler_params=pltpu.CompilerParams(vmem_limit_bytes=VMEM_GRANT),
        )(*operands)

    px = jnp.stack([lax.axis_index("slab") % 2, TILE // 2]).astype(jnp.int32)
    py = (lax.axis_index("comp") % 2).astype(jnp.int32).reshape(1)
    fields = (current_field, earlier_field, wave_coef)
    local_comps = frequency.shape[0]
    own_block, *faces = call(
        prepare_kernel,
        (
            py, *fields, wave_vector, frequency.reshape(1, local_comps), amplitude,
            phase_index.reshape(1, local_comps), phase_table.reshape(1, -1),
        ),
        [(8, local_comps)] + [(5, cx, TILE, nz)] * 2,
        scalars=1,
        from_hbm=tuple(range(1, 9)),
    )
    if comp_count == 4:
        near_block = lax.ppermute(own_block, "comp", pair_list(4, 0))
        first_blocks = [own_block, near_block]
        ring = pair_list(4, 1) + [(0, 3), (3, 0)]
        far_block = lax.ppermute(jnp.concatenate(first_blocks, axis=1), "comp", ring)
        last_blocks = [far_block]
    else:
        first_blocks = [own_block]
        last_blocks = [
            lax.ppermute(own_block, "comp", [(i, (i + k) % comp_count) for i in range(comp_count)])
            for k in range(1, comp_count)
        ]
    ye, yo = swap_faces(faces, "comp")
    (sum_one, total_one) = call(
        lambda *refs: first_incident_kernel(len(first_blocks), *refs),
        (*first_blocks, point_xyz),
        [(32, point_count), (16, 256)],
        [(8, point_count)],
        from_hbm=(len(first_blocks),),
    )
    sent = side_planes_sent(cy)
    sides = call(
        field_side_kernel,
        (px, py, *fields, layer_mask, ye, yo),
        [(sent, cy, nz)] * 2,
        [(2, sent - SIDE_PLANES, cy, nz), (2, MID, cy, nz), pltpu.SemaphoreType.DMA((2, len(FIELD_PLAN) + 1))],
        scalars=2,
        from_hbm=(5,),
        left_in_hbm=(2, 3, 4),
        to_hbm=True,
        raw_outputs=True,
    )
    xe, xo = swap_faces(sides, "slab")
    (packed,) = call(
        lambda *refs: last_incident_kernel(len(last_blocks), comp_count, *refs),
        (
            *last_blocks, sum_one, total_one, point_xyz,
            point_owner.reshape(1, point_count), cell_offset.reshape(1, point_count),
        ),
        [(device_count, 1, LIST_ROWS * 2 * HALF)],
        [(8, point_count), (32, point_count)],
        from_hbm=tuple(len(last_blocks) + k for k in (2, 3, 4)),
    )
    arrived = lax.all_to_all(packed, ("slab", "comp"), split_axis=0, concat_axis=0, tiled=True)
    free_final, free_prior, wide_coef, wide_sign = call(
        first_wave_kernel,
        (px, py, *fields, layer_mask, ye, yo, xe, xo),
        [current_field.shape, current_field.shape, plane_stack(cx + 2 * NEAR), (cx + 2 * MID, cy, nz)],
        [
            plane_stack(3, cx + 2 * DEEP), plane_stack(3, cx + 2 * MID), plane_stack(cx + 2 * MID),
            plane_stack(3, cx + 2 * MID), plane_stack(3, cx + 2 * NEAR),
        ],
        scalars=2,
        from_hbm=(2, 3, 4, 5),
        to_hbm=True,
    )
    held = (device_count // 2 * ROWS_HELD, 2 * HALF)
    zero, one, face_even, face_odd = call(
        near_scatter_kernel,
        (py, arrived, wide_sign),
        [(3, cx + 2 * NEAR, cy, nz), (3, cx, cy, nz)] + [(3, cx, TILE, nz)] * 2,
        [(3, (cx + 2 * NEAR) * cy, nz), (3, cx * cy, nz), held, held],
        scalars=1,
        from_hbm=(2,),
    )
    fye, fyo = swap_faces((face_even, face_odd), "comp")
    zero_far, one_side, two = call(
        rest_scatter_kernel,
        (arrived, wide_sign),
        [(3, 2 * NEAR, cy, nz), (3, 2 * NEAR, cy, nz), (3, cx, cy, nz)],
        [(3, 2 * NEAR * cy, nz), (3, 2 * NEAR * cy, nz), (3, cx * cy, nz), held, held],
        from_hbm=(1,),
    )
    final, prior = call(
        last_wave_kernel,
        (px, py, free_final, free_prior, wide_coef, zero, zero_far, one, one_side, two, fye, fyo),
        [current_field.shape, current_field.shape],
        [plane_stack(3, cx + 2 * MID), plane_stack(3, cx + 2 * NEAR)],
        scalars=2,
        from_hbm=(2, 3, 4),
    )
    return (final, prior)


def solution(mesh):
    in_specs = (
        P(None, "slab", "comp", None),
        P(None, "slab", "comp", None),
        P("slab", "comp", None),
        P("slab", "comp", None),
        P(None, ("slab", "comp")),
        P(("slab", "comp"), None),
        P(("slab", "comp")),
        P(None, "comp"),
        P("comp"),
        P(None, "comp"),
        P("comp"),
        P(),
    )
    out_specs = (P(None, "slab", "comp", None), P(None, "slab", "comp", None))
    return jax.shard_map(local, mesh=mesh, in_specs=in_specs, out_specs=out_specs, check_vma=False)
```

```python
import jax
import jax.numpy as jnp
from jax import lax
from jax.experimental import pallas as pl
from jax.experimental.pallas import tpu as pltpu
from jax.sharding import PartitionSpec as P

step_size = 0.05
near_weight = 4.0 / 3.0
far_weight = -1.0 / 12.0
centre_weight = -7.5
inv_two_pi = 0.15915494309189535

LEAD = -0.7713118195533752
SIN_C = (4.442834854125977 / LEAD, -7.306587219238281 / LEAD, 3.588636875152588 / LEAD)
SIN_SCALE = LEAD * abs(LEAD)
VER_SCALE = LEAD * LEAD
HALF = 64
OWN_TILES = 5
SIDE_TILES = 4
HIGH_LIST = OWN_TILES
LOW_LIST = OWN_TILES + SIDE_TILES
LIST_ROWS = OWN_TILES + 2 * SIDE_TILES
VMEM_GRANT = 16 * 2**20

F32 = jnp.float32
BF16 = jnp.bfloat16


def sin_versine(u):
    r = u - jnp.round(u)
    z = r * r
    s = r * (((z + SIN_C[2]) * z + SIN_C[1]) * z + SIN_C[0])
    q = s * s
    w = 2.0 / VER_SCALE - q
    return s * (w * lax.rsqrt(w)), q


def split_three(x):
    hi = x.astype(BF16).astype(F32)
    rest = x - hi
    mid = rest.astype(BF16).astype(F32)
    return hi, mid, rest - mid


def row_ids(shape):
    return lax.broadcasted_iota(jnp.int32, shape, 0)


def add_components(par_refs, xyz_ref, x8_ref, acc_ref):
    points = xyz_ref.shape[1]
    kc = 256
    tile = 256
    x8_ref[...] = jnp.zeros(x8_ref.shape, F32)
    x8_ref[0:3, :] = xyz_ref[...]
    xhi, xmid, xlo = split_three(x8_ref[...])
    right = jnp.concatenate([xhi, xmid, xlo, xhi, xmid, xhi], axis=0).astype(BF16)
    rows8 = row_ids((8, kc))
    times = step_size * (rows8 + 1).astype(F32)
    rows16 = row_ids((16, kc))
    comp_row = jnp.where(rows16 < 6, rows16 % 3, (rows16 + 2) % 3)
    valued = (rows16 < 10) & (rows16 != 6)

    def body(par_ref, step, total):
        blk = par_ref[:, pl.ds(pl.multiple_of(step * kc, kc), kc)]
        kv = jnp.where(rows8 < 3, blk * inv_two_pi, 0.0)
        khi, kmid, klo = split_three(kv)
        left = jnp.concatenate([khi, khi, khi, kmid, kmid, klo], axis=0).astype(BF16)
        delays = times * blk[3:4, :] - blk[7:8, :]
        sd, qd = sin_versine(delays * inv_two_pi)
        sd, cd = SIN_SCALE * sd, 1.0 - VER_SCALE * qd
        amp = jnp.where(comp_row == 0, blk[4:5, :], jnp.where(comp_row == 1, blk[5:6, :], blk[6:7, :]))
        amp = jnp.where(valued, amp, 0.0)

        def rows_of(t):
            w = amp * jnp.where(rows16 < 3, t[0:1, :], jnp.where(rows16 < 6, t[1:2, :], t[2:3, :]))
            hi = w.astype(BF16)
            lo = (w - hi.astype(F32)).astype(BF16)
            return w, jnp.concatenate([hi, lo], axis=0)

        wc = rows_of(cd)[0]
        lc = rows_of(-VER_SCALE * cd)[1]
        ls = rows_of(SIN_SCALE * sd)[1]
        for t in range(points // tile):
            cols = slice(t * tile, (t + 1) * tile)
            u = lax.dot_general(left, right[:, cols], (((0,), (0,)), ((), ())), preferred_element_type=F32)
            highs, lows = [], []
            for j in range(kc // 32):
                for value in sin_versine(u[32 * j : 32 * j + 32]):
                    high = value.astype(BF16)
                    highs.append(high)
                    lows.append((value - high.astype(F32)).astype(BF16))
            part = jnp.dot(ls, jnp.concatenate(highs[0::2], axis=0), preferred_element_type=F32)
            part += jnp.dot(lc, jnp.concatenate(highs[1::2], axis=0), preferred_element_type=F32)
            part += jnp.dot(ls, jnp.concatenate(lows[0::2], axis=0), preferred_element_type=F32)
            part += jnp.dot(lc, jnp.concatenate(lows[1::2], axis=0), preferred_element_type=F32)
            acc_ref[:, cols] += part
        return total + wc

    total = jnp.zeros((16, kc), F32)
    for par_ref in par_refs:
        steps = par_ref.shape[1] // kc
        total = lax.fori_loop(0, steps, lambda step, t, ref=par_ref: body(ref, step, t), total)
    return total


def first_incident_kernel(count, *refs):
    par_refs, (xyz_ref, acc_ref, total_ref, x8_ref) = refs[:count], refs[count:]
    acc_ref[...] = jnp.zeros(acc_ref.shape, F32)
    total_ref[...] = add_components(par_refs, xyz_ref, x8_ref, acc_ref)


def last_incident_kernel(count, step, *refs):
    par_refs, refs = refs[:count], refs[count:]
    first_ref, first_total_ref, xyz_ref, own_ref, off_ref, out_ref, x8_ref, acc_ref = refs
    points = xyz_ref.shape[1]
    owners = out_ref.shape[0]
    acc_ref[...] = first_ref[...]
    total = add_components(par_refs, xyz_ref, x8_ref, acc_ref) + first_total_ref[...]
    vals = acc_ref[0:16, :] + acc_ref[16:32, :] + jnp.sum(total, axis=1, keepdims=True)
    vals = jnp.where(row_ids((16, points)) == 6, off_ref[...].astype(F32), vals)
    v1, v2, v3 = split_three(vals)
    named = own_ref[...] == row_ids((owners, points))
    named_one = named.astype(F32).astype(BF16)
    earlier = row_ids((points, points)) < lax.broadcasted_iota(jnp.int32, (points, points), 1)
    before = jnp.dot(named_one, earlier.astype(F32).astype(BF16), preferred_element_type=F32)
    rank = jnp.sum(jnp.where(named, before, 0.0), axis=0, keepdims=True).astype(jnp.int32)
    terms = [v.astype(BF16) for v in (v1, v2, v3)]
    tiles = 0.0
    for odd in (0, 1):
        left = jnp.concatenate(
            [named_one * t[2 * j + odd : 2 * j + odd + 1, :] for t in terms for j in range(OWN_TILES)], axis=0
        )
        spots = (row_ids((2 * HALF, points)) == rank + odd * HALF).astype(F32).astype(BF16)
        got = lax.dot_general(left, spots, (((1,), (1,)), ((), ())), preferred_element_type=F32)
        size = OWN_TILES * owners
        tiles = tiles + (got[0:size] + got[size : 2 * size] + got[2 * size :])
    owner_row = row_ids((owners, 2 * HALF))

    def put(j, tile):
        out_ref[:, 0, 2 * HALF * j : 2 * HALF * (j + 1)] = tile

    for j in range(OWN_TILES):
        tile = tiles[j * owners : (j + 1) * owners]
        put(j, tile)
        if j < SIDE_TILES:
            above = pltpu.roll(tile, owners - step, 0)
            put(HIGH_LIST + j, jnp.where(owner_row < owners - step, above, 0.0))
            put(LOW_LIST + j, jnp.where(owner_row >= step, pltpu.roll(tile, step, 0), 0.0))


TILE = 8
DEEP = 6
MID = 4
NEAR = 2


def half_turn(tile):
    return pltpu.roll(tile, TILE // 2, 0)


ROWS_HELD = 16


def scatter_lists(val_ref, even_ref, odd_ref, jobs, cy, nz):
    lanes = 2 * HALF
    sources = val_ref.shape[0]
    groups = sources // 2
    chunk = 2 * lanes
    left_half = lax.broadcasted_iota(jnp.int32, (groups, lanes), 1) < lanes // 2
    for ref in {id(job[4]): job[4] for job in jobs}.values():
        ref[...] = jnp.zeros(ref.shape, F32)
    for j in range(LIST_ROWS):
        rows = val_ref[:, 0, lanes * j : lanes * (j + 1)]
        first, second = rows[0:groups], rows[groups:]
        at = pl.ds(j, groups, stride=ROWS_HELD)
        even_ref[at, :] = jnp.where(left_half, first, pltpu.roll(second, lanes // 2, 1))
        odd_ref[at, :] = jnp.where(left_half, pltpu.roll(first, lanes // 2, 1), second)

    def body(step, carry):
        evens, odds = [], []
        for pair in range(2):
            at = pl.ds(pl.multiple_of((2 * step + pair) * ROWS_HELD, ROWS_HELD), ROWS_HELD)
            evens.append(even_ref[at, :])
            odds.append(odd_ref[at, :])
        values = [jnp.concatenate(evens, axis=1), jnp.concatenate(odds, axis=1)]
        high = [v.astype(BF16) for v in values]
        low = [(v - h.astype(F32)).astype(BF16) for v, h in zip(values, high)]
        for base in (0, HIGH_LIST, LOW_LIST):
            own_jobs = [job for job in jobs if job[0] == base]
            off = values[0][base + 3 : base + 4, :].astype(jnp.int32)
            row = off // nz
            zt = (row_ids((nz, chunk)) == off - row * nz).astype(F32).astype(BF16)
            masks, left = {}, []
            for _, ranks, plane, planes, ref, start in own_jobs:
                if (plane, planes) not in masks:
                    ids = row_ids((planes * cy, chunk)) + plane * cy
                    masks[plane, planes] = (ids == row).astype(F32).astype(BF16)
                for r in ranks:
                    at = base + r // 2
                    left += [masks[plane, planes] * t[r % 2][at : at + 1, :] for t in (high, low)]
            left = jnp.concatenate(left, axis=0)
            got = lax.dot_general(left, zt, (((1,), (1,)), ((), ())), preferred_element_type=F32)
            at = 0
            for _, ranks, _, planes, ref, start in own_jobs:
                size = planes * cy
                for i in range(len(ranks)):
                    ref[i, start : start + size] += got[at : at + size] + got[at + size : at + 2 * size]
                    at += 2 * size
        return carry

    lax.fori_loop(0, groups // 2, body, 0)


STEP_ROWS = ((0, 1, 2), (3, 4, 5), (7, 8, 9))


def near_scatter_kernel(
    ready, par_ref, val_ref, sign_ref, zero_out, one_out, even_out, odd_out, zero_ref, one_ref, even_ref, odd_ref
):
    _, cx, cy, nz = one_out.shape
    jobs = (
        (0, STEP_ROWS[0], 0, cx, zero_ref, NEAR * cy),
        (0, STEP_ROWS[1], 0, cx, one_ref, 0),
        (HIGH_LIST, STEP_ROWS[0], 0, NEAR, zero_ref, (NEAR + cx) * cy),
        (LOW_LIST, STEP_ROWS[0], cx - NEAR, NEAR, zero_ref, 0),
    )
    scatter_lists(val_ref, even_ref, odd_ref, jobs, cy, nz)
    ready()
    sign = sign_ref[...]
    for i in range(3):
        zero_out[i] = zero_ref[i].reshape(zero_out.shape[1:]) * sign[MID - NEAR : MID + cx + NEAR]
        one_out[i] = one_ref[i].reshape(one_out.shape[1:]) * sign[MID : MID + cx]
    at = row_ids((TILE, nz))

    def write(is_high, face_ref):
        ys = slice(cy - TILE, cy) if is_high else slice(0, TILE)
        half = at >= TILE // 2 if is_high else at < TILE // 2
        corner = at < NEAR if is_high else at >= TILE - NEAR
        for i in range(3):
            for x in range(cx):
                tile = jnp.where(half, zero_out[i, NEAR + x, ys], half_turn(one_out[i, x, ys]))
                if x < 2 * NEAR:
                    moved = pltpu.roll(zero_out[i, NEAR + corner_plane(x, cx), ys], NEAR if is_high else TILE - NEAR, 0)
                    tile = jnp.where(corner, moved, tile)
                face_ref[i, x] = tile

    write_faces(par_ref[0], write, even_out, odd_out)


def rest_scatter_kernel(
    ready, val_ref, sign_ref, zero_out, one_out, two_out, zero_ref, one_ref, two_ref, even_ref, odd_ref
):
    _, cx, cy, nz = two_out.shape
    jobs = (
        (0, STEP_ROWS[2], 0, cx, two_ref, 0),
        (HIGH_LIST, STEP_ROWS[0], NEAR, MID - NEAR, zero_ref, NEAR * cy),
        (LOW_LIST, STEP_ROWS[0], cx - MID, MID - NEAR, zero_ref, 0),
        (HIGH_LIST, STEP_ROWS[1], 0, NEAR, one_ref, NEAR * cy),
        (LOW_LIST, STEP_ROWS[1], cx - NEAR, NEAR, one_ref, 0),
    )
    scatter_lists(val_ref, even_ref, odd_ref, jobs, cy, nz)
    ready()
    sign = sign_ref[...]
    last = cx + 2 * MID
    far = jnp.concatenate([sign[0 : MID - NEAR], sign[last - (MID - NEAR) :]], axis=0)
    side = jnp.concatenate([sign[MID - NEAR : MID], sign[MID + cx : MID + cx + NEAR]], axis=0)
    for i in range(3):
        zero_out[i] = zero_ref[i].reshape(zero_out.shape[1:]) * far
        one_out[i] = one_ref[i].reshape(one_out.shape[1:]) * side
        two_out[i] = two_ref[i].reshape(two_out.shape[1:]) * sign[MID : MID + cx]


def corner_plane(x, cx):
    return x - NEAR if x < NEAR else cx + x - NEAR


def write_faces(parity, write, even_out, odd_out):
    @pl.when(parity == 0)
    def _():
        write(True, even_out)
        write(False, odd_out)

    @pl.when(parity != 0)
    def _():
        write(False, even_out)
        write(True, odd_out)


def pair_list(count, odd):
    first = 1 if odd else 0
    pairs = [(i, i + 1) for i in range(first, count - 1, 2)]
    return pairs + [(j, i) for i, j in pairs]


def swap_faces(faces, axis):
    count = lax.axis_size(axis)
    out = []
    for k in (0, 1):
        out.append(lax.ppermute(faces[k], axis, pair_list(count, k)))
    return out


def prepare_kernel(
    ready, par_ref, cur_ref, ear_ref, coef_ref, wave_ref, freq_ref, amp_ref, index_ref, table_ref,
    block_out, even_out, odd_out,
):
    ready()
    entries = table_ref.shape[1]
    comps = index_ref.shape[1]
    picked = (row_ids((entries, comps)) == index_ref[...]).astype(F32).astype(BF16)
    terms = jnp.concatenate(list(split_three(jnp.broadcast_to(table_ref[...], (TILE, entries)))), axis=0).astype(BF16)
    phase = jnp.dot(terms, picked, preferred_element_type=F32)
    block_out[0:3, :] = wave_ref[...]
    block_out[3:4, :] = freq_ref[...]
    block_out[4:7, :] = amp_ref[...]
    block_out[7:8, :] = phase[0:1] + phase[TILE : TILE + 1] + phase[2 * TILE : 2 * TILE + 1]
    _, cx, cy, nz = cur_ref.shape
    upper = row_ids((TILE, nz)) >= TILE // 2

    def write(high, face_ref):
        ys = slice(cy - TILE, cy) if high else slice(0, TILE)
        keep = upper if high else ~upper
        for x in range(cx):
            for i in range(3):
                face_ref[i, x] = cur_ref[i, x, ys]
            face_ref[3, x] = jnp.where(keep, ear_ref[0, x, ys], half_turn(ear_ref[1, x, ys]))
            face_ref[4, x] = jnp.where(keep, ear_ref[2, x, ys], half_turn(coef_ref[x, ys]))

    write_faces(par_ref[0], write, even_out, odd_out)


def face_tile(ref, name, x):
    if name < 3:
        return ref[name, x]
    tile = ref[3 + (name - 3) // 2, x]
    return half_turn(tile) if name in (4, 6) else tile


def select_side(parity, even_ref, odd_ref, high):
    from_even = (parity == 0) if high else (parity == 1)

    def read(get):
        return jnp.where(from_even, get(even_ref), get(odd_ref))

    return read


FIELD_PLAN = [(DEEP, MID)] * 3 + [(MID, NEAR)] * 4 + [(MID, 0)]
SIDE_PLANES = sum(planes for planes, _ in FIELD_PLAN)
CORNERS = [(name, dist) for name, (_, corners) in enumerate(FIELD_PLAN) for dist in range(1, corners + 1)]


def side_plane(name, dist, is_high):
    planes = FIELD_PLAN[name][0]
    first = sum(n for n, _ in FIELD_PLAN[:name])
    return first + (dist - 1 if is_high else planes - dist)


def corner_place(k, cy):
    per_plane = cy // TILE
    start = k % per_plane * TILE
    return SIDE_PLANES + k // per_plane, slice(start, start + TILE)


def side_planes_sent(cy):
    return SIDE_PLANES + -(-len(CORNERS) // (cy // TILE))


def sign_of(mask):
    return (mask == 1).astype(F32) - (mask == 2).astype(F32)


def field_side_kernel(
    ready, px_ref, py_ref, cur_ref, ear_ref, coef_ref, mask_ref, even_ref, odd_ref, even_out, odd_out, sems
):
    cx, cy, nz = mask_ref.shape
    upper = row_ids((TILE, nz)) >= TILE // 2
    low = select_side(py_ref[0], even_ref, odd_ref, False)
    high = select_side(py_ref[0], even_ref, odd_ref, True)
    sources = [cur_ref.at[i] for i in range(3)] + [ear_ref.at[i] for i in range(3)] + [coef_ref]

    def run(high_out, low_out):
        faces = ((True, 0, high_out), (False, 1, low_out))
        copies = []
        for is_high, face, out in faces:
            for name, source in enumerate(sources):
                planes = FIELD_PLAN[name][0]
                first = sum(n for n, _ in FIELD_PLAN[:name])
                x = cx - planes if is_high else 0
                copies.append(
                    pltpu.make_async_copy(
                        source.at[pl.ds(x, planes)], out.at[pl.ds(first, planes)], sems.at[face, name]
                    )
                )
        for copy in copies:
            copy.start()
        for is_high, face, out in faces:
            for k, (name, dist) in enumerate(CORNERS):
                x = cx - dist if is_high else dist - 1
                below = low(lambda ref: face_tile(ref, name, x))
                above = high(lambda ref: face_tile(ref, name, x))
                plane, rows = corner_place(k, cy)
                out[plane, rows] = jnp.where(upper, below, above)
        ready()
        for is_high, face, out in faces:
            for k in range(MID):
                out[SIDE_PLANES - MID + k] = sign_of(mask_ref[cx - MID + k if is_high else k])
        for copy in copies:
            copy.wait()

    @pl.when(px_ref[0] == 0)
    def _():
        run(even_out, odd_out)

    @pl.when(px_ref[0] != 0)
    def _():
        run(odd_out, even_out)


LANES = 128


def put_rows(ref, index, rows, value):
    for h in range(value.shape[1] // LANES):
        ref[(*index, h, rows)] = value[:, h * LANES : (h + 1) * LANES]


def laplacian_rows(ref, i, x, start, count):
    tiles = ref.shape[2]
    lane = lax.broadcasted_iota(jnp.int32, (count, LANES), 1)

    def rows(h, dx, dy):
        return ref[i, x + dx, h, pl.ds(start + dy, count)]

    centre = [rows(h, 0, 0) for h in range(tiles)]
    out = [centre_weight * c for c in centre]
    for k, weight in ((1, near_weight), (2, far_weight)):
        up = [pltpu.roll(c, k, 1) for c in centre]
        down = [pltpu.roll(c, LANES - k, 1) for c in centre]
        for h in range(tiles):
            below = jnp.where(lane >= k, up[h], up[h - 1] if h else 0.0)
            above = jnp.where(lane < LANES - k, down[h], down[h + 1] if h + 1 < tiles else 0.0)
            across = (rows(h, -k, 0) + rows(h, k, 0)) + (rows(h, 0, -k) + rows(h, 0, k))
            out[h] = out[h] + weight * (across + (below + above))
    return centre, out


def run_planes(first, last, body):
    lax.fori_loop(first, last, lambda x, carry: (body(x), carry)[1], 0, unroll=2)


def first_wave_kernel(
    ready, px_ref, py_ref, cur_ref, ear_ref, coef_ref, mask_ref, ye_ref, yo_ref, xe_ref, xo_ref,
    final_ref, prior_ref, wide_coef_ref, wide_sign_ref, u_ref, e_ref, c_ref, one_ref, two_ref,
):
    _, cx, cy, _ = cur_ref.shape
    own = slice(TILE, TILE + cy)
    lower, higher = slice(0, TILE), slice(TILE + cy, 2 * TILE + cy)
    low = select_side(py_ref[0], ye_ref, yo_ref, False)
    high = select_side(py_ref[0], ye_ref, yo_ref, True)
    ready()

    def put(name, x, rows, value):
        if name < 3:
            put_rows(u_ref, (name, DEEP + x), rows, value)
        elif name < 6:
            put_rows(e_ref, (name - 3, MID + x), rows, value)
        elif name == 6:
            put_rows(c_ref, (MID + x,), rows, value)
            if -NEAR <= x < cx + NEAR:
                put_rows(wide_coef_ref, (NEAR + x,), rows, value)
        else:
            wide_sign_ref[MID + x, slice(rows.start - TILE, rows.stop - TILE)] = value

    for x in range(cx):
        for name in range(7):
            value = cur_ref[name, x] if name < 3 else ear_ref[name - 3, x] if name < 6 else coef_ref[x]
            put(name, x, own, value)
            put(name, x, lower, low(lambda ref: face_tile(ref, name, x)))
            put(name, x, higher, high(lambda ref: face_tile(ref, name, x)))
        put(7, x, own, sign_of(mask_ref[x]))
    for is_high in (False, True):
        read = select_side(px_ref[0], xe_ref, xo_ref, is_high)
        for name, (planes, _) in enumerate(FIELD_PLAN):
            for dist in range(1, planes + 1):
                x = cx - 1 + dist if is_high else -dist
                put(name, x, own, read(lambda ref: ref[side_plane(name, dist, is_high)]))
        for k, (name, dist) in enumerate(CORNERS):
            x = cx - 1 + dist if is_high else -dist
            plane, rows = corner_place(k, cy)
            tile = read(lambda ref: ref[plane, rows])
            put(name, x, lower, tile)
            put(name, x, higher, tile)

    begin = px_ref[1]
    deep = cy + TILE

    def first(start, count):
        def body(x):
            for i in range(3):
                centre, lap = laplacian_rows(u_ref, i, x + DEEP - MID, start, count)
                for h, (c, l) in enumerate(zip(centre, lap)):
                    rows = pl.ds(start, count)
                    one_ref[i, x, h, rows] = 2.0 * c - e_ref[i, x, h, rows] + c_ref[x, h, rows] * l

        return body

    def second(start, count):
        def body(x):
            for i in range(3):
                centre, lap = laplacian_rows(one_ref, i, x + MID - NEAR, start, count)
                for h, (c, l) in enumerate(zip(centre, lap)):
                    rows = pl.ds(start, count)
                    moved = 2.0 * c - u_ref[i, x + DEEP - NEAR, h, rows]
                    two_ref[i, x, h, rows] = moved + c_ref[x + MID - NEAR, h, rows] * l

        return body

    def third(x):
        for i in range(3):
            centre, lap = laplacian_rows(two_ref, i, x + NEAR, TILE, cy)
            for h, (c, l) in enumerate(zip(centre, lap)):
                lanes = slice(h * LANES, (h + 1) * LANES)
                moved = 2.0 * c - one_ref[i, x + MID, h, own]
                final_ref[i, x, :, lanes] = moved + c_ref[x + MID, h, own] * l
                prior_ref[i, x, :, lanes] = c

    run_planes(0, NEAR, first(TILE, cy))
    run_planes(NEAR, cx + 2 * MID - NEAR, first(begin, deep))
    run_planes(cx + 2 * MID - NEAR, cx + 2 * MID, first(TILE, cy))
    run_planes(0, NEAR, second(TILE, cy))
    run_planes(NEAR, cx + NEAR, second(begin, deep))
    run_planes(cx + NEAR, cx + 2 * NEAR, second(TILE, cy))
    run_planes(0, cx, third)


def last_wave_kernel(
    ready, px_ref, py_ref, free_final_ref, free_prior_ref, coef_ref, zero_in, zero_far_in, one_in, one_side_in, two_in,
    ye_ref, yo_ref, final_ref, prior_ref, one_ref, two_ref,
):
    _, cx, cy, _ = two_in.shape
    own = slice(TILE, TILE + cy)
    lower, higher = slice(0, TILE), slice(TILE + cy, 2 * TILE + cy)
    low = select_side(py_ref[0], ye_ref, yo_ref, False)
    high = select_side(py_ref[0], ye_ref, yo_ref, True)
    for i in range(3):
        for x in range(cx + 2 * NEAR):
            put_rows(one_ref, (i, x + MID - NEAR), own, zero_in[i, x])
        for k in range(NEAR):
            put_rows(one_ref, (i, k), own, zero_far_in[i, k])
            put_rows(one_ref, (i, cx + 2 * MID - NEAR + k), own, zero_far_in[i, NEAR + k])
            put_rows(two_ref, (i, k), own, one_side_in[i, k])
            put_rows(two_ref, (i, cx + NEAR + k), own, one_side_in[i, NEAR + k])
        for x in range(cx):
            put_rows(two_ref, (i, NEAR + x), own, one_in[i, x])
            for rows, read, turn in ((lower, low, TILE - NEAR), (higher, high, NEAR)):
                tile = read(lambda ref: ref[i, x])
                put_rows(one_ref, (i, MID + x), rows, tile)
                put_rows(two_ref, (i, NEAR + x), rows, half_turn(tile))
                if x < 2 * NEAR:
                    put_rows(one_ref, (i, MID + corner_plane(x, cx)), rows, pltpu.roll(tile, turn, 0))

    def second(start, count):
        def body(x):
            for i in range(3):
                centre, lap = laplacian_rows(one_ref, i, x + MID - NEAR, start, count)
                for h, (c, l) in enumerate(zip(centre, lap)):
                    rows = pl.ds(start, count)
                    two_ref[i, x, h, rows] = 2.0 * c + coef_ref[x, h, rows] * l + two_ref[i, x, h, rows]

        return body

    def third(x):
        for i in range(3):
            centre, lap = laplacian_rows(two_ref, i, x + NEAR, TILE, cy)
            for h, (c, l) in enumerate(zip(centre, lap)):
                lanes = slice(h * LANES, (h + 1) * LANES)
                moved = 2.0 * c - one_ref[i, x + MID, h, own] + coef_ref[x + NEAR, h, own] * l
                final_ref[i, x, :, lanes] = free_final_ref[i, x, :, lanes] + (moved + two_in[i, x, :, lanes])
                prior_ref[i, x, :, lanes] = free_prior_ref[i, x, :, lanes] + c

    ready()
    run_planes(0, NEAR, second(TILE, cy))
    run_planes(NEAR, cx + NEAR, second(px_ref[1], cy + TILE))
    run_planes(cx + NEAR, cx + 2 * NEAR, second(TILE, cy))
    run_planes(0, cx, third)


def staged(kernel, positions, operand_count):
    def run(*refs):
        refs, stages, sems = refs[: -len(positions) - 1], refs[-len(positions) - 1 : -1], refs[-1]
        ins = list(refs[:operand_count])
        copies = []
        for k, (at, stage) in enumerate(zip(positions, stages)):
            copies.append(pltpu.make_async_copy(ins[at], stage, sems.at[k]))
            ins[at] = stage
        for copy in copies:
            copy.start()

        def ready():
            for copy in copies:
                copy.wait()

        kernel(ready, *ins, *refs[operand_count:])

    return run


def local(
    current_field,
    earlier_field,
    wave_coef,
    layer_mask,
    point_xyz,
    point_owner,
    cell_offset,
    wave_vector,
    frequency,
    amplitude,
    phase_index,
    phase_table,
):
    point_count = point_xyz.shape[1]
    slab_count = lax.axis_size("slab")
    comp_count = lax.axis_size("comp")
    device_count = slab_count * comp_count
    slot_count = max(2, 2 * point_count // device_count)
    _, cx, cy, nz = current_field.shape
    assert slot_count <= HALF and device_count % 8 == 0
    assert cx >= DEEP and cy >= 2 * TILE and cy % TILE == 0
    wide = cy + 2 * TILE
    assert nz % LANES == 0 and MID == 2 * NEAR

    def plane_stack(*lead):
        return (*lead, nz // LANES, wide, LANES)

    smem = pl.BlockSpec(memory_space=pltpu.SMEM)
    vmem = pl.BlockSpec(memory_space=pltpu.VMEM)

    def call(kernel, operands, shapes, scratch=(), scalars=0, from_hbm=(), left_in_hbm=(), to_hbm=False):
        shapes = [(pltpu.HBM if to_hbm else jax.ShapeDtypeStruct)(shape, F32) for shape in shapes]
        operands = list(operands)
        in_specs = [smem] * scalars + [vmem] * (len(operands) - scalars)
        scratch_shapes = [pltpu.VMEM(shape, F32) if isinstance(shape, tuple) else shape for shape in scratch]
        hbm = pl.BlockSpec(memory_space=pltpu.HBM)
        for at in left_in_hbm:
            operands[at] = pltpu.with_memory_space_constraint(operands[at], pltpu.HBM)
            in_specs[at] = hbm
        if from_hbm:
            for at in from_hbm:
                operands[at] = pltpu.with_memory_space_constraint(operands[at], pltpu.HBM)
                in_specs[at] = hbm
                scratch_shapes.append(pltpu.VMEM(operands[at].shape, operands[at].dtype))
            scratch_shapes.append(pltpu.SemaphoreType.DMA((len(from_hbm),)))
            kernel = staged(kernel, from_hbm, len(operands))
        return pl.pallas_call(
            kernel,
            out_shape=shapes,
            in_specs=in_specs,
            out_specs=[vmem] * len(shapes),
            scratch_shapes=scratch_shapes,
            compiler_params=pltpu.CompilerParams(vmem_limit_bytes=VMEM_GRANT),
        )(*operands)

    px = jnp.stack([lax.axis_index("slab") % 2, TILE // 2]).astype(jnp.int32)
    py = (lax.axis_index("comp") % 2).astype(jnp.int32).reshape(1)
    fields = (current_field, earlier_field, wave_coef)
    local_comps = frequency.shape[0]
    own_block, *faces = call(
        prepare_kernel,
        (
            py, *fields, wave_vector, frequency.reshape(1, local_comps), amplitude,
            phase_index.reshape(1, local_comps), phase_table.reshape(1, -1),
        ),
        [(8, local_comps)] + [(5, cx, TILE, nz)] * 2,
        scalars=1,
        from_hbm=tuple(range(1, 9)),
    )
    if comp_count == 4:
        near_block = lax.ppermute(own_block, "comp", pair_list(4, 0))
        first_blocks = [own_block, near_block]
        ring = pair_list(4, 1) + [(0, 3), (3, 0)]
        far_block = lax.ppermute(jnp.concatenate(first_blocks, axis=1), "comp", ring)
        last_blocks = [far_block]
    else:
        first_blocks = [own_block]
        last_blocks = [
            lax.ppermute(own_block, "comp", [(i, (i + k) % comp_count) for i in range(comp_count)])
            for k in range(1, comp_count)
        ]
    ye, yo = swap_faces(faces, "comp")
    (sum_one, total_one) = call(
        lambda *refs: first_incident_kernel(len(first_blocks), *refs),
        (*first_blocks, point_xyz),
        [(32, point_count), (16, 256)],
        [(8, point_count)],
    )
    sent = side_planes_sent(cy)
    sides = call(
        field_side_kernel,
        (px, py, *fields, layer_mask, ye, yo),
        [(sent, cy, nz)] * 2,
        [pltpu.SemaphoreType.DMA((2, len(FIELD_PLAN) - 1))],
        scalars=2,
        from_hbm=(5,),
        left_in_hbm=(2, 3, 4),
    )
    xe, xo = swap_faces(sides, "slab")
    (packed,) = call(
        lambda *refs: last_incident_kernel(len(last_blocks), comp_count, *refs),
        (
            *last_blocks, sum_one, total_one, point_xyz,
            point_owner.reshape(1, point_count), cell_offset.reshape(1, point_count),
        ),
        [(device_count, 1, LIST_ROWS * 2 * HALF)],
        [(8, point_count), (32, point_count)],
    )
    arrived = lax.all_to_all(packed, ("slab", "comp"), split_axis=0, concat_axis=0, tiled=True)
    free_final, free_prior, wide_coef, wide_sign = call(
        first_wave_kernel,
        (px, py, *fields, layer_mask, ye, yo, xe, xo),
        [current_field.shape, current_field.shape, plane_stack(cx + 2 * NEAR), (cx + 2 * MID, cy, nz)],
        [
            plane_stack(3, cx + 2 * DEEP), plane_stack(3, cx + 2 * MID), plane_stack(cx + 2 * MID),
            plane_stack(3, cx + 2 * MID), plane_stack(3, cx + 2 * NEAR),
        ],
        scalars=2,
        from_hbm=(2, 3, 4, 5),
        to_hbm=True,
    )
    held = (device_count // 2 * ROWS_HELD, 2 * HALF)
    zero, one, face_even, face_odd = call(
        near_scatter_kernel,
        (py, arrived, wide_sign),
        [(3, cx + 2 * NEAR, cy, nz), (3, cx, cy, nz)] + [(3, cx, TILE, nz)] * 2,
        [(3, (cx + 2 * NEAR) * cy, nz), (3, cx * cy, nz), held, held],
        scalars=1,
        from_hbm=(2,),
    )
    fye, fyo = swap_faces((face_even, face_odd), "comp")
    zero_far, one_side, two = call(
        rest_scatter_kernel,
        (arrived, wide_sign),
        [(3, 2 * NEAR, cy, nz), (3, 2 * NEAR, cy, nz), (3, cx, cy, nz)],
        [(3, 2 * NEAR * cy, nz), (3, 2 * NEAR * cy, nz), (3, cx * cy, nz), held, held],
        from_hbm=(1,),
    )
    final, prior = call(
        last_wave_kernel,
        (px, py, free_final, free_prior, wide_coef, zero, zero_far, one, one_side, two, fye, fyo),
        [current_field.shape, current_field.shape],
        [plane_stack(3, cx + 2 * MID), plane_stack(3, cx + 2 * NEAR)],
        scalars=2,
        from_hbm=(2, 3, 4),
    )
    return (final, prior)


def solution(mesh):
    in_specs = (
        P(None, "slab", "comp", None),
        P(None, "slab", "comp", None),
        P("slab", "comp", None),
        P("slab", "comp", None),
        P(None, ("slab", "comp")),
        P(("slab", "comp"), None),
        P(("slab", "comp")),
        P(None, "comp"),
        P("comp"),
        P(None, "comp"),
        P("comp"),
        P(),
    )
    out_specs = (P(None, "slab", "comp", None), P(None, "slab", "comp", None))
    return jax.shard_map(local, mesh=mesh, in_specs=in_specs, out_specs=out_specs, check_vma=False)
```

```python
import jax
import jax.numpy as jnp
from jax import lax
from jax.experimental import pallas as pl
from jax.experimental.pallas import tpu as pltpu
from jax.sharding import PartitionSpec as P

step_size = 0.05
near_weight = 4.0 / 3.0
far_weight = -1.0 / 12.0
centre_weight = -7.5
inv_two_pi = 0.15915494309189535

LEAD = -0.7713118195533752
SIN_C = (4.442834854125977 / LEAD, -7.306587219238281 / LEAD, 3.588636875152588 / LEAD)
SIN_SCALE = LEAD * abs(LEAD)
VER_SCALE = LEAD * LEAD
KC = 256
AHEAD = 2
HALF = 64
OWN_TILES = 5
SIDE_TILES = 4
HIGH_LIST = OWN_TILES
LOW_LIST = OWN_TILES + SIDE_TILES
LIST_ROWS = OWN_TILES + 2 * SIDE_TILES
VMEM_GRANT = 16 * 2**20

F32 = jnp.float32
BF16 = jnp.bfloat16


def sin_versine(u):
    r = u - jnp.round(u)
    z = r * r
    s = r * (((z + SIN_C[2]) * z + SIN_C[1]) * z + SIN_C[0])
    q = s * s
    w = 2.0 / VER_SCALE - q
    return s * (w * lax.rsqrt(w)), q


def split_three(x):
    hi = x.astype(BF16).astype(F32)
    rest = x - hi
    mid = rest.astype(BF16).astype(F32)
    return hi, mid, rest - mid


def row_ids(shape):
    return lax.broadcasted_iota(jnp.int32, shape, 0)


def add_components(par_refs, right_ref, acc_ref, u_ref):
    points = right_ref.shape[1]
    ahead, kc, tile = u_ref.shape
    rows8 = row_ids((8, kc))
    times = step_size * (rows8 + 1).astype(F32)
    rows16 = row_ids((16, kc))
    comp_row = jnp.where(rows16 < 6, rows16 % 3, (rows16 + 2) % 3)
    valued = (rows16 < 10) & (rows16 != 6)

    def block_of(par_ref, step):
        return par_ref[:, pl.ds(pl.multiple_of(step * kc, kc), kc)]

    def left_of(blk):
        khi, kmid, klo = split_three(jnp.where(rows8 < 3, blk * inv_two_pi, 0.0))
        return jnp.concatenate([khi, khi, khi, kmid, kmid, klo], axis=0).astype(BF16)

    def angles(left, t):
        cols = slice(t * tile, (t + 1) * tile)
        return lax.dot_general(left, right_ref[:, cols], (((0,), (0,)), ((), ())), preferred_element_type=F32)

    def body(par_ref, steps, step, total):
        blk = block_of(par_ref, step)
        left = left_of(blk)
        later = left_of(block_of(par_ref, jnp.minimum(step + 1, steps - 1)))
        delays = times * blk[3:4, :] - blk[7:8, :]
        sd, qd = sin_versine(delays * inv_two_pi)
        sd, cd = SIN_SCALE * sd, 1.0 - VER_SCALE * qd
        amp = jnp.where(comp_row == 0, blk[4:5, :], jnp.where(comp_row == 1, blk[5:6, :], blk[6:7, :]))
        amp = jnp.where(valued, amp, 0.0)

        def rows_of(t):
            w = amp * jnp.where(rows16 < 3, t[0:1, :], jnp.where(rows16 < 6, t[1:2, :], t[2:3, :]))
            hi = w.astype(BF16)
            lo = (w - hi.astype(F32)).astype(BF16)
            return w, jnp.concatenate([hi, lo], axis=0)

        wc = rows_of(cd)[0]
        lc = rows_of(-VER_SCALE * cd)[1]
        ls = rows_of(SIN_SCALE * sd)[1]

        def add_tile(t, u):
            highs, lows = [], []
            for j in range(kc // 32):
                for value in sin_versine(u[32 * j : 32 * j + 32]):
                    high = value.astype(BF16)
                    highs.append(high)
                    lows.append((value - high.astype(F32)).astype(BF16))
            part = jnp.dot(ls, jnp.concatenate(highs[0::2], axis=0), preferred_element_type=F32)
            part += jnp.dot(lc, jnp.concatenate(highs[1::2], axis=0), preferred_element_type=F32)
            part += jnp.dot(ls, jnp.concatenate(lows[0::2], axis=0), preferred_element_type=F32)
            part += jnp.dot(lc, jnp.concatenate(lows[1::2], axis=0), preferred_element_type=F32)
            acc_ref[:, t * tile : (t + 1) * tile] += part

        tiles = points // tile
        rest = {t: angles(left, t) for t in range(ahead, tiles)}
        for t in range(ahead):
            add_tile(t, u_ref[t])
        for t in range(ahead):
            u_ref[t] = angles(later, t)
        for t, u in rest.items():
            add_tile(t, u)
        return total + wc

    total = jnp.zeros((16, kc), F32)
    for par_ref in par_refs:
        steps = par_ref.shape[1] // kc
        left = left_of(block_of(par_ref, 0))
        for t in range(ahead):
            u_ref[t] = angles(left, t)
        total = lax.fori_loop(0, steps, lambda step, t, ref=par_ref, n=steps: body(ref, n, step, t), total)
    return total


def first_incident_kernel(count, *refs):
    par_refs, (right_ref, acc_ref, total_ref, u_ref) = refs[:count], refs[count:]
    acc_ref[...] = jnp.zeros(acc_ref.shape, F32)
    total_ref[...] = add_components(par_refs, right_ref, acc_ref, u_ref)


def last_incident_kernel(count, step, ready, *refs):
    par_refs, refs = refs[:count], refs[count:]
    first_ref, first_total_ref, right_ref, own_ref, off_ref, out_ref, acc_ref, u_ref = refs
    points = right_ref.shape[1]
    owners = out_ref.shape[0]
    acc_ref[...] = first_ref[...]
    total = add_components(par_refs, right_ref, acc_ref, u_ref) + first_total_ref[...]
    ready()
    vals = acc_ref[0:16, :] + acc_ref[16:32, :] + jnp.sum(total, axis=1, keepdims=True)
    vals = jnp.where(row_ids((16, points)) == 6, off_ref[...].astype(F32), vals)
    v1, v2, v3 = split_three(vals)
    named = own_ref[...] == row_ids((owners, points))
    named_one = named.astype(F32).astype(BF16)
    width = 128
    square = (width, width)
    earlier = (row_ids(square) < lax.broadcasted_iota(jnp.int32, square, 1)).astype(F32).astype(BF16)
    sums = jnp.concatenate([earlier, jnp.ones(square, BF16)], axis=1)
    before, past = [], jnp.zeros((owners, width), F32)
    for k in range(0, points, width):
        got = jnp.dot(named_one[:, k : k + width], sums, preferred_element_type=F32)
        before.append(got[:, 0:width] + past)
        past = past + got[:, width:]
    before = jnp.concatenate(before, axis=1)
    rank = jnp.sum(jnp.where(named, before, 0.0), axis=0, keepdims=True).astype(jnp.int32)
    terms = [v.astype(BF16) for v in (v1, v2, v3)]
    tiles = 0.0
    for odd in (0, 1):
        left = jnp.concatenate(
            [named_one * t[2 * j + odd : 2 * j + odd + 1, :] for t in terms for j in range(OWN_TILES)], axis=0
        )
        spots = (row_ids((2 * HALF, points)) == rank + odd * HALF).astype(F32).astype(BF16)
        got = lax.dot_general(left, spots, (((1,), (1,)), ((), ())), preferred_element_type=F32)
        size = OWN_TILES * owners
        tiles = tiles + (got[0:size] + got[size : 2 * size] + got[2 * size :])
    owner_row = row_ids((owners, 2 * HALF))

    def put(j, tile):
        out_ref[:, 0, 2 * HALF * j : 2 * HALF * (j + 1)] = tile

    for j in range(OWN_TILES):
        tile = tiles[j * owners : (j + 1) * owners]
        put(j, tile)
        if j < SIDE_TILES:
            above = pltpu.roll(tile, owners - step, 0)
            put(HIGH_LIST + j, jnp.where(owner_row < owners - step, above, 0.0))
            put(LOW_LIST + j, jnp.where(owner_row >= step, pltpu.roll(tile, step, 0), 0.0))


TILE = 8
DEEP = 6
MID = 4
NEAR = 2


def half_turn(tile):
    return pltpu.roll(tile, TILE // 2, 0)


ROWS_HELD = 16


def scatter_lists(val_ref, even_ref, odd_ref, jobs, cy, nz):
    lanes = 2 * HALF
    sources = val_ref.shape[0]
    groups = sources // 2
    chunk = 2 * lanes
    left_half = lax.broadcasted_iota(jnp.int32, (groups, lanes), 1) < lanes // 2
    for ref in {id(job[4]): job[4] for job in jobs}.values():
        ref[...] = jnp.zeros(ref.shape, F32)
    for j in range(LIST_ROWS):
        rows = val_ref[:, 0, lanes * j : lanes * (j + 1)]
        first, second = rows[0:groups], rows[groups:]
        at = pl.ds(j, groups, stride=ROWS_HELD)
        even_ref[at, :] = jnp.where(left_half, first, pltpu.roll(second, lanes // 2, 1))
        odd_ref[at, :] = jnp.where(left_half, pltpu.roll(first, lanes // 2, 1), second)

    def body(step, carry):
        evens, odds = [], []
        for pair in range(2):
            at = pl.ds(pl.multiple_of((2 * step + pair) * ROWS_HELD, ROWS_HELD), ROWS_HELD)
            evens.append(even_ref[at, :])
            odds.append(odd_ref[at, :])
        values = [jnp.concatenate(evens, axis=1), jnp.concatenate(odds, axis=1)]
        high = [v.astype(BF16) for v in values]
        low = [(v - h.astype(F32)).astype(BF16) for v, h in zip(values, high)]
        for base in (0, HIGH_LIST, LOW_LIST):
            own_jobs = [job for job in jobs if job[0] == base]
            off = values[0][base + 3 : base + 4, :].astype(jnp.int32)
            row = off // nz
            zt = (row_ids((nz, chunk)) == off - row * nz).astype(F32).astype(BF16)
            masks, left = {}, []
            for _, ranks, plane, planes, ref, start in own_jobs:
                if (plane, planes) not in masks:
                    ids = row_ids((planes * cy, chunk)) + plane * cy
                    masks[plane, planes] = (ids == row).astype(F32).astype(BF16)
                for r in ranks:
                    at = base + r // 2
                    left += [masks[plane, planes] * t[r % 2][at : at + 1, :] for t in (high, low)]
            left = jnp.concatenate(left, axis=0)
            got = lax.dot_general(left, zt, (((1,), (1,)), ((), ())), preferred_element_type=F32)
            at = 0
            for _, ranks, _, planes, ref, start in own_jobs:
                size = planes * cy
                for i in range(len(ranks)):
                    ref[i, start : start + size] += got[at : at + size] + got[at + size : at + 2 * size]
                    at += 2 * size
        return carry

    lax.fori_loop(0, groups // 2, body, 0)


STEP_ROWS = ((0, 1, 2), (3, 4, 5), (7, 8, 9))


def near_scatter_kernel(
    ready, par_ref, val_ref, sign_ref, zero_out, one_out, even_out, odd_out, zero_ref, one_ref, even_ref, odd_ref
):
    _, cx, cy, nz = one_out.shape
    jobs = (
        (0, STEP_ROWS[0], 0, cx, zero_ref, NEAR * cy),
        (0, STEP_ROWS[1], 0, cx, one_ref, 0),
        (HIGH_LIST, STEP_ROWS[0], 0, NEAR, zero_ref, (NEAR + cx) * cy),
        (LOW_LIST, STEP_ROWS[0], cx - NEAR, NEAR, zero_ref, 0),
    )
    scatter_lists(val_ref, even_ref, odd_ref, jobs, cy, nz)
    ready()
    sign = sign_ref[...]
    for i in range(3):
        zero_out[i] = zero_ref[i].reshape(zero_out.shape[1:]) * sign[MID - NEAR : MID + cx + NEAR]
        one_out[i] = one_ref[i].reshape(one_out.shape[1:]) * sign[MID : MID + cx]
    at = row_ids((TILE, nz))

    def write(is_high, face_ref):
        ys = slice(cy - TILE, cy) if is_high else slice(0, TILE)
        half = at >= TILE // 2 if is_high else at < TILE // 2
        corner = at < NEAR if is_high else at >= TILE - NEAR
        for i in range(3):
            for x in range(cx):
                tile = jnp.where(half, zero_out[i, NEAR + x, ys], half_turn(one_out[i, x, ys]))
                if x < 2 * NEAR:
                    moved = pltpu.roll(zero_out[i, NEAR + corner_plane(x, cx), ys], NEAR if is_high else TILE - NEAR, 0)
                    tile = jnp.where(corner, moved, tile)
                face_ref[i, x] = tile

    write_faces(par_ref[0], write, even_out, odd_out)


def rest_scatter_kernel(
    ready, val_ref, sign_ref, zero_out, one_out, two_out, zero_ref, one_ref, two_ref, even_ref, odd_ref
):
    _, cx, cy, nz = two_out.shape
    jobs = (
        (0, STEP_ROWS[2], 0, cx, two_ref, 0),
        (HIGH_LIST, STEP_ROWS[0], NEAR, MID - NEAR, zero_ref, NEAR * cy),
        (LOW_LIST, STEP_ROWS[0], cx - MID, MID - NEAR, zero_ref, 0),
        (HIGH_LIST, STEP_ROWS[1], 0, NEAR, one_ref, NEAR * cy),
        (LOW_LIST, STEP_ROWS[1], cx - NEAR, NEAR, one_ref, 0),
    )
    scatter_lists(val_ref, even_ref, odd_ref, jobs, cy, nz)
    ready()
    sign = sign_ref[...]
    last = cx + 2 * MID
    far = jnp.concatenate([sign[0 : MID - NEAR], sign[last - (MID - NEAR) :]], axis=0)
    side = jnp.concatenate([sign[MID - NEAR : MID], sign[MID + cx : MID + cx + NEAR]], axis=0)
    for i in range(3):
        zero_out[i] = zero_ref[i].reshape(zero_out.shape[1:]) * far
        one_out[i] = one_ref[i].reshape(one_out.shape[1:]) * side
        two_out[i] = two_ref[i].reshape(two_out.shape[1:]) * sign[MID : MID + cx]


def corner_plane(x, cx):
    return x - NEAR if x < NEAR else cx + x - NEAR


def write_faces(parity, write, even_out, odd_out):
    @pl.when(parity == 0)
    def _():
        write(True, even_out)
        write(False, odd_out)

    @pl.when(parity != 0)
    def _():
        write(False, even_out)
        write(True, odd_out)


def pair_list(count, odd):
    first = 1 if odd else 0
    pairs = [(i, i + 1) for i in range(first, count - 1, 2)]
    return pairs + [(j, i) for i, j in pairs]


def swap_faces(faces, axis):
    count = lax.axis_size(axis)
    out = []
    for k in (0, 1):
        out.append(lax.ppermute(faces[k], axis, pair_list(count, k)))
    return out


def prepare_kernel(
    ready, par_ref, cur_ref, ear_ref, coef_ref, wave_ref, freq_ref, amp_ref, index_ref, table_ref, xyz_ref,
    block_out, right_out, even_out, odd_out, x8_ref,
):
    x8_ref[...] = jnp.zeros(x8_ref.shape, F32)
    ready()
    x8_ref[0:3, :] = xyz_ref[...]
    xhi, xmid, xlo = split_three(x8_ref[...])
    right_out[...] = jnp.concatenate([xhi, xmid, xlo, xhi, xmid, xhi], axis=0).astype(BF16)
    entries = table_ref.shape[1]
    comps = index_ref.shape[1]
    picked = (row_ids((entries, comps)) == index_ref[...]).astype(F32).astype(BF16)
    terms = jnp.concatenate(list(split_three(jnp.broadcast_to(table_ref[...], (TILE, entries)))), axis=0).astype(BF16)
    phase = jnp.dot(terms, picked, preferred_element_type=F32)
    block_out[0:3, :] = wave_ref[...]
    block_out[3:4, :] = freq_ref[...]
    block_out[4:7, :] = amp_ref[...]
    block_out[7:8, :] = phase[0:1] + phase[TILE : TILE + 1] + phase[2 * TILE : 2 * TILE + 1]
    _, cx, cy, nz = cur_ref.shape
    upper = row_ids((TILE, nz)) >= TILE // 2

    def write(high, face_ref):
        ys = slice(cy - TILE, cy) if high else slice(0, TILE)
        keep = upper if high else ~upper
        for x in range(cx):
            for i in range(3):
                face_ref[i, x] = cur_ref[i, x, ys]
            face_ref[3, x] = jnp.where(keep, ear_ref[0, x, ys], half_turn(ear_ref[1, x, ys]))
            face_ref[4, x] = jnp.where(keep, ear_ref[2, x, ys], half_turn(coef_ref[x, ys]))

    write_faces(par_ref[0], write, even_out, odd_out)


def face_tile(ref, name, x):
    if name < 3:
        return ref[name, x]
    tile = ref[3 + (name - 3) // 2, x]
    return half_turn(tile) if name in (4, 6) else tile


def select_side(parity, even_ref, odd_ref, high):
    from_even = (parity == 0) if high else (parity == 1)

    def read(get):
        return jnp.where(from_even, get(even_ref), get(odd_ref))

    return read


FIELD_PLAN = [(DEEP, MID)] * 3 + [(MID, NEAR)] * 4 + [(MID, 0)]
SIDE_PLANES = sum(planes for planes, _ in FIELD_PLAN)
CORNERS = [(name, dist) for name, (_, corners) in enumerate(FIELD_PLAN) for dist in range(1, corners + 1)]


def side_plane(name, dist, is_high):
    planes = FIELD_PLAN[name][0]
    first = sum(n for n, _ in FIELD_PLAN[:name])
    return first + (dist - 1 if is_high else planes - dist)


def corner_place(k, cy):
    per_plane = cy // TILE
    start = k % per_plane * TILE
    return SIDE_PLANES + k // per_plane, slice(start, start + TILE)


def side_planes_sent(cy):
    return SIDE_PLANES + -(-len(CORNERS) // (cy // TILE))


def sign_of(mask):
    return (mask == 1).astype(F32) - (mask == 2).astype(F32)


def field_side_kernel(
    ready, px_ref, py_ref, cur_ref, ear_ref, coef_ref, mask_ref, even_ref, odd_ref, even_out, odd_out, sems
):
    cx, cy, nz = mask_ref.shape
    upper = row_ids((TILE, nz)) >= TILE // 2
    low = select_side(py_ref[0], even_ref, odd_ref, False)
    high = select_side(py_ref[0], even_ref, odd_ref, True)
    sources = [cur_ref.at[i] for i in range(3)] + [ear_ref.at[i] for i in range(3)] + [coef_ref]

    def run(high_out, low_out):
        faces = ((True, 0, high_out), (False, 1, low_out))
        copies = []
        for is_high, face, out in faces:
            for name, source in enumerate(sources):
                planes = FIELD_PLAN[name][0]
                first = sum(n for n, _ in FIELD_PLAN[:name])
                x = cx - planes if is_high else 0
                copies.append(
                    pltpu.make_async_copy(
                        source.at[pl.ds(x, planes)], out.at[pl.ds(first, planes)], sems.at[face, name]
                    )
                )
        for copy in copies:
            copy.start()
        for is_high, face, out in faces:
            for k, (name, dist) in enumerate(CORNERS):
                x = cx - dist if is_high else dist - 1
                below = low(lambda ref: face_tile(ref, name, x))
                above = high(lambda ref: face_tile(ref, name, x))
                plane, rows = corner_place(k, cy)
                out[plane, rows] = jnp.where(upper, below, above)
        ready()
        for is_high, face, out in faces:
            for k in range(MID):
                out[SIDE_PLANES - MID + k] = sign_of(mask_ref[cx - MID + k if is_high else k])
        for copy in copies:
            copy.wait()

    @pl.when(px_ref[0] == 0)
    def _():
        run(even_out, odd_out)

    @pl.when(px_ref[0] != 0)
    def _():
        run(odd_out, even_out)


LANES = 128


def put_rows(ref, index, rows, value):
    for h in range(value.shape[1] // LANES):
        ref[(*index, h, rows)] = value[:, h * LANES : (h + 1) * LANES]


def laplacian_rows(ref, i, x, start, count):
    tiles = ref.shape[2]
    lane = lax.broadcasted_iota(jnp.int32, (count, LANES), 1)

    def rows(h, dx, dy):
        return ref[i, x + dx, h, pl.ds(start + dy, count)]

    centre = [rows(h, 0, 0) for h in range(tiles)]
    out = [centre_weight * c for c in centre]
    for k, weight in ((1, near_weight), (2, far_weight)):
        up = [pltpu.roll(c, k, 1) for c in centre]
        down = [pltpu.roll(c, LANES - k, 1) for c in centre]
        for h in range(tiles):
            below = jnp.where(lane >= k, up[h], up[h - 1] if h else 0.0)
            above = jnp.where(lane < LANES - k, down[h], down[h + 1] if h + 1 < tiles else 0.0)
            across = (rows(h, -k, 0) + rows(h, k, 0)) + (rows(h, 0, -k) + rows(h, 0, k))
            out[h] = out[h] + weight * (across + (below + above))
    return centre, out


def run_planes(first, last, body):
    lax.fori_loop(first, last, lambda x, carry: (body(x), carry)[1], 0, unroll=2)


def first_wave_kernel(
    ready, px_ref, py_ref, cur_ref, ear_ref, coef_ref, mask_ref, ye_ref, yo_ref, xe_ref, xo_ref,
    final_ref, prior_ref, wide_coef_ref, wide_sign_ref, u_ref, e_ref, c_ref, one_ref, two_ref,
):
    _, cx, cy, _ = cur_ref.shape
    own = slice(TILE, TILE + cy)
    lower, higher = slice(0, TILE), slice(TILE + cy, 2 * TILE + cy)
    low = select_side(py_ref[0], ye_ref, yo_ref, False)
    high = select_side(py_ref[0], ye_ref, yo_ref, True)
    ready()

    def put(name, x, rows, value):
        if name < 3:
            put_rows(u_ref, (name, DEEP + x), rows, value)
        elif name < 6:
            put_rows(e_ref, (name - 3, MID + x), rows, value)
        elif name == 6:
            put_rows(c_ref, (MID + x,), rows, value)
            if -NEAR <= x < cx + NEAR:
                put_rows(wide_coef_ref, (NEAR + x,), rows, value)
        else:
            wide_sign_ref[MID + x, slice(rows.start - TILE, rows.stop - TILE)] = value

    for x in range(cx):
        for name in range(7):
            value = cur_ref[name, x] if name < 3 else ear_ref[name - 3, x] if name < 6 else coef_ref[x]
            put(name, x, own, value)
            put(name, x, lower, low(lambda ref: face_tile(ref, name, x)))
            put(name, x, higher, high(lambda ref: face_tile(ref, name, x)))
        put(7, x, own, sign_of(mask_ref[x]))
    for is_high in (False, True):
        read = select_side(px_ref[0], xe_ref, xo_ref, is_high)
        for name, (planes, _) in enumerate(FIELD_PLAN):
            for dist in range(1, planes + 1):
                x = cx - 1 + dist if is_high else -dist
                put(name, x, own, read(lambda ref: ref[side_plane(name, dist, is_high)]))
        for k, (name, dist) in enumerate(CORNERS):
            x = cx - 1 + dist if is_high else -dist
            plane, rows = corner_place(k, cy)
            tile = read(lambda ref: ref[plane, rows])
            put(name, x, lower, tile)
            put(name, x, higher, tile)

    begin = px_ref[1]
    deep = cy + TILE

    def first(start, count):
        def body(x):
            for i in range(3):
                centre, lap = laplacian_rows(u_ref, i, x + DEEP - MID, start, count)
                for h, (c, l) in enumerate(zip(centre, lap)):
                    rows = pl.ds(start, count)
                    one_ref[i, x, h, rows] = 2.0 * c - e_ref[i, x, h, rows] + c_ref[x, h, rows] * l

        return body

    def second(start, count):
        def body(x):
            for i in range(3):
                centre, lap = laplacian_rows(one_ref, i, x + MID - NEAR, start, count)
                for h, (c, l) in enumerate(zip(centre, lap)):
                    rows = pl.ds(start, count)
                    moved = 2.0 * c - u_ref[i, x + DEEP - NEAR, h, rows]
                    two_ref[i, x, h, rows] = moved + c_ref[x + MID - NEAR, h, rows] * l

        return body

    def third(x):
        for i in range(3):
            centre, lap = laplacian_rows(two_ref, i, x + NEAR, TILE, cy)
            for h, (c, l) in enumerate(zip(centre, lap)):
                lanes = slice(h * LANES, (h + 1) * LANES)
                moved = 2.0 * c - one_ref[i, x + MID, h, own]
                final_ref[i, x, :, lanes] = moved + c_ref[x + MID, h, own] * l
                prior_ref[i, x, :, lanes] = c

    run_planes(0, NEAR, first(TILE, cy))
    run_planes(NEAR, cx + 2 * MID - NEAR, first(begin, deep))
    run_planes(cx + 2 * MID - NEAR, cx + 2 * MID, first(TILE, cy))
    run_planes(0, NEAR, second(TILE, cy))
    run_planes(NEAR, cx + NEAR, second(begin, deep))
    run_planes(cx + NEAR, cx + 2 * NEAR, second(TILE, cy))
    run_planes(0, cx, third)


def last_wave_kernel(
    ready, px_ref, py_ref, free_final_ref, free_prior_ref, coef_ref, zero_in, zero_far_in, one_in, one_side_in, two_in,
    ye_ref, yo_ref, final_ref, prior_ref, one_ref, two_ref,
):
    _, cx, cy, _ = two_in.shape
    own = slice(TILE, TILE + cy)
    lower, higher = slice(0, TILE), slice(TILE + cy, 2 * TILE + cy)
    low = select_side(py_ref[0], ye_ref, yo_ref, False)
    high = select_side(py_ref[0], ye_ref, yo_ref, True)
    for i in range(3):
        for x in range(cx + 2 * NEAR):
            put_rows(one_ref, (i, x + MID - NEAR), own, zero_in[i, x])
        for k in range(NEAR):
            put_rows(one_ref, (i, k), own, zero_far_in[i, k])
            put_rows(one_ref, (i, cx + 2 * MID - NEAR + k), own, zero_far_in[i, NEAR + k])
            put_rows(two_ref, (i, k), own, one_side_in[i, k])
            put_rows(two_ref, (i, cx + NEAR + k), own, one_side_in[i, NEAR + k])
        for x in range(cx):
            put_rows(two_ref, (i, NEAR + x), own, one_in[i, x])
            for rows, read, turn in ((lower, low, TILE - NEAR), (higher, high, NEAR)):
                tile = read(lambda ref: ref[i, x])
                put_rows(one_ref, (i, MID + x), rows, tile)
                put_rows(two_ref, (i, NEAR + x), rows, half_turn(tile))
                if x < 2 * NEAR:
                    put_rows(one_ref, (i, MID + corner_plane(x, cx)), rows, pltpu.roll(tile, turn, 0))

    def second(start, count):
        def body(x):
            for i in range(3):
                centre, lap = laplacian_rows(one_ref, i, x + MID - NEAR, start, count)
                for h, (c, l) in enumerate(zip(centre, lap)):
                    rows = pl.ds(start, count)
                    two_ref[i, x, h, rows] = 2.0 * c + coef_ref[x, h, rows] * l + two_ref[i, x, h, rows]

        return body

    def third(x):
        for i in range(3):
            centre, lap = laplacian_rows(two_ref, i, x + NEAR, TILE, cy)
            for h, (c, l) in enumerate(zip(centre, lap)):
                lanes = slice(h * LANES, (h + 1) * LANES)
                moved = 2.0 * c - one_ref[i, x + MID, h, own] + coef_ref[x + NEAR, h, own] * l
                final_ref[i, x, :, lanes] = free_final_ref[i, x, :, lanes] + (moved + two_in[i, x, :, lanes])
                prior_ref[i, x, :, lanes] = free_prior_ref[i, x, :, lanes] + c

    ready()
    run_planes(0, NEAR, second(TILE, cy))
    run_planes(NEAR, cx + NEAR, second(px_ref[1], cy + TILE))
    run_planes(cx + NEAR, cx + 2 * NEAR, second(TILE, cy))
    run_planes(0, cx, third)


def staged(kernel, positions, operand_count):
    def run(*refs):
        refs, stages, sems = refs[: -len(positions) - 1], refs[-len(positions) - 1 : -1], refs[-1]
        ins = list(refs[:operand_count])
        copies = []
        for k, (at, stage) in enumerate(zip(positions, stages)):
            copies.append(pltpu.make_async_copy(ins[at], stage, sems.at[k]))
            ins[at] = stage
        for copy in copies:
            copy.start()

        def ready():
            for copy in copies:
                copy.wait()

        kernel(ready, *ins, *refs[operand_count:])

    return run


def local(
    current_field,
    earlier_field,
    wave_coef,
    layer_mask,
    point_xyz,
    point_owner,
    cell_offset,
    wave_vector,
    frequency,
    amplitude,
    phase_index,
    phase_table,
):
    point_count = point_xyz.shape[1]
    slab_count = lax.axis_size("slab")
    comp_count = lax.axis_size("comp")
    device_count = slab_count * comp_count
    slot_count = max(2, 2 * point_count // device_count)
    _, cx, cy, nz = current_field.shape
    assert slot_count <= HALF and device_count % 8 == 0
    assert cx >= DEEP and cy >= 2 * TILE and cy % TILE == 0
    wide = cy + 2 * TILE
    assert nz % LANES == 0 and MID == 2 * NEAR

    def plane_stack(*lead):
        return (*lead, nz // LANES, wide, LANES)

    smem = pl.BlockSpec(memory_space=pltpu.SMEM)
    vmem = pl.BlockSpec(memory_space=pltpu.VMEM)

    def call(kernel, operands, shapes, scratch=(), scalars=0, from_hbm=(), left_in_hbm=(), to_hbm=False):
        kind = pltpu.HBM if to_hbm else jax.ShapeDtypeStruct
        shapes = [kind(shape, F32) if isinstance(shape, tuple) else shape for shape in shapes]
        operands = list(operands)
        in_specs = [smem] * scalars + [vmem] * (len(operands) - scalars)
        scratch_shapes = [pltpu.VMEM(shape, F32) if isinstance(shape, tuple) else shape for shape in scratch]
        hbm = pl.BlockSpec(memory_space=pltpu.HBM)
        for at in left_in_hbm:
            operands[at] = pltpu.with_memory_space_constraint(operands[at], pltpu.HBM)
            in_specs[at] = hbm
        if from_hbm:
            for at in from_hbm:
                operands[at] = pltpu.with_memory_space_constraint(operands[at], pltpu.HBM)
                in_specs[at] = hbm
                scratch_shapes.append(pltpu.VMEM(operands[at].shape, operands[at].dtype))
            scratch_shapes.append(pltpu.SemaphoreType.DMA((len(from_hbm),)))
            kernel = staged(kernel, from_hbm, len(operands))
        return pl.pallas_call(
            kernel,
            out_shape=shapes,
            in_specs=in_specs,
            out_specs=[vmem] * len(shapes),
            scratch_shapes=scratch_shapes,
            compiler_params=pltpu.CompilerParams(vmem_limit_bytes=VMEM_GRANT),
        )(*operands)

    px = jnp.stack([lax.axis_index("slab") % 2, TILE // 2]).astype(jnp.int32)
    py = (lax.axis_index("comp") % 2).astype(jnp.int32).reshape(1)
    fields = (current_field, earlier_field, wave_coef)
    local_comps = frequency.shape[0]
    own_block, right, *faces = call(
        prepare_kernel,
        (
            py, *fields, wave_vector, frequency.reshape(1, local_comps), amplitude,
            phase_index.reshape(1, local_comps), phase_table.reshape(1, -1), point_xyz,
        ),
        [(8, local_comps), jax.ShapeDtypeStruct((48, point_count), BF16)] + [(5, cx, TILE, nz)] * 2,
        [(8, point_count)],
        scalars=1,
        from_hbm=tuple(range(1, 10)),
    )
    if comp_count == 4:
        near_block = lax.ppermute(own_block, "comp", pair_list(4, 0))
        first_blocks = [own_block, near_block]
        ring = pair_list(4, 1) + [(0, 3), (3, 0)]
        far_block = lax.ppermute(jnp.concatenate(first_blocks, axis=1), "comp", ring)
        last_blocks = [far_block]
    else:
        first_blocks = [own_block]
        last_blocks = [
            lax.ppermute(own_block, "comp", [(i, (i + k) % comp_count) for i in range(comp_count)])
            for k in range(1, comp_count)
        ]
    ye, yo = swap_faces(faces, "comp")
    (sum_one, total_one) = call(
        lambda *refs: first_incident_kernel(len(first_blocks), *refs),
        (*first_blocks, right),
        [(32, point_count), (16, KC)],
        [(AHEAD, KC, KC)],
    )
    sent = side_planes_sent(cy)
    sides = call(
        field_side_kernel,
        (px, py, *fields, layer_mask, ye, yo),
        [(sent, cy, nz)] * 2,
        [pltpu.SemaphoreType.DMA((2, len(FIELD_PLAN) - 1))],
        scalars=2,
        from_hbm=(5,),
        left_in_hbm=(2, 3, 4),
    )
    xe, xo = swap_faces(sides, "slab")
    (packed,) = call(
        lambda *refs: last_incident_kernel(len(last_blocks), comp_count, *refs),
        (
            *last_blocks, sum_one, total_one, right,
            point_owner.reshape(1, point_count), cell_offset.reshape(1, point_count),
        ),
        [(device_count, 1, LIST_ROWS * 2 * HALF)],
        [(32, point_count), (AHEAD, KC, KC)],
        from_hbm=tuple(len(last_blocks) + k for k in (3, 4)),
    )
    arrived = lax.all_to_all(packed, ("slab", "comp"), split_axis=0, concat_axis=0, tiled=True)
    free_final, free_prior, wide_coef, wide_sign = call(
        first_wave_kernel,
        (px, py, *fields, layer_mask, ye, yo, xe, xo),
        [current_field.shape, current_field.shape, plane_stack(cx + 2 * NEAR), (cx + 2 * MID, cy, nz)],
        [
            plane_stack(3, cx + 2 * DEEP), plane_stack(3, cx + 2 * MID), plane_stack(cx + 2 * MID),
            plane_stack(3, cx + 2 * MID), plane_stack(3, cx + 2 * NEAR),
        ],
        scalars=2,
        from_hbm=(2, 3, 4, 5),
        to_hbm=True,
    )
    held = (device_count // 2 * ROWS_HELD, 2 * HALF)
    zero, one, face_even, face_odd = call(
        near_scatter_kernel,
        (py, arrived, wide_sign),
        [(3, cx + 2 * NEAR, cy, nz), (3, cx, cy, nz)] + [(3, cx, TILE, nz)] * 2,
        [(3, (cx + 2 * NEAR) * cy, nz), (3, cx * cy, nz), held, held],
        scalars=1,
        from_hbm=(2,),
    )
    fye, fyo = swap_faces((face_even, face_odd), "comp")
    zero_far, one_side, two = call(
        rest_scatter_kernel,
        (arrived, wide_sign),
        [(3, 2 * NEAR, cy, nz), (3, 2 * NEAR, cy, nz), (3, cx, cy, nz)],
        [(3, 2 * NEAR * cy, nz), (3, 2 * NEAR * cy, nz), (3, cx * cy, nz), held, held],
        from_hbm=(1,),
    )
    final, prior = call(
        last_wave_kernel,
        (px, py, free_final, free_prior, wide_coef, zero, zero_far, one, one_side, two, fye, fyo),
        [current_field.shape, current_field.shape],
        [plane_stack(3, cx + 2 * MID), plane_stack(3, cx + 2 * NEAR)],
        scalars=2,
        from_hbm=(2, 3, 4),
    )
    return (final, prior)


def solution(mesh):
    in_specs = (
        P(None, "slab", "comp", None),
        P(None, "slab", "comp", None),
        P("slab", "comp", None),
        P("slab", "comp", None),
        P(None, ("slab", "comp")),
        P(("slab", "comp"), None),
        P(("slab", "comp")),
        P(None, "comp"),
        P("comp"),
        P(None, "comp"),
        P("comp"),
        P(),
    )
    out_specs = (P(None, "slab", "comp", None), P(None, "slab", "comp", None))
    return jax.shard_map(local, mesh=mesh, in_specs=in_specs, out_specs=out_specs, check_vma=False)
```

```python
import jax
import jax.numpy as jnp
from jax import lax
from jax.experimental import pallas as pl
from jax.experimental.pallas import tpu as pltpu
from jax.sharding import PartitionSpec as P

step_size = 0.05
near_weight = 4.0 / 3.0
far_weight = -1.0 / 12.0
centre_weight = -7.5
inv_two_pi = 0.15915494309189535

LEAD = -0.7713118195533752
SIN_C = (4.442834854125977 / LEAD, -7.306587219238281 / LEAD, 3.588636875152588 / LEAD)
SIN_SCALE = LEAD * abs(LEAD)
VER_SCALE = LEAD * LEAD
KC = 256
AHEAD = 2
HALF = 64
OWN_TILES = 5
SIDE_TILES = 4
HIGH_LIST = OWN_TILES
LOW_LIST = OWN_TILES + SIDE_TILES
LIST_ROWS = OWN_TILES + 2 * SIDE_TILES
VMEM_GRANT = 16 * 2**20

F32 = jnp.float32
BF16 = jnp.bfloat16


def sin_versine(u):
    r = u - jnp.round(u)
    z = r * r
    s = r * (((z + SIN_C[2]) * z + SIN_C[1]) * z + SIN_C[0])
    q = s * s
    w = 2.0 / VER_SCALE - q
    return s * (w * lax.rsqrt(w)), q


def split_three(x):
    hi = x.astype(BF16).astype(F32)
    rest = x - hi
    mid = rest.astype(BF16).astype(F32)
    return hi, mid, rest - mid


def row_ids(shape):
    return lax.broadcasted_iota(jnp.int32, shape, 0)


def add_components(par_refs, right_ref, acc_ref, u_ref):
    points = right_ref.shape[1]
    ahead, kc, tile = u_ref.shape
    rows8 = row_ids((8, kc))
    times = step_size * (rows8 + 1).astype(F32)
    rows16 = row_ids((16, kc))
    comp_row = jnp.where(rows16 < 6, rows16 % 3, (rows16 + 2) % 3)
    valued = (rows16 < 10) & (rows16 != 6)

    def block_of(par_ref, step):
        return par_ref[:, pl.ds(pl.multiple_of(step * kc, kc), kc)]

    def left_of(blk):
        khi, kmid, klo = split_three(jnp.where(rows8 < 3, blk * inv_two_pi, 0.0))
        return jnp.concatenate([khi, khi, khi, kmid, kmid, klo], axis=0).astype(BF16)

    def angles(left, t):
        cols = slice(t * tile, (t + 1) * tile)
        return lax.dot_general(left, right_ref[:, cols], (((0,), (0,)), ((), ())), preferred_element_type=F32)

    def body(par_ref, steps, step, total):
        blk = block_of(par_ref, step)
        left = left_of(blk)
        later = left_of(block_of(par_ref, jnp.minimum(step + 1, steps - 1)))
        delays = times * blk[3:4, :] - blk[7:8, :]
        sd, qd = sin_versine(delays * inv_two_pi)
        sd, cd = SIN_SCALE * sd, 1.0 - VER_SCALE * qd
        amp = jnp.where(comp_row == 0, blk[4:5, :], jnp.where(comp_row == 1, blk[5:6, :], blk[6:7, :]))
        amp = jnp.where(valued, amp, 0.0)

        def rows_of(t):
            w = amp * jnp.where(rows16 < 3, t[0:1, :], jnp.where(rows16 < 6, t[1:2, :], t[2:3, :]))
            hi = w.astype(BF16)
            lo = (w - hi.astype(F32)).astype(BF16)
            return w, jnp.concatenate([hi, lo], axis=0)

        wc = rows_of(cd)[0]
        lc = rows_of(-VER_SCALE * cd)[1]
        ls = rows_of(SIN_SCALE * sd)[1]

        def add_tile(t, u):
            highs, lows = [], []
            for j in range(kc // 32):
                for value in sin_versine(u[32 * j : 32 * j + 32]):
                    high = value.astype(BF16)
                    highs.append(high)
                    lows.append((value - high.astype(F32)).astype(BF16))
            part = jnp.dot(ls, jnp.concatenate(highs[0::2], axis=0), preferred_element_type=F32)
            part += jnp.dot(lc, jnp.concatenate(highs[1::2], axis=0), preferred_element_type=F32)
            part += jnp.dot(ls, jnp.concatenate(lows[0::2], axis=0), preferred_element_type=F32)
            part += jnp.dot(lc, jnp.concatenate(lows[1::2], axis=0), preferred_element_type=F32)
            acc_ref[:, t * tile : (t + 1) * tile] += part

        tiles = points // tile
        rest = {t: angles(left, t) for t in range(ahead, tiles)}
        for t in range(ahead):
            add_tile(t, u_ref[t])
        for t in range(ahead):
            u_ref[t] = angles(later, t)
        for t, u in rest.items():
            add_tile(t, u)
        return total + wc

    total = jnp.zeros((16, kc), F32)
    for par_ref in par_refs:
        steps = par_ref.shape[1] // kc
        left = left_of(block_of(par_ref, 0))
        for t in range(ahead):
            u_ref[t] = angles(left, t)
        total = lax.fori_loop(0, steps, lambda step, t, ref=par_ref, n=steps: body(ref, n, step, t), total)
    return total


def first_incident_kernel(count, ready, px_ref, *refs):
    par_refs, refs = refs[:count], refs[count:]
    right_ref, cur_ref, ear_ref, coef_ref, mask_ref, acc_ref, total_ref, even_out, odd_out, u_ref, face_ref = refs[:11]
    load_sems, store_sems = refs[11:]
    cx = mask_ref.shape[0]
    sources = [cur_ref.at[i] for i in range(3)] + [ear_ref.at[i] for i in range(3)] + [coef_ref]
    loads = []
    for face in (0, 1):
        for name, source in enumerate(sources):
            planes = FIELD_PLAN[name][0]
            first = sum(n for n, _ in FIELD_PLAN[:name])
            x = cx - planes if face == 0 else 0
            held = face_ref.at[face, pl.ds(first, planes)]
            loads.append(pltpu.make_async_copy(source.at[pl.ds(x, planes)], held, load_sems.at[face, name]))
    for copy in loads:
        copy.start()

    def stores(high_out, low_out):
        return [
            pltpu.make_async_copy(face_ref.at[face], out.at[pl.ds(0, SIDE_PLANES)], store_sems.at[face])
            for face, out in ((0, high_out), (1, low_out))
        ]

    def each_store(act):
        for parity, outs in ((0, (even_out, odd_out)), (1, (odd_out, even_out))):

            @pl.when(px_ref[0] == parity)
            def _():
                for copy in stores(*outs):
                    act(copy)

    acc_ref[...] = jnp.zeros(acc_ref.shape, F32)
    total = add_components(par_refs[:1], right_ref, acc_ref, u_ref)
    for copy in loads:
        copy.wait()
    ready()
    for face in (0, 1):
        for k in range(MID):
            x = cx - MID + k if face == 0 else k
            face_ref[face, SIDE_PLANES - MID + k] = sign_of(mask_ref[x])
    each_store(lambda copy: copy.start())
    total_ref[...] = total + add_components(par_refs[1:], right_ref, acc_ref, u_ref)
    each_store(lambda copy: copy.wait())


def last_incident_kernel(count, step, ready, *refs):
    par_refs, refs = refs[:count], refs[count:]
    first_ref, first_total_ref, right_ref, own_ref, off_ref, out_ref, acc_ref, u_ref = refs
    points = right_ref.shape[1]
    owners = out_ref.shape[0]
    acc_ref[...] = first_ref[...]
    total = add_components(par_refs, right_ref, acc_ref, u_ref) + first_total_ref[...]
    ready()
    vals = acc_ref[0:16, :] + acc_ref[16:32, :] + jnp.sum(total, axis=1, keepdims=True)
    vals = jnp.where(row_ids((16, points)) == 6, off_ref[...].astype(F32), vals)
    v1, v2, v3 = split_three(vals)
    named = own_ref[...] == row_ids((owners, points))
    named_one = named.astype(F32).astype(BF16)
    width = 128
    square = (width, width)
    earlier = (row_ids(square) < lax.broadcasted_iota(jnp.int32, square, 1)).astype(F32).astype(BF16)
    sums = jnp.concatenate([earlier, jnp.ones(square, BF16)], axis=1)
    before, past = [], jnp.zeros((owners, width), F32)
    for k in range(0, points, width):
        got = jnp.dot(named_one[:, k : k + width], sums, preferred_element_type=F32)
        before.append(got[:, 0:width] + past)
        past = past + got[:, width:]
    before = jnp.concatenate(before, axis=1)
    rank = jnp.sum(jnp.where(named, before, 0.0), axis=0, keepdims=True).astype(jnp.int32)
    terms = [v.astype(BF16) for v in (v1, v2, v3)]
    tiles = 0.0
    for odd in (0, 1):
        left = jnp.concatenate(
            [named_one * t[2 * j + odd : 2 * j + odd + 1, :] for t in terms for j in range(OWN_TILES)], axis=0
        )
        spots = (row_ids((2 * HALF, points)) == rank + odd * HALF).astype(F32).astype(BF16)
        got = lax.dot_general(left, spots, (((1,), (1,)), ((), ())), preferred_element_type=F32)
        size = OWN_TILES * owners
        tiles = tiles + (got[0:size] + got[size : 2 * size] + got[2 * size :])
    owner_row = row_ids((owners, 2 * HALF))

    def put(j, tile):
        out_ref[:, 0, 2 * HALF * j : 2 * HALF * (j + 1)] = tile

    for j in range(OWN_TILES):
        tile = tiles[j * owners : (j + 1) * owners]
        put(j, tile)
        if j < SIDE_TILES:
            above = pltpu.roll(tile, owners - step, 0)
            put(HIGH_LIST + j, jnp.where(owner_row < owners - step, above, 0.0))
            put(LOW_LIST + j, jnp.where(owner_row >= step, pltpu.roll(tile, step, 0), 0.0))


TILE = 8
DEEP = 6
MID = 4
NEAR = 2


def half_turn(tile):
    return pltpu.roll(tile, TILE // 2, 0)


ROWS_HELD = 16


def scatter_lists(val_ref, even_ref, odd_ref, jobs, cy, nz):
    lanes = 2 * HALF
    sources = val_ref.shape[0]
    groups = sources // 2
    chunk = 2 * lanes
    left_half = lax.broadcasted_iota(jnp.int32, (groups, lanes), 1) < lanes // 2
    for ref in {id(job[4]): job[4] for job in jobs}.values():
        ref[...] = jnp.zeros(ref.shape, F32)
    for j in range(LIST_ROWS):
        rows = val_ref[:, 0, lanes * j : lanes * (j + 1)]
        first, second = rows[0:groups], rows[groups:]
        at = pl.ds(j, groups, stride=ROWS_HELD)
        even_ref[at, :] = jnp.where(left_half, first, pltpu.roll(second, lanes // 2, 1))
        odd_ref[at, :] = jnp.where(left_half, pltpu.roll(first, lanes // 2, 1), second)

    def body(step, carry):
        evens, odds = [], []
        for pair in range(2):
            at = pl.ds(pl.multiple_of((2 * step + pair) * ROWS_HELD, ROWS_HELD), ROWS_HELD)
            evens.append(even_ref[at, :])
            odds.append(odd_ref[at, :])
        values = [jnp.concatenate(evens, axis=1), jnp.concatenate(odds, axis=1)]
        high = [v.astype(BF16) for v in values]
        low = [(v - h.astype(F32)).astype(BF16) for v, h in zip(values, high)]
        for base in (0, HIGH_LIST, LOW_LIST):
            own_jobs = [job for job in jobs if job[0] == base]
            off = values[0][base + 3 : base + 4, :].astype(jnp.int32)
            row = off // nz
            zt = (row_ids((nz, chunk)) == off - row * nz).astype(F32).astype(BF16)
            masks, left = {}, []
            for _, ranks, plane, planes, ref, start in own_jobs:
                if (plane, planes) not in masks:
                    ids = row_ids((planes * cy, chunk)) + plane * cy
                    masks[plane, planes] = (ids == row).astype(F32).astype(BF16)
                for r in ranks:
                    at = base + r // 2
                    left += [masks[plane, planes] * t[r % 2][at : at + 1, :] for t in (high, low)]
            left = jnp.concatenate(left, axis=0)
            got = lax.dot_general(left, zt, (((1,), (1,)), ((), ())), preferred_element_type=F32)
            at = 0
            for _, ranks, _, planes, ref, start in own_jobs:
                size = planes * cy
                for i in range(len(ranks)):
                    ref[i, start : start + size] += got[at : at + size] + got[at + size : at + 2 * size]
                    at += 2 * size
        return carry

    lax.fori_loop(0, groups // 2, body, 0, unroll=4)


STEP_ROWS = ((0, 1, 2), (3, 4, 5), (7, 8, 9))


def near_scatter_kernel(
    ready, par_ref, val_ref, sign_ref, zero_out, one_out, even_out, odd_out, zero_ref, one_ref, even_ref, odd_ref
):
    _, cx, cy, nz = one_out.shape
    jobs = (
        (0, STEP_ROWS[0], 0, cx, zero_ref, NEAR * cy),
        (0, STEP_ROWS[1], 0, cx, one_ref, 0),
        (HIGH_LIST, STEP_ROWS[0], 0, NEAR, zero_ref, (NEAR + cx) * cy),
        (LOW_LIST, STEP_ROWS[0], cx - NEAR, NEAR, zero_ref, 0),
    )
    scatter_lists(val_ref, even_ref, odd_ref, jobs, cy, nz)
    ready()
    sign = sign_ref[...]
    for i in range(3):
        zero_out[i] = zero_ref[i].reshape(zero_out.shape[1:]) * sign[MID - NEAR : MID + cx + NEAR]
        one_out[i] = one_ref[i].reshape(one_out.shape[1:]) * sign[MID : MID + cx]
    at = row_ids((TILE, nz))

    def write(is_high, face_ref):
        ys = slice(cy - TILE, cy) if is_high else slice(0, TILE)
        half = at >= TILE // 2 if is_high else at < TILE // 2
        corner = at < NEAR if is_high else at >= TILE - NEAR
        for i in range(3):
            for x in range(cx):
                tile = jnp.where(half, zero_out[i, NEAR + x, ys], half_turn(one_out[i, x, ys]))
                if x < 2 * NEAR:
                    moved = pltpu.roll(zero_out[i, NEAR + corner_plane(x, cx), ys], NEAR if is_high else TILE - NEAR, 0)
                    tile = jnp.where(corner, moved, tile)
                face_ref[i, x] = tile

    write_faces(par_ref[0], write, even_out, odd_out)


def rest_scatter_kernel(
    ready, val_ref, sign_ref, zero_out, one_out, two_out, zero_ref, one_ref, two_ref, even_ref, odd_ref
):
    _, cx, cy, nz = two_out.shape
    jobs = (
        (0, STEP_ROWS[2], 0, cx, two_ref, 0),
        (HIGH_LIST, STEP_ROWS[0], NEAR, MID - NEAR, zero_ref, NEAR * cy),
        (LOW_LIST, STEP_ROWS[0], cx - MID, MID - NEAR, zero_ref, 0),
        (HIGH_LIST, STEP_ROWS[1], 0, NEAR, one_ref, NEAR * cy),
        (LOW_LIST, STEP_ROWS[1], cx - NEAR, NEAR, one_ref, 0),
    )
    scatter_lists(val_ref, even_ref, odd_ref, jobs, cy, nz)
    ready()
    sign = sign_ref[...]
    last = cx + 2 * MID
    far = jnp.concatenate([sign[0 : MID - NEAR], sign[last - (MID - NEAR) :]], axis=0)
    side = jnp.concatenate([sign[MID - NEAR : MID], sign[MID + cx : MID + cx + NEAR]], axis=0)
    for i in range(3):
        zero_out[i] = zero_ref[i].reshape(zero_out.shape[1:]) * far
        one_out[i] = one_ref[i].reshape(one_out.shape[1:]) * side
        two_out[i] = two_ref[i].reshape(two_out.shape[1:]) * sign[MID : MID + cx]


def corner_plane(x, cx):
    return x - NEAR if x < NEAR else cx + x - NEAR


def write_faces(parity, write, even_out, odd_out):
    @pl.when(parity == 0)
    def _():
        write(True, even_out)
        write(False, odd_out)

    @pl.when(parity != 0)
    def _():
        write(False, even_out)
        write(True, odd_out)


def pair_list(count, odd):
    first = 1 if odd else 0
    pairs = [(i, i + 1) for i in range(first, count - 1, 2)]
    return pairs + [(j, i) for i, j in pairs]


def swap_faces(faces, axis):
    count = lax.axis_size(axis)
    out = []
    for k in (0, 1):
        out.append(lax.ppermute(faces[k], axis, pair_list(count, k)))
    return out


def prepare_kernel(
    ready, par_ref, cur_ref, ear_ref, coef_ref, wave_ref, freq_ref, amp_ref, index_ref, table_ref, xyz_ref,
    block_out, right_out, even_out, odd_out, x8_ref,
):
    x8_ref[...] = jnp.zeros(x8_ref.shape, F32)
    ready()
    x8_ref[0:3, :] = xyz_ref[...]
    xhi, xmid, xlo = split_three(x8_ref[...])
    right_out[...] = jnp.concatenate([xhi, xmid, xlo, xhi, xmid, xhi], axis=0).astype(BF16)
    entries = table_ref.shape[1]
    comps = index_ref.shape[1]
    picked = (row_ids((entries, comps)) == index_ref[...]).astype(F32).astype(BF16)
    terms = jnp.concatenate(list(split_three(jnp.broadcast_to(table_ref[...], (TILE, entries)))), axis=0).astype(BF16)
    phase = jnp.dot(terms, picked, preferred_element_type=F32)
    block_out[0:3, :] = wave_ref[...]
    block_out[3:4, :] = freq_ref[...]
    block_out[4:7, :] = amp_ref[...]
    block_out[7:8, :] = phase[0:1] + phase[TILE : TILE + 1] + phase[2 * TILE : 2 * TILE + 1]
    _, cx, cy, nz = cur_ref.shape
    upper = row_ids((TILE, nz)) >= TILE // 2

    def write(high, face_ref):
        ys = slice(cy - TILE, cy) if high else slice(0, TILE)
        keep = upper if high else ~upper
        for x in range(cx):
            for i in range(3):
                face_ref[i, x] = cur_ref[i, x, ys]
            face_ref[3, x] = jnp.where(keep, ear_ref[0, x, ys], half_turn(ear_ref[1, x, ys]))
            face_ref[4, x] = jnp.where(keep, ear_ref[2, x, ys], half_turn(coef_ref[x, ys]))

    write_faces(par_ref[0], write, even_out, odd_out)


def face_tile(ref, name, x):
    if name < 3:
        return ref[name, x]
    tile = ref[3 + (name - 3) // 2, x]
    return half_turn(tile) if name in (4, 6) else tile


def select_side(parity, even_ref, odd_ref, high):
    from_even = (parity == 0) if high else (parity == 1)

    def read(get):
        return jnp.where(from_even, get(even_ref), get(odd_ref))

    return read


FIELD_PLAN = [(DEEP, MID)] * 3 + [(MID, NEAR)] * 4 + [(MID, 0)]
SIDE_PLANES = sum(planes for planes, _ in FIELD_PLAN)
CORNERS = [(name, dist) for name, (_, corners) in enumerate(FIELD_PLAN) for dist in range(1, corners + 1)]


def side_plane(name, dist, is_high):
    planes = FIELD_PLAN[name][0]
    first = sum(n for n, _ in FIELD_PLAN[:name])
    return first + (dist - 1 if is_high else planes - dist)


def corner_place(k, cy):
    per_plane = cy // TILE
    start = k % per_plane * TILE
    return SIDE_PLANES + k // per_plane, slice(start, start + TILE)


def side_planes_sent(cy):
    return SIDE_PLANES + -(-len(CORNERS) // (cy // TILE))


def sign_of(mask):
    return (mask == 1).astype(F32) - (mask == 2).astype(F32)


def corner_kernel(
    px_ref, py_ref, even_ref, odd_ref, even_in, odd_in, even_out, odd_out, corner_ref, sems
):
    cx, nz = even_ref.shape[1], even_ref.shape[3]
    cy = corner_ref.shape[2]
    upper = row_ids((TILE, nz)) >= TILE // 2
    low = select_side(py_ref[0], even_ref, odd_ref, False)
    high = select_side(py_ref[0], even_ref, odd_ref, True)
    for face in (0, 1):
        for k, (name, dist) in enumerate(CORNERS):
            x = cx - dist if face == 0 else dist - 1
            below = low(lambda ref: face_tile(ref, name, x))
            above = high(lambda ref: face_tile(ref, name, x))
            plane, rows = corner_place(k, cy)
            corner_ref[face, plane - SIDE_PLANES, rows] = jnp.where(upper, below, above)
    rest = pl.ds(SIDE_PLANES, corner_ref.shape[1])

    def run(*outs):
        copies = [
            pltpu.make_async_copy(corner_ref.at[face], out.at[rest], sems.at[face]) for face, out in enumerate(outs)
        ]
        for copy in copies:
            copy.start()
        for copy in copies:
            copy.wait()

    @pl.when(px_ref[0] == 0)
    def _():
        run(even_out, odd_out)

    @pl.when(px_ref[0] != 0)
    def _():
        run(odd_out, even_out)


LANES = 128


def put_rows(ref, index, rows, value):
    for h in range(value.shape[1] // LANES):
        ref[(*index, h, rows)] = value[:, h * LANES : (h + 1) * LANES]


def laplacian_rows(ref, i, x, start, count):
    tiles = ref.shape[2]
    lane = lax.broadcasted_iota(jnp.int32, (count, LANES), 1)

    def rows(h, dx, dy):
        return ref[i, x + dx, h, pl.ds(start + dy, count)]

    centre = [rows(h, 0, 0) for h in range(tiles)]
    out = [centre_weight * c for c in centre]
    for k, weight in ((1, near_weight), (2, far_weight)):
        up = [pltpu.roll(c, k, 1) for c in centre]
        down = [pltpu.roll(c, LANES - k, 1) for c in centre]
        for h in range(tiles):
            below = jnp.where(lane >= k, up[h], up[h - 1] if h else 0.0)
            above = jnp.where(lane < LANES - k, down[h], down[h + 1] if h + 1 < tiles else 0.0)
            across = (rows(h, -k, 0) + rows(h, k, 0)) + (rows(h, 0, -k) + rows(h, 0, k))
            out[h] = out[h] + weight * (across + (below + above))
    return centre, out


def run_planes(first, last, body):
    lax.fori_loop(first, last, lambda x, carry: (body(x), carry)[1], 0, unroll=2)


def first_wave_kernel(
    ready, px_ref, py_ref, cur_ref, ear_ref, coef_ref, mask_ref, ye_ref, yo_ref, xe_ref, xo_ref,
    final_ref, prior_ref, wide_coef_ref, wide_sign_ref, u_ref, e_ref, c_ref, one_ref, two_ref,
):
    _, cx, cy, _ = cur_ref.shape
    own = slice(TILE, TILE + cy)
    lower, higher = slice(0, TILE), slice(TILE + cy, 2 * TILE + cy)
    low = select_side(py_ref[0], ye_ref, yo_ref, False)
    high = select_side(py_ref[0], ye_ref, yo_ref, True)
    ready()

    def put(name, x, rows, value):
        if name < 3:
            put_rows(u_ref, (name, DEEP + x), rows, value)
        elif name < 6:
            put_rows(e_ref, (name - 3, MID + x), rows, value)
        elif name == 6:
            put_rows(c_ref, (MID + x,), rows, value)
            if -NEAR <= x < cx + NEAR:
                put_rows(wide_coef_ref, (NEAR + x,), rows, value)
        else:
            wide_sign_ref[MID + x, slice(rows.start - TILE, rows.stop - TILE)] = value

    for x in range(cx):
        for name in range(7):
            value = cur_ref[name, x] if name < 3 else ear_ref[name - 3, x] if name < 6 else coef_ref[x]
            put(name, x, own, value)
            put(name, x, lower, low(lambda ref: face_tile(ref, name, x)))
            put(name, x, higher, high(lambda ref: face_tile(ref, name, x)))
        put(7, x, own, sign_of(mask_ref[x]))
    for is_high in (False, True):
        read = select_side(px_ref[0], xe_ref, xo_ref, is_high)
        for name, (planes, _) in enumerate(FIELD_PLAN):
            for dist in range(1, planes + 1):
                x = cx - 1 + dist if is_high else -dist
                put(name, x, own, read(lambda ref: ref[side_plane(name, dist, is_high)]))
        for k, (name, dist) in enumerate(CORNERS):
            x = cx - 1 + dist if is_high else -dist
            plane, rows = corner_place(k, cy)
            tile = read(lambda ref: ref[plane, rows])
            put(name, x, lower, tile)
            put(name, x, higher, tile)

    begin = px_ref[1]
    deep = cy + TILE

    def first(start, count):
        def body(x):
            for i in range(3):
                centre, lap = laplacian_rows(u_ref, i, x + DEEP - MID, start, count)
                for h, (c, l) in enumerate(zip(centre, lap)):
                    rows = pl.ds(start, count)
                    one_ref[i, x, h, rows] = 2.0 * c - e_ref[i, x, h, rows] + c_ref[x, h, rows] * l

        return body

    def second(start, count):
        def body(x):
            for i in range(3):
                centre, lap = laplacian_rows(one_ref, i, x + MID - NEAR, start, count)
                for h, (c, l) in enumerate(zip(centre, lap)):
                    rows = pl.ds(start, count)
                    moved = 2.0 * c - u_ref[i, x + DEEP - NEAR, h, rows]
                    two_ref[i, x, h, rows] = moved + c_ref[x + MID - NEAR, h, rows] * l

        return body

    def third(x):
        for i in range(3):
            centre, lap = laplacian_rows(two_ref, i, x + NEAR, TILE, cy)
            for h, (c, l) in enumerate(zip(centre, lap)):
                lanes = slice(h * LANES, (h + 1) * LANES)
                moved = 2.0 * c - one_ref[i, x + MID, h, own]
                final_ref[i, x, :, lanes] = moved + c_ref[x + MID, h, own] * l
                prior_ref[i, x, :, lanes] = c

    run_planes(0, NEAR, first(TILE, cy))
    run_planes(NEAR, cx + 2 * MID - NEAR, first(begin, deep))
    run_planes(cx + 2 * MID - NEAR, cx + 2 * MID, first(TILE, cy))
    run_planes(0, NEAR, second(TILE, cy))
    run_planes(NEAR, cx + NEAR, second(begin, deep))
    run_planes(cx + NEAR, cx + 2 * NEAR, second(TILE, cy))
    run_planes(0, cx, third)


def last_wave_kernel(
    ready, px_ref, py_ref, free_final_ref, free_prior_ref, coef_ref, zero_in, zero_far_in, one_in, one_side_in, two_in,
    ye_ref, yo_ref, final_ref, prior_ref, one_ref, two_ref,
):
    _, cx, cy, _ = two_in.shape
    own = slice(TILE, TILE + cy)
    lower, higher = slice(0, TILE), slice(TILE + cy, 2 * TILE + cy)
    low = select_side(py_ref[0], ye_ref, yo_ref, False)
    high = select_side(py_ref[0], ye_ref, yo_ref, True)
    for i in range(3):
        for x in range(cx + 2 * NEAR):
            put_rows(one_ref, (i, x + MID - NEAR), own, zero_in[i, x])
        for k in range(NEAR):
            put_rows(one_ref, (i, k), own, zero_far_in[i, k])
            put_rows(one_ref, (i, cx + 2 * MID - NEAR + k), own, zero_far_in[i, NEAR + k])
            put_rows(two_ref, (i, k), own, one_side_in[i, k])
            put_rows(two_ref, (i, cx + NEAR + k), own, one_side_in[i, NEAR + k])
        for x in range(cx):
            put_rows(two_ref, (i, NEAR + x), own, one_in[i, x])
            for rows, read, turn in ((lower, low, TILE - NEAR), (higher, high, NEAR)):
                tile = read(lambda ref: ref[i, x])
                put_rows(one_ref, (i, MID + x), rows, tile)
                put_rows(two_ref, (i, NEAR + x), rows, half_turn(tile))
                if x < 2 * NEAR:
                    put_rows(one_ref, (i, MID + corner_plane(x, cx)), rows, pltpu.roll(tile, turn, 0))

    def second(start, count):
        def body(x):
            for i in range(3):
                centre, lap = laplacian_rows(one_ref, i, x + MID - NEAR, start, count)
                for h, (c, l) in enumerate(zip(centre, lap)):
                    rows = pl.ds(start, count)
                    two_ref[i, x, h, rows] = 2.0 * c + coef_ref[x, h, rows] * l + two_ref[i, x, h, rows]

        return body

    def third(x):
        for i in range(3):
            centre, lap = laplacian_rows(two_ref, i, x + NEAR, TILE, cy)
            for h, (c, l) in enumerate(zip(centre, lap)):
                lanes = slice(h * LANES, (h + 1) * LANES)
                moved = 2.0 * c - one_ref[i, x + MID, h, own] + coef_ref[x + NEAR, h, own] * l
                final_ref[i, x, :, lanes] = free_final_ref[i, x, :, lanes] + (moved + two_in[i, x, :, lanes])
                prior_ref[i, x, :, lanes] = free_prior_ref[i, x, :, lanes] + c

    ready()
    run_planes(0, NEAR, second(TILE, cy))
    run_planes(NEAR, cx + NEAR, second(px_ref[1], cy + TILE))
    run_planes(cx + NEAR, cx + 2 * NEAR, second(TILE, cy))
    run_planes(0, cx, third)


def staged(kernel, positions, operand_count):
    def run(*refs):
        refs, stages, sems = refs[: -len(positions) - 1], refs[-len(positions) - 1 : -1], refs[-1]
        ins = list(refs[:operand_count])
        copies = []
        for k, (at, stage) in enumerate(zip(positions, stages)):
            copies.append(pltpu.make_async_copy(ins[at], stage, sems.at[k]))
            ins[at] = stage
        for copy in copies:
            copy.start()

        def ready():
            for copy in copies:
                copy.wait()

        kernel(ready, *ins, *refs[operand_count:])

    return run


def local(
    current_field,
    earlier_field,
    wave_coef,
    layer_mask,
    point_xyz,
    point_owner,
    cell_offset,
    wave_vector,
    frequency,
    amplitude,
    phase_index,
    phase_table,
):
    point_count = point_xyz.shape[1]
    slab_count = lax.axis_size("slab")
    comp_count = lax.axis_size("comp")
    device_count = slab_count * comp_count
    slot_count = max(2, 2 * point_count // device_count)
    _, cx, cy, nz = current_field.shape
    assert slot_count <= HALF and device_count % 8 == 0
    assert cx >= DEEP and cy >= 2 * TILE and cy % TILE == 0
    wide = cy + 2 * TILE
    assert nz % LANES == 0 and MID == 2 * NEAR

    def plane_stack(*lead):
        return (*lead, nz // LANES, wide, LANES)

    smem = pl.BlockSpec(memory_space=pltpu.SMEM)
    vmem = pl.BlockSpec(memory_space=pltpu.VMEM)

    def call(kernel, operands, shapes, scratch=(), scalars=0, from_hbm=(), left_in_hbm=(), to_hbm=False, raw=0, aliases=None):
        kind = pltpu.HBM if to_hbm else jax.ShapeDtypeStruct
        shapes = [kind(shape, F32) if isinstance(shape, tuple) else shape for shape in shapes]
        out_specs = [vmem] * (len(shapes) - raw) + [pl.BlockSpec(memory_space=pltpu.HBM)] * raw
        operands = list(operands)
        in_specs = [smem] * scalars + [vmem] * (len(operands) - scalars)
        scratch_shapes = [pltpu.VMEM(shape, F32) if isinstance(shape, tuple) else shape for shape in scratch]
        hbm = pl.BlockSpec(memory_space=pltpu.HBM)
        for at in left_in_hbm:
            operands[at] = pltpu.with_memory_space_constraint(operands[at], pltpu.HBM)
            in_specs[at] = hbm
        if from_hbm:
            for at in from_hbm:
                operands[at] = pltpu.with_memory_space_constraint(operands[at], pltpu.HBM)
                in_specs[at] = hbm
                scratch_shapes.append(pltpu.VMEM(operands[at].shape, operands[at].dtype))
            scratch_shapes.append(pltpu.SemaphoreType.DMA((len(from_hbm),)))
            kernel = staged(kernel, from_hbm, len(operands))
        return pl.pallas_call(
            kernel,
            out_shape=shapes,
            in_specs=in_specs,
            out_specs=out_specs,
            input_output_aliases=aliases or {},
            scratch_shapes=scratch_shapes,
            compiler_params=pltpu.CompilerParams(vmem_limit_bytes=VMEM_GRANT),
        )(*operands)

    px = jnp.stack([lax.axis_index("slab") % 2, TILE // 2]).astype(jnp.int32)
    py = (lax.axis_index("comp") % 2).astype(jnp.int32).reshape(1)
    fields = (current_field, earlier_field, wave_coef)
    local_comps = frequency.shape[0]
    own_block, right, *faces = call(
        prepare_kernel,
        (
            py, *fields, wave_vector, frequency.reshape(1, local_comps), amplitude,
            phase_index.reshape(1, local_comps), phase_table.reshape(1, -1), point_xyz,
        ),
        [(8, local_comps), jax.ShapeDtypeStruct((48, point_count), BF16)] + [(5, cx, TILE, nz)] * 2,
        [(8, point_count)],
        scalars=1,
        from_hbm=tuple(range(1, 10)),
    )
    if comp_count == 4:
        near_block = lax.ppermute(own_block, "comp", pair_list(4, 0))
        first_blocks = [own_block, near_block]
        ring = pair_list(4, 1) + [(0, 3), (3, 0)]
        far_block = lax.ppermute(jnp.concatenate(first_blocks, axis=1), "comp", ring)
        last_blocks = [far_block]
    else:
        first_blocks = [own_block]
        last_blocks = [
            lax.ppermute(own_block, "comp", [(i, (i + k) % comp_count) for i in range(comp_count)])
            for k in range(1, comp_count)
        ]
    ye, yo = swap_faces(faces, "comp")
    sent = side_planes_sent(cy)
    side_kind = pltpu.HBM((sent, cy, nz), F32)
    count = len(first_blocks)
    sum_one, total_one, *sides = call(
        lambda *refs: first_incident_kernel(count, *refs),
        (px, *first_blocks, right, *fields, layer_mask),
        [(32, point_count), (16, KC), side_kind, side_kind],
        [
            (AHEAD, KC, KC), (2, SIDE_PLANES, cy, nz),
            pltpu.SemaphoreType.DMA((2, len(FIELD_PLAN) - 1)), pltpu.SemaphoreType.DMA((2,)),
        ],
        scalars=1,
        left_in_hbm=tuple(range(count + 2, count + 5)),
        from_hbm=(count + 5,),
        raw=2,
    )
    sides = call(
        corner_kernel,
        (px, py, ye, yo, *sides),
        [side_kind, side_kind],
        [(2, sent - SIDE_PLANES, cy, nz), pltpu.SemaphoreType.DMA((2,))],
        scalars=2,
        left_in_hbm=(4, 5),
        raw=2,
        aliases={4: 0, 5: 1},
    )
    xe, xo = swap_faces(sides, "slab")
    (packed,) = call(
        lambda *refs: last_incident_kernel(len(last_blocks), comp_count, *refs),
        (
            *last_blocks, sum_one, total_one, right,
            point_owner.reshape(1, point_count), cell_offset.reshape(1, point_count),
        ),
        [(device_count, 1, LIST_ROWS * 2 * HALF)],
        [(32, point_count), (AHEAD, KC, KC)],
        from_hbm=tuple(len(last_blocks) + k for k in (3, 4)),
    )
    arrived = lax.all_to_all(packed, ("slab", "comp"), split_axis=0, concat_axis=0, tiled=True)
    free_final, free_prior, wide_coef, wide_sign = call(
        first_wave_kernel,
        (px, py, *fields, layer_mask, ye, yo, xe, xo),
        [current_field.shape, current_field.shape, plane_stack(cx + 2 * NEAR), (cx + 2 * MID, cy, nz)],
        [
            plane_stack(3, cx + 2 * DEEP), plane_stack(3, cx + 2 * MID), plane_stack(cx + 2 * MID),
            plane_stack(3, cx + 2 * MID), plane_stack(3, cx + 2 * NEAR),
        ],
        scalars=2,
        from_hbm=(2, 3, 4, 5),
        to_hbm=True,
    )
    held = (device_count // 2 * ROWS_HELD, 2 * HALF)
    zero, one, face_even, face_odd = call(
        near_scatter_kernel,
        (py, arrived, wide_sign),
        [(3, cx + 2 * NEAR, cy, nz), (3, cx, cy, nz)] + [(3, cx, TILE, nz)] * 2,
        [(3, (cx + 2 * NEAR) * cy, nz), (3, cx * cy, nz), held, held],
        scalars=1,
        from_hbm=(2,),
    )
    fye, fyo = swap_faces((face_even, face_odd), "comp")
    zero_far, one_side, two = call(
        rest_scatter_kernel,
        (arrived, wide_sign),
        [(3, 2 * NEAR, cy, nz), (3, 2 * NEAR, cy, nz), (3, cx, cy, nz)],
        [(3, 2 * NEAR * cy, nz), (3, 2 * NEAR * cy, nz), (3, cx * cy, nz), held, held],
        from_hbm=(1,),
    )
    final, prior = call(
        last_wave_kernel,
        (px, py, free_final, free_prior, wide_coef, zero, zero_far, one, one_side, two, fye, fyo),
        [current_field.shape, current_field.shape],
        [plane_stack(3, cx + 2 * MID), plane_stack(3, cx + 2 * NEAR)],
        scalars=2,
        from_hbm=(2, 3, 4),
    )
    return (final, prior)


def solution(mesh):
    in_specs = (
        P(None, "slab", "comp", None),
        P(None, "slab", "comp", None),
        P("slab", "comp", None),
        P("slab", "comp", None),
        P(None, ("slab", "comp")),
        P(("slab", "comp"), None),
        P(("slab", "comp")),
        P(None, "comp"),
        P("comp"),
        P(None, "comp"),
        P("comp"),
        P(),
    )
    out_specs = (P(None, "slab", "comp", None), P(None, "slab", "comp", None))
    return jax.shard_map(local, mesh=mesh, in_specs=in_specs, out_specs=out_specs, check_vma=False)
```

```python
import jax
import jax.numpy as jnp
from jax import lax
from jax.experimental import pallas as pl
from jax.experimental.pallas import tpu as pltpu
from jax.sharding import PartitionSpec as P

step_size = 0.05
near_weight = 4.0 / 3.0
far_weight = -1.0 / 12.0
centre_weight = -7.5
inv_two_pi = 0.15915494309189535

LEAD = -0.7713118195533752
SIN_C = (4.442834854125977 / LEAD, -7.306587219238281 / LEAD, 3.588636875152588 / LEAD)
SIN_SCALE = LEAD * abs(LEAD)
VER_SCALE = LEAD * LEAD
KC = 256
AHEAD = 2
HALF = 64
OWN_TILES = 5
SIDE_TILES = 4
HIGH_LIST = OWN_TILES
LOW_LIST = OWN_TILES + SIDE_TILES
LIST_ROWS = OWN_TILES + 2 * SIDE_TILES
VMEM_GRANT = 16 * 2**20

F32 = jnp.float32
BF16 = jnp.bfloat16


def sin_versine(u):
    r = u - jnp.round(u)
    z = r * r
    s = r * (((z + SIN_C[2]) * z + SIN_C[1]) * z + SIN_C[0])
    q = s * s
    w = 2.0 / VER_SCALE - q
    return s * (w * lax.rsqrt(w)), q


def split_three(x):
    hi = x.astype(BF16).astype(F32)
    rest = x - hi
    mid = rest.astype(BF16).astype(F32)
    return hi, mid, rest - mid


def row_ids(shape):
    return lax.broadcasted_iota(jnp.int32, shape, 0)


def add_components(par_refs, right_ref, acc_ref, u_ref):
    points = right_ref.shape[1]
    ahead, kc, tile = u_ref.shape
    rows8 = row_ids((8, kc))
    times = step_size * (rows8 + 1).astype(F32)
    rows16 = row_ids((16, kc))
    comp_row = jnp.where(rows16 < 6, rows16 % 3, (rows16 + 2) % 3)
    valued = (rows16 < 10) & (rows16 != 6)

    def block_of(par_ref, step):
        return par_ref[:, pl.ds(pl.multiple_of(step * kc, kc), kc)]

    def left_of(blk):
        khi, kmid, klo = split_three(jnp.where(rows8 < 3, blk * inv_two_pi, 0.0))
        return jnp.concatenate([khi, khi, khi, kmid, kmid, klo], axis=0).astype(BF16)

    def angles(left, t):
        cols = slice(t * tile, (t + 1) * tile)
        return lax.dot_general(left, right_ref[:, cols], (((0,), (0,)), ((), ())), preferred_element_type=F32)

    def body(par_ref, steps, step, total):
        blk = block_of(par_ref, step)
        left = left_of(blk)
        later = left_of(block_of(par_ref, jnp.minimum(step + 1, steps - 1)))
        delays = times * blk[3:4, :] - blk[7:8, :]
        sd, qd = sin_versine(delays * inv_two_pi)
        sd, cd = SIN_SCALE * sd, 1.0 - VER_SCALE * qd
        amp = jnp.where(comp_row == 0, blk[4:5, :], jnp.where(comp_row == 1, blk[5:6, :], blk[6:7, :]))
        amp = jnp.where(valued, amp, 0.0)

        def rows_of(t):
            w = amp * jnp.where(rows16 < 3, t[0:1, :], jnp.where(rows16 < 6, t[1:2, :], t[2:3, :]))
            hi = w.astype(BF16)
            lo = (w - hi.astype(F32)).astype(BF16)
            return w, jnp.concatenate([hi, lo], axis=0)

        wc = rows_of(cd)[0]
        lc = rows_of(-VER_SCALE * cd)[1]
        ls = rows_of(SIN_SCALE * sd)[1]

        def add_tile(t, u):
            highs, lows = [], []
            for j in range(kc // 32):
                for value in sin_versine(u[32 * j : 32 * j + 32]):
                    high = value.astype(BF16)
                    highs.append(high)
                    lows.append((value - high.astype(F32)).astype(BF16))
            part = jnp.dot(ls, jnp.concatenate(highs[0::2], axis=0), preferred_element_type=F32)
            part += jnp.dot(lc, jnp.concatenate(highs[1::2], axis=0), preferred_element_type=F32)
            part += jnp.dot(ls, jnp.concatenate(lows[0::2], axis=0), preferred_element_type=F32)
            part += jnp.dot(lc, jnp.concatenate(lows[1::2], axis=0), preferred_element_type=F32)
            acc_ref[:, t * tile : (t + 1) * tile] += part

        tiles = points // tile
        rest = {t: angles(left, t) for t in range(ahead, tiles)}
        for t in range(ahead):
            add_tile(t, u_ref[t])
        for t in range(ahead):
            u_ref[t] = angles(later, t)
        for t, u in rest.items():
            add_tile(t, u)
        return total + wc

    total = jnp.zeros((16, kc), F32)
    for par_ref in par_refs:
        steps = par_ref.shape[1] // kc
        left = left_of(block_of(par_ref, 0))
        for t in range(ahead):
            u_ref[t] = angles(left, t)
        total = lax.fori_loop(0, steps, lambda step, t, ref=par_ref, n=steps: body(ref, n, step, t), total)
    return total


def first_incident_kernel(count, ready, px_ref, *refs):
    par_refs, refs = refs[:count], refs[count:]
    right_ref, cur_ref, ear_ref, coef_ref, mask_ref, acc_ref, total_ref, even_out, odd_out, u_ref, face_ref = refs[:11]
    load_sems, store_sems = refs[11:]
    cx = mask_ref.shape[0]
    sources = [cur_ref.at[i] for i in range(3)] + [ear_ref.at[i] for i in range(3)] + [coef_ref]
    loads = []
    for face in (0, 1):
        for name, source in enumerate(sources):
            planes = FIELD_PLAN[name][0]
            first = sum(n for n, _ in FIELD_PLAN[:name])
            x = cx - planes if face == 0 else 0
            held = face_ref.at[face, pl.ds(first, planes)]
            loads.append(pltpu.make_async_copy(source.at[pl.ds(x, planes)], held, load_sems.at[face, name]))
    for copy in loads:
        copy.start()

    def stores(high_out, low_out):
        return [
            pltpu.make_async_copy(face_ref.at[face], out.at[pl.ds(0, SIDE_PLANES)], store_sems.at[face])
            for face, out in ((0, high_out), (1, low_out))
        ]

    def each_store(act):
        for parity, outs in ((0, (even_out, odd_out)), (1, (odd_out, even_out))):

            @pl.when(px_ref[0] == parity)
            def _():
                for copy in stores(*outs):
                    act(copy)

    acc_ref[...] = jnp.zeros(acc_ref.shape, F32)
    total = add_components(par_refs[:1], right_ref, acc_ref, u_ref)
    for copy in loads:
        copy.wait()
    ready()
    for face in (0, 1):
        for k in range(MID):
            x = cx - MID + k if face == 0 else k
            face_ref[face, SIDE_PLANES - MID + k] = sign_of(mask_ref[x])
    each_store(lambda copy: copy.start())
    total_ref[...] = total + add_components(par_refs[1:], right_ref, acc_ref, u_ref)
    each_store(lambda copy: copy.wait())


def last_incident_kernel(count, step, ready, *refs):
    par_refs, refs = refs[:count], refs[count:]
    first_ref, first_total_ref, right_ref, own_ref, off_ref, out_ref, acc_ref, u_ref = refs
    points = right_ref.shape[1]
    owners = out_ref.shape[0]
    acc_ref[...] = first_ref[...]
    total = add_components(par_refs, right_ref, acc_ref, u_ref) + first_total_ref[...]
    ready()
    vals = acc_ref[0:16, :] + acc_ref[16:32, :] + jnp.sum(total, axis=1, keepdims=True)
    vals = jnp.where(row_ids((16, points)) == 6, off_ref[...].astype(F32), vals)
    v1, v2, v3 = split_three(vals)
    named = own_ref[...] == row_ids((owners, points))
    named_one = named.astype(F32).astype(BF16)
    width = 128
    square = (width, width)
    earlier = (row_ids(square) < lax.broadcasted_iota(jnp.int32, square, 1)).astype(F32).astype(BF16)
    sums = jnp.concatenate([earlier, jnp.ones(square, BF16)], axis=1)
    before, past = [], jnp.zeros((owners, width), F32)
    for k in range(0, points, width):
        got = jnp.dot(named_one[:, k : k + width], sums, preferred_element_type=F32)
        before.append(got[:, 0:width] + past)
        past = past + got[:, width:]
    before = jnp.concatenate(before, axis=1)
    rank = jnp.sum(jnp.where(named, before, 0.0), axis=0, keepdims=True).astype(jnp.int32)
    terms = [v.astype(BF16) for v in (v1, v2, v3)]
    tiles = 0.0
    for odd in (0, 1):
        left = jnp.concatenate(
            [named_one * t[2 * j + odd : 2 * j + odd + 1, :] for t in terms for j in range(OWN_TILES)], axis=0
        )
        spots = (row_ids((2 * HALF, points)) == rank + odd * HALF).astype(F32).astype(BF16)
        got = lax.dot_general(left, spots, (((1,), (1,)), ((), ())), preferred_element_type=F32)
        size = OWN_TILES * owners
        tiles = tiles + (got[0:size] + got[size : 2 * size] + got[2 * size :])
    owner_row = row_ids((owners, 2 * HALF))

    def put(j, tile):
        out_ref[:, 0, 2 * HALF * j : 2 * HALF * (j + 1)] = tile

    for j in range(OWN_TILES):
        tile = tiles[j * owners : (j + 1) * owners]
        put(j, tile)
        if j < SIDE_TILES:
            above = pltpu.roll(tile, owners - step, 0)
            put(HIGH_LIST + j, jnp.where(owner_row < owners - step, above, 0.0))
            put(LOW_LIST + j, jnp.where(owner_row >= step, pltpu.roll(tile, step, 0), 0.0))


TILE = 8
DEEP = 6
MID = 4
NEAR = 2


def half_turn(tile):
    return pltpu.roll(tile, TILE // 2, 0)


ROWS_HELD = 16


def scatter_lists(val_ref, even_ref, odd_ref, jobs, cy, nz):
    lanes = 2 * HALF
    sources = val_ref.shape[0]
    groups = sources // 2
    chunk = 2 * lanes
    left_half = lax.broadcasted_iota(jnp.int32, (groups, lanes), 1) < lanes // 2
    for ref in {id(job[4]): job[4] for job in jobs}.values():
        ref[...] = jnp.zeros(ref.shape, F32)
    for j in range(LIST_ROWS):
        rows = val_ref[:, 0, lanes * j : lanes * (j + 1)]
        first, second = rows[0:groups], rows[groups:]
        at = pl.ds(j, groups, stride=ROWS_HELD)
        even_ref[at, :] = jnp.where(left_half, first, pltpu.roll(second, lanes // 2, 1))
        odd_ref[at, :] = jnp.where(left_half, pltpu.roll(first, lanes // 2, 1), second)

    def body(step, carry):
        evens, odds = [], []
        for pair in range(2):
            at = pl.ds(pl.multiple_of((2 * step + pair) * ROWS_HELD, ROWS_HELD), ROWS_HELD)
            evens.append(even_ref[at, :])
            odds.append(odd_ref[at, :])
        values = [jnp.concatenate(evens, axis=1), jnp.concatenate(odds, axis=1)]
        high = [v.astype(BF16) for v in values]
        low = [(v - h.astype(F32)).astype(BF16) for v, h in zip(values, high)]
        for base in (0, HIGH_LIST, LOW_LIST):
            own_jobs = [job for job in jobs if job[0] == base]
            off = values[0][base + 3 : base + 4, :].astype(jnp.int32)
            row = off // nz
            zt = (row_ids((nz, chunk)) == off - row * nz).astype(F32).astype(BF16)
            masks, left = {}, []
            for _, ranks, plane, planes, ref, start in own_jobs:
                if (plane, planes) not in masks:
                    ids = row_ids((planes * cy, chunk)) + plane * cy
                    masks[plane, planes] = (ids == row).astype(F32).astype(BF16)
                for r in ranks:
                    at = base + r // 2
                    left += [masks[plane, planes] * t[r % 2][at : at + 1, :] for t in (high, low)]
            left = jnp.concatenate(left, axis=0)
            got = lax.dot_general(left, zt, (((1,), (1,)), ((), ())), preferred_element_type=F32)
            at = 0
            for _, ranks, _, planes, ref, start in own_jobs:
                size = planes * cy
                for i in range(len(ranks)):
                    ref[i, start : start + size] += got[at : at + size] + got[at + size : at + 2 * size]
                    at += 2 * size
        return carry

    lax.fori_loop(0, groups // 2, body, 0, unroll=4)


STEP_ROWS = ((0, 1, 2), (3, 4, 5), (7, 8, 9))


def near_scatter_kernel(
    ready, par_ref, val_ref, sign_ref, zero_out, one_out, even_out, odd_out, zero_ref, one_ref, even_ref, odd_ref
):
    _, cx, cy, nz = one_out.shape
    jobs = (
        (0, STEP_ROWS[0], 0, cx, zero_ref, NEAR * cy),
        (0, STEP_ROWS[1], 0, cx, one_ref, 0),
        (HIGH_LIST, STEP_ROWS[0], 0, NEAR, zero_ref, (NEAR + cx) * cy),
        (LOW_LIST, STEP_ROWS[0], cx - NEAR, NEAR, zero_ref, 0),
    )
    scatter_lists(val_ref, even_ref, odd_ref, jobs, cy, nz)
    ready()
    sign = sign_ref[...]
    for i in range(3):
        zero_out[i] = zero_ref[i].reshape(zero_out.shape[1:]) * sign[MID - NEAR : MID + cx + NEAR]
        one_out[i] = one_ref[i].reshape(one_out.shape[1:]) * sign[MID : MID + cx]
    at = row_ids((TILE, nz))

    def write(is_high, face_ref):
        ys = slice(cy - TILE, cy) if is_high else slice(0, TILE)
        half = at >= TILE // 2 if is_high else at < TILE // 2
        corner = at < NEAR if is_high else at >= TILE - NEAR
        for i in range(3):
            for x in range(cx):
                tile = jnp.where(half, zero_out[i, NEAR + x, ys], half_turn(one_out[i, x, ys]))
                if x < 2 * NEAR:
                    moved = pltpu.roll(zero_out[i, NEAR + corner_plane(x, cx), ys], NEAR if is_high else TILE - NEAR, 0)
                    tile = jnp.where(corner, moved, tile)
                face_ref[i, x] = tile

    write_faces(par_ref[0], write, even_out, odd_out)


def rest_scatter_kernel(
    ready, val_ref, sign_ref, zero_out, one_out, two_out, zero_ref, one_ref, two_ref, even_ref, odd_ref
):
    _, cx, cy, nz = two_out.shape
    jobs = (
        (0, STEP_ROWS[2], 0, cx, two_ref, 0),
        (HIGH_LIST, STEP_ROWS[0], NEAR, MID - NEAR, zero_ref, NEAR * cy),
        (LOW_LIST, STEP_ROWS[0], cx - MID, MID - NEAR, zero_ref, 0),
        (HIGH_LIST, STEP_ROWS[1], 0, NEAR, one_ref, NEAR * cy),
        (LOW_LIST, STEP_ROWS[1], cx - NEAR, NEAR, one_ref, 0),
    )
    scatter_lists(val_ref, even_ref, odd_ref, jobs, cy, nz)
    ready()
    sign = sign_ref[...]
    last = cx + 2 * MID
    far = jnp.concatenate([sign[0 : MID - NEAR], sign[last - (MID - NEAR) :]], axis=0)
    side = jnp.concatenate([sign[MID - NEAR : MID], sign[MID + cx : MID + cx + NEAR]], axis=0)
    for i in range(3):
        zero_out[i] = zero_ref[i].reshape(zero_out.shape[1:]) * far
        one_out[i] = one_ref[i].reshape(one_out.shape[1:]) * side
        two_out[i] = two_ref[i].reshape(two_out.shape[1:]) * sign[MID : MID + cx]


def corner_plane(x, cx):
    return x - NEAR if x < NEAR else cx + x - NEAR


def write_faces(parity, write, even_out, odd_out):
    @pl.when(parity == 0)
    def _():
        write(True, even_out)
        write(False, odd_out)

    @pl.when(parity != 0)
    def _():
        write(False, even_out)
        write(True, odd_out)


def pair_list(count, odd):
    first = 1 if odd else 0
    pairs = [(i, i + 1) for i in range(first, count - 1, 2)]
    return pairs + [(j, i) for i, j in pairs]


def swap_faces(faces, axis):
    count = lax.axis_size(axis)
    out = []
    for k in (0, 1):
        out.append(lax.ppermute(faces[k], axis, pair_list(count, k)))
    return out


def prepare_kernel(
    ready, par_ref, cur_ref, ear_ref, coef_ref, wave_ref, freq_ref, amp_ref, index_ref, table_ref, xyz_ref,
    block_out, right_out, even_out, odd_out, x8_ref,
):
    x8_ref[...] = jnp.zeros(x8_ref.shape, F32)
    ready()
    x8_ref[0:3, :] = xyz_ref[...]
    xhi, xmid, xlo = split_three(x8_ref[...])
    right_out[...] = jnp.concatenate([xhi, xmid, xlo, xhi, xmid, xhi], axis=0).astype(BF16)
    entries = table_ref.shape[1]
    comps = index_ref.shape[1]
    picked = (row_ids((entries, comps)) == index_ref[...]).astype(F32).astype(BF16)
    terms = jnp.concatenate(list(split_three(jnp.broadcast_to(table_ref[...], (TILE, entries)))), axis=0).astype(BF16)
    phase = jnp.dot(terms, picked, preferred_element_type=F32)
    block_out[0:3, :] = wave_ref[...]
    block_out[3:4, :] = freq_ref[...]
    block_out[4:7, :] = amp_ref[...]
    block_out[7:8, :] = phase[0:1] + phase[TILE : TILE + 1] + phase[2 * TILE : 2 * TILE + 1]
    _, cx, cy, nz = cur_ref.shape
    upper = row_ids((TILE, nz)) >= TILE // 2

    def write(high, face_ref):
        ys = slice(cy - TILE, cy) if high else slice(0, TILE)
        keep = upper if high else ~upper
        for x in range(cx):
            for i in range(3):
                face_ref[i, x] = cur_ref[i, x, ys]
            face_ref[3, x] = jnp.where(keep, ear_ref[0, x, ys], half_turn(ear_ref[1, x, ys]))
            face_ref[4, x] = jnp.where(keep, ear_ref[2, x, ys], half_turn(coef_ref[x, ys]))

    write_faces(par_ref[0], write, even_out, odd_out)


def face_tile(ref, name, x):
    if name < 3:
        return ref[name, x]
    tile = ref[3 + (name - 3) // 2, x]
    return half_turn(tile) if name in (4, 6) else tile


def select_side(parity, even_ref, odd_ref, high):
    from_even = (parity == 0) if high else (parity == 1)

    def read(get):
        return jnp.where(from_even, get(even_ref), get(odd_ref))

    return read


FIELD_PLAN = [(DEEP, MID)] * 3 + [(MID, NEAR)] * 4 + [(MID, 0)]
SIDE_PLANES = sum(planes for planes, _ in FIELD_PLAN)
CORNERS = [(name, dist) for name, (_, corners) in enumerate(FIELD_PLAN) for dist in range(1, corners + 1)]


def side_plane(name, dist, is_high):
    planes = FIELD_PLAN[name][0]
    first = sum(n for n, _ in FIELD_PLAN[:name])
    return first + (dist - 1 if is_high else planes - dist)


def corner_place(k, cy):
    per_plane = cy // TILE
    start = k % per_plane * TILE
    return SIDE_PLANES + k // per_plane, slice(start, start + TILE)


def side_planes_sent(cy):
    return SIDE_PLANES + -(-len(CORNERS) // (cy // TILE))


def sign_of(mask):
    return (mask == 1).astype(F32) - (mask == 2).astype(F32)


def corner_kernel(
    px_ref, py_ref, even_ref, odd_ref, even_in, odd_in, even_out, odd_out, corner_ref, sems
):
    cx, nz = even_ref.shape[1], even_ref.shape[3]
    cy = corner_ref.shape[2]
    upper = row_ids((TILE, nz)) >= TILE // 2
    low = select_side(py_ref[0], even_ref, odd_ref, False)
    high = select_side(py_ref[0], even_ref, odd_ref, True)
    for face in (0, 1):
        for k, (name, dist) in enumerate(CORNERS):
            x = cx - dist if face == 0 else dist - 1
            below = low(lambda ref: face_tile(ref, name, x))
            above = high(lambda ref: face_tile(ref, name, x))
            plane, rows = corner_place(k, cy)
            corner_ref[face, plane - SIDE_PLANES, rows] = jnp.where(upper, below, above)
    rest = pl.ds(SIDE_PLANES, corner_ref.shape[1])

    def run(*outs):
        copies = [
            pltpu.make_async_copy(corner_ref.at[face], out.at[rest], sems.at[face]) for face, out in enumerate(outs)
        ]
        for copy in copies:
            copy.start()
        for copy in copies:
            copy.wait()

    @pl.when(px_ref[0] == 0)
    def _():
        run(even_out, odd_out)

    @pl.when(px_ref[0] != 0)
    def _():
        run(odd_out, even_out)


LANES = 128


def put_rows(ref, index, rows, value):
    for h in range(value.shape[1] // LANES):
        ref[(*index, h, rows)] = value[:, h * LANES : (h + 1) * LANES]


def laplacian_rows(ref, i, x, start, count):
    tiles = ref.shape[2]
    lane = lax.broadcasted_iota(jnp.int32, (count, LANES), 1)

    def rows(h, dx, dy):
        return ref[i, x + dx, h, pl.ds(start + dy, count)]

    centre = [rows(h, 0, 0) for h in range(tiles)]
    out = [centre_weight * c for c in centre]
    for k, weight in ((1, near_weight), (2, far_weight)):
        up = [pltpu.roll(c, k, 1) for c in centre]
        down = [pltpu.roll(c, LANES - k, 1) for c in centre]
        for h in range(tiles):
            below = jnp.where(lane >= k, up[h], up[h - 1] if h else 0.0)
            above = jnp.where(lane < LANES - k, down[h], down[h + 1] if h + 1 < tiles else 0.0)
            across = (rows(h, -k, 0) + rows(h, k, 0)) + (rows(h, 0, -k) + rows(h, 0, k))
            out[h] = out[h] + weight * (across + (below + above))
    return centre, out


def run_planes(first, last, body):
    lax.fori_loop(first, last, lambda x, carry: (body(x), carry)[1], 0, unroll=2)


def first_wave_kernel(
    ready, px_ref, py_ref, cur_ref, ear_ref, coef_ref, mask_ref, ye_ref, yo_ref, xe_ref, xo_ref,
    final_ref, prior_ref, wide_coef_ref, wide_sign_ref, u_ref, e_ref, c_ref, one_ref, two_ref,
):
    _, cx, cy, _ = cur_ref.shape
    own = slice(TILE, TILE + cy)
    lower, higher = slice(0, TILE), slice(TILE + cy, 2 * TILE + cy)
    low = select_side(py_ref[0], ye_ref, yo_ref, False)
    high = select_side(py_ref[0], ye_ref, yo_ref, True)
    ready()

    def put(name, x, rows, value):
        if name < 3:
            put_rows(u_ref, (name, DEEP + x), rows, value)
        elif name < 6:
            put_rows(e_ref, (name - 3, MID + x), rows, value)
        elif name == 6:
            put_rows(c_ref, (MID + x,), rows, value)
            if -NEAR <= x < cx + NEAR:
                put_rows(wide_coef_ref, (NEAR + x,), rows, value)
        else:
            wide_sign_ref[MID + x, slice(rows.start - TILE, rows.stop - TILE)] = value

    for x in range(cx):
        for name in range(7):
            value = cur_ref[name, x] if name < 3 else ear_ref[name - 3, x] if name < 6 else coef_ref[x]
            put(name, x, own, value)
            put(name, x, lower, low(lambda ref: face_tile(ref, name, x)))
            put(name, x, higher, high(lambda ref: face_tile(ref, name, x)))
        put(7, x, own, sign_of(mask_ref[x]))
    for is_high in (False, True):
        read = select_side(px_ref[0], xe_ref, xo_ref, is_high)
        for name, (planes, _) in enumerate(FIELD_PLAN):
            for dist in range(1, planes + 1):
                x = cx - 1 + dist if is_high else -dist
                put(name, x, own, read(lambda ref: ref[side_plane(name, dist, is_high)]))
        for k, (name, dist) in enumerate(CORNERS):
            x = cx - 1 + dist if is_high else -dist
            plane, rows = corner_place(k, cy)
            tile = read(lambda ref: ref[plane, rows])
            put(name, x, lower, tile)
            put(name, x, higher, tile)

    begin = px_ref[1]
    deep = cy + TILE

    def first(start, count):
        def body(x):
            for i in range(3):
                centre, lap = laplacian_rows(u_ref, i, x + DEEP - MID, start, count)
                for h, (c, l) in enumerate(zip(centre, lap)):
                    rows = pl.ds(start, count)
                    one_ref[i, x, h, rows] = 2.0 * c - e_ref[i, x, h, rows] + c_ref[x, h, rows] * l

        return body

    def second(start, count):
        def body(x):
            for i in range(3):
                centre, lap = laplacian_rows(one_ref, i, x + MID - NEAR, start, count)
                for h, (c, l) in enumerate(zip(centre, lap)):
                    rows = pl.ds(start, count)
                    moved = 2.0 * c - u_ref[i, x + DEEP - NEAR, h, rows]
                    two_ref[i, x, h, rows] = moved + c_ref[x + MID - NEAR, h, rows] * l

        return body

    def third(x):
        for i in range(3):
            centre, lap = laplacian_rows(two_ref, i, x + NEAR, TILE, cy)
            for h, (c, l) in enumerate(zip(centre, lap)):
                lanes = slice(h * LANES, (h + 1) * LANES)
                moved = 2.0 * c - one_ref[i, x + MID, h, own]
                final_ref[i, x, :, lanes] = moved + c_ref[x + MID, h, own] * l
                prior_ref[i, x, :, lanes] = c

    run_planes(0, NEAR, first(TILE, cy))
    run_planes(NEAR, cx + 2 * MID - NEAR, first(begin, deep))
    run_planes(cx + 2 * MID - NEAR, cx + 2 * MID, first(TILE, cy))
    run_planes(0, NEAR, second(TILE, cy))
    run_planes(NEAR, cx + NEAR, second(begin, deep))
    run_planes(cx + NEAR, cx + 2 * NEAR, second(TILE, cy))
    run_planes(0, cx, third)


def last_wave_kernel(
    ready, px_ref, py_ref, free_final_ref, free_prior_ref, coef_ref, zero_in, zero_far_in, one_in, one_side_in, two_in,
    ye_ref, yo_ref, final_out, prior_out, one_ref, two_ref, final_ref, prior_ref, sems,
):
    _, cx, cy, nz = two_in.shape
    own = slice(TILE, TILE + cy)
    lower, higher = slice(0, TILE), slice(TILE + cy, 2 * TILE + cy)
    low = select_side(py_ref[0], ye_ref, yo_ref, False)
    high = select_side(py_ref[0], ye_ref, yo_ref, True)
    for i in range(3):
        for x in range(cx + 2 * NEAR):
            put_rows(one_ref, (i, x + MID - NEAR), own, zero_in[i, x])
        for k in range(NEAR):
            put_rows(one_ref, (i, k), own, zero_far_in[i, k])
            put_rows(one_ref, (i, cx + 2 * MID - NEAR + k), own, zero_far_in[i, NEAR + k])
            put_rows(two_ref, (i, k), own, one_side_in[i, k])
            put_rows(two_ref, (i, cx + NEAR + k), own, one_side_in[i, NEAR + k])
        for x in range(cx):
            put_rows(two_ref, (i, NEAR + x), own, one_in[i, x])
            for rows, read, turn in ((lower, low, TILE - NEAR), (higher, high, NEAR)):
                tile = read(lambda ref: ref[i, x])
                put_rows(one_ref, (i, MID + x), rows, tile)
                put_rows(two_ref, (i, NEAR + x), rows, half_turn(tile))
                if x < 2 * NEAR:
                    put_rows(one_ref, (i, MID + corner_plane(x, cx)), rows, pltpu.roll(tile, turn, 0))

    def second(start, count):
        def body(x):
            for i in range(3):
                centre, lap = laplacian_rows(one_ref, i, x + MID - NEAR, start, count)
                for h, (c, l) in enumerate(zip(centre, lap)):
                    rows = pl.ds(start, count)
                    two_ref[i, x, h, rows] = 2.0 * c + coef_ref[x, h, rows] * l + two_ref[i, x, h, rows]

        return body

    def third(x):
        for i in range(3):
            centre, lap = laplacian_rows(two_ref, i, x + NEAR, TILE, cy)
            for h, (c, l) in enumerate(zip(centre, lap)):
                lanes = slice(h * LANES, (h + 1) * LANES)
                moved = 2.0 * c - one_ref[i, x + MID, h, own] + coef_ref[x + NEAR, h, own] * l
                final_ref[i, x, :, lanes] = free_final_ref[i, x, :, lanes] + (moved + two_in[i, x, :, lanes])

    def keep(x):
        for i in range(3):
            for h in range(nz // LANES):
                lanes = slice(h * LANES, (h + 1) * LANES)
                prior_ref[i, x, :, lanes] = free_prior_ref[i, x, :, lanes] + two_ref[i, x + NEAR, h, own]

    ready()
    run_planes(0, NEAR, second(TILE, cy))
    run_planes(NEAR, cx + NEAR, second(px_ref[1], cy + TILE))
    run_planes(cx + NEAR, cx + 2 * NEAR, second(TILE, cy))
    run_planes(0, cx, keep)
    copies = [pltpu.make_async_copy(prior_ref, prior_out, sems.at[0])]
    copies[0].start()
    for part, (begin, end) in enumerate(((0, cx // 2), (cx // 2, cx))):
        run_planes(begin, end, third)
        planes = pl.ds(begin, end - begin)
        copy = pltpu.make_async_copy(final_ref.at[:, planes], final_out.at[:, planes], sems.at[1 + part])
        copy.start()
        copies.append(copy)
    for copy in copies:
        copy.wait()


def staged(kernel, positions, operand_count):
    def run(*refs):
        refs, stages, sems = refs[: -len(positions) - 1], refs[-len(positions) - 1 : -1], refs[-1]
        ins = list(refs[:operand_count])
        copies = []
        for k, (at, stage) in enumerate(zip(positions, stages)):
            copies.append(pltpu.make_async_copy(ins[at], stage, sems.at[k]))
            ins[at] = stage
        for copy in copies:
            copy.start()

        def ready():
            for copy in copies:
                copy.wait()

        kernel(ready, *ins, *refs[operand_count:])

    return run


def local(
    current_field,
    earlier_field,
    wave_coef,
    layer_mask,
    point_xyz,
    point_owner,
    cell_offset,
    wave_vector,
    frequency,
    amplitude,
    phase_index,
    phase_table,
):
    point_count = point_xyz.shape[1]
    slab_count = lax.axis_size("slab")
    comp_count = lax.axis_size("comp")
    device_count = slab_count * comp_count
    slot_count = max(2, 2 * point_count // device_count)
    _, cx, cy, nz = current_field.shape
    assert slot_count <= HALF and device_count % 8 == 0
    assert cx >= DEEP and cy >= 2 * TILE and cy % TILE == 0
    wide = cy + 2 * TILE
    assert nz % LANES == 0 and MID == 2 * NEAR

    def plane_stack(*lead):
        return (*lead, nz // LANES, wide, LANES)

    smem = pl.BlockSpec(memory_space=pltpu.SMEM)
    vmem = pl.BlockSpec(memory_space=pltpu.VMEM)

    def call(kernel, operands, shapes, scratch=(), scalars=0, from_hbm=(), left_in_hbm=(), to_hbm=False, raw=0, aliases=None):
        kind = pltpu.HBM if to_hbm else jax.ShapeDtypeStruct
        shapes = [kind(shape, F32) if isinstance(shape, tuple) else shape for shape in shapes]
        out_specs = [vmem] * (len(shapes) - raw) + [pl.BlockSpec(memory_space=pltpu.HBM)] * raw
        operands = list(operands)
        in_specs = [smem] * scalars + [vmem] * (len(operands) - scalars)
        scratch_shapes = [pltpu.VMEM(shape, F32) if isinstance(shape, tuple) else shape for shape in scratch]
        hbm = pl.BlockSpec(memory_space=pltpu.HBM)
        for at in left_in_hbm:
            operands[at] = pltpu.with_memory_space_constraint(operands[at], pltpu.HBM)
            in_specs[at] = hbm
        if from_hbm:
            for at in from_hbm:
                operands[at] = pltpu.with_memory_space_constraint(operands[at], pltpu.HBM)
                in_specs[at] = hbm
                scratch_shapes.append(pltpu.VMEM(operands[at].shape, operands[at].dtype))
            scratch_shapes.append(pltpu.SemaphoreType.DMA((len(from_hbm),)))
            kernel = staged(kernel, from_hbm, len(operands))
        return pl.pallas_call(
            kernel,
            out_shape=shapes,
            in_specs=in_specs,
            out_specs=out_specs,
            input_output_aliases=aliases or {},
            scratch_shapes=scratch_shapes,
            compiler_params=pltpu.CompilerParams(vmem_limit_bytes=VMEM_GRANT),
        )(*operands)

    px = jnp.stack([lax.axis_index("slab") % 2, TILE // 2]).astype(jnp.int32)
    py = (lax.axis_index("comp") % 2).astype(jnp.int32).reshape(1)
    fields = (current_field, earlier_field, wave_coef)
    local_comps = frequency.shape[0]
    own_block, right, *faces = call(
        prepare_kernel,
        (
            py, *fields, wave_vector, frequency.reshape(1, local_comps), amplitude,
            phase_index.reshape(1, local_comps), phase_table.reshape(1, -1), point_xyz,
        ),
        [(8, local_comps), jax.ShapeDtypeStruct((48, point_count), BF16)] + [(5, cx, TILE, nz)] * 2,
        [(8, point_count)],
        scalars=1,
        from_hbm=tuple(range(1, 10)),
    )
    if comp_count == 4:
        near_block = lax.ppermute(own_block, "comp", pair_list(4, 0))
        first_blocks = [own_block, near_block]
        ring = pair_list(4, 1) + [(0, 3), (3, 0)]
        far_block = lax.ppermute(jnp.concatenate(first_blocks, axis=1), "comp", ring)
        last_blocks = [far_block]
    else:
        first_blocks = [own_block]
        last_blocks = [
            lax.ppermute(own_block, "comp", [(i, (i + k) % comp_count) for i in range(comp_count)])
            for k in range(1, comp_count)
        ]
    ye, yo = swap_faces(faces, "comp")
    sent = side_planes_sent(cy)
    side_kind = pltpu.HBM((sent, cy, nz), F32)
    count = len(first_blocks)
    sum_one, total_one, *sides = call(
        lambda *refs: first_incident_kernel(count, *refs),
        (px, *first_blocks, right, *fields, layer_mask),
        [(32, point_count), (16, KC), side_kind, side_kind],
        [
            (AHEAD, KC, KC), (2, SIDE_PLANES, cy, nz),
            pltpu.SemaphoreType.DMA((2, len(FIELD_PLAN) - 1)), pltpu.SemaphoreType.DMA((2,)),
        ],
        scalars=1,
        left_in_hbm=tuple(range(count + 2, count + 5)),
        from_hbm=(count + 5,),
        raw=2,
    )
    sides = call(
        corner_kernel,
        (px, py, ye, yo, *sides),
        [side_kind, side_kind],
        [(2, sent - SIDE_PLANES, cy, nz), pltpu.SemaphoreType.DMA((2,))],
        scalars=2,
        left_in_hbm=(4, 5),
        raw=2,
        aliases={4: 0, 5: 1},
    )
    xe, xo = swap_faces(sides, "slab")
    (packed,) = call(
        lambda *refs: last_incident_kernel(len(last_blocks), comp_count, *refs),
        (
            *last_blocks, sum_one, total_one, right,
            point_owner.reshape(1, point_count), cell_offset.reshape(1, point_count),
        ),
        [(device_count, 1, LIST_ROWS * 2 * HALF)],
        [(32, point_count), (AHEAD, KC, KC)],
        from_hbm=tuple(len(last_blocks) + k for k in (3, 4)),
    )
    arrived = lax.all_to_all(packed, ("slab", "comp"), split_axis=0, concat_axis=0, tiled=True)
    free_final, free_prior, wide_coef, wide_sign = call(
        first_wave_kernel,
        (px, py, *fields, layer_mask, ye, yo, xe, xo),
        [current_field.shape, current_field.shape, plane_stack(cx + 2 * NEAR), (cx + 2 * MID, cy, nz)],
        [
            plane_stack(3, cx + 2 * DEEP), plane_stack(3, cx + 2 * MID), plane_stack(cx + 2 * MID),
            plane_stack(3, cx + 2 * MID), plane_stack(3, cx + 2 * NEAR),
        ],
        scalars=2,
        from_hbm=(2, 3, 4, 5),
        to_hbm=True,
    )
    held = (device_count // 2 * ROWS_HELD, 2 * HALF)
    zero, one, face_even, face_odd = call(
        near_scatter_kernel,
        (py, arrived, wide_sign),
        [(3, cx + 2 * NEAR, cy, nz), (3, cx, cy, nz)] + [(3, cx, TILE, nz)] * 2,
        [(3, (cx + 2 * NEAR) * cy, nz), (3, cx * cy, nz), held, held],
        scalars=1,
        from_hbm=(2,),
    )
    fye, fyo = swap_faces((face_even, face_odd), "comp")
    zero_far, one_side, two = call(
        rest_scatter_kernel,
        (arrived, wide_sign),
        [(3, 2 * NEAR, cy, nz), (3, 2 * NEAR, cy, nz), (3, cx, cy, nz)],
        [(3, 2 * NEAR * cy, nz), (3, 2 * NEAR * cy, nz), (3, cx * cy, nz), held, held],
        from_hbm=(1,),
    )
    final, prior = call(
        last_wave_kernel,
        (px, py, free_final, free_prior, wide_coef, zero, zero_far, one, one_side, two, fye, fyo),
        [current_field.shape, current_field.shape],
        [
            plane_stack(3, cx + 2 * MID), plane_stack(3, cx + 2 * NEAR),
            current_field.shape, current_field.shape, pltpu.SemaphoreType.DMA((3,)),
        ],
        scalars=2,
        from_hbm=(2, 3, 4),
        to_hbm=True,
        raw=2,
    )
    return (final, prior)


def solution(mesh):
    in_specs = (
        P(None, "slab", "comp", None),
        P(None, "slab", "comp", None),
        P("slab", "comp", None),
        P("slab", "comp", None),
        P(None, ("slab", "comp")),
        P(("slab", "comp"), None),
        P(("slab", "comp")),
        P(None, "comp"),
        P("comp"),
        P(None, "comp"),
        P("comp"),
        P(),
    )
    out_specs = (P(None, "slab", "comp", None), P(None, "slab", "comp", None))
    return jax.shard_map(local, mesh=mesh, in_specs=in_specs, out_specs=out_specs, check_vma=False)
```

```python
import jax
import jax.numpy as jnp
from jax import lax
from jax.experimental import pallas as pl
from jax.experimental.pallas import tpu as pltpu
from jax.sharding import PartitionSpec as P

step_size = 0.05
near_weight = 4.0 / 3.0
far_weight = -1.0 / 12.0
centre_weight = -7.5
inv_two_pi = 0.15915494309189535

LEAD = -0.7713118195533752
SIN_C = (4.442834854125977 / LEAD, -7.306587219238281 / LEAD, 3.588636875152588 / LEAD)
SIN_SCALE = LEAD * abs(LEAD)
VER_SCALE = LEAD * LEAD
KC = 256
AHEAD = 2
HALF = 64
OWN_TILES = 5
SIDE_TILES = 4
HIGH_LIST = OWN_TILES
LOW_LIST = OWN_TILES + SIDE_TILES
LIST_ROWS = OWN_TILES + 2 * SIDE_TILES
VMEM_GRANT = 16 * 2**20

F32 = jnp.float32
BF16 = jnp.bfloat16


def sin_versine(u):
    r = u - jnp.round(u)
    z = r * r
    s = r * (((z + SIN_C[2]) * z + SIN_C[1]) * z + SIN_C[0])
    q = s * s
    w = 2.0 / VER_SCALE - q
    return s * (w * lax.rsqrt(w)), q


def split_three(x):
    hi = x.astype(BF16).astype(F32)
    rest = x - hi
    mid = rest.astype(BF16).astype(F32)
    return hi, mid, rest - mid


def row_ids(shape):
    return lax.broadcasted_iota(jnp.int32, shape, 0)


def add_components(par_refs, right_ref, acc_ref, u_ref):
    points = right_ref.shape[1]
    ahead, kc, tile = u_ref.shape
    rows8 = row_ids((8, kc))
    times = step_size * (rows8 + 1).astype(F32)
    rows16 = row_ids((16, kc))
    comp_row = jnp.where(rows16 < 6, rows16 % 3, (rows16 + 2) % 3)
    valued = (rows16 < 10) & (rows16 != 6)

    def block_of(par_ref, step):
        return par_ref[:, pl.ds(pl.multiple_of(step * kc, kc), kc)]

    def left_of(blk):
        khi, kmid, klo = split_three(jnp.where(rows8 < 3, blk * inv_two_pi, 0.0))
        return jnp.concatenate([khi, khi, khi, kmid, kmid, klo], axis=0).astype(BF16)

    def angles(left, t):
        cols = slice(t * tile, (t + 1) * tile)
        return lax.dot_general(left, right_ref[:, cols], (((0,), (0,)), ((), ())), preferred_element_type=F32)

    def body(par_ref, steps, step, total):
        blk = block_of(par_ref, step)
        left = left_of(blk)
        later = left_of(block_of(par_ref, jnp.minimum(step + 1, steps - 1)))
        delays = times * blk[3:4, :] - blk[7:8, :]
        sd, qd = sin_versine(delays * inv_two_pi)
        sd, cd = SIN_SCALE * sd, 1.0 - VER_SCALE * qd
        amp = jnp.where(comp_row == 0, blk[4:5, :], jnp.where(comp_row == 1, blk[5:6, :], blk[6:7, :]))
        amp = jnp.where(valued, amp, 0.0)

        def rows_of(t):
            w = amp * jnp.where(rows16 < 3, t[0:1, :], jnp.where(rows16 < 6, t[1:2, :], t[2:3, :]))
            hi = w.astype(BF16)
            lo = (w - hi.astype(F32)).astype(BF16)
            return w, jnp.concatenate([hi, lo], axis=0)

        wc = rows_of(cd)[0]
        lc = rows_of(-VER_SCALE * cd)[1]
        ls = rows_of(SIN_SCALE * sd)[1]

        def add_tile(t, u):
            highs, lows = [], []
            for j in range(kc // 32):
                for value in sin_versine(u[32 * j : 32 * j + 32]):
                    high = value.astype(BF16)
                    highs.append(high)
                    lows.append((value - high.astype(F32)).astype(BF16))
            part = jnp.dot(ls, jnp.concatenate(highs[0::2], axis=0), preferred_element_type=F32)
            part += jnp.dot(lc, jnp.concatenate(highs[1::2], axis=0), preferred_element_type=F32)
            part += jnp.dot(ls, jnp.concatenate(lows[0::2], axis=0), preferred_element_type=F32)
            part += jnp.dot(lc, jnp.concatenate(lows[1::2], axis=0), preferred_element_type=F32)
            acc_ref[:, t * tile : (t + 1) * tile] += part

        tiles = points // tile
        rest = {t: angles(left, t) for t in range(ahead, tiles)}
        for t in range(ahead):
            add_tile(t, u_ref[t])
        for t in range(ahead):
            u_ref[t] = angles(later, t)
        for t, u in rest.items():
            add_tile(t, u)
        return total + wc

    total = jnp.zeros((16, kc), F32)
    for par_ref in par_refs:
        steps = par_ref.shape[1] // kc
        left = left_of(block_of(par_ref, 0))
        for t in range(ahead):
            u_ref[t] = angles(left, t)
        total = lax.fori_loop(0, steps, lambda step, t, ref=par_ref, n=steps: body(ref, n, step, t), total)
    return total


def first_incident_kernel(count, ready, px_ref, *refs):
    par_refs, refs = refs[:count], refs[count:]
    right_ref, cur_ref, ear_ref, coef_ref, mask_ref, acc_ref, total_ref, even_out, odd_out, u_ref, face_ref = refs[:11]
    load_sems, store_sems = refs[11:]
    cx = mask_ref.shape[0]
    sources = [cur_ref.at[i] for i in range(3)] + [ear_ref.at[i] for i in range(3)] + [coef_ref]
    loads = []
    for face in (0, 1):
        for name, source in enumerate(sources):
            planes = FIELD_PLAN[name][0]
            first = sum(n for n, _ in FIELD_PLAN[:name])
            x = cx - planes if face == 0 else 0
            held = face_ref.at[face, pl.ds(first, planes)]
            loads.append(pltpu.make_async_copy(source.at[pl.ds(x, planes)], held, load_sems.at[face, name]))
    for copy in loads:
        copy.start()

    def stores(high_out, low_out):
        return [
            pltpu.make_async_copy(face_ref.at[face], out.at[pl.ds(0, SIDE_PLANES)], store_sems.at[face])
            for face, out in ((0, high_out), (1, low_out))
        ]

    def each_store(act):
        for parity, outs in ((0, (even_out, odd_out)), (1, (odd_out, even_out))):

            @pl.when(px_ref[0] == parity)
            def _():
                for copy in stores(*outs):
                    act(copy)

    acc_ref[...] = jnp.zeros(acc_ref.shape, F32)
    total = add_components(par_refs[:1], right_ref, acc_ref, u_ref)
    for copy in loads:
        copy.wait()
    ready()
    for face in (0, 1):
        for k in range(MID):
            x = cx - MID + k if face == 0 else k
            face_ref[face, SIDE_PLANES - MID + k] = sign_of(mask_ref[x])
    each_store(lambda copy: copy.start())
    total_ref[...] = total + add_components(par_refs[1:], right_ref, acc_ref, u_ref)
    each_store(lambda copy: copy.wait())


def last_incident_kernel(count, step, ready, *refs):
    par_refs, refs = refs[:count], refs[count:]
    first_ref, first_total_ref, right_ref, own_ref, off_ref, out_ref, acc_ref, u_ref = refs
    points = right_ref.shape[1]
    owners = out_ref.shape[0]
    acc_ref[...] = first_ref[...]
    total = add_components(par_refs, right_ref, acc_ref, u_ref) + first_total_ref[...]
    ready()
    vals = acc_ref[0:16, :] + acc_ref[16:32, :] + jnp.sum(total, axis=1, keepdims=True)
    vals = jnp.where(row_ids((16, points)) == 6, off_ref[...].astype(F32), vals)
    v1, v2, v3 = split_three(vals)
    named = own_ref[...] == row_ids((owners, points))
    named_one = named.astype(F32).astype(BF16)
    width = 128
    square = (width, width)
    earlier = (row_ids(square) < lax.broadcasted_iota(jnp.int32, square, 1)).astype(F32).astype(BF16)
    sums = jnp.concatenate([earlier, jnp.ones(square, BF16)], axis=1)
    before, past = [], jnp.zeros((owners, width), F32)
    for k in range(0, points, width):
        got = jnp.dot(named_one[:, k : k + width], sums, preferred_element_type=F32)
        before.append(got[:, 0:width] + past)
        past = past + got[:, width:]
    before = jnp.concatenate(before, axis=1)
    rank = jnp.sum(jnp.where(named, before, 0.0), axis=0, keepdims=True).astype(jnp.int32)
    terms = [v.astype(BF16) for v in (v1, v2, v3)]
    tiles = 0.0
    for odd in (0, 1):
        left = jnp.concatenate(
            [named_one * t[2 * j + odd : 2 * j + odd + 1, :] for t in terms for j in range(OWN_TILES)], axis=0
        )
        spots = (row_ids((2 * HALF, points)) == rank + odd * HALF).astype(F32).astype(BF16)
        got = lax.dot_general(left, spots, (((1,), (1,)), ((), ())), preferred_element_type=F32)
        size = OWN_TILES * owners
        tiles = tiles + (got[0:size] + got[size : 2 * size] + got[2 * size :])
    owner_row = row_ids((owners, 2 * HALF))

    def put(j, tile):
        out_ref[:, 0, 2 * HALF * j : 2 * HALF * (j + 1)] = tile

    for j in range(OWN_TILES):
        tile = tiles[j * owners : (j + 1) * owners]
        put(j, tile)
        if j < SIDE_TILES:
            above = pltpu.roll(tile, owners - step, 0)
            put(HIGH_LIST + j, jnp.where(owner_row < owners - step, above, 0.0))
            put(LOW_LIST + j, jnp.where(owner_row >= step, pltpu.roll(tile, step, 0), 0.0))


TILE = 8
DEEP = 6
MID = 4
NEAR = 2


def half_turn(tile):
    return pltpu.roll(tile, TILE // 2, 0)


ROWS_HELD = 16


def scatter_lists(val_ref, even_ref, odd_ref, jobs, cy, nz):
    lanes = 2 * HALF
    sources = val_ref.shape[0]
    groups = sources // 2
    chunk = 2 * lanes
    left_half = lax.broadcasted_iota(jnp.int32, (groups, lanes), 1) < lanes // 2
    for ref in {id(job[4]): job[4] for job in jobs}.values():
        ref[...] = jnp.zeros(ref.shape, F32)
    for j in range(LIST_ROWS):
        rows = val_ref[:, 0, lanes * j : lanes * (j + 1)]
        first, second = rows[0:groups], rows[groups:]
        at = pl.ds(j, groups, stride=ROWS_HELD)
        even_ref[at, :] = jnp.where(left_half, first, pltpu.roll(second, lanes // 2, 1))
        odd_ref[at, :] = jnp.where(left_half, pltpu.roll(first, lanes // 2, 1), second)

    def body(step, carry):
        evens, odds = [], []
        for pair in range(2):
            at = pl.ds(pl.multiple_of((2 * step + pair) * ROWS_HELD, ROWS_HELD), ROWS_HELD)
            evens.append(even_ref[at, :])
            odds.append(odd_ref[at, :])
        values = [jnp.concatenate(evens, axis=1), jnp.concatenate(odds, axis=1)]
        high = [v.astype(BF16) for v in values]
        low = [(v - h.astype(F32)).astype(BF16) for v, h in zip(values, high)]
        for base in (0, HIGH_LIST, LOW_LIST):
            own_jobs = [job for job in jobs if job[0] == base]
            off = values[0][base + 3 : base + 4, :].astype(jnp.int32)
            row = off // nz
            zt = (row_ids((nz, chunk)) == off - row * nz).astype(F32).astype(BF16)
            masks, left = {}, []
            for _, ranks, plane, planes, ref, start in own_jobs:
                if (plane, planes) not in masks:
                    if plane is None:
                        ids = face_row_ids(planes, cy, chunk)
                    else:
                        ids = row_ids((planes * cy, chunk)) + plane * cy
                    masks[plane, planes] = (ids == row).astype(F32).astype(BF16)
                for r in ranks:
                    at = base + r // 2
                    left += [masks[plane, planes] * t[r % 2][at : at + 1, :] for t in (high, low)]
            left = jnp.concatenate(left, axis=0)
            got = lax.dot_general(left, zt, (((1,), (1,)), ((), ())), preferred_element_type=F32)
            at = 0
            for _, ranks, plane, planes, ref, start in own_jobs:
                size = planes * (TILE if plane is None else cy)
                for i in range(len(ranks)):
                    ref[i, start : start + size] += got[at : at + size] + got[at + size : at + 2 * size]
                    at += 2 * size
        return carry

    lax.fori_loop(0, groups // 2, body, 0, unroll=4)


STEP_ROWS = ((0, 1, 2), (3, 4, 5), (7, 8, 9))


def face_row_ids(planes, cy, width):
    rid = row_ids((planes * TILE, width))
    at = rid % TILE
    middle = TILE // 2
    y = jnp.where(at < middle, cy - middle + at, at - middle)
    used = (at >= middle - NEAR) & (at < middle + NEAR)
    return jnp.where(used, rid // TILE * cy + y, -1)


def near_scatter_kernel(
    ready, par_ref, val_ref, sign_ref, zero_out, even_out, odd_out, zero_ref, one_ref, even_ref, odd_ref
):
    _, planes, cy, nz = zero_out.shape
    cx = planes - 2 * NEAR
    jobs = (
        (0, STEP_ROWS[0], 0, cx, zero_ref, NEAR * cy),
        (0, STEP_ROWS[1], None, cx, one_ref, 0),
        (HIGH_LIST, STEP_ROWS[0], 0, NEAR, zero_ref, (NEAR + cx) * cy),
        (LOW_LIST, STEP_ROWS[0], cx - NEAR, NEAR, zero_ref, 0),
    )
    scatter_lists(val_ref, even_ref, odd_ref, jobs, cy, nz)
    ready()
    sign = sign_ref[...]
    for i in range(3):
        zero_out[i] = zero_ref[i].reshape(zero_out.shape[1:]) * sign[MID - NEAR : MID + cx + NEAR]
    at = row_ids((TILE, nz))

    def write(is_high, face_ref):
        ys = slice(cy - TILE, cy) if is_high else slice(0, TILE)
        half = at >= TILE // 2 if is_high else at < TILE // 2
        corner = at < NEAR if is_high else at >= TILE - NEAR
        for i in range(3):
            for x in range(cx):
                one = one_ref[i, x * TILE : (x + 1) * TILE] * half_turn(sign_ref[MID + x, ys])
                tile = jnp.where(half, zero_out[i, NEAR + x, ys], one)
                if x < 2 * NEAR:
                    moved = pltpu.roll(zero_out[i, NEAR + corner_plane(x, cx), ys], NEAR if is_high else TILE - NEAR, 0)
                    tile = jnp.where(corner, moved, tile)
                face_ref[i, x] = tile

    write_faces(par_ref[0], write, even_out, odd_out)


def rest_scatter_kernel(
    ready, val_ref, sign_ref, zero_out, one_out, side_out, two_out,
    zero_ref, one_ref, side_ref, two_ref, even_ref, odd_ref,
):
    _, cx, cy, nz = two_out.shape
    jobs = (
        (0, STEP_ROWS[1], 0, cx, one_ref, 0),
        (0, STEP_ROWS[2], 0, cx, two_ref, 0),
        (HIGH_LIST, STEP_ROWS[0], NEAR, MID - NEAR, zero_ref, NEAR * cy),
        (LOW_LIST, STEP_ROWS[0], cx - MID, MID - NEAR, zero_ref, 0),
        (HIGH_LIST, STEP_ROWS[1], 0, NEAR, side_ref, NEAR * cy),
        (LOW_LIST, STEP_ROWS[1], cx - NEAR, NEAR, side_ref, 0),
    )
    scatter_lists(val_ref, even_ref, odd_ref, jobs, cy, nz)
    ready()
    sign = sign_ref[...]
    last = cx + 2 * MID
    far = jnp.concatenate([sign[0 : MID - NEAR], sign[last - (MID - NEAR) :]], axis=0)
    side = jnp.concatenate([sign[MID - NEAR : MID], sign[MID + cx : MID + cx + NEAR]], axis=0)
    for i in range(3):
        zero_out[i] = zero_ref[i].reshape(zero_out.shape[1:]) * far
        one_out[i] = one_ref[i].reshape(one_out.shape[1:]) * sign[MID : MID + cx]
        side_out[i] = side_ref[i].reshape(side_out.shape[1:]) * side
        two_out[i] = two_ref[i].reshape(two_out.shape[1:]) * sign[MID : MID + cx]


def corner_plane(x, cx):
    return x - NEAR if x < NEAR else cx + x - NEAR


def write_faces(parity, write, even_out, odd_out):
    @pl.when(parity == 0)
    def _():
        write(True, even_out)
        write(False, odd_out)

    @pl.when(parity != 0)
    def _():
        write(False, even_out)
        write(True, odd_out)


def pair_list(count, odd):
    first = 1 if odd else 0
    pairs = [(i, i + 1) for i in range(first, count - 1, 2)]
    return pairs + [(j, i) for i, j in pairs]


def swap_faces(faces, axis):
    count = lax.axis_size(axis)
    out = []
    for k in (0, 1):
        out.append(lax.ppermute(faces[k], axis, pair_list(count, k)))
    return out


def prepare_kernel(
    ready, par_ref, cur_ref, ear_ref, coef_ref, wave_ref, freq_ref, amp_ref, index_ref, table_ref, xyz_ref,
    block_out, right_out, even_out, odd_out, x8_ref,
):
    x8_ref[...] = jnp.zeros(x8_ref.shape, F32)
    ready()
    x8_ref[0:3, :] = xyz_ref[...]
    xhi, xmid, xlo = split_three(x8_ref[...])
    right_out[...] = jnp.concatenate([xhi, xmid, xlo, xhi, xmid, xhi], axis=0).astype(BF16)
    entries = table_ref.shape[1]
    comps = index_ref.shape[1]
    picked = (row_ids((entries, comps)) == index_ref[...]).astype(F32).astype(BF16)
    terms = jnp.concatenate(list(split_three(jnp.broadcast_to(table_ref[...], (TILE, entries)))), axis=0).astype(BF16)
    phase = jnp.dot(terms, picked, preferred_element_type=F32)
    block_out[0:3, :] = wave_ref[...]
    block_out[3:4, :] = freq_ref[...]
    block_out[4:7, :] = amp_ref[...]
    block_out[7:8, :] = phase[0:1] + phase[TILE : TILE + 1] + phase[2 * TILE : 2 * TILE + 1]
    _, cx, cy, nz = cur_ref.shape
    upper = row_ids((TILE, nz)) >= TILE // 2

    def write(high, face_ref):
        ys = slice(cy - TILE, cy) if high else slice(0, TILE)
        keep = upper if high else ~upper
        for x in range(cx):
            for i in range(3):
                face_ref[i, x] = cur_ref[i, x, ys]
            face_ref[3, x] = jnp.where(keep, ear_ref[0, x, ys], half_turn(ear_ref[1, x, ys]))
            face_ref[4, x] = jnp.where(keep, ear_ref[2, x, ys], half_turn(coef_ref[x, ys]))

    write_faces(par_ref[0], write, even_out, odd_out)


def face_tile(ref, name, x):
    if name < 3:
        return ref[name, x]
    tile = ref[3 + (name - 3) // 2, x]
    return half_turn(tile) if name in (4, 6) else tile


def select_side(parity, even_ref, odd_ref, high):
    from_even = (parity == 0) if high else (parity == 1)

    def read(get):
        return jnp.where(from_even, get(even_ref), get(odd_ref))

    return read


FIELD_PLAN = [(DEEP, MID)] * 3 + [(MID, NEAR)] * 4 + [(MID, 0)]
SIDE_PLANES = sum(planes for planes, _ in FIELD_PLAN)
CORNERS = [(name, dist) for name, (_, corners) in enumerate(FIELD_PLAN) for dist in range(1, corners + 1)]


def side_plane(name, dist, is_high):
    planes = FIELD_PLAN[name][0]
    first = sum(n for n, _ in FIELD_PLAN[:name])
    return first + (dist - 1 if is_high else planes - dist)


def corner_place(k, cy):
    per_plane = cy // TILE
    start = k % per_plane * TILE
    return SIDE_PLANES + k // per_plane, slice(start, start + TILE)


def side_planes_sent(cy):
    return SIDE_PLANES + -(-len(CORNERS) // (cy // TILE))


def sign_of(mask):
    return (mask == 1).astype(F32) - (mask == 2).astype(F32)


def corner_kernel(
    px_ref, py_ref, even_ref, odd_ref, even_in, odd_in, even_out, odd_out, corner_ref, sems
):
    cx, nz = even_ref.shape[1], even_ref.shape[3]
    cy = corner_ref.shape[2]
    upper = row_ids((TILE, nz)) >= TILE // 2
    low = select_side(py_ref[0], even_ref, odd_ref, False)
    high = select_side(py_ref[0], even_ref, odd_ref, True)
    for face in (0, 1):
        for k, (name, dist) in enumerate(CORNERS):
            x = cx - dist if face == 0 else dist - 1
            below = low(lambda ref: face_tile(ref, name, x))
            above = high(lambda ref: face_tile(ref, name, x))
            plane, rows = corner_place(k, cy)
            corner_ref[face, plane - SIDE_PLANES, rows] = jnp.where(upper, below, above)
    rest = pl.ds(SIDE_PLANES, corner_ref.shape[1])

    def run(*outs):
        copies = [
            pltpu.make_async_copy(corner_ref.at[face], out.at[rest], sems.at[face]) for face, out in enumerate(outs)
        ]
        for copy in copies:
            copy.start()
        for copy in copies:
            copy.wait()

    @pl.when(px_ref[0] == 0)
    def _():
        run(even_out, odd_out)

    @pl.when(px_ref[0] != 0)
    def _():
        run(odd_out, even_out)


LANES = 128


def put_rows(ref, index, rows, value):
    for h in range(value.shape[1] // LANES):
        ref[(*index, h, rows)] = value[:, h * LANES : (h + 1) * LANES]


def laplacian_rows(ref, i, x, start, count):
    tiles = ref.shape[2]
    lane = lax.broadcasted_iota(jnp.int32, (count, LANES), 1)

    def rows(h, dx, dy):
        return ref[i, x + dx, h, pl.ds(start + dy, count)]

    centre = [rows(h, 0, 0) for h in range(tiles)]
    out = [centre_weight * c for c in centre]
    for k, weight in ((1, near_weight), (2, far_weight)):
        up = [pltpu.roll(c, k, 1) for c in centre]
        down = [pltpu.roll(c, LANES - k, 1) for c in centre]
        for h in range(tiles):
            below = jnp.where(lane >= k, up[h], up[h - 1] if h else 0.0)
            above = jnp.where(lane < LANES - k, down[h], down[h + 1] if h + 1 < tiles else 0.0)
            across = (rows(h, -k, 0) + rows(h, k, 0)) + (rows(h, 0, -k) + rows(h, 0, k))
            out[h] = out[h] + weight * (across + (below + above))
    return centre, out


def run_planes(first, last, body):
    lax.fori_loop(first, last, lambda x, carry: (body(x), carry)[1], 0, unroll=2)


def first_wave_kernel(
    ready, px_ref, py_ref, cur_ref, ear_ref, coef_ref, mask_ref, ye_ref, yo_ref, xe_ref, xo_ref,
    final_ref, prior_ref, wide_coef_ref, wide_sign_ref, u_ref, e_ref, c_ref, one_ref, two_ref,
):
    _, cx, cy, _ = cur_ref.shape
    own = slice(TILE, TILE + cy)
    lower, higher = slice(0, TILE), slice(TILE + cy, 2 * TILE + cy)
    low = select_side(py_ref[0], ye_ref, yo_ref, False)
    high = select_side(py_ref[0], ye_ref, yo_ref, True)
    ready()

    def put(name, x, rows, value):
        if name < 3:
            put_rows(u_ref, (name, DEEP + x), rows, value)
        elif name < 6:
            put_rows(e_ref, (name - 3, MID + x), rows, value)
        elif name == 6:
            put_rows(c_ref, (MID + x,), rows, value)
            if -NEAR <= x < cx + NEAR:
                put_rows(wide_coef_ref, (NEAR + x,), rows, value)
        else:
            wide_sign_ref[MID + x, slice(rows.start - TILE, rows.stop - TILE)] = value

    for x in range(cx):
        for name in range(7):
            value = cur_ref[name, x] if name < 3 else ear_ref[name - 3, x] if name < 6 else coef_ref[x]
            put(name, x, own, value)
            put(name, x, lower, low(lambda ref: face_tile(ref, name, x)))
            put(name, x, higher, high(lambda ref: face_tile(ref, name, x)))
        put(7, x, own, sign_of(mask_ref[x]))
    for is_high in (False, True):
        read = select_side(px_ref[0], xe_ref, xo_ref, is_high)
        for name, (planes, _) in enumerate(FIELD_PLAN):
            for dist in range(1, planes + 1):
                x = cx - 1 + dist if is_high else -dist
                put(name, x, own, read(lambda ref: ref[side_plane(name, dist, is_high)]))
        for k, (name, dist) in enumerate(CORNERS):
            x = cx - 1 + dist if is_high else -dist
            plane, rows = corner_place(k, cy)
            tile = read(lambda ref: ref[plane, rows])
            put(name, x, lower, tile)
            put(name, x, higher, tile)

    begin = px_ref[1]
    deep = cy + TILE

    def first(start, count):
        def body(x):
            for i in range(3):
                centre, lap = laplacian_rows(u_ref, i, x + DEEP - MID, start, count)
                for h, (c, l) in enumerate(zip(centre, lap)):
                    rows = pl.ds(start, count)
                    one_ref[i, x, h, rows] = 2.0 * c - e_ref[i, x, h, rows] + c_ref[x, h, rows] * l

        return body

    def second(start, count):
        def body(x):
            for i in range(3):
                centre, lap = laplacian_rows(one_ref, i, x + MID - NEAR, start, count)
                for h, (c, l) in enumerate(zip(centre, lap)):
                    rows = pl.ds(start, count)
                    moved = 2.0 * c - u_ref[i, x + DEEP - NEAR, h, rows]
                    two_ref[i, x, h, rows] = moved + c_ref[x + MID - NEAR, h, rows] * l

        return body

    def third(x):
        for i in range(3):
            centre, lap = laplacian_rows(two_ref, i, x + NEAR, TILE, cy)
            for h, (c, l) in enumerate(zip(centre, lap)):
                lanes = slice(h * LANES, (h + 1) * LANES)
                moved = 2.0 * c - one_ref[i, x + MID, h, own]
                final_ref[i, x, :, lanes] = moved + c_ref[x + MID, h, own] * l
                prior_ref[i, x, :, lanes] = c

    run_planes(0, NEAR, first(TILE, cy))
    run_planes(NEAR, cx + 2 * MID - NEAR, first(begin, deep))
    run_planes(cx + 2 * MID - NEAR, cx + 2 * MID, first(TILE, cy))
    run_planes(0, NEAR, second(TILE, cy))
    run_planes(NEAR, cx + NEAR, second(begin, deep))
    run_planes(cx + NEAR, cx + 2 * NEAR, second(TILE, cy))
    run_planes(0, cx, third)


def last_wave_kernel(
    ready, px_ref, py_ref, free_final_ref, free_prior_ref, coef_ref, zero_in, zero_far_in, one_in, one_side_in, two_in,
    ye_ref, yo_ref, final_ref, prior_ref, one_ref, two_ref,
):
    _, cx, cy, _ = two_in.shape
    own = slice(TILE, TILE + cy)
    lower, higher = slice(0, TILE), slice(TILE + cy, 2 * TILE + cy)
    low = select_side(py_ref[0], ye_ref, yo_ref, False)
    high = select_side(py_ref[0], ye_ref, yo_ref, True)
    for i in range(3):
        for x in range(cx + 2 * NEAR):
            put_rows(one_ref, (i, x + MID - NEAR), own, zero_in[i, x])
        for k in range(NEAR):
            put_rows(one_ref, (i, k), own, zero_far_in[i, k])
            put_rows(one_ref, (i, cx + 2 * MID - NEAR + k), own, zero_far_in[i, NEAR + k])
            put_rows(two_ref, (i, k), own, one_side_in[i, k])
            put_rows(two_ref, (i, cx + NEAR + k), own, one_side_in[i, NEAR + k])
        for x in range(cx):
            put_rows(two_ref, (i, NEAR + x), own, one_in[i, x])
            for rows, read, turn in ((lower, low, TILE - NEAR), (higher, high, NEAR)):
                tile = read(lambda ref: ref[i, x])
                put_rows(one_ref, (i, MID + x), rows, tile)
                put_rows(two_ref, (i, NEAR + x), rows, half_turn(tile))
                if x < 2 * NEAR:
                    put_rows(one_ref, (i, MID + corner_plane(x, cx)), rows, pltpu.roll(tile, turn, 0))

    def second(start, count):
        def body(x):
            for i in range(3):
                centre, lap = laplacian_rows(one_ref, i, x + MID - NEAR, start, count)
                for h, (c, l) in enumerate(zip(centre, lap)):
                    rows = pl.ds(start, count)
                    two_ref[i, x, h, rows] = 2.0 * c + coef_ref[x, h, rows] * l + two_ref[i, x, h, rows]

        return body

    def third(x):
        for i in range(3):
            centre, lap = laplacian_rows(two_ref, i, x + NEAR, TILE, cy)
            for h, (c, l) in enumerate(zip(centre, lap)):
                lanes = slice(h * LANES, (h + 1) * LANES)
                moved = 2.0 * c - one_ref[i, x + MID, h, own] + coef_ref[x + NEAR, h, own] * l
                final_ref[i, x, :, lanes] = free_final_ref[i, x, :, lanes] + (moved + two_in[i, x, :, lanes])
                prior_ref[i, x, :, lanes] = free_prior_ref[i, x, :, lanes] + c

    ready()
    run_planes(0, NEAR, second(TILE, cy))
    run_planes(NEAR, cx + NEAR, second(px_ref[1], cy + TILE))
    run_planes(cx + NEAR, cx + 2 * NEAR, second(TILE, cy))
    run_planes(0, cx, third)


def staged(kernel, positions, operand_count):
    def run(*refs):
        refs, stages, sems = refs[: -len(positions) - 1], refs[-len(positions) - 1 : -1], refs[-1]
        ins = list(refs[:operand_count])
        copies = []
        for k, (at, stage) in enumerate(zip(positions, stages)):
            copies.append(pltpu.make_async_copy(ins[at], stage, sems.at[k]))
            ins[at] = stage
        for copy in copies:
            copy.start()

        def ready():
            for copy in copies:
                copy.wait()

        kernel(ready, *ins, *refs[operand_count:])

    return run


def local(
    current_field,
    earlier_field,
    wave_coef,
    layer_mask,
    point_xyz,
    point_owner,
    cell_offset,
    wave_vector,
    frequency,
    amplitude,
    phase_index,
    phase_table,
):
    point_count = point_xyz.shape[1]
    slab_count = lax.axis_size("slab")
    comp_count = lax.axis_size("comp")
    device_count = slab_count * comp_count
    slot_count = max(2, 2 * point_count // device_count)
    _, cx, cy, nz = current_field.shape
    assert slot_count <= HALF and device_count % 8 == 0
    assert cx >= DEEP and cy >= 2 * TILE and cy % TILE == 0
    wide = cy + 2 * TILE
    assert nz % LANES == 0 and MID == 2 * NEAR

    def plane_stack(*lead):
        return (*lead, nz // LANES, wide, LANES)

    smem = pl.BlockSpec(memory_space=pltpu.SMEM)
    vmem = pl.BlockSpec(memory_space=pltpu.VMEM)

    def call(kernel, operands, shapes, scratch=(), scalars=0, from_hbm=(), left_in_hbm=(), to_hbm=False, raw=0, aliases=None):
        kind = pltpu.HBM if to_hbm else jax.ShapeDtypeStruct
        shapes = [kind(shape, F32) if isinstance(shape, tuple) else shape for shape in shapes]
        out_specs = [vmem] * (len(shapes) - raw) + [pl.BlockSpec(memory_space=pltpu.HBM)] * raw
        operands = list(operands)
        in_specs = [smem] * scalars + [vmem] * (len(operands) - scalars)
        scratch_shapes = [pltpu.VMEM(shape, F32) if isinstance(shape, tuple) else shape for shape in scratch]
        hbm = pl.BlockSpec(memory_space=pltpu.HBM)
        for at in left_in_hbm:
            operands[at] = pltpu.with_memory_space_constraint(operands[at], pltpu.HBM)
            in_specs[at] = hbm
        if from_hbm:
            for at in from_hbm:
                operands[at] = pltpu.with_memory_space_constraint(operands[at], pltpu.HBM)
                in_specs[at] = hbm
                scratch_shapes.append(pltpu.VMEM(operands[at].shape, operands[at].dtype))
            scratch_shapes.append(pltpu.SemaphoreType.DMA((len(from_hbm),)))
            kernel = staged(kernel, from_hbm, len(operands))
        return pl.pallas_call(
            kernel,
            out_shape=shapes,
            in_specs=in_specs,
            out_specs=out_specs,
            input_output_aliases=aliases or {},
            scratch_shapes=scratch_shapes,
            compiler_params=pltpu.CompilerParams(vmem_limit_bytes=VMEM_GRANT),
        )(*operands)

    px = jnp.stack([lax.axis_index("slab") % 2, TILE // 2]).astype(jnp.int32)
    py = (lax.axis_index("comp") % 2).astype(jnp.int32).reshape(1)
    fields = (current_field, earlier_field, wave_coef)
    local_comps = frequency.shape[0]
    own_block, right, *faces = call(
        prepare_kernel,
        (
            py, *fields, wave_vector, frequency.reshape(1, local_comps), amplitude,
            phase_index.reshape(1, local_comps), phase_table.reshape(1, -1), point_xyz,
        ),
        [(8, local_comps), jax.ShapeDtypeStruct((48, point_count), BF16)] + [(5, cx, TILE, nz)] * 2,
        [(8, point_count)],
        scalars=1,
        from_hbm=tuple(range(1, 10)),
    )
    if comp_count == 4:
        near_block = lax.ppermute(own_block, "comp", pair_list(4, 0))
        first_blocks = [own_block, near_block]
        ring = pair_list(4, 1) + [(0, 3), (3, 0)]
        far_block = lax.ppermute(jnp.concatenate(first_blocks, axis=1), "comp", ring)
        last_blocks = [far_block]
    else:
        first_blocks = [own_block]
        last_blocks = [
            lax.ppermute(own_block, "comp", [(i, (i + k) % comp_count) for i in range(comp_count)])
            for k in range(1, comp_count)
        ]
    ye, yo = swap_faces(faces, "comp")
    sent = side_planes_sent(cy)
    side_kind = pltpu.HBM((sent, cy, nz), F32)
    count = len(first_blocks)
    sum_one, total_one, *sides = call(
        lambda *refs: first_incident_kernel(count, *refs),
        (px, *first_blocks, right, *fields, layer_mask),
        [(32, point_count), (16, KC), side_kind, side_kind],
        [
            (AHEAD, KC, KC), (2, SIDE_PLANES, cy, nz),
            pltpu.SemaphoreType.DMA((2, len(FIELD_PLAN) - 1)), pltpu.SemaphoreType.DMA((2,)),
        ],
        scalars=1,
        left_in_hbm=tuple(range(count + 2, count + 5)),
        from_hbm=(count + 5,),
        raw=2,
    )
    sides = call(
        corner_kernel,
        (px, py, ye, yo, *sides),
        [side_kind, side_kind],
        [(2, sent - SIDE_PLANES, cy, nz), pltpu.SemaphoreType.DMA((2,))],
        scalars=2,
        left_in_hbm=(4, 5),
        raw=2,
        aliases={4: 0, 5: 1},
    )
    xe, xo = swap_faces(sides, "slab")
    (packed,) = call(
        lambda *refs: last_incident_kernel(len(last_blocks), comp_count, *refs),
        (
            *last_blocks, sum_one, total_one, right,
            point_owner.reshape(1, point_count), cell_offset.reshape(1, point_count),
        ),
        [(device_count, 1, LIST_ROWS * 2 * HALF)],
        [(32, point_count), (AHEAD, KC, KC)],
        from_hbm=tuple(len(last_blocks) + k for k in (3, 4)),
    )
    arrived = lax.all_to_all(packed, ("slab", "comp"), split_axis=0, concat_axis=0, tiled=True)
    free_final, free_prior, wide_coef, wide_sign = call(
        first_wave_kernel,
        (px, py, *fields, layer_mask, ye, yo, xe, xo),
        [current_field.shape, current_field.shape, plane_stack(cx + 2 * NEAR), (cx + 2 * MID, cy, nz)],
        [
            plane_stack(3, cx + 2 * DEEP), plane_stack(3, cx + 2 * MID), plane_stack(cx + 2 * MID),
            plane_stack(3, cx + 2 * MID), plane_stack(3, cx + 2 * NEAR),
        ],
        scalars=2,
        from_hbm=(2, 3, 4, 5),
        to_hbm=True,
    )
    held = (device_count // 2 * ROWS_HELD, 2 * HALF)
    zero, face_even, face_odd = call(
        near_scatter_kernel,
        (py, arrived, wide_sign),
        [(3, cx + 2 * NEAR, cy, nz)] + [(3, cx, TILE, nz)] * 2,
        [(3, (cx + 2 * NEAR) * cy, nz), (3, cx * TILE, nz), held, held],
        scalars=1,
        from_hbm=(2,),
    )
    fye, fyo = swap_faces((face_even, face_odd), "comp")
    zero_far, one, one_side, two = call(
        rest_scatter_kernel,
        (arrived, wide_sign),
        [(3, 2 * NEAR, cy, nz), (3, cx, cy, nz), (3, 2 * NEAR, cy, nz), (3, cx, cy, nz)],
        [
            (3, 2 * NEAR * cy, nz), (3, cx * cy, nz), (3, 2 * NEAR * cy, nz), (3, cx * cy, nz),
            held, held,
        ],
        from_hbm=(1,),
    )
    final, prior = call(
        last_wave_kernel,
        (px, py, free_final, free_prior, wide_coef, zero, zero_far, one, one_side, two, fye, fyo),
        [current_field.shape, current_field.shape],
        [plane_stack(3, cx + 2 * MID), plane_stack(3, cx + 2 * NEAR)],
        scalars=2,
        from_hbm=(2, 3, 4),
    )
    return (final, prior)


def solution(mesh):
    in_specs = (
        P(None, "slab", "comp", None),
        P(None, "slab", "comp", None),
        P("slab", "comp", None),
        P("slab", "comp", None),
        P(None, ("slab", "comp")),
        P(("slab", "comp"), None),
        P(("slab", "comp")),
        P(None, "comp"),
        P("comp"),
        P(None, "comp"),
        P("comp"),
        P(),
    )
    out_specs = (P(None, "slab", "comp", None), P(None, "slab", "comp", None))
    return jax.shard_map(local, mesh=mesh, in_specs=in_specs, out_specs=out_specs, check_vma=False)
```

```python
import jax
import jax.numpy as jnp
from jax import lax
from jax.experimental import pallas as pl
from jax.experimental.pallas import tpu as pltpu
from jax.sharding import PartitionSpec as P

step_size = 0.05
near_weight = 4.0 / 3.0
far_weight = -1.0 / 12.0
centre_weight = -7.5
inv_two_pi = 0.15915494309189535

LEAD = -0.7713118195533752
SIN_C = (4.442834854125977 / LEAD, -7.306587219238281 / LEAD, 3.588636875152588 / LEAD)
SIN_SCALE = LEAD * abs(LEAD)
VER_SCALE = LEAD * LEAD
KC = 256
AHEAD = 2
HALF = 64
OWN_TILES = 5
SIDE_TILES = 3
OFFSET_TILE = 3
HIGH_LIST = OWN_TILES
LOW_LIST = OWN_TILES + SIDE_TILES
SIDE_OFFSETS = OWN_TILES + 2 * SIDE_TILES
LIST_ROWS = SIDE_OFFSETS + 1
VMEM_GRANT = 16 * 2**20

F32 = jnp.float32
BF16 = jnp.bfloat16


def sin_versine(u):
    r = u - jnp.round(u)
    z = r * r
    s = r * (((z + SIN_C[2]) * z + SIN_C[1]) * z + SIN_C[0])
    q = s * s
    w = 2.0 / VER_SCALE - q
    return s * (w * lax.rsqrt(w)), q


def split_three(x):
    hi = x.astype(BF16).astype(F32)
    rest = x - hi
    mid = rest.astype(BF16).astype(F32)
    return hi, mid, rest - mid


def row_ids(shape):
    return lax.broadcasted_iota(jnp.int32, shape, 0)


def add_components(par_refs, right_ref, acc_ref, u_ref):
    points = right_ref.shape[1]
    ahead, kc, tile = u_ref.shape
    rows8 = row_ids((8, kc))
    times = step_size * (rows8 + 1).astype(F32)
    rows16 = row_ids((16, kc))
    comp_row = jnp.where(rows16 < 6, rows16 % 3, (rows16 + 2) % 3)
    valued = (rows16 < 10) & (rows16 != 6)

    def block_of(par_ref, step):
        return par_ref[:, pl.ds(pl.multiple_of(step * kc, kc), kc)]

    def left_of(blk):
        khi, kmid, klo = split_three(jnp.where(rows8 < 3, blk * inv_two_pi, 0.0))
        return jnp.concatenate([khi, khi, khi, kmid, kmid, klo], axis=0).astype(BF16)

    def angles(left, t):
        cols = slice(t * tile, (t + 1) * tile)
        return lax.dot_general(left, right_ref[:, cols], (((0,), (0,)), ((), ())), preferred_element_type=F32)

    def body(par_ref, steps, step, total):
        blk = block_of(par_ref, step)
        left = left_of(blk)
        later = left_of(block_of(par_ref, jnp.minimum(step + 1, steps - 1)))
        delays = times * blk[3:4, :] - blk[7:8, :]
        sd, qd = sin_versine(delays * inv_two_pi)
        sd, cd = SIN_SCALE * sd, 1.0 - VER_SCALE * qd
        amp = jnp.where(comp_row == 0, blk[4:5, :], jnp.where(comp_row == 1, blk[5:6, :], blk[6:7, :]))
        amp = jnp.where(valued, amp, 0.0)

        def rows_of(t):
            w = amp * jnp.where(rows16 < 3, t[0:1, :], jnp.where(rows16 < 6, t[1:2, :], t[2:3, :]))
            hi = w.astype(BF16)
            lo = (w - hi.astype(F32)).astype(BF16)
            return w, jnp.concatenate([hi, lo], axis=0)

        wc = rows_of(cd)[0]
        lc = rows_of(-VER_SCALE * cd)[1]
        ls = rows_of(SIN_SCALE * sd)[1]

        def add_tile(t, u):
            highs, lows = [], []
            for j in range(kc // 32):
                for value in sin_versine(u[32 * j : 32 * j + 32]):
                    high = value.astype(BF16)
                    highs.append(high)
                    lows.append((value - high.astype(F32)).astype(BF16))
            part = jnp.dot(ls, jnp.concatenate(highs[0::2], axis=0), preferred_element_type=F32)
            part += jnp.dot(lc, jnp.concatenate(highs[1::2], axis=0), preferred_element_type=F32)
            part += jnp.dot(ls, jnp.concatenate(lows[0::2], axis=0), preferred_element_type=F32)
            part += jnp.dot(lc, jnp.concatenate(lows[1::2], axis=0), preferred_element_type=F32)
            acc_ref[:, t * tile : (t + 1) * tile] += part

        tiles = points // tile
        rest = {t: angles(left, t) for t in range(ahead, tiles)}
        for t in range(ahead):
            add_tile(t, u_ref[t])
        for t in range(ahead):
            u_ref[t] = angles(later, t)
        for t, u in rest.items():
            add_tile(t, u)
        return total + wc

    total = jnp.zeros((16, kc), F32)
    for par_ref in par_refs:
        steps = par_ref.shape[1] // kc
        left = left_of(block_of(par_ref, 0))
        for t in range(ahead):
            u_ref[t] = angles(left, t)
        total = lax.fori_loop(0, steps, lambda step, t, ref=par_ref, n=steps: body(ref, n, step, t), total)
    return total


def first_incident_kernel(count, ready, px_ref, *refs):
    par_refs, refs = refs[:count], refs[count:]
    right_ref, cur_ref, ear_ref, coef_ref, mask_ref, acc_ref, total_ref, even_out, odd_out, u_ref, face_ref = refs[:11]
    load_sems, store_sems = refs[11:]
    cx = mask_ref.shape[0]
    sources = [cur_ref.at[i] for i in range(3)] + [ear_ref.at[i] for i in range(3)] + [coef_ref]
    loads = []
    for face in (0, 1):
        for name, source in enumerate(sources):
            planes = FIELD_PLAN[name][0]
            first = sum(n for n, _ in FIELD_PLAN[:name])
            x = cx - planes if face == 0 else 0
            held = face_ref.at[face, pl.ds(first, planes)]
            loads.append(pltpu.make_async_copy(source.at[pl.ds(x, planes)], held, load_sems.at[face, name]))
    for copy in loads:
        copy.start()

    def stores(high_out, low_out):
        return [
            pltpu.make_async_copy(face_ref.at[face], out.at[pl.ds(0, SIDE_PLANES)], store_sems.at[face])
            for face, out in ((0, high_out), (1, low_out))
        ]

    def each_store(act):
        for parity, outs in ((0, (even_out, odd_out)), (1, (odd_out, even_out))):

            @pl.when(px_ref[0] == parity)
            def _():
                for copy in stores(*outs):
                    act(copy)

    acc_ref[...] = jnp.zeros(acc_ref.shape, F32)
    total = add_components(par_refs[:1], right_ref, acc_ref, u_ref)
    for copy in loads:
        copy.wait()
    ready()
    for face in (0, 1):
        for k in range(MID):
            x = cx - MID + k if face == 0 else k
            face_ref[face, SIDE_PLANES - MID + k] = sign_of(mask_ref[x])
    each_store(lambda copy: copy.start())
    total_ref[...] = total + add_components(par_refs[1:], right_ref, acc_ref, u_ref)
    each_store(lambda copy: copy.wait())


def last_incident_kernel(count, step, ready, *refs):
    par_refs, refs = refs[:count], refs[count:]
    first_ref, first_total_ref, right_ref, own_ref, off_ref, out_ref, acc_ref, u_ref = refs
    points = right_ref.shape[1]
    owners = out_ref.shape[0]
    acc_ref[...] = first_ref[...]
    total = add_components(par_refs, right_ref, acc_ref, u_ref) + first_total_ref[...]
    ready()
    vals = acc_ref[0:16, :] + acc_ref[16:32, :] + jnp.sum(total, axis=1, keepdims=True)
    vals = jnp.where(row_ids((16, points)) == 6, off_ref[...].astype(F32), vals)
    v1, v2, v3 = split_three(vals)
    named = own_ref[...] == row_ids((owners, points))
    named_one = named.astype(F32).astype(BF16)
    width = 128
    square = (width, width)
    earlier = (row_ids(square) < lax.broadcasted_iota(jnp.int32, square, 1)).astype(F32).astype(BF16)
    sums = jnp.concatenate([earlier, jnp.ones(square, BF16)], axis=1)
    before, past = [], jnp.zeros((owners, width), F32)
    for k in range(0, points, width):
        got = jnp.dot(named_one[:, k : k + width], sums, preferred_element_type=F32)
        before.append(got[:, 0:width] + past)
        past = past + got[:, width:]
    before = jnp.concatenate(before, axis=1)
    rank = jnp.sum(jnp.where(named, before, 0.0), axis=0, keepdims=True).astype(jnp.int32)
    terms = [v.astype(BF16) for v in (v1, v2, v3)]
    tiles = 0.0
    for odd in (0, 1):
        left = jnp.concatenate(
            [named_one * t[2 * j + odd : 2 * j + odd + 1, :] for t in terms for j in range(OWN_TILES)], axis=0
        )
        spots = (row_ids((2 * HALF, points)) == rank + odd * HALF).astype(F32).astype(BF16)
        got = lax.dot_general(left, spots, (((1,), (1,)), ((), ())), preferred_element_type=F32)
        size = OWN_TILES * owners
        tiles = tiles + (got[0:size] + got[size : 2 * size] + got[2 * size :])
    owner_row = row_ids((owners, 2 * HALF))

    def put(j, tile):
        out_ref[:, 0, 2 * HALF * j : 2 * HALF * (j + 1)] = tile

    def shifted(tile):
        above = jnp.where(owner_row < owners - step, pltpu.roll(tile, owners - step, 0), 0.0)
        return above, jnp.where(owner_row >= step, pltpu.roll(tile, step, 0), 0.0)

    for j in range(OWN_TILES):
        tile = tiles[j * owners : (j + 1) * owners]
        put(j, tile)
        above, below = shifted(tile)
        if j < SIDE_TILES:
            put(HIGH_LIST + j, above)
            put(LOW_LIST + j, below)
        if j == OFFSET_TILE:
            first = lax.broadcasted_iota(jnp.int32, (owners, 2 * HALF), 1) < HALF
            put(SIDE_OFFSETS, jnp.where(first, above, pltpu.roll(below, HALF, 1)))


TILE = 8
DEEP = 6
MID = 4
NEAR = 2


def half_turn(tile):
    return pltpu.roll(tile, TILE // 2, 0)


ROWS_HELD = 16


def scatter_lists(val_ref, even_ref, odd_ref, jobs, cy, nz):
    lanes = 2 * HALF
    sources = val_ref.shape[0]
    groups = sources // 2
    chunk = 2 * lanes
    left_half = lax.broadcasted_iota(jnp.int32, (groups, lanes), 1) < lanes // 2
    for ref in {id(job[4]): job[4] for job in jobs}.values():
        ref[...] = jnp.zeros(ref.shape, F32)
    for j in range(LIST_ROWS):
        rows = val_ref[:, 0, lanes * j : lanes * (j + 1)]
        first, second = rows[0:groups], rows[groups:]
        at = pl.ds(j, groups, stride=ROWS_HELD)
        even_ref[at, :] = jnp.where(left_half, first, pltpu.roll(second, lanes // 2, 1))
        odd_ref[at, :] = jnp.where(left_half, pltpu.roll(first, lanes // 2, 1), second)

    def body(step, carry):
        evens, odds = [], []
        for pair in range(2):
            at = pl.ds(pl.multiple_of((2 * step + pair) * ROWS_HELD, ROWS_HELD), ROWS_HELD)
            evens.append(even_ref[at, :])
            odds.append(odd_ref[at, :])
        values = [jnp.concatenate(evens, axis=1), jnp.concatenate(odds, axis=1)]
        high = [v.astype(BF16) for v in values]
        low = [(v - h.astype(F32)).astype(BF16) for v, h in zip(values, high)]
        for base in (0, HIGH_LIST, LOW_LIST):
            own_jobs = [job for job in jobs if job[0] == base]
            at = OFFSET_TILE if base == 0 else SIDE_OFFSETS
            off = values[1 if base == LOW_LIST else 0][at : at + 1, :].astype(jnp.int32)
            row = off // nz
            zt = (row_ids((nz, chunk)) == off - row * nz).astype(F32).astype(BF16)
            masks, left = {}, []
            for _, ranks, plane, planes, ref, start in own_jobs:
                if (plane, planes) not in masks:
                    if plane is None:
                        ids = face_row_ids(planes, cy, chunk)
                    else:
                        ids = row_ids((planes * cy, chunk)) + plane * cy
                    masks[plane, planes] = (ids == row).astype(F32).astype(BF16)
                for r in ranks:
                    at = base + r // 2
                    left += [masks[plane, planes] * t[r % 2][at : at + 1, :] for t in (high, low)]
            left = jnp.concatenate(left, axis=0)
            got = lax.dot_general(left, zt, (((1,), (1,)), ((), ())), preferred_element_type=F32)
            at = 0
            for _, ranks, plane, planes, ref, start in own_jobs:
                size = planes * (TILE if plane is None else cy)
                for i in range(len(ranks)):
                    ref[i, start : start + size] += got[at : at + size] + got[at + size : at + 2 * size]
                    at += 2 * size
        return carry

    lax.fori_loop(0, groups // 2, body, 0, unroll=4)


STEP_ROWS = ((0, 1, 2), (3, 4, 5), (7, 8, 9))


def face_row_ids(planes, cy, width):
    rid = row_ids((planes * TILE, width))
    at = rid % TILE
    middle = TILE // 2
    y = jnp.where(at < middle, cy - middle + at, at - middle)
    used = (at >= middle - NEAR) & (at < middle + NEAR)
    return jnp.where(used, rid // TILE * cy + y, -1)


def near_scatter_kernel(
    ready, par_ref, val_ref, sign_ref, zero_out, even_out, odd_out, zero_ref, one_ref, even_ref, odd_ref
):
    _, planes, cy, nz = zero_out.shape
    cx = planes - 2 * NEAR
    jobs = (
        (0, STEP_ROWS[0], 0, cx, zero_ref, NEAR * cy),
        (0, STEP_ROWS[1], None, cx, one_ref, 0),
        (HIGH_LIST, STEP_ROWS[0], 0, NEAR, zero_ref, (NEAR + cx) * cy),
        (LOW_LIST, STEP_ROWS[0], cx - NEAR, NEAR, zero_ref, 0),
    )
    scatter_lists(val_ref, even_ref, odd_ref, jobs, cy, nz)
    ready()
    sign = sign_ref[...]
    for i in range(3):
        zero_out[i] = zero_ref[i].reshape(zero_out.shape[1:]) * sign[MID - NEAR : MID + cx + NEAR]
    at = row_ids((TILE, nz))

    def write(is_high, face_ref):
        ys = slice(cy - TILE, cy) if is_high else slice(0, TILE)
        half = at >= TILE // 2 if is_high else at < TILE // 2
        corner = at < NEAR if is_high else at >= TILE - NEAR
        for i in range(3):
            for x in range(cx):
                one = one_ref[i, x * TILE : (x + 1) * TILE] * half_turn(sign_ref[MID + x, ys])
                tile = jnp.where(half, zero_out[i, NEAR + x, ys], one)
                if x < 2 * NEAR:
                    moved = pltpu.roll(zero_out[i, NEAR + corner_plane(x, cx), ys], NEAR if is_high else TILE - NEAR, 0)
                    tile = jnp.where(corner, moved, tile)
                face_ref[i, x] = tile

    write_faces(par_ref[0], write, even_out, odd_out)


def rest_scatter_kernel(
    ready, val_ref, sign_ref, zero_out, one_out, side_out, two_out,
    zero_ref, one_ref, side_ref, two_ref, even_ref, odd_ref,
):
    _, cx, cy, nz = two_out.shape
    jobs = (
        (0, STEP_ROWS[1], 0, cx, one_ref, 0),
        (0, STEP_ROWS[2], 0, cx, two_ref, 0),
        (HIGH_LIST, STEP_ROWS[0], NEAR, MID - NEAR, zero_ref, NEAR * cy),
        (LOW_LIST, STEP_ROWS[0], cx - MID, MID - NEAR, zero_ref, 0),
        (HIGH_LIST, STEP_ROWS[1], 0, NEAR, side_ref, NEAR * cy),
        (LOW_LIST, STEP_ROWS[1], cx - NEAR, NEAR, side_ref, 0),
    )
    scatter_lists(val_ref, even_ref, odd_ref, jobs, cy, nz)
    ready()
    sign = sign_ref[...]
    last = cx + 2 * MID
    far = jnp.concatenate([sign[0 : MID - NEAR], sign[last - (MID - NEAR) :]], axis=0)
    side = jnp.concatenate([sign[MID - NEAR : MID], sign[MID + cx : MID + cx + NEAR]], axis=0)
    for i in range(3):
        zero_out[i] = zero_ref[i].reshape(zero_out.shape[1:]) * far
        one_out[i] = one_ref[i].reshape(one_out.shape[1:]) * sign[MID : MID + cx]
        side_out[i] = side_ref[i].reshape(side_out.shape[1:]) * side
        two_out[i] = two_ref[i].reshape(two_out.shape[1:]) * sign[MID : MID + cx]


def corner_plane(x, cx):
    return x - NEAR if x < NEAR else cx + x - NEAR


def write_faces(parity, write, even_out, odd_out):
    @pl.when(parity == 0)
    def _():
        write(True, even_out)
        write(False, odd_out)

    @pl.when(parity != 0)
    def _():
        write(False, even_out)
        write(True, odd_out)


def pair_list(count, odd):
    first = 1 if odd else 0
    pairs = [(i, i + 1) for i in range(first, count - 1, 2)]
    return pairs + [(j, i) for i, j in pairs]


def swap_faces(faces, axis):
    count = lax.axis_size(axis)
    out = []
    for k in (0, 1):
        out.append(lax.ppermute(faces[k], axis, pair_list(count, k)))
    return out


def prepare_kernel(
    ready, par_ref, cur_ref, ear_ref, coef_ref, wave_ref, freq_ref, amp_ref, index_ref, table_ref, xyz_ref,
    block_out, right_out, even_out, odd_out, x8_ref,
):
    x8_ref[...] = jnp.zeros(x8_ref.shape, F32)
    ready()
    x8_ref[0:3, :] = xyz_ref[...]
    xhi, xmid, xlo = split_three(x8_ref[...])
    right_out[...] = jnp.concatenate([xhi, xmid, xlo, xhi, xmid, xhi], axis=0).astype(BF16)
    entries = table_ref.shape[1]
    comps = index_ref.shape[1]
    picked = (row_ids((entries, comps)) == index_ref[...]).astype(F32).astype(BF16)
    terms = jnp.concatenate(list(split_three(jnp.broadcast_to(table_ref[...], (TILE, entries)))), axis=0).astype(BF16)
    phase = jnp.dot(terms, picked, preferred_element_type=F32)
    block_out[0:3, :] = wave_ref[...]
    block_out[3:4, :] = freq_ref[...]
    block_out[4:7, :] = amp_ref[...]
    block_out[7:8, :] = phase[0:1] + phase[TILE : TILE + 1] + phase[2 * TILE : 2 * TILE + 1]
    _, cx, cy, nz = cur_ref.shape
    upper = row_ids((TILE, nz)) >= TILE // 2

    def write(high, face_ref):
        ys = slice(cy - TILE, cy) if high else slice(0, TILE)
        keep = upper if high else ~upper
        for x in range(cx):
            for i in range(3):
                face_ref[i, x] = cur_ref[i, x, ys]
            face_ref[3, x] = jnp.where(keep, ear_ref[0, x, ys], half_turn(ear_ref[1, x, ys]))
            face_ref[4, x] = jnp.where(keep, ear_ref[2, x, ys], half_turn(coef_ref[x, ys]))

    write_faces(par_ref[0], write, even_out, odd_out)


def face_tile(ref, name, x):
    if name < 3:
        return ref[name, x]
    tile = ref[3 + (name - 3) // 2, x]
    return half_turn(tile) if name in (4, 6) else tile


def select_side(parity, even_ref, odd_ref, high):
    from_even = (parity == 0) if high else (parity == 1)

    def read(get):
        return jnp.where(from_even, get(even_ref), get(odd_ref))

    return read


FIELD_PLAN = [(DEEP, MID)] * 3 + [(MID, NEAR)] * 4 + [(MID, 0)]
SIDE_PLANES = sum(planes for planes, _ in FIELD_PLAN)
CORNERS = [(name, dist) for name, (_, corners) in enumerate(FIELD_PLAN) for dist in range(1, corners + 1)]


def side_plane(name, dist, is_high):
    planes = FIELD_PLAN[name][0]
    first = sum(n for n, _ in FIELD_PLAN[:name])
    return first + (dist - 1 if is_high else planes - dist)


def corner_place(k, cy):
    per_plane = cy // TILE
    start = k % per_plane * TILE
    return SIDE_PLANES + k // per_plane, slice(start, start + TILE)


def side_planes_sent(cy):
    return SIDE_PLANES + -(-len(CORNERS) // (cy // TILE))


def sign_of(mask):
    return (mask == 1).astype(F32) - (mask == 2).astype(F32)


def corner_kernel(
    px_ref, py_ref, even_ref, odd_ref, even_in, odd_in, even_out, odd_out, corner_ref, sems
):
    cx, nz = even_ref.shape[1], even_ref.shape[3]
    cy = corner_ref.shape[2]
    upper = row_ids((TILE, nz)) >= TILE // 2
    low = select_side(py_ref[0], even_ref, odd_ref, False)
    high = select_side(py_ref[0], even_ref, odd_ref, True)
    for face in (0, 1):
        for k, (name, dist) in enumerate(CORNERS):
            x = cx - dist if face == 0 else dist - 1
            below = low(lambda ref: face_tile(ref, name, x))
            above = high(lambda ref: face_tile(ref, name, x))
            plane, rows = corner_place(k, cy)
            corner_ref[face, plane - SIDE_PLANES, rows] = jnp.where(upper, below, above)
    rest = pl.ds(SIDE_PLANES, corner_ref.shape[1])

    def run(*outs):
        copies = [
            pltpu.make_async_copy(corner_ref.at[face], out.at[rest], sems.at[face]) for face, out in enumerate(outs)
        ]
        for copy in copies:
            copy.start()
        for copy in copies:
            copy.wait()

    @pl.when(px_ref[0] == 0)
    def _():
        run(even_out, odd_out)

    @pl.when(px_ref[0] != 0)
    def _():
        run(odd_out, even_out)


LANES = 128


def put_rows(ref, index, rows, value):
    for h in range(value.shape[1] // LANES):
        ref[(*index, h, rows)] = value[:, h * LANES : (h + 1) * LANES]


def laplacian_rows(ref, i, x, start, count):
    tiles = ref.shape[2]
    lane = lax.broadcasted_iota(jnp.int32, (count, LANES), 1)

    def rows(h, dx, dy):
        return ref[i, x + dx, h, pl.ds(start + dy, count)]

    centre = [rows(h, 0, 0) for h in range(tiles)]
    out = [centre_weight * c for c in centre]
    for k, weight in ((1, near_weight), (2, far_weight)):
        up = [pltpu.roll(c, k, 1) for c in centre]
        down = [pltpu.roll(c, LANES - k, 1) for c in centre]
        for h in range(tiles):
            below = jnp.where(lane >= k, up[h], up[h - 1] if h else 0.0)
            above = jnp.where(lane < LANES - k, down[h], down[h + 1] if h + 1 < tiles else 0.0)
            across = (rows(h, -k, 0) + rows(h, k, 0)) + (rows(h, 0, -k) + rows(h, 0, k))
            out[h] = out[h] + weight * (across + (below + above))
    return centre, out


def run_planes(first, last, body):
    lax.fori_loop(first, last, lambda x, carry: (body(x), carry)[1], 0, unroll=2)


def first_wave_kernel(
    ready, px_ref, py_ref, cur_ref, ear_ref, coef_ref, mask_ref, ye_ref, yo_ref, xe_ref, xo_ref,
    final_ref, prior_ref, wide_coef_ref, wide_sign_ref, u_ref, e_ref, c_ref, one_ref, two_ref,
):
    _, cx, cy, _ = cur_ref.shape
    own = slice(TILE, TILE + cy)
    lower, higher = slice(0, TILE), slice(TILE + cy, 2 * TILE + cy)
    low = select_side(py_ref[0], ye_ref, yo_ref, False)
    high = select_side(py_ref[0], ye_ref, yo_ref, True)
    ready()

    def put(name, x, rows, value):
        if name < 3:
            put_rows(u_ref, (name, DEEP + x), rows, value)
        elif name < 6:
            put_rows(e_ref, (name - 3, MID + x), rows, value)
        elif name == 6:
            put_rows(c_ref, (MID + x,), rows, value)
            if -NEAR <= x < cx + NEAR:
                put_rows(wide_coef_ref, (NEAR + x,), rows, value)
        else:
            wide_sign_ref[MID + x, slice(rows.start - TILE, rows.stop - TILE)] = value

    for x in range(cx):
        for name in range(7):
            value = cur_ref[name, x] if name < 3 else ear_ref[name - 3, x] if name < 6 else coef_ref[x]
            put(name, x, own, value)
            put(name, x, lower, low(lambda ref: face_tile(ref, name, x)))
            put(name, x, higher, high(lambda ref: face_tile(ref, name, x)))
        put(7, x, own, sign_of(mask_ref[x]))
    for is_high in (False, True):
        read = select_side(px_ref[0], xe_ref, xo_ref, is_high)
        for name, (planes, _) in enumerate(FIELD_PLAN):
            for dist in range(1, planes + 1):
                x = cx - 1 + dist if is_high else -dist
                put(name, x, own, read(lambda ref: ref[side_plane(name, dist, is_high)]))
        for k, (name, dist) in enumerate(CORNERS):
            x = cx - 1 + dist if is_high else -dist
            plane, rows = corner_place(k, cy)
            tile = read(lambda ref: ref[plane, rows])
            put(name, x, lower, tile)
            put(name, x, higher, tile)

    begin = px_ref[1]
    deep = cy + TILE

    def first(start, count):
        def body(x):
            for i in range(3):
                centre, lap = laplacian_rows(u_ref, i, x + DEEP - MID, start, count)
                for h, (c, l) in enumerate(zip(centre, lap)):
                    rows = pl.ds(start, count)
                    one_ref[i, x, h, rows] = 2.0 * c - e_ref[i, x, h, rows] + c_ref[x, h, rows] * l

        return body

    def second(start, count):
        def body(x):
            for i in range(3):
                centre, lap = laplacian_rows(one_ref, i, x + MID - NEAR, start, count)
                for h, (c, l) in enumerate(zip(centre, lap)):
                    rows = pl.ds(start, count)
                    moved = 2.0 * c - u_ref[i, x + DEEP - NEAR, h, rows]
                    two_ref[i, x, h, rows] = moved + c_ref[x + MID - NEAR, h, rows] * l

        return body

    def third(x):
        for i in range(3):
            centre, lap = laplacian_rows(two_ref, i, x + NEAR, TILE, cy)
            for h, (c, l) in enumerate(zip(centre, lap)):
                lanes = slice(h * LANES, (h + 1) * LANES)
                moved = 2.0 * c - one_ref[i, x + MID, h, own]
                final_ref[i, x, :, lanes] = moved + c_ref[x + MID, h, own] * l
                prior_ref[i, x, :, lanes] = c

    run_planes(0, NEAR, first(TILE, cy))
    run_planes(NEAR, cx + 2 * MID - NEAR, first(begin, deep))
    run_planes(cx + 2 * MID - NEAR, cx + 2 * MID, first(TILE, cy))
    run_planes(0, NEAR, second(TILE, cy))
    run_planes(NEAR, cx + NEAR, second(begin, deep))
    run_planes(cx + NEAR, cx + 2 * NEAR, second(TILE, cy))
    run_planes(0, cx, third)


def last_wave_kernel(
    ready, px_ref, py_ref, free_final_ref, free_prior_ref, coef_ref, zero_in, zero_far_in, one_in, one_side_in, two_in,
    ye_ref, yo_ref, final_ref, prior_ref, one_ref, two_ref,
):
    _, cx, cy, _ = two_in.shape
    own = slice(TILE, TILE + cy)
    lower, higher = slice(0, TILE), slice(TILE + cy, 2 * TILE + cy)
    low = select_side(py_ref[0], ye_ref, yo_ref, False)
    high = select_side(py_ref[0], ye_ref, yo_ref, True)
    for i in range(3):
        for x in range(cx + 2 * NEAR):
            put_rows(one_ref, (i, x + MID - NEAR), own, zero_in[i, x])
        for k in range(NEAR):
            put_rows(one_ref, (i, k), own, zero_far_in[i, k])
            put_rows(one_ref, (i, cx + 2 * MID - NEAR + k), own, zero_far_in[i, NEAR + k])
            put_rows(two_ref, (i, k), own, one_side_in[i, k])
            put_rows(two_ref, (i, cx + NEAR + k), own, one_side_in[i, NEAR + k])
        for x in range(cx):
            put_rows(two_ref, (i, NEAR + x), own, one_in[i, x])
            for rows, read, turn in ((lower, low, TILE - NEAR), (higher, high, NEAR)):
                tile = read(lambda ref: ref[i, x])
                put_rows(one_ref, (i, MID + x), rows, tile)
                put_rows(two_ref, (i, NEAR + x), rows, half_turn(tile))
                if x < 2 * NEAR:
                    put_rows(one_ref, (i, MID + corner_plane(x, cx)), rows, pltpu.roll(tile, turn, 0))

    def second(start, count):
        def body(x):
            for i in range(3):
                centre, lap = laplacian_rows(one_ref, i, x + MID - NEAR, start, count)
                for h, (c, l) in enumerate(zip(centre, lap)):
                    rows = pl.ds(start, count)
                    two_ref[i, x, h, rows] = 2.0 * c + coef_ref[x, h, rows] * l + two_ref[i, x, h, rows]

        return body

    def third(x):
        for i in range(3):
            centre, lap = laplacian_rows(two_ref, i, x + NEAR, TILE, cy)
            for h, (c, l) in enumerate(zip(centre, lap)):
                lanes = slice(h * LANES, (h + 1) * LANES)
                moved = 2.0 * c - one_ref[i, x + MID, h, own] + coef_ref[x + NEAR, h, own] * l
                final_ref[i, x, :, lanes] = free_final_ref[i, x, :, lanes] + (moved + two_in[i, x, :, lanes])
                prior_ref[i, x, :, lanes] = free_prior_ref[i, x, :, lanes] + c

    ready()
    run_planes(0, NEAR, second(TILE, cy))
    run_planes(NEAR, cx + NEAR, second(px_ref[1], cy + TILE))
    run_planes(cx + NEAR, cx + 2 * NEAR, second(TILE, cy))
    run_planes(0, cx, third)


def staged(kernel, positions, operand_count):
    def run(*refs):
        refs, stages, sems = refs[: -len(positions) - 1], refs[-len(positions) - 1 : -1], refs[-1]
        ins = list(refs[:operand_count])
        copies = []
        for k, (at, stage) in enumerate(zip(positions, stages)):
            copies.append(pltpu.make_async_copy(ins[at], stage, sems.at[k]))
            ins[at] = stage
        for copy in copies:
            copy.start()

        def ready():
            for copy in copies:
                copy.wait()

        kernel(ready, *ins, *refs[operand_count:])

    return run


def local(
    current_field,
    earlier_field,
    wave_coef,
    layer_mask,
    point_xyz,
    point_owner,
    cell_offset,
    wave_vector,
    frequency,
    amplitude,
    phase_index,
    phase_table,
):
    point_count = point_xyz.shape[1]
    slab_count = lax.axis_size("slab")
    comp_count = lax.axis_size("comp")
    device_count = slab_count * comp_count
    slot_count = max(2, 2 * point_count // device_count)
    _, cx, cy, nz = current_field.shape
    assert slot_count <= HALF and device_count % 8 == 0
    assert cx >= DEEP and cy >= 2 * TILE and cy % TILE == 0
    wide = cy + 2 * TILE
    assert nz % LANES == 0 and MID == 2 * NEAR

    def plane_stack(*lead):
        return (*lead, nz // LANES, wide, LANES)

    smem = pl.BlockSpec(memory_space=pltpu.SMEM)
    vmem = pl.BlockSpec(memory_space=pltpu.VMEM)

    def call(kernel, operands, shapes, scratch=(), scalars=0, from_hbm=(), left_in_hbm=(), to_hbm=False, raw=0, aliases=None):
        kind = pltpu.HBM if to_hbm else jax.ShapeDtypeStruct
        shapes = [kind(shape, F32) if isinstance(shape, tuple) else shape for shape in shapes]
        out_specs = [vmem] * (len(shapes) - raw) + [pl.BlockSpec(memory_space=pltpu.HBM)] * raw
        operands = list(operands)
        in_specs = [smem] * scalars + [vmem] * (len(operands) - scalars)
        scratch_shapes = [pltpu.VMEM(shape, F32) if isinstance(shape, tuple) else shape for shape in scratch]
        hbm = pl.BlockSpec(memory_space=pltpu.HBM)
        for at in left_in_hbm:
            operands[at] = pltpu.with_memory_space_constraint(operands[at], pltpu.HBM)
            in_specs[at] = hbm
        if from_hbm:
            for at in from_hbm:
                operands[at] = pltpu.with_memory_space_constraint(operands[at], pltpu.HBM)
                in_specs[at] = hbm
                scratch_shapes.append(pltpu.VMEM(operands[at].shape, operands[at].dtype))
            scratch_shapes.append(pltpu.SemaphoreType.DMA((len(from_hbm),)))
            kernel = staged(kernel, from_hbm, len(operands))
        return pl.pallas_call(
            kernel,
            out_shape=shapes,
            in_specs=in_specs,
            out_specs=out_specs,
            input_output_aliases=aliases or {},
            scratch_shapes=scratch_shapes,
            compiler_params=pltpu.CompilerParams(vmem_limit_bytes=VMEM_GRANT),
        )(*operands)

    px = jnp.stack([lax.axis_index("slab") % 2, TILE // 2]).astype(jnp.int32)
    py = (lax.axis_index("comp") % 2).astype(jnp.int32).reshape(1)
    fields = (current_field, earlier_field, wave_coef)
    local_comps = frequency.shape[0]
    own_block, right, *faces = call(
        prepare_kernel,
        (
            py, *fields, wave_vector, frequency.reshape(1, local_comps), amplitude,
            phase_index.reshape(1, local_comps), phase_table.reshape(1, -1), point_xyz,
        ),
        [(8, local_comps), jax.ShapeDtypeStruct((48, point_count), BF16)] + [(5, cx, TILE, nz)] * 2,
        [(8, point_count)],
        scalars=1,
        from_hbm=tuple(range(1, 10)),
    )
    if comp_count == 4:
        near_block = lax.ppermute(own_block, "comp", pair_list(4, 0))
        first_blocks = [own_block, near_block]
        ring = pair_list(4, 1) + [(0, 3), (3, 0)]
        far_block = lax.ppermute(jnp.concatenate(first_blocks, axis=1), "comp", ring)
        last_blocks = [far_block]
    else:
        first_blocks = [own_block]
        last_blocks = [
            lax.ppermute(own_block, "comp", [(i, (i + k) % comp_count) for i in range(comp_count)])
            for k in range(1, comp_count)
        ]
    ye, yo = swap_faces(faces, "comp")
    sent = side_planes_sent(cy)
    side_kind = pltpu.HBM((sent, cy, nz), F32)
    count = len(first_blocks)
    sum_one, total_one, *sides = call(
        lambda *refs: first_incident_kernel(count, *refs),
        (px, *first_blocks, right, *fields, layer_mask),
        [(32, point_count), (16, KC), side_kind, side_kind],
        [
            (AHEAD, KC, KC), (2, SIDE_PLANES, cy, nz),
            pltpu.SemaphoreType.DMA((2, len(FIELD_PLAN) - 1)), pltpu.SemaphoreType.DMA((2,)),
        ],
        scalars=1,
        left_in_hbm=tuple(range(count + 2, count + 5)),
        from_hbm=(count + 5,),
        raw=2,
    )
    sides = call(
        corner_kernel,
        (px, py, ye, yo, *sides),
        [side_kind, side_kind],
        [(2, sent - SIDE_PLANES, cy, nz), pltpu.SemaphoreType.DMA((2,))],
        scalars=2,
        left_in_hbm=(4, 5),
        raw=2,
        aliases={4: 0, 5: 1},
    )
    xe, xo = swap_faces(sides, "slab")
    (packed,) = call(
        lambda *refs: last_incident_kernel(len(last_blocks), comp_count, *refs),
        (
            *last_blocks, sum_one, total_one, right,
            point_owner.reshape(1, point_count), cell_offset.reshape(1, point_count),
        ),
        [(device_count, 1, LIST_ROWS * 2 * HALF)],
        [(32, point_count), (AHEAD, KC, KC)],
        from_hbm=tuple(len(last_blocks) + k for k in (3, 4)),
    )
    arrived = lax.all_to_all(packed, ("slab", "comp"), split_axis=0, concat_axis=0, tiled=True)
    free_final, free_prior, wide_coef, wide_sign = call(
        first_wave_kernel,
        (px, py, *fields, layer_mask, ye, yo, xe, xo),
        [current_field.shape, current_field.shape, plane_stack(cx + 2 * NEAR), (cx + 2 * MID, cy, nz)],
        [
            plane_stack(3, cx + 2 * DEEP), plane_stack(3, cx + 2 * MID), plane_stack(cx + 2 * MID),
            plane_stack(3, cx + 2 * MID), plane_stack(3, cx + 2 * NEAR),
        ],
        scalars=2,
        from_hbm=(2, 3, 4, 5),
        to_hbm=True,
    )
    held = (device_count // 2 * ROWS_HELD, 2 * HALF)
    zero, face_even, face_odd = call(
        near_scatter_kernel,
        (py, arrived, wide_sign),
        [(3, cx + 2 * NEAR, cy, nz)] + [(3, cx, TILE, nz)] * 2,
        [(3, (cx + 2 * NEAR) * cy, nz), (3, cx * TILE, nz), held, held],
        scalars=1,
        from_hbm=(2,),
    )
    fye, fyo = swap_faces((face_even, face_odd), "comp")
    zero_far, one, one_side, two = call(
        rest_scatter_kernel,
        (arrived, wide_sign),
        [(3, 2 * NEAR, cy, nz), (3, cx, cy, nz), (3, 2 * NEAR, cy, nz), (3, cx, cy, nz)],
        [
            (3, 2 * NEAR * cy, nz), (3, cx * cy, nz), (3, 2 * NEAR * cy, nz), (3, cx * cy, nz),
            held, held,
        ],
        from_hbm=(1,),
    )
    final, prior = call(
        last_wave_kernel,
        (px, py, free_final, free_prior, wide_coef, zero, zero_far, one, one_side, two, fye, fyo),
        [current_field.shape, current_field.shape],
        [plane_stack(3, cx + 2 * MID), plane_stack(3, cx + 2 * NEAR)],
        scalars=2,
        from_hbm=(2, 3, 4),
    )
    return (final, prior)


def solution(mesh):
    in_specs = (
        P(None, "slab", "comp", None),
        P(None, "slab", "comp", None),
        P("slab", "comp", None),
        P("slab", "comp", None),
        P(None, ("slab", "comp")),
        P(("slab", "comp"), None),
        P(("slab", "comp")),
        P(None, "comp"),
        P("comp"),
        P(None, "comp"),
        P("comp"),
        P(),
    )
    out_specs = (P(None, "slab", "comp", None), P(None, "slab", "comp", None))
    return jax.shard_map(local, mesh=mesh, in_specs=in_specs, out_specs=out_specs, check_vma=False)
```
